32 devices in a mesh: dp: 16 (over z, y, x), head: 2 (over core).
Axes of the slice: x: 2, y: 2, z: 4, core: 2. Of those that a mesh axis runs over, the one named last changes fastest.
Arguments:
- block_in: bfloat16 [4096, 2048], P('dp'), may hold values from -6 to 6
- out_grad: bfloat16 [4096, 2048], P('dp'), may hold values from -6 to 6
- attn_gain: float32 [2048], replicated, may hold values from 0.5 to 1.5
- mlp_gain: float32 [2048], replicated, may hold values from 0.5 to 1.5
- w_query: bfloat16 [2048, 2048], P(None, 'head'), may hold values from -0.25 to 0.25
- w_key: bfloat16 [2048, 2048], P(None, 'head'), may hold values from -0.125 to 0.125
- w_value: bfloat16 [2048, 2048], P(None, 'head'), may hold values from -0.125 to 0.125
- w_forget: bfloat16 [2048, 256], P(None, 'head'), may hold values from -0.125 to 0.125
- w_output: bfloat16 [2048, 2048], P(None, 'head'), may hold values from -0.375 to 0.375
- w_gate: bfloat16 [2048, 5632], P('dp', 'head'), may hold values from -0.125 to 0.125
- w_up: bfloat16 [2048, 5632], P('dp', 'head'), may hold values from -0.125 to 0.125
- w_down: bfloat16 [2048, 5632], P('dp', 'head'), may hold values from -0.15625 to 0.15625
- doc_starts: int32 [16, 3], P('dp'), may hold values from 1 to 255, as said below
Outputs:
- block_out: bfloat16 [4096, 2048], P('dp')
- block_in_grad: float32 [4096, 2048], P('dp')
- attn_gain_grad: float32 [2048], P('dp')
- mlp_gain_grad: float32 [2048], P('dp')
- w_query_grad: float32 [2048, 2048], P('dp', 'head')
- w_key_grad: float32 [2048, 2048], P('dp', 'head')
- w_value_grad: float32 [2048, 2048], P('dp', 'head')
- w_forget_grad: float32 [2048, 256], P('dp', 'head')
- w_output_grad: float32 [2048, 2048], P('dp', 'head')
- w_gate_grad: float32 [2048, 5632], P('dp', 'head')
- w_up_grad: float32 [2048, 5632], P('dp', 'head')
- w_down_grad: float32 [2048, 5632], P('dp', 'head')
The draws below stay inside these ranges and needn't reach their ends.
Inputs may be any that keep to these rules, and one draw needn't show every extreme that they name: `doc_starts`: each row holds 3 distinct positions in increasing order, from 1 to 255; position 0 always begins a document.
All inputs are finite; a program needn't handle non-finite values.
Results may differ from the reference program's by a relative error of at most 0.015.
Values may be sent and summed in bfloat16 or wider, within the bound.
No kernel may reach another device: no remote copies, remote signals or barrier semaphores. Data moves between devices by JAX's collectives and lax.ppermute only.
A program may use at most 256 MiB of HBM per device.

```python
import math
import jax
import jax.numpy as jnp
from jax import lax

D = 2048
H = 4
DK = 512
DV = 512
M = 64
FF = 5632
SEQ = 256
DOCS = 3
TOKENS = 4096
N_DP = 16


def draw_doc_starts(key, part):
    row_keys = jax.random.split(jax.random.fold_in(key, 1), N_DP)
    chosen_row = jax.random.randint(jax.random.fold_in(key, 2), (), 0, N_DP)

    def one_row(row_key):
        chosen = jax.random.permutation(row_key, SEQ - 1)[:DOCS] + 1
        return jnp.sort(chosen).astype(jnp.int32)

    def edge_row(row_key):
        inner = jax.random.permutation(row_key, SEQ - 3)[:DOCS - 2] + 2
        ends = jnp.array([1, SEQ - 1], dtype=jnp.int32)
        return jnp.sort(jnp.concatenate([ends, inner.astype(jnp.int32)])).astype(jnp.int32)
    drawn = jax.vmap(one_row)(row_keys)
    edged = jax.vmap(edge_row)(row_keys)
    rows = jnp.arange(N_DP, dtype=jnp.int32)
    return jnp.where((rows == chosen_row)[:, None], edged, drawn).astype(jnp.int32)


def shard_levels(rng, dims, pieces, smallest, top_value):
    loudness = 1.0
    for dim, shards_of in pieces:
        steps = jax.random.uniform(jax.random.fold_in(jax.random.fold_in(rng, 6), dim), (shards_of,), jnp.float32, smallest / len(pieces), top_value / len(pieces))
        loudness = loudness * jnp.repeat(jnp.exp(steps), dims[dim] // shards_of).reshape((-1,) + (1,) * (len(dims) - 1 - dim))
    return loudness


def normal_values(key, dims, width, most, cuts=(), kind=jnp.bfloat16):
    values = jax.random.normal(key, dims, jnp.float32) * width
    if len(cuts) > 0:
        values = shard_levels(key, dims, cuts, -0.22, 0.18) * values
    return jnp.clip(values, min=-most, max=most).astype(kind)


def setup_inputs(seed: int = 0) -> dict:
    key_list = jax.random.split(jax.random.key(seed), 14)
    block_in = normal_values(key_list[0], (TOKENS, D), 1.0, 6.0, ((0, 16),))
    out_grad = normal_values(key_list[1], (TOKENS, D), 1.0, 6.0, ((0, 16),))
    attn_gain = jnp.clip(1.0 + 0.1 * jax.random.normal(key_list[2], (D,), jnp.float32), 0.5, 1.5)
    mlp_gain = jnp.clip(1.0 + 0.1 * jax.random.normal(key_list[3], (D,), jnp.float32), 0.5, 1.5)
    w_query = normal_values(key_list[4], (D, H * DK), (D // 4) ** -0.5, 0.25, ((1, 2),))
    w_key = normal_values(key_list[5], (D, H * DK), D ** -0.5, 0.125, ((1, 2),))
    w_value = normal_values(key_list[6], (D, H * DV), D ** -0.5, 0.125, ((1, 2),))
    w_forget = normal_values(key_list[7], (D, H * M), D ** -0.5, 0.125, ((1, 2),))
    w_output = normal_values(key_list[8], (D, H * DV), (H * DV // 8) ** -0.5, 0.375, ((1, 2),))
    w_gate = normal_values(key_list[9], (D, FF), D ** -0.5, 0.125, ((0, 16), (1, 2)))
    w_up = normal_values(key_list[10], (D, FF), D ** -0.5, 0.125, ((0, 16), (1, 2)))
    w_down = normal_values(key_list[11], (D, FF), (FF // 4) ** -0.5, 0.15625, ((0, 16), (1, 2)))
    doc_starts = draw_doc_starts(jax.random.fold_in(key_list[13], 71), 0)
    return dict(block_in=block_in, out_grad=out_grad, attn_gain=attn_gain, mlp_gain=mlp_gain, w_query=w_query, w_key=w_key, w_value=w_value, w_forget=w_forget, w_output=w_output, w_gate=w_gate, w_up=w_up, w_down=w_down, doc_starts=doc_starts)


eps = 1e-06
tau_inv = 0.125
highest_precision = lax.Precision.HIGHEST

@jax.custom_vjp
def low(v):
    return lax.optimization_barrier(v.astype(jnp.bfloat16)).astype(jnp.float32)

@jax.custom_vjp
def low_back(v):
    return v

def low_keep(v):
    return (low(v), None)

def low_pass(kept, grad):
    return (grad,)

def back_keep(v):
    return (v, None)

def back_low(kept, grad):
    return (low(grad),)
low.defvjp(low_keep, low_pass)
low_back.defvjp(back_keep, back_low)

def rms_norm(values, gain):
    return values * lax.rsqrt(lax.optimization_barrier(jnp.mean(values * values, axis=-1, keepdims=True)) + eps) * gain

def project(left, right):
    return jnp.einsum('gtd,de->gte', left, right, precision=highest_precision)

def project_back(left, right):
    return jnp.einsum('gte,de->gtd', left, right, precision=highest_precision)

def token_step(state_pair, scan_item):
    slot_key_state, slot_value_state = state_pair
    query_now, key_now, value_now, log_now, keep_now = scan_item
    decay_now = jnp.exp(log_now)
    kept_now = decay_now * keep_now[:, None, None]
    written = 1.0 - decay_now
    slot_key_state = kept_now[..., None] * slot_key_state + written[..., None] * key_now[:, :, None, :]
    logit_scores = jnp.einsum('ghmd,ghd->ghm', slot_key_state, query_now, precision=highest_precision)
    weights_now = jax.nn.softmax(logit_scores, axis=-1)
    slot_value_state = kept_now[..., None] * slot_value_state + written[..., None] * value_now[:, :, None, :]
    block_output = jnp.einsum('ghm,ghmd->ghd', weights_now, slot_value_state, precision=highest_precision)
    return ((slot_key_state, slot_value_state), block_output)

def block_scan(state_pair, block_data):
    return lax.scan(token_step, state_pair, block_data)

def slot_attention(query_matrix, key_matrix, value_matrix, log_keep, keep_rows):
    groups = query_matrix.shape[0]
    head_count = query_matrix.shape[2]
    block_len = math.gcd(SEQ, 64)

    def arrange(values):
        time_major = jnp.moveaxis(values, 1, 0)
        return time_major.reshape((SEQ // block_len, block_len) + time_major.shape[1:])
    initial = (jnp.zeros((groups, head_count, M, DK), jnp.float32), jnp.zeros((groups, head_count, M, DV), jnp.float32))
    scaled = query_matrix * (1.0 / math.sqrt(DK))
    inputs = (arrange(scaled), arrange(key_matrix), arrange(value_matrix), arrange(log_keep), arrange(keep_rows))
    unused, outputs = lax.scan(jax.checkpoint(block_scan), initial, inputs)
    outputs = outputs.reshape((SEQ,) + outputs.shape[2:])
    return jnp.moveaxis(outputs, 0, 1)

def forward(block_in, attn_gain, mlp_gain, w_query, w_key, w_value, w_forget, w_output, w_gate, w_up, w_down, keep_rows):
    groups = block_in.shape[0]
    normed = low(rms_norm(block_in, attn_gain))
    query_matrix = low(jax.nn.silu(low_back(project(normed, w_query))))
    key_matrix = low(jax.nn.silu(low_back(project(normed, w_key))))
    value_matrix = low(jax.nn.silu(low_back(project(normed, w_value))))
    forget = low_back(project(normed, w_forget))
    log_keep = jax.nn.log_sigmoid(forget) * tau_inv
    mixed_heads = slot_attention(query_matrix.reshape(groups, SEQ, H, DK), key_matrix.reshape(groups, SEQ, H, DK), value_matrix.reshape(groups, SEQ, H, DV), log_keep.reshape(groups, SEQ, H, M), keep_rows)
    mixed_heads = low(mixed_heads.reshape(groups, SEQ, H * DV))
    branch = low_back(project_back(mixed_heads, w_output))
    hidden = block_in + branch
    normed_two = low(rms_norm(hidden, mlp_gain))
    gate_act = low_back(project(normed_two, w_gate))
    up_act = low_back(project(normed_two, w_up))
    inner_act = low(jax.nn.silu(gate_act) * up_act)
    return hidden + project_back(inner_act, w_down)

def reference(block_in, out_grad, attn_gain, mlp_gain, w_query, w_key, w_value, w_forget, w_output, w_gate, w_up, w_down, doc_starts):
    weights = tuple((weight.astype(jnp.float32) for weight in (attn_gain, mlp_gain, w_query, w_key, w_value, w_forget, w_output, w_gate, w_up, w_down)))
    row_count = N_DP
    group_size = math.gcd(row_count, 4)
    positions = jnp.arange(SEQ, dtype=jnp.int32)
    starts_here = jnp.any(doc_starts[:, :, None] == positions[None, None, :], axis=1)
    keep_all = 1.0 - starts_here.astype(jnp.float32)
    inputs = (block_in.astype(jnp.float32).reshape(row_count // group_size, group_size, SEQ, D), out_grad.astype(jnp.float32).reshape(row_count // group_size, group_size, SEQ, D), keep_all.reshape(row_count // group_size, group_size, SEQ))

    def group_step(totals, scan_item):
        rows_in, cotangent, keep_rows = scan_item

        def apply_block(rows_value, *params):
            return forward(rows_value, *params, keep_rows)
        result, pullback = jax.vjp(apply_block, rows_in, *weights)
        gradients = pullback(cotangent)
        totals = tuple((total + grad for total, grad in zip(totals, gradients[1:])))
        return (totals, (result, gradients[0]))
    initial = tuple((jnp.zeros_like(weight) for weight in weights))
    totals, (results, input_grads) = lax.scan(group_step, initial, inputs)
    return (results.reshape(TOKENS, D).astype(jnp.bfloat16), input_grads.reshape(TOKENS, D), totals[0], totals[1], totals[2], totals[3], totals[4], totals[5], totals[6], totals[7], totals[8], totals[9])
```

```python
import math
from functools import partial
import jax
import jax.numpy as jnp
from jax import lax
from jax.experimental import pallas as pl
from jax.experimental.pallas import tpu as pltpu
from jax.sharding import PartitionSpec as P

DK = 512
DV = 512
M = 64
B = 16
f32 = jnp.float32
bf16 = jnp.bfloat16


def nn(a, b):
    return jnp.dot(a.astype(bf16), b.astype(bf16), preferred_element_type=f32)


def nt(a, b):
    return lax.dot_general(
        a.astype(bf16), b.astype(bf16), (((1,), (1,)), ((), ())), preferred_element_type=f32
    )


def tn(a, b):
    return lax.dot_general(
        a.astype(bf16), b.astype(bf16), (((0,), (0,)), ((), ())), preferred_element_type=f32
    )


def nn3(a, b):
    ah, bh = a.astype(bf16), b.astype(bf16)
    al, bl = (a - ah.astype(f32)).astype(bf16), (b - bh.astype(f32)).astype(bf16)
    return nn(ah, bh) + (nn(al, bh) + nn(ah, bl))


def shift_up(x, s):
    return pltpu.roll(x, x.shape[0] - s, 0)


def shift_down(x, s):
    return pltpu.roll(x, s, 0)


def segment_at(pos, starts):
    seg = jnp.zeros(pos.shape, jnp.int32)
    for s in starts:
        seg = seg + (pos >= s).astype(jnp.int32)
    return seg


def same_document(t, j, starts):
    ok = None
    for s in starts:
        same = (t >= s) == (j >= s)
        ok = same if ok is None else ok & same
    return ok


def level_sizes(length):
    sizes = []
    h = length // 2
    while h >= B:
        sizes.append(h)
        h //= 2
    return sizes


def row_pick(x, size, row):
    n, lanes = x.shape
    x3 = x.reshape(n // size, size, lanes)
    return jnp.broadcast_to(x3[:, row : row + 1, :], x3.shape).reshape(n, lanes)


class Common:
    def __init__(self, la, starts):
        length, lanes = la.shape
        self.length, self.lanes = length, lanes
        rows = lax.broadcasted_iota(jnp.int32, (length, lanes), 0)
        self.rows = rows
        self.lane_head = lax.broadcasted_iota(jnp.int32, (length, lanes), 1) // M
        c = la
        s = 1
        while s < length:
            c = c + jnp.where(rows >= s, shift_down(c, s), 0.0)
            s *= 2
        self.c = c
        self.alpha = jnp.exp(la)
        self.om = 1.0 - self.alpha
        self.levels = level_sizes(length)
        self.x = []
        for h in self.levels:
            mid = row_pick(c, 2 * h, h - 1)
            self.x.append(jnp.exp(-jnp.abs(c - mid)))
        t = lax.broadcasted_iota(jnp.int32, (length, length), 0)
        j = lax.broadcasted_iota(jnp.int32, (length, length), 1)
        same = same_document(t, j, starts)
        self.masks = [
            same & ((t // (2 * h)) == (j // (2 * h))) & ((t & h) != 0) & ((j & h) == 0)
            for h in self.levels
        ]
        tc = lax.broadcasted_iota(jnp.int32, (length, B), 0)
        off = lax.broadcasted_iota(jnp.int32, (length, B), 1)
        jc = (tc - tc % B) + off
        self.mask_c = same_document(tc, jc, starts) & (jc <= tc)

    def by_head(self, parts):
        out = parts[0]
        for i in range(1, len(parts)):
            out = jnp.where(self.lane_head == i, parts[i], out)
        return out

    def only(self, x, i):
        return jnp.where(self.lane_head == i, x, 0.0)

    def decay_from(self, jj):
        return jnp.exp(jnp.minimum(self.c - row_pick(self.c, B, jj), 0.0))

    def om_at(self, jj):
        return row_pick(self.om, B, jj)


def blocks(x):
    return x.reshape(x.shape[0] // B, B, x.shape[1])


def block_nt(a, b):
    r = lax.dot_general(
        blocks(a.astype(bf16)),
        blocks(b.astype(bf16)),
        (((2,), (2,)), ((0,), (0,))),
        preferred_element_type=f32,
    )
    return r.reshape(a.shape[0], B)


def block_nn(a, b):
    r = lax.dot_general(
        blocks(a.astype(bf16)),
        blocks(b.astype(bf16)),
        (((2,), (1,)), ((0,), (0,))),
        preferred_element_type=f32,
    )
    return r.reshape(a.shape[0], b.shape[1])


def block_tn(a, b):
    at = jnp.swapaxes(blocks(a), 1, 2).astype(bf16)
    r = lax.dot_general(
        at, blocks(b.astype(bf16)), (((2,), (1,)), ((0,), (0,))), preferred_element_type=f32
    )
    return r.reshape(a.shape[0], b.shape[1])


def collect(lanes, heads):
    r = lax.broadcasted_iota(jnp.int32, (B * lanes, heads * 128), 0)
    col = lax.broadcasted_iota(jnp.int32, (B * lanes, heads * 128), 1)
    jj, head = r // lanes, (r % lanes) // M
    return jnp.where(col == head * 128 + jj, 1.0, 0.0).astype(bf16)


def wide(x, jj):
    return jnp.broadcast_to(x[:, jj : jj + 1], (x.shape[0], 128))


def forward_math(q, k, v, la, starts):
    heads = q.shape[1] // DK
    scale = 1.0 / math.sqrt(DK)
    cm = Common(la, starts)
    qs = [q[:, i * DK : (i + 1) * DK] for i in range(heads)]
    ks = [k[:, i * DK : (i + 1) * DK] for i in range(heads)]
    vs = [v[:, i * DV : (i + 1) * DV] for i in range(heads)]
    aff = [nt(qs[i], ks[i]) * scale for i in range(heads)]
    affc = [jnp.where(cm.mask_c, block_nt(qs[i], ks[i]) * scale, 0.0) for i in range(heads)]
    s = jnp.zeros_like(la)
    parts = []
    for x, mask in zip(cm.x, cm.masks):
        g = x * cm.om
        part = x * cm.by_head([nn3(jnp.where(mask, aff[i], 0.0), g) for i in range(heads)])
        parts.append(part)
        s = s + part
    for jj in range(B):
        s = s + cm.by_head([wide(affc[i], jj) for i in range(heads)]) * (
            cm.decay_from(jj) * cm.om_at(jj)
        )
    top = cm.by_head(
        [
            jnp.max(jnp.where(cm.lane_head == i, s, -jnp.inf), axis=1, keepdims=True)
            for i in range(heads)
        ]
    )
    e = jnp.exp(s - top)
    total = cm.by_head([jnp.sum(cm.only(e, i), axis=1, keepdims=True) for i in range(heads)])
    p = e / total
    mix = [jnp.zeros((cm.length, cm.length), f32) for _ in range(heads)]
    for x, mask in zip(cm.x, cm.masks):
        g = x * cm.om
        px = p * x
        for i in range(heads):
            mix[i] = mix[i] + jnp.where(mask, nt(cm.only(px, i), g), 0.0)
    mix = [m.astype(bf16) for m in mix]
    pieces = [(p * (cm.decay_from(jj) * cm.om_at(jj))).astype(bf16) for jj in range(B)]
    mixc = nn(jnp.concatenate(pieces, axis=1), collect(cm.lanes, heads))
    mixc = [
        jnp.where(cm.mask_c, mixc[:, i * 128 : i * 128 + B], 0.0) for i in range(heads)
    ]
    outs = [nn(mix[i], vs[i]) + block_nn(mixc[i], vs[i]) for i in range(heads)]
    return outs, p, parts, mix, mixc


def backward_math(q, k, v, la, starts, p, parts, mix, mixc, dout):
    heads = q.shape[1] // DK
    scale = 1.0 / math.sqrt(DK)
    cm = Common(la, starts)
    qs = [q[:, i * DK : (i + 1) * DK] for i in range(heads)]
    ks = [k[:, i * DK : (i + 1) * DK] for i in range(heads)]
    vs = [v[:, i * DV : (i + 1) * DV] for i in range(heads)]
    dos = [dout[:, i * DV : (i + 1) * DV].astype(bf16) for i in range(heads)]
    aff = [nt(qs[i], ks[i]) * scale for i in range(heads)]
    affc = [jnp.where(cm.mask_c, block_nt(qs[i], ks[i]) * scale, 0.0) for i in range(heads)]
    dmix = [nt(dos[i], vs[i]) for i in range(heads)]
    dmixc = [jnp.where(cm.mask_c, block_nt(dos[i], vs[i]), 0.0) for i in range(heads)]
    dp = jnp.zeros_like(la)
    dparts = []
    for x, mask in zip(cm.x, cm.masks):
        g = x * cm.om
        part = x * cm.by_head([nn3(jnp.where(mask, dmix[i], 0.0), g) for i in range(heads)])
        dparts.append(part)
        dp = dp + part
    for jj in range(B):
        dp = dp + cm.by_head([wide(dmixc[i], jj) for i in range(heads)]) * (
            cm.decay_from(jj) * cm.om_at(jj)
        )
    pdp = p * dp
    inner = cm.by_head([jnp.sum(cm.only(pdp, i), axis=1, keepdims=True) for i in range(heads)])
    ds = pdp - p * inner
    daff = [jnp.zeros((cm.length, cm.length), f32) for _ in range(heads)]
    dla = jnp.zeros_like(la)
    reach = jnp.zeros_like(la)
    for n, h in enumerate(cm.levels):
        x, mask = cm.x[n], cm.masks[n]
        g = x * cm.om
        dsx, px = ds * x, p * x
        both = jnp.concatenate([dsx, px], axis=0).astype(bf16)
        cols = []
        for i in range(heads):
            daff[i] = daff[i] + jnp.where(mask, nt(cm.only(dsx, i), g), 0.0)
            left = jnp.concatenate(
                [jnp.where(mask, aff[i], 0.0), jnp.where(mask, dmix[i], 0.0)], axis=0
            )
            cols.append(tn(left, both))
        r = x * cm.by_head(cols)
        reach = reach + r
        right = (cm.rows & h) != 0
        flow = jnp.where(right, ds * parts[n] + p * dparts[n], cm.om * r)
        s = 1
        while s < h:
            flow = flow + jnp.where((cm.rows & (h - 1)) < h - s, shift_up(flow, s), 0.0)
            s *= 2
        dla = dla + jnp.where(right, flow, row_pick(flow, h, 0) - flow)
    flow = jnp.zeros_like(la)
    near = jnp.zeros_like(la)
    pieces = []
    for jj in range(B):
        w = cm.decay_from(jj)
        omj = cm.om_at(jj)
        aj = cm.by_head([wide(affc[i], jj) for i in range(heads)])
        dj = cm.by_head([wide(dmixc[i], jj) for i in range(heads)])
        pieces.append((ds * (w * omj)).astype(bf16))
        z = w * (aj * ds + dj * p)
        flow = flow + omj * z
        z3 = blocks(z)
        tot = jnp.broadcast_to(jnp.sum(z3, axis=1, keepdims=True), z3.shape).reshape(z.shape)
        near = jnp.where((cm.rows & (B - 1)) == jj, tot, near)
    flow = flow - cm.om * near
    s = 1
    while s < B:
        flow = flow + jnp.where((cm.rows & (B - 1)) < B - s, shift_up(flow, s), 0.0)
        s *= 2
    dla = dla + flow - cm.alpha * (reach + near)
    daffc = nn(jnp.concatenate(pieces, axis=1), collect(cm.lanes, heads))
    daffc = [
        jnp.where(cm.mask_c, daffc[:, i * 128 : i * 128 + B], 0.0) for i in range(heads)
    ]
    dq, dk, dv = [], [], []
    for i in range(heads):
        da = daff[i].astype(bf16)
        dq.append((nn(da, ks[i]) + block_nn(daffc[i], ks[i])) * scale)
        dk.append((tn(da, qs[i]) + block_tn(daffc[i], qs[i])) * scale)
        dv.append(tn(mix[i], dos[i]) + block_tn(mixc[i], dos[i]))
    return dq, dk, dv, dla


def head_split(outs, ref, width):
    for i, x in enumerate(outs):
        ref[:, i * width : (i + 1) * width] = x.astype(ref.dtype)


def forward_kernel(starts_ref, q_ref, k_ref, v_ref, la_ref, o_ref, p_ref, parts_ref, mix_ref, mixc_ref):
    starts = [starts_ref[0, n] for n in range(starts_ref.shape[1])]
    outs, p, parts, mix, mixc = forward_math(
        q_ref[...], k_ref[...], v_ref[...], la_ref[...], starts
    )
    head_split(outs, o_ref, DV)
    p_ref[...] = p
    for n, x in enumerate(parts):
        parts_ref[n] = x
    for i in range(len(mix)):
        mix_ref[i] = mix[i]
        mixc_ref[i] = mixc[i].astype(bf16)


def backward_kernel(
    starts_ref, q_ref, k_ref, v_ref, la_ref, p_ref, parts_ref, mix_ref, mixc_ref, do_ref,
    dq_ref, dk_ref, dv_ref, dla_ref,
):
    starts = [starts_ref[0, n] for n in range(starts_ref.shape[1])]
    heads = mix_ref.shape[0]
    dq, dk, dv, dla = backward_math(
        q_ref[...],
        k_ref[...],
        v_ref[...],
        la_ref[...],
        starts,
        p_ref[...],
        [parts_ref[n] for n in range(parts_ref.shape[0])],
        [mix_ref[i] for i in range(heads)],
        [mixc_ref[i] for i in range(heads)],
        do_ref[...],
    )
    head_split(dq, dq_ref, DK)
    head_split(dk, dk_ref, DK)
    head_split(dv, dv_ref, DV)
    dla_ref[...] = dla


SMEM = pl.BlockSpec(memory_space=pltpu.SMEM)
VMEM = pl.BlockSpec(memory_space=pltpu.VMEM)


def attend_forward(q, k, v, la, starts):
    length, lanes = la.shape
    heads = q.shape[1] // DK
    sds = jax.ShapeDtypeStruct
    return pl.pallas_call(
        forward_kernel,
        out_shape=(
            sds((length, heads * DV), bf16),
            sds((length, lanes), f32),
            sds((len(level_sizes(length)), length, lanes), f32),
            sds((heads, length, length), bf16),
            sds((heads, length, B), bf16),
        ),
        in_specs=[SMEM] + [VMEM] * 4,
        out_specs=(VMEM,) * 5,
        cost_estimate=pl.CostEstimate(
            flops=4 * 10**9, transcendentals=10**6, bytes_accessed=4 * 10**6
        ),
        name="slot_forward",
    )(starts, q, k, v, la)


def attend_backward(q, k, v, la, starts, saved, dout):
    length, lanes = la.shape
    sds = jax.ShapeDtypeStruct
    return pl.pallas_call(
        backward_kernel,
        out_shape=(
            sds(q.shape, f32),
            sds(k.shape, f32),
            sds(v.shape, f32),
            sds((length, lanes), f32),
        ),
        in_specs=[SMEM] + [VMEM] * 9,
        out_specs=(VMEM,) * 4,
        cost_estimate=pl.CostEstimate(
            flops=12 * 10**9, transcendentals=10**6, bytes_accessed=8 * 10**6
        ),
        name="slot_backward",
    )(starts, q, k, v, la, *saved, dout)


eps = 1e-06
tau_inv = 0.125
INNER = 4
LAP = (0, 1, 3, 2)


def rms_scale(values):
    return lax.rsqrt(jnp.mean(values * values, axis=-1, keepdims=True) + eps)


def norm_back(values, scale, gain, upstream):
    gain_grad = jnp.sum(upstream * values * scale, axis=0)
    weighted = upstream * gain
    input_grad = scale * weighted - values * (scale * scale * scale) * jnp.mean(
        weighted * values, axis=-1, keepdims=True
    )
    return (gain_grad, input_grad)


def silu_slope(values):
    sigmoid_val = jax.nn.sigmoid(values)
    return sigmoid_val * (1.0 + values * (1.0 - sigmoid_val))


class Grid:
    def __init__(self, dp):
        self.dp = dp
        self.outer = dp // INNER
        self.rows = [[o * INNER + i for i in LAP] for o in range(self.outer)]
        self.cols = [[o * INNER + i for o in range(self.outer)] for i in range(INNER)]
        self.gathered = [o * INNER + i for i in LAP for o in range(self.outer)]
        walk = [0]
        for n, i in enumerate((1, 3, 2)):
            column = [o * INNER + i for o in range(self.outer)]
            walk += column if n % 2 == 0 else column[::-1]
        walk += [o * INNER for o in range(self.outer - 1, 0, -1)]
        self.walk = walk


def reorder(x, order):
    n = len(order)
    size = x.shape[-1] // n
    return jnp.concatenate([x[..., b * size : (b + 1) * size] for b in order], axis=-1)


def inverse(order):
    back = [0] * len(order)
    for n, b in enumerate(order):
        back[b] = n
    return back


def swap(x):
    return lax.ppermute(x, "head", [(0, 1), (1, 0)])


def half_of(x, which):
    size = x.shape[0] // 2
    return lax.dynamic_slice_in_dim(x, which * size, size, 0)


def join(mine, other, core):
    size = mine.shape[0]
    out = jnp.zeros((2 * size,) + mine.shape[1:], mine.dtype)
    out = lax.dynamic_update_slice_in_dim(out, mine, core * size, 0)
    return lax.dynamic_update_slice_in_dim(out, other, (1 - core) * size, 0)


def spread_columns(w, grid, place):
    rows, size = w.shape[0], w.shape[1] // grid.outer
    if grid.outer > 4:
        return lax.all_to_all(w, "dp", 1, 0, tiled=True, axis_index_groups=grid.cols)
    out = jnp.zeros((grid.outer, rows, size), w.dtype)
    for s in range(grid.outer):
        mate = place ^ s
        piece = lax.dynamic_slice_in_dim(w, mate * size, size, 1)
        if s:
            pairs = [
                (o * INNER + i, (o ^ s) * INNER + i) for o in range(grid.outer) for i in range(INNER)
            ]
            piece = lax.ppermute(piece, "dp", pairs)
        out = lax.dynamic_update_slice_in_dim(out, piece[None], mate, 0)
    return out.reshape(grid.outer * rows, size)


def gather_rows(w, grid):
    return lax.all_gather(w, "dp", axis=0, tiled=True, axis_index_groups=grid.rows)


def scatter_rows(g, grid):
    g = lax.psum_scatter(
        g, "dp", scatter_dimension=0, tiled=True, axis_index_groups=grid.rows
    )
    return lax.all_to_all(g, "dp", 0, 1, tiled=True, axis_index_groups=grid.cols)


def gather_tokens(x, grid):
    x = reorder(x, grid.gathered)
    own = lax.all_gather(x, "dp", axis=0, tiled=True, axis_index_groups=grid.cols)
    return jnp.concatenate([own, swap(own)], axis=0)


def scatter_tokens(x, grid):
    size = x.shape[0] // 2
    other = swap(x[size:].astype(bf16))
    mine = (x[:size] + other.astype(f32)).astype(bf16)
    mine = lax.psum_scatter(
        mine, "dp", scatter_dimension=0, tiled=True, axis_index_groups=grid.cols
    )
    return reorder(mine.astype(f32), inverse(grid.gathered))


def on_device(
    block_in,
    out_grad,
    attn_gain,
    mlp_gain,
    w_query,
    w_key,
    w_value,
    w_forget,
    w_output,
    w_gate,
    w_up,
    w_down,
    doc_starts,
    grid,
):
    core = lax.axis_index("head")
    place = lax.axis_index("dp") // INNER
    cot_half = half_of(out_grad, core)
    cot_all = gather_tokens(cot_half, grid)
    full_gate = gather_rows(spread_columns(w_gate, grid, place), grid)
    full_up = gather_rows(spread_columns(w_up, grid, place), grid)
    full_down = gather_rows(spread_columns(w_down, grid, place), grid)

    inputs_f = block_in.astype(f32)
    scale_one = rms_scale(inputs_f)
    normed = (inputs_f * scale_one * attn_gain).astype(bf16)
    query_pre = nn(normed, w_query)
    key_pre = nn(normed, w_key)
    value_pre = nn(normed, w_value)
    forget_pre = nn(normed, w_forget)
    query = jax.nn.silu(query_pre).astype(bf16)
    key = jax.nn.silu(key_pre).astype(bf16)
    value = jax.nn.silu(value_pre).astype(bf16)
    log_keep = jax.nn.log_sigmoid(forget_pre) * tau_inv
    mixed, *saved = attend_forward(query, key, value, log_keep, doc_starts)

    branch = nt(mixed, w_output)
    hidden = half_of(inputs_f, core) + half_of(branch, core) + swap(half_of(branch, 1 - core))
    scale_two = rms_scale(hidden)
    normed_two = (hidden * scale_two * mlp_gain).astype(bf16)
    tokens = gather_tokens(normed_two, grid)

    gate_act = nn(tokens, full_gate)
    up_act = nn(tokens, full_up)
    inner_grad = nn(cot_all, full_down)
    gate_grad = (inner_grad * up_act * silu_slope(gate_act)).astype(bf16)
    up_grad = (inner_grad * jax.nn.silu(gate_act)).astype(bf16)
    inner_act = (jax.nn.silu(gate_act) * up_act).astype(bf16)
    normed_two_grad = scatter_tokens(nt(gate_grad, full_gate) + nt(up_grad, full_up), grid)
    mlp_out = scatter_tokens(nt(inner_act, full_down), grid)
    result = (hidden + mlp_out).astype(bf16)
    result = join(result, swap(result), core)

    mlp_gain_part, hidden_grad = norm_back(hidden, scale_two, mlp_gain, normed_two_grad)
    hidden_grad = hidden_grad + cot_half.astype(f32)
    branch_half = hidden_grad.astype(bf16)
    branch_grad = join(branch_half, swap(branch_half), core)
    mixed_grad = nn(branch_grad, w_output).astype(bf16)

    gate_sum = scatter_rows(tn(tokens, gate_grad).astype(bf16), grid).astype(f32)
    up_sum = scatter_rows(tn(tokens, up_grad).astype(bf16), grid).astype(f32)
    down_sum = scatter_rows(tn(cot_all, inner_act).astype(bf16), grid).astype(f32)

    def walk_sum(g):
        return lax.psum_scatter(
            g.astype(bf16), "dp", scatter_dimension=0, tiled=True, axis_index_groups=[grid.walk]
        ).astype(f32)

    output_sum = walk_sum(tn(reorder(branch_grad, grid.walk), mixed))
    query_grad, key_grad, value_grad, log_grad = attend_backward(
        query, key, value, log_keep, doc_starts, saved, mixed_grad
    )
    query_pre_grad = (query_grad * silu_slope(query_pre)).astype(bf16)
    key_pre_grad = (key_grad * silu_slope(key_pre)).astype(bf16)
    value_pre_grad = (value_grad * silu_slope(value_pre)).astype(bf16)
    forget_pre_grad = (log_grad * tau_inv * jax.nn.sigmoid(-forget_pre)).astype(bf16)
    pre_grads = (query_pre_grad, key_pre_grad, value_pre_grad, forget_pre_grad)
    sums = walk_sum(tn(reorder(normed, grid.walk), jnp.concatenate(pre_grads, axis=1)))
    normed_part = nt(query_pre_grad, w_query) + nt(key_pre_grad, w_key)
    normed_part = normed_part + nt(value_pre_grad, w_value) + nt(forget_pre_grad, w_forget)
    normed_grad = half_of(normed_part, core) + swap(half_of(normed_part, 1 - core))
    attn_gain_part, input_grad = norm_back(
        half_of(inputs_f, core), half_of(scale_one, core), attn_gain, normed_grad
    )
    input_grad = input_grad + hidden_grad
    input_grad = join(input_grad, swap(input_grad), core)

    gains = jnp.stack([attn_gain_part, mlp_gain_part])
    gains = gains + swap(gains)
    gains = jnp.swapaxes(gains.reshape(2, grid.dp, -1), 0, 1)
    gains = jnp.sum(lax.all_to_all(gains, "dp", 0, 0, tiled=True), axis=0)

    widths = [g.shape[1] for g in pre_grads]
    ends = [sum(widths[: n + 1]) for n in range(4)]
    query_sum, key_sum, value_sum, forget_sum = (
        sums[:, e - w : e] for e, w in zip(ends, widths)
    )
    return (
        result,
        input_grad,
        gains[0],
        gains[1],
        query_sum,
        key_sum,
        value_sum,
        forget_sum,
        output_sum,
        gate_sum,
        up_sum,
        down_sum,
    )


def solution(mesh):
    placed = (
        P("dp", None),
        P("dp", None),
        P(),
        P(),
        P(None, "head"),
        P(None, "head"),
        P(None, "head"),
        P(None, "head"),
        P(None, "head"),
        P("dp", "head"),
        P("dp", "head"),
        P("dp", "head"),
        P("dp", None),
    )
    return jax.shard_map(
        partial(on_device, grid=Grid(mesh.shape["dp"])),
        mesh=mesh,
        in_specs=placed,
        out_specs=(P("dp", None), P("dp", None), P("dp"), P("dp")) + (P("dp", "head"),) * 8,
        check_vma=False,
    )
```

```python
import math
from functools import partial
import jax
import jax.numpy as jnp
from jax import lax
from jax.experimental import pallas as pl
from jax.experimental.pallas import tpu as pltpu
from jax.sharding import PartitionSpec as P

DK = 512
DV = 512
M = 64
B = 16
f32 = jnp.float32
bf16 = jnp.bfloat16


def nn(a, b):
    return jnp.dot(a.astype(bf16), b.astype(bf16), preferred_element_type=f32)


def nt(a, b):
    return lax.dot_general(
        a.astype(bf16), b.astype(bf16), (((1,), (1,)), ((), ())), preferred_element_type=f32
    )


def tn(a, b):
    return lax.dot_general(
        a.astype(bf16), b.astype(bf16), (((0,), (0,)), ((), ())), preferred_element_type=f32
    )


def nn3(a, b):
    ah, bh = a.astype(bf16), b.astype(bf16)
    al, bl = (a - ah.astype(f32)).astype(bf16), (b - bh.astype(f32)).astype(bf16)
    return nn(ah, bh) + (nn(al, bh) + nn(ah, bl))


def shift_up(x, s):
    return pltpu.roll(x, x.shape[0] - s, 0)


def shift_down(x, s):
    return pltpu.roll(x, s, 0)


def segment_at(pos, starts):
    seg = jnp.zeros(pos.shape, jnp.int32)
    for s in starts:
        seg = seg + (pos >= s).astype(jnp.int32)
    return seg


def same_document(t, j, starts):
    ok = None
    for s in starts:
        same = (t >= s) == (j >= s)
        ok = same if ok is None else ok & same
    return ok


def level_sizes(length):
    sizes = []
    h = length // 2
    while h >= B:
        sizes.append(h)
        h //= 2
    return sizes


def row_pick(x, size, row):
    n, lanes = x.shape
    x3 = x.reshape(n // size, size, lanes)
    return jnp.broadcast_to(x3[:, row : row + 1, :], x3.shape).reshape(n, lanes)


class Common:
    def __init__(self, la, starts):
        length, lanes = la.shape
        self.length, self.lanes = length, lanes
        rows = lax.broadcasted_iota(jnp.int32, (length, lanes), 0)
        self.rows = rows
        self.lane_head = lax.broadcasted_iota(jnp.int32, (length, lanes), 1) // M
        c = la
        s = 1
        while s < length:
            c = c + jnp.where(rows >= s, shift_down(c, s), 0.0)
            s *= 2
        self.c = c
        self.alpha = jnp.exp(la)
        self.om = 1.0 - self.alpha
        self.levels = level_sizes(length)
        self.x = []
        for h in self.levels:
            mid = row_pick(c, 2 * h, h - 1)
            self.x.append(jnp.exp(-jnp.abs(c - mid)))
        t = lax.broadcasted_iota(jnp.int32, (length, length), 0)
        j = lax.broadcasted_iota(jnp.int32, (length, length), 1)
        same = same_document(t, j, starts)
        self.masks = [
            same & ((t // (2 * h)) == (j // (2 * h))) & ((t & h) != 0) & ((j & h) == 0)
            for h in self.levels
        ]
        tc = lax.broadcasted_iota(jnp.int32, (length, B), 0)
        off = lax.broadcasted_iota(jnp.int32, (length, B), 1)
        jc = (tc - tc % B) + off
        self.mask_c = same_document(tc, jc, starts) & (jc <= tc)

    def by_head(self, parts):
        out = parts[0]
        for i in range(1, len(parts)):
            out = jnp.where(self.lane_head == i, parts[i], out)
        return out

    def only(self, x, i):
        return jnp.where(self.lane_head == i, x, 0.0)

    def decay_from(self, jj):
        return jnp.exp(jnp.minimum(self.c - row_pick(self.c, B, jj), 0.0))

    def om_at(self, jj):
        return row_pick(self.om, B, jj)


def blocks(x):
    return x.reshape(x.shape[0] // B, B, x.shape[1])


def block_nt(a, b):
    r = lax.dot_general(
        blocks(a.astype(bf16)),
        blocks(b.astype(bf16)),
        (((2,), (2,)), ((0,), (0,))),
        preferred_element_type=f32,
    )
    return r.reshape(a.shape[0], B)


def block_nn(a, b):
    r = lax.dot_general(
        blocks(a.astype(bf16)),
        blocks(b.astype(bf16)),
        (((2,), (1,)), ((0,), (0,))),
        preferred_element_type=f32,
    )
    return r.reshape(a.shape[0], b.shape[1])


def block_tn(a, b):
    at = jnp.swapaxes(blocks(a), 1, 2).astype(bf16)
    r = lax.dot_general(
        at, blocks(b.astype(bf16)), (((2,), (1,)), ((0,), (0,))), preferred_element_type=f32
    )
    return r.reshape(a.shape[0], b.shape[1])


def collect(lanes, heads):
    r = lax.broadcasted_iota(jnp.int32, (B * lanes, heads * 128), 0)
    col = lax.broadcasted_iota(jnp.int32, (B * lanes, heads * 128), 1)
    jj, head = r // lanes, (r % lanes) // M
    return jnp.where(col == head * 128 + jj, 1.0, 0.0).astype(bf16)


def wide(x, jj):
    return jnp.broadcast_to(x[:, jj : jj + 1], (x.shape[0], 128))


def forward_math(q, k, v, la, starts):
    heads = q.shape[1] // DK
    scale = 1.0 / math.sqrt(DK)
    cm = Common(la, starts)
    qs = [q[:, i * DK : (i + 1) * DK] for i in range(heads)]
    ks = [k[:, i * DK : (i + 1) * DK] for i in range(heads)]
    vs = [v[:, i * DV : (i + 1) * DV] for i in range(heads)]
    aff = [nt(qs[i], ks[i]) * scale for i in range(heads)]
    affc = [jnp.where(cm.mask_c, block_nt(qs[i], ks[i]) * scale, 0.0) for i in range(heads)]
    s = jnp.zeros_like(la)
    parts = []
    for x, mask in zip(cm.x, cm.masks):
        g = x * cm.om
        part = x * cm.by_head([nn3(jnp.where(mask, aff[i], 0.0), g) for i in range(heads)])
        parts.append(part)
        s = s + part
    for jj in range(B):
        s = s + cm.by_head([wide(affc[i], jj) for i in range(heads)]) * (
            cm.decay_from(jj) * cm.om_at(jj)
        )
    top = cm.by_head(
        [
            jnp.max(jnp.where(cm.lane_head == i, s, -jnp.inf), axis=1, keepdims=True)
            for i in range(heads)
        ]
    )
    e = jnp.exp(s - top)
    total = cm.by_head([jnp.sum(cm.only(e, i), axis=1, keepdims=True) for i in range(heads)])
    p = e / total
    mix = [jnp.zeros((cm.length, cm.length), f32) for _ in range(heads)]
    for x, mask in zip(cm.x, cm.masks):
        g = x * cm.om
        px = p * x
        for i in range(heads):
            mix[i] = mix[i] + jnp.where(mask, nt(cm.only(px, i), g), 0.0)
    mix = [m.astype(bf16) for m in mix]
    pieces = [(p * (cm.decay_from(jj) * cm.om_at(jj))).astype(bf16) for jj in range(B)]
    mixc = nn(jnp.concatenate(pieces, axis=1), collect(cm.lanes, heads))
    mixc = [
        jnp.where(cm.mask_c, mixc[:, i * 128 : i * 128 + B], 0.0) for i in range(heads)
    ]
    outs = [nn(mix[i], vs[i]) + block_nn(mixc[i], vs[i]) for i in range(heads)]
    return outs, p, parts, mix, mixc


def backward_math(q, k, v, la, starts, p, parts, mix, mixc, dout):
    heads = q.shape[1] // DK
    scale = 1.0 / math.sqrt(DK)
    cm = Common(la, starts)
    qs = [q[:, i * DK : (i + 1) * DK] for i in range(heads)]
    ks = [k[:, i * DK : (i + 1) * DK] for i in range(heads)]
    vs = [v[:, i * DV : (i + 1) * DV] for i in range(heads)]
    dos = [dout[:, i * DV : (i + 1) * DV].astype(bf16) for i in range(heads)]
    aff = [nt(qs[i], ks[i]) * scale for i in range(heads)]
    affc = [jnp.where(cm.mask_c, block_nt(qs[i], ks[i]) * scale, 0.0) for i in range(heads)]
    dmix = [nt(dos[i], vs[i]) for i in range(heads)]
    dmixc = [jnp.where(cm.mask_c, block_nt(dos[i], vs[i]), 0.0) for i in range(heads)]
    dp = jnp.zeros_like(la)
    dparts = []
    for x, mask in zip(cm.x, cm.masks):
        g = x * cm.om
        part = x * cm.by_head([nn3(jnp.where(mask, dmix[i], 0.0), g) for i in range(heads)])
        dparts.append(part)
        dp = dp + part
    for jj in range(B):
        dp = dp + cm.by_head([wide(dmixc[i], jj) for i in range(heads)]) * (
            cm.decay_from(jj) * cm.om_at(jj)
        )
    pdp = p * dp
    inner = cm.by_head([jnp.sum(cm.only(pdp, i), axis=1, keepdims=True) for i in range(heads)])
    ds = pdp - p * inner
    daff = [jnp.zeros((cm.length, cm.length), f32) for _ in range(heads)]
    dla = jnp.zeros_like(la)
    reach = jnp.zeros_like(la)
    for n, h in enumerate(cm.levels):
        x, mask = cm.x[n], cm.masks[n]
        g = x * cm.om
        dsx, px = ds * x, p * x
        both = jnp.concatenate([dsx, px], axis=0).astype(bf16)
        cols = []
        for i in range(heads):
            daff[i] = daff[i] + jnp.where(mask, nt(cm.only(dsx, i), g), 0.0)
            left = jnp.concatenate(
                [jnp.where(mask, aff[i], 0.0), jnp.where(mask, dmix[i], 0.0)], axis=0
            )
            cols.append(tn(left, both))
        r = x * cm.by_head(cols)
        reach = reach + r
        right = (cm.rows & h) != 0
        flow = jnp.where(right, ds * parts[n] + p * dparts[n], cm.om * r)
        s = 1
        while s < h:
            flow = flow + jnp.where((cm.rows & (h - 1)) < h - s, shift_up(flow, s), 0.0)
            s *= 2
        dla = dla + jnp.where(right, flow, row_pick(flow, h, 0) - flow)
    flow = jnp.zeros_like(la)
    near = jnp.zeros_like(la)
    pieces = []
    for jj in range(B):
        w = cm.decay_from(jj)
        omj = cm.om_at(jj)
        aj = cm.by_head([wide(affc[i], jj) for i in range(heads)])
        dj = cm.by_head([wide(dmixc[i], jj) for i in range(heads)])
        pieces.append((ds * (w * omj)).astype(bf16))
        z = w * (aj * ds + dj * p)
        flow = flow + omj * z
        z3 = blocks(z)
        tot = jnp.broadcast_to(jnp.sum(z3, axis=1, keepdims=True), z3.shape).reshape(z.shape)
        near = jnp.where((cm.rows & (B - 1)) == jj, tot, near)
    flow = flow - cm.om * near
    s = 1
    while s < B:
        flow = flow + jnp.where((cm.rows & (B - 1)) < B - s, shift_up(flow, s), 0.0)
        s *= 2
    dla = dla + flow - cm.alpha * (reach + near)
    daffc = nn(jnp.concatenate(pieces, axis=1), collect(cm.lanes, heads))
    daffc = [
        jnp.where(cm.mask_c, daffc[:, i * 128 : i * 128 + B], 0.0) for i in range(heads)
    ]
    dq, dk, dv = [], [], []
    for i in range(heads):
        da = daff[i].astype(bf16)
        dq.append((nn(da, ks[i]) + block_nn(daffc[i], ks[i])) * scale)
        dk.append((tn(da, qs[i]) + block_tn(daffc[i], qs[i])) * scale)
        dv.append(tn(mix[i], dos[i]) + block_tn(mixc[i], dos[i]))
    return dq, dk, dv, dla


def head_split(outs, ref, width):
    for i, x in enumerate(outs):
        ref[:, i * width : (i + 1) * width] = x.astype(ref.dtype)


def forward_kernel(starts_ref, q_ref, k_ref, v_ref, la_ref, o_ref, p_ref, parts_ref, mix_ref, mixc_ref):
    starts = [starts_ref[0, n] for n in range(starts_ref.shape[1])]
    outs, p, parts, mix, mixc = forward_math(
        q_ref[...], k_ref[...], v_ref[...], la_ref[...], starts
    )
    head_split(outs, o_ref, DV)
    p_ref[...] = p
    for n, x in enumerate(parts):
        parts_ref[n] = x
    for i in range(len(mix)):
        mix_ref[i] = mix[i]
        mixc_ref[i] = mixc[i].astype(bf16)


def backward_kernel(
    starts_ref, q_ref, k_ref, v_ref, la_ref, p_ref, parts_ref, mix_ref, mixc_ref, do_ref,
    dq_ref, dk_ref, dv_ref, dla_ref,
):
    starts = [starts_ref[0, n] for n in range(starts_ref.shape[1])]
    heads = mix_ref.shape[0]
    dq, dk, dv, dla = backward_math(
        q_ref[...],
        k_ref[...],
        v_ref[...],
        la_ref[...],
        starts,
        p_ref[...],
        [parts_ref[n] for n in range(parts_ref.shape[0])],
        [mix_ref[i] for i in range(heads)],
        [mixc_ref[i] for i in range(heads)],
        do_ref[...],
    )
    head_split(dq, dq_ref, DK)
    head_split(dk, dk_ref, DK)
    head_split(dv, dv_ref, DV)
    dla_ref[...] = dla


SMEM = pl.BlockSpec(memory_space=pltpu.SMEM)
VMEM = pl.BlockSpec(memory_space=pltpu.VMEM)


def attend_forward(q, k, v, la, starts):
    length, lanes = la.shape
    heads = q.shape[1] // DK
    sds = jax.ShapeDtypeStruct
    return pl.pallas_call(
        forward_kernel,
        out_shape=(
            sds((length, heads * DV), bf16),
            sds((length, lanes), f32),
            sds((len(level_sizes(length)), length, lanes), f32),
            sds((heads, length, length), bf16),
            sds((heads, length, B), bf16),
        ),
        in_specs=[SMEM] + [VMEM] * 4,
        out_specs=(VMEM,) * 5,
        cost_estimate=pl.CostEstimate(
            flops=4 * 10**9, transcendentals=10**6, bytes_accessed=4 * 10**6
        ),
        name="slot_forward",
    )(starts, q, k, v, la)


def attend_backward(q, k, v, la, starts, saved, dout):
    length, lanes = la.shape
    sds = jax.ShapeDtypeStruct
    return pl.pallas_call(
        backward_kernel,
        out_shape=(
            sds(q.shape, f32),
            sds(k.shape, f32),
            sds(v.shape, f32),
            sds((length, lanes), f32),
        ),
        in_specs=[SMEM] + [VMEM] * 9,
        out_specs=(VMEM,) * 4,
        cost_estimate=pl.CostEstimate(
            flops=12 * 10**9, transcendentals=10**6, bytes_accessed=8 * 10**6
        ),
        name="slot_backward",
    )(starts, q, k, v, la, *saved, dout)


eps = 1e-06
tau_inv = 0.125
INNER = 4
LAP = (0, 1, 3, 2)


def rms_scale(values):
    return lax.rsqrt(jnp.mean(values * values, axis=-1, keepdims=True) + eps)


def norm_back(values, scale, gain, upstream):
    gain_grad = jnp.sum(upstream * values * scale, axis=0, keepdims=True)
    weighted = upstream * gain
    input_grad = scale * weighted - values * (scale * scale * scale) * jnp.mean(
        weighted * values, axis=-1, keepdims=True
    )
    return (gain_grad, input_grad)


def silu_slope(values):
    sigmoid_val = jax.nn.sigmoid(values)
    return sigmoid_val * (1.0 + values * (1.0 - sigmoid_val))


class Grid:
    def __init__(self, dp):
        self.dp = dp
        self.outer = dp // INNER
        self.laps = [[o * INNER + i for i in LAP] for o in range(self.outer)]
        self.rows = [[o * INNER + i for i in range(INNER)] for o in range(self.outer)]
        self.cols = [[o * INNER + i for o in range(self.outer)] for i in range(INNER)]
        self.gathered = [o * INNER + i for i in LAP for o in range(self.outer)]
        self.natural = inverse(self.gathered)
        self.up = [(d, d + INNER) for d in range(dp - INNER)]
        self.down = [(d + INNER, d) for d in range(dp - INNER)]


def reorder(x, order):
    size = x.shape[-1] // len(order)
    return jnp.concatenate([x[..., b * size : (b + 1) * size] for b in order], axis=-1)


def inverse(order):
    back = [0] * len(order)
    for n, b in enumerate(order):
        back[b] = n
    return back


def swap(x):
    return lax.ppermute(x, "head", [(0, 1), (1, 0)])


def half_of(x, which):
    size = x.shape[0] // 2
    return lax.dynamic_slice_in_dim(x, which * size, size, 0)


def join(mine, other, core):
    size = mine.shape[0]
    out = jnp.zeros((2 * size,) + mine.shape[1:], mine.dtype)
    out = lax.dynamic_update_slice_in_dim(out, mine, core * size, 0)
    return lax.dynamic_update_slice_in_dim(out, other, (1 - core) * size, 0)


def on_rows(kernel, name, core, halves, wholes, outs):
    rows = halves[0].shape[0] // 2
    specs = [pl.BlockSpec((rows, x.shape[1]), lambda i, c: (c[0], 0)) for x in halves]
    specs += [pl.BlockSpec(x.shape, lambda i, c: (0, 0)) for x in wholes]
    return pl.pallas_call(
        kernel,
        out_shape=outs,
        grid_spec=pltpu.PrefetchScalarGridSpec(
            num_scalar_prefetch=1,
            grid=(1,),
            in_specs=specs,
            out_specs=[pl.BlockSpec(x.shape, lambda i, c: (0, 0)) for x in outs],
        ),
        name=name,
    )(core.reshape(1), *halves, *wholes)


def aligned(grid, width):
    return (width // grid.dp) % 128 == 0


def put_in_order(x, order, grid, inside):
    return reorder(x, order) if aligned(grid, x.shape[1]) == inside else x


def cotangent_rows(out_grad, core, grid):
    rows, width = out_grad.shape

    def kernel(core_ref, cot_ref, out_ref):
        out_ref[...] = put_in_order(cot_ref[...], grid.gathered, grid, True)

    outs = [jax.ShapeDtypeStruct((rows // 2, width), bf16)]
    (x,) = on_rows(kernel, "cotangent_rows", core, [out_grad], [], outs)
    return put_in_order(x, grid.gathered, grid, False)


def second_norm(block_in, mine, other, gain, core, grid):
    rows, width = mine.shape

    def kernel(core_ref, in_ref, mine_ref, other_ref, gain_ref, hidden_ref, normed_ref):
        hidden = in_ref[...].astype(f32) + (mine_ref[...] + other_ref[...])
        hidden_ref[...] = hidden
        normed = (hidden * rms_scale(hidden) * gain_ref[...]).astype(bf16)
        normed_ref[...] = put_in_order(normed, grid.gathered, grid, True)

    outs = [jax.ShapeDtypeStruct((rows, width), f32), jax.ShapeDtypeStruct((rows, width), bf16)]
    hidden, normed = on_rows(
        kernel, "second_norm", core, [block_in], [mine, other, gain[None]], outs
    )
    return hidden, put_in_order(normed, grid.gathered, grid, False)


def second_norm_back(out_grad, hidden, gain, parts, core, grid):
    rows, width = hidden.shape
    parts = [put_in_order(x, grid.natural, grid, False) for x in parts]

    def kernel(core_ref, cot_ref, hidden_ref, gain_ref, *refs):
        upstream = sum(x[...].astype(f32) for x in refs[: len(parts)])
        upstream = put_in_order(upstream, grid.natural, grid, True)
        grad_ref, low_ref, gain_grad_ref = refs[len(parts) :]
        hidden = hidden_ref[...]
        gain_grad, grad = norm_back(hidden, rms_scale(hidden), gain_ref[...], upstream)
        grad = grad + cot_ref[...].astype(f32)
        grad_ref[...] = grad
        low_ref[...] = grad.astype(bf16)
        gain_grad_ref[...] = gain_grad

    sds = jax.ShapeDtypeStruct
    outs = [sds((rows, width), f32), sds((rows, width), bf16), sds((1, width), f32)]
    return on_rows(
        kernel, "second_norm_back", core, [out_grad], [hidden, gain[None], *parts], outs
    )


def first_norm_back(block_in, grad, gain, mine, other, core):
    rows, width = grad.shape

    def kernel(core_ref, in_ref, grad_ref, gain_ref, mine_ref, other_ref, out_ref, gain_grad_ref):
        inputs = in_ref[...].astype(f32)
        upstream = mine_ref[...] + other_ref[...]
        gain_grad, out = norm_back(inputs, rms_scale(inputs), gain_ref[...], upstream)
        out_ref[...] = out + grad_ref[...]
        gain_grad_ref[...] = gain_grad

    sds = jax.ShapeDtypeStruct
    outs = [sds((rows, width), f32), sds((1, width), f32)]
    return on_rows(
        kernel, "first_norm_back", core, [block_in], [grad, gain[None], mine, other], outs
    )


def block_result(block_in, hidden, parts, core, grid):
    rows, width = hidden.shape
    parts = [put_in_order(x, grid.natural, grid, False) for x in parts]

    def kernel(core_ref, in_ref, hidden_ref, *refs):
        out = sum(x[...].astype(f32) for x in refs[: len(parts)])
        out = put_in_order(out, grid.natural, grid, True)
        refs[-1][...] = (hidden_ref[...] + out).astype(bf16)

    outs = [jax.ShapeDtypeStruct((rows, width), bf16)]
    (x,) = on_rows(kernel, "block_result", core, [block_in], [hidden, *parts], outs)
    return x


def exchange(x, split, concat, groups):
    return lax.all_to_all(x, "dp", split, concat, tiled=True, axis_index_groups=groups)


def gather_along(x, grid, place):
    n = grid.outer
    above = below = x
    from_below, from_above = [], []
    for _ in range(n - 1):
        below = lax.ppermute(below, "dp", grid.up)
        above = lax.ppermute(above, "dp", grid.down)
        from_below.append(below)
        from_above.append(above)
    blocks = [x]
    for k in range(1, n):
        blocks.append(jnp.where(place + k < n, from_above[k - 1], from_below[n - 1 - k]))
    return jnp.concatenate(blocks, axis=0)


def gather_tokens(x, grid, place):
    own = gather_along(x, grid, place)
    return jnp.concatenate([own, swap(own)], axis=0)


def scatter_tokens(x, grid):
    n = grid.outer
    size = x.shape[0] // (2 * n)
    block = [x[k * size : (k + 1) * size] for k in range(2 * n)]
    order = [k for s in range(1, n) for k in (n - s, s)]
    order = list(dict.fromkeys(order)) + [0]
    swapped = {k: swap(block[n + k].astype(bf16)) for k in order}
    own = {k: block[k] + swapped[k].astype(f32) for k in order}
    up = down = None
    for k in range(n - 1):
        send = own[n - 1 - k] if up is None else own[n - 1 - k] + up.astype(f32)
        up = lax.ppermute(send.astype(bf16), "dp", grid.up)
        send = own[1 + k] if down is None else own[1 + k] + down.astype(f32)
        down = lax.ppermute(send.astype(bf16), "dp", grid.down)
    return own[0], up, down


def on_device(
    block_in,
    out_grad,
    attn_gain,
    mlp_gain,
    w_query,
    w_key,
    w_value,
    w_forget,
    w_output,
    w_gate,
    w_up,
    w_down,
    doc_starts,
    grid,
):
    core = lax.axis_index("head")
    place = lax.axis_index("dp") // INNER
    width = block_in.shape[1]

    def columns(w):
        return exchange(w, 1, 0, grid.cols)

    def gather_rows(w):
        return lax.all_gather(w, "dp", axis=0, tiled=True, axis_index_groups=grid.laps)

    gate_piece, up_piece, down_piece = columns(w_gate), columns(w_up), columns(w_down)

    inputs_f = block_in.astype(f32)
    normed = (inputs_f * rms_scale(inputs_f) * attn_gain).astype(bf16)
    normed, gate_piece = lax.optimization_barrier((normed, gate_piece))
    full_gate = gather_rows(gate_piece)
    query_pre = nn(normed, w_query)
    key_pre = nn(normed, w_key)
    value_pre = nn(normed, w_value)
    forget_pre = nn(normed, w_forget)
    query = jax.nn.silu(query_pre).astype(bf16)
    key = jax.nn.silu(key_pre).astype(bf16)
    value = jax.nn.silu(value_pre).astype(bf16)
    log_keep = jax.nn.log_sigmoid(forget_pre) * tau_inv
    query, up_piece = lax.optimization_barrier((query, up_piece))
    full_up = gather_rows(up_piece)
    mixed, *saved = attend_forward(query, key, value, log_keep, doc_starts)

    branch_other = swap(nt(half_of(mixed, 1 - core), w_output))
    branch_mine = nt(half_of(mixed, core), w_output)
    hidden, normed_two = second_norm(block_in, branch_mine, branch_other, mlp_gain, core, grid)
    normed_two, down_piece = lax.optimization_barrier((normed_two, down_piece))
    full_down = gather_rows(down_piece)
    tokens = gather_tokens(normed_two, grid, place)
    cot_rows = cotangent_rows(out_grad, core, grid)
    cot_rows, tokens = lax.optimization_barrier((cot_rows, tokens))
    cot_all = gather_tokens(cot_rows, grid, place)

    def plane_tokens(half):
        own = lax.all_gather(half, "dp", axis=0, tiled=True, axis_index_groups=grid.rows)
        return own, swap(own)

    def plane_columns(parts):
        rows = parts[0].shape[0]
        x = jnp.concatenate([p.reshape(rows, INNER, -1) for p in parts], axis=2)
        size = x.shape[2]
        x = exchange(x.reshape(rows, INNER * size), 1, 0, grid.rows)
        x = x.reshape(INNER, 2, rows // 2, size)
        return tuple(
            lax.dynamic_index_in_dim(x, c, 1, keepdims=False).reshape(-1, size)
            for c in (core, 1 - core)
        )

    def plane_grad(left, right):
        g = (tn(left[0], right[0]) + tn(left[1], right[1])).astype(bf16)
        g = lax.psum_scatter(
            g, "dp", scatter_dimension=0, tiled=True, axis_index_groups=grid.cols
        )
        size = g.shape[1]
        g = exchange(g, 0, 1, grid.rows).reshape(-1, INNER, size)
        return g.astype(f32)

    normed_plane = plane_tokens(half_of(normed, core))
    mixed_plane = plane_columns([mixed])

    gate_act = nn(tokens, full_gate)
    up_act = nn(tokens, full_up)
    inner_grad = nn(cot_all, full_down)
    gate_grad = (inner_grad * up_act * silu_slope(gate_act)).astype(bf16)
    up_grad = (inner_grad * jax.nn.silu(gate_act)).astype(bf16)
    inner_act = (jax.nn.silu(gate_act) * up_act).astype(bf16)
    back_parts = scatter_tokens(nt(gate_grad, full_gate) + nt(up_grad, full_up), grid)
    hidden_grad, low_half, mlp_gain_part = second_norm_back(
        out_grad, hidden, mlp_gain, back_parts, core, grid
    )
    branch_grad = join(low_half, swap(low_half), core)
    mixed_grad = nn(branch_grad, w_output).astype(bf16)

    def scatter_rows(g):
        return lax.psum_scatter(
            g.astype(bf16), "dp", scatter_dimension=0, tiled=True, axis_index_groups=grid.laps
        )

    down_rows = scatter_rows(tn(cot_all, inner_act))
    gate_rows = scatter_rows(tn(tokens, gate_grad))
    up_rows = scatter_rows(tn(tokens, up_grad))
    out_parts = scatter_tokens(nt(inner_act, full_down), grid)
    result = block_result(block_in, hidden, out_parts, core, grid)
    result = join(result, swap(result), core)

    output_sum = plane_grad(plane_tokens(low_half), mixed_plane)
    query_grad, key_grad, value_grad, log_grad = attend_backward(
        query, key, value, log_keep, doc_starts, saved, mixed_grad
    )
    query_pre_grad = (query_grad * silu_slope(query_pre)).astype(bf16)
    key_pre_grad = (key_grad * silu_slope(key_pre)).astype(bf16)
    value_pre_grad = (value_grad * silu_slope(value_pre)).astype(bf16)
    forget_pre_grad = (log_grad * tau_inv * jax.nn.sigmoid(-forget_pre)).astype(bf16)
    pre_grads = (query_pre_grad, key_pre_grad, value_pre_grad, forget_pre_grad)
    sums = plane_grad(normed_plane, plane_columns(pre_grads))
    ends = [0]
    for g in pre_grads:
        ends.append(ends[-1] + g.shape[1] // INNER)
    query_sum, key_sum, value_sum, forget_sum = (
        sums[:, :, a:b].reshape(sums.shape[0], -1) for a, b in zip(ends, ends[1:])
    )

    def normed_part(which):
        q, k, v, f = (half_of(g, which) for g in pre_grads)
        return nt(q, w_query) + nt(k, w_key) + nt(v, w_value) + nt(f, w_forget)

    part_other = swap(normed_part(1 - core))
    input_grad, attn_gain_part = first_norm_back(
        block_in, hidden_grad, attn_gain, normed_part(core), part_other, core
    )
    input_grad = join(input_grad, swap(input_grad), core)

    gains = jnp.concatenate([attn_gain_part, mlp_gain_part], axis=0)
    gains = gains + swap(gains)
    gains = jnp.swapaxes(gains.reshape(2, grid.dp, -1), 0, 1)
    gains = jnp.sum(lax.all_to_all(gains, "dp", 0, 0, tiled=True), axis=0)

    def to_columns(g):
        return exchange(g, 0, 1, grid.cols).astype(f32)

    return (
        result,
        input_grad,
        gains[0],
        gains[1],
        query_sum,
        key_sum,
        value_sum,
        forget_sum,
        output_sum.reshape(output_sum.shape[0], -1),
        to_columns(gate_rows),
        to_columns(up_rows),
        to_columns(down_rows),
    )


def solution(mesh):
    placed = (
        P("dp", None),
        P("dp", None),
        P(),
        P(),
        P(None, "head"),
        P(None, "head"),
        P(None, "head"),
        P(None, "head"),
        P(None, "head"),
        P("dp", "head"),
        P("dp", "head"),
        P("dp", "head"),
        P("dp", None),
    )
    return jax.shard_map(
        partial(on_device, grid=Grid(mesh.shape["dp"])),
        mesh=mesh,
        in_specs=placed,
        out_specs=(P("dp", None), P("dp", None), P("dp"), P("dp")) + (P("dp", "head"),) * 8,
        check_vma=False,
    )
```

```python
import math
from functools import partial
import jax
import jax.numpy as jnp
from jax import lax
from jax.experimental import pallas as pl
from jax.experimental.pallas import tpu as pltpu
from jax.sharding import PartitionSpec as P

DK = 512
DV = 512
M = 64
B = 16
f32 = jnp.float32
bf16 = jnp.bfloat16


def nn(a, b):
    return jnp.dot(a.astype(bf16), b.astype(bf16), preferred_element_type=f32)


def nt(a, b):
    return lax.dot_general(
        a.astype(bf16), b.astype(bf16), (((1,), (1,)), ((), ())), preferred_element_type=f32
    )


def tn(a, b):
    return lax.dot_general(
        a.astype(bf16), b.astype(bf16), (((0,), (0,)), ((), ())), preferred_element_type=f32
    )


def nn3(a, b):
    ah, bh = a.astype(bf16), b.astype(bf16)
    al, bl = (a - ah.astype(f32)).astype(bf16), (b - bh.astype(f32)).astype(bf16)
    return nn(ah, bh) + (nn(al, bh) + nn(ah, bl))


def shift_up(x, s):
    return pltpu.roll(x, x.shape[0] - s, 0)


def shift_down(x, s):
    return pltpu.roll(x, s, 0)


def segment_at(pos, starts):
    seg = jnp.zeros(pos.shape, jnp.int32)
    for s in starts:
        seg = seg + (pos >= s).astype(jnp.int32)
    return seg


def same_document(t, j, starts):
    ok = None
    for s in starts:
        same = (t >= s) == (j >= s)
        ok = same if ok is None else ok & same
    return ok


def level_sizes(length):
    sizes = []
    h = length // 2
    while h >= B:
        sizes.append(h)
        h //= 2
    return sizes


def row_pick(x, size, row):
    n, lanes = x.shape
    x3 = x.reshape(n // size, size, lanes)
    return jnp.broadcast_to(x3[:, row : row + 1, :], x3.shape).reshape(n, lanes)


class Common:
    def __init__(self, la, starts):
        length, lanes = la.shape
        self.length, self.lanes = length, lanes
        rows = lax.broadcasted_iota(jnp.int32, (length, lanes), 0)
        self.rows = rows
        self.lane_head = lax.broadcasted_iota(jnp.int32, (length, lanes), 1) // M
        c = la
        s = 1
        while s < length:
            c = c + jnp.where(rows >= s, shift_down(c, s), 0.0)
            s *= 2
        self.c = c
        self.alpha = jnp.exp(la)
        self.om = 1.0 - self.alpha
        self.levels = level_sizes(length)
        self.x = []
        for h in self.levels:
            mid = row_pick(c, 2 * h, h - 1)
            self.x.append(jnp.exp(-jnp.abs(c - mid)))
        t = lax.broadcasted_iota(jnp.int32, (length, length), 0)
        j = lax.broadcasted_iota(jnp.int32, (length, length), 1)
        same = same_document(t, j, starts)
        self.masks = [
            same & ((t // (2 * h)) == (j // (2 * h))) & ((t & h) != 0) & ((j & h) == 0)
            for h in self.levels
        ]
        tc = lax.broadcasted_iota(jnp.int32, (length, B), 0)
        off = lax.broadcasted_iota(jnp.int32, (length, B), 1)
        jc = (tc - tc % B) + off
        self.mask_c = same_document(tc, jc, starts) & (jc <= tc)

    def by_head(self, parts):
        out = parts[0]
        for i in range(1, len(parts)):
            out = jnp.where(self.lane_head == i, parts[i], out)
        return out

    def only(self, x, i):
        return jnp.where(self.lane_head == i, x, 0.0)

    def decay_from(self, jj):
        return jnp.exp(jnp.minimum(self.c - row_pick(self.c, B, jj), 0.0))

    def om_at(self, jj):
        return row_pick(self.om, B, jj)


def blocks(x):
    return x.reshape(x.shape[0] // B, B, x.shape[1])


def block_nt(a, b):
    r = lax.dot_general(
        blocks(a.astype(bf16)),
        blocks(b.astype(bf16)),
        (((2,), (2,)), ((0,), (0,))),
        preferred_element_type=f32,
    )
    return r.reshape(a.shape[0], B)


def block_nn(a, b):
    r = lax.dot_general(
        blocks(a.astype(bf16)),
        blocks(b.astype(bf16)),
        (((2,), (1,)), ((0,), (0,))),
        preferred_element_type=f32,
    )
    return r.reshape(a.shape[0], b.shape[1])


def block_tn(a, b):
    at = jnp.swapaxes(blocks(a), 1, 2).astype(bf16)
    r = lax.dot_general(
        at, blocks(b.astype(bf16)), (((2,), (1,)), ((0,), (0,))), preferred_element_type=f32
    )
    return r.reshape(a.shape[0], b.shape[1])


def collect(lanes, heads):
    r = lax.broadcasted_iota(jnp.int32, (B * lanes, heads * 128), 0)
    col = lax.broadcasted_iota(jnp.int32, (B * lanes, heads * 128), 1)
    jj, head = r // lanes, (r % lanes) // M
    return jnp.where(col == head * 128 + jj, 1.0, 0.0).astype(bf16)


def wide(x, jj):
    return jnp.broadcast_to(x[:, jj : jj + 1], (x.shape[0], 128))


def forward_math(q, k, v, la, starts):
    heads = q.shape[1] // DK
    scale = 1.0 / math.sqrt(DK)
    cm = Common(la, starts)
    qs = [q[:, i * DK : (i + 1) * DK] for i in range(heads)]
    ks = [k[:, i * DK : (i + 1) * DK] for i in range(heads)]
    vs = [v[:, i * DV : (i + 1) * DV] for i in range(heads)]
    aff = [nt(qs[i], ks[i]) * scale for i in range(heads)]
    affc = [jnp.where(cm.mask_c, block_nt(qs[i], ks[i]) * scale, 0.0) for i in range(heads)]
    s = jnp.zeros_like(la)
    parts = []
    for x, mask in zip(cm.x, cm.masks):
        g = x * cm.om
        part = x * cm.by_head([nn3(jnp.where(mask, aff[i], 0.0), g) for i in range(heads)])
        parts.append(part)
        s = s + part
    for jj in range(B):
        s = s + cm.by_head([wide(affc[i], jj) for i in range(heads)]) * (
            cm.decay_from(jj) * cm.om_at(jj)
        )
    top = cm.by_head(
        [
            jnp.max(jnp.where(cm.lane_head == i, s, -jnp.inf), axis=1, keepdims=True)
            for i in range(heads)
        ]
    )
    e = jnp.exp(s - top)
    total = cm.by_head([jnp.sum(cm.only(e, i), axis=1, keepdims=True) for i in range(heads)])
    p = e / total
    mix = [jnp.zeros((cm.length, cm.length), f32) for _ in range(heads)]
    for x, mask in zip(cm.x, cm.masks):
        g = x * cm.om
        px = p * x
        for i in range(heads):
            mix[i] = mix[i] + jnp.where(mask, nt(cm.only(px, i), g), 0.0)
    mix = [m.astype(bf16) for m in mix]
    pieces = [(p * (cm.decay_from(jj) * cm.om_at(jj))).astype(bf16) for jj in range(B)]
    mixc = nn(jnp.concatenate(pieces, axis=1), collect(cm.lanes, heads))
    mixc = [
        jnp.where(cm.mask_c, mixc[:, i * 128 : i * 128 + B], 0.0) for i in range(heads)
    ]
    outs = [nn(mix[i], vs[i]) + block_nn(mixc[i], vs[i]) for i in range(heads)]
    return outs, p, parts, mix, mixc


def backward_math(q, k, v, la, starts, p, parts, mix, mixc, dout):
    heads = q.shape[1] // DK
    scale = 1.0 / math.sqrt(DK)
    cm = Common(la, starts)
    qs = [q[:, i * DK : (i + 1) * DK] for i in range(heads)]
    ks = [k[:, i * DK : (i + 1) * DK] for i in range(heads)]
    vs = [v[:, i * DV : (i + 1) * DV] for i in range(heads)]
    dos = [dout[:, i * DV : (i + 1) * DV].astype(bf16) for i in range(heads)]
    aff = [nt(qs[i], ks[i]) * scale for i in range(heads)]
    affc = [jnp.where(cm.mask_c, block_nt(qs[i], ks[i]) * scale, 0.0) for i in range(heads)]
    dmix = [nt(dos[i], vs[i]) for i in range(heads)]
    dmixc = [jnp.where(cm.mask_c, block_nt(dos[i], vs[i]), 0.0) for i in range(heads)]
    dp = jnp.zeros_like(la)
    dparts = []
    for x, mask in zip(cm.x, cm.masks):
        g = x * cm.om
        part = x * cm.by_head([nn3(jnp.where(mask, dmix[i], 0.0), g) for i in range(heads)])
        dparts.append(part)
        dp = dp + part
    for jj in range(B):
        dp = dp + cm.by_head([wide(dmixc[i], jj) for i in range(heads)]) * (
            cm.decay_from(jj) * cm.om_at(jj)
        )
    pdp = p * dp
    inner = cm.by_head([jnp.sum(cm.only(pdp, i), axis=1, keepdims=True) for i in range(heads)])
    ds = pdp - p * inner
    daff = [jnp.zeros((cm.length, cm.length), f32) for _ in range(heads)]
    dla = jnp.zeros_like(la)
    reach = jnp.zeros_like(la)
    for n, h in enumerate(cm.levels):
        x, mask = cm.x[n], cm.masks[n]
        g = x * cm.om
        dsx, px = ds * x, p * x
        both = jnp.concatenate([dsx, px], axis=0).astype(bf16)
        cols = []
        for i in range(heads):
            daff[i] = daff[i] + jnp.where(mask, nt(cm.only(dsx, i), g), 0.0)
            left = jnp.concatenate(
                [jnp.where(mask, aff[i], 0.0), jnp.where(mask, dmix[i], 0.0)], axis=0
            )
            cols.append(tn(left, both))
        r = x * cm.by_head(cols)
        reach = reach + r
        right = (cm.rows & h) != 0
        flow = jnp.where(right, ds * parts[n] + p * dparts[n], cm.om * r)
        s = 1
        while s < h:
            flow = flow + jnp.where((cm.rows & (h - 1)) < h - s, shift_up(flow, s), 0.0)
            s *= 2
        dla = dla + jnp.where(right, flow, row_pick(flow, h, 0) - flow)
    flow = jnp.zeros_like(la)
    near = jnp.zeros_like(la)
    pieces = []
    for jj in range(B):
        w = cm.decay_from(jj)
        omj = cm.om_at(jj)
        aj = cm.by_head([wide(affc[i], jj) for i in range(heads)])
        dj = cm.by_head([wide(dmixc[i], jj) for i in range(heads)])
        pieces.append((ds * (w * omj)).astype(bf16))
        z = w * (aj * ds + dj * p)
        flow = flow + omj * z
        z3 = blocks(z)
        tot = jnp.broadcast_to(jnp.sum(z3, axis=1, keepdims=True), z3.shape).reshape(z.shape)
        near = jnp.where((cm.rows & (B - 1)) == jj, tot, near)
    flow = flow - cm.om * near
    s = 1
    while s < B:
        flow = flow + jnp.where((cm.rows & (B - 1)) < B - s, shift_up(flow, s), 0.0)
        s *= 2
    dla = dla + flow - cm.alpha * (reach + near)
    daffc = nn(jnp.concatenate(pieces, axis=1), collect(cm.lanes, heads))
    daffc = [
        jnp.where(cm.mask_c, daffc[:, i * 128 : i * 128 + B], 0.0) for i in range(heads)
    ]
    dq, dk, dv = [], [], []
    for i in range(heads):
        da = daff[i].astype(bf16)
        dq.append((nn(da, ks[i]) + block_nn(daffc[i], ks[i])) * scale)
        dk.append((tn(da, qs[i]) + block_tn(daffc[i], qs[i])) * scale)
        dv.append(tn(mix[i], dos[i]) + block_tn(mixc[i], dos[i]))
    return dq, dk, dv, dla


def head_split(outs, ref, width):
    for i, x in enumerate(outs):
        ref[:, i * width : (i + 1) * width] = x.astype(ref.dtype)


def forward_kernel(starts_ref, q_ref, k_ref, v_ref, la_ref, o_ref, p_ref, parts_ref, mix_ref, mixc_ref):
    starts = [starts_ref[0, n] for n in range(starts_ref.shape[1])]
    outs, p, parts, mix, mixc = forward_math(
        q_ref[...], k_ref[...], v_ref[...], la_ref[...], starts
    )
    head_split(outs, o_ref, DV)
    p_ref[...] = p
    for n, x in enumerate(parts):
        parts_ref[n] = x
    for i in range(len(mix)):
        mix_ref[i] = mix[i]
        mixc_ref[i] = mixc[i].astype(bf16)


def backward_kernel(
    starts_ref, q_ref, k_ref, v_ref, la_ref, p_ref, parts_ref, mix_ref, mixc_ref, do_ref,
    dq_ref, dk_ref, dv_ref, dla_ref,
):
    starts = [starts_ref[0, n] for n in range(starts_ref.shape[1])]
    heads = mix_ref.shape[0]
    dq, dk, dv, dla = backward_math(
        q_ref[...],
        k_ref[...],
        v_ref[...],
        la_ref[...],
        starts,
        p_ref[...],
        [parts_ref[n] for n in range(parts_ref.shape[0])],
        [mix_ref[i] for i in range(heads)],
        [mixc_ref[i] for i in range(heads)],
        do_ref[...],
    )
    head_split(dq, dq_ref, DK)
    head_split(dk, dk_ref, DK)
    head_split(dv, dv_ref, DV)
    dla_ref[...] = dla


SMEM = pl.BlockSpec(memory_space=pltpu.SMEM)
VMEM = pl.BlockSpec(memory_space=pltpu.VMEM)


def attend_forward(q, k, v, la, starts):
    length, lanes = la.shape
    heads = q.shape[1] // DK
    sds = jax.ShapeDtypeStruct
    return pl.pallas_call(
        forward_kernel,
        out_shape=(
            sds((length, heads * DV), bf16),
            sds((length, lanes), f32),
            sds((len(level_sizes(length)), length, lanes), f32),
            sds((heads, length, length), bf16),
            sds((heads, length, B), bf16),
        ),
        in_specs=[SMEM] + [VMEM] * 4,
        out_specs=(VMEM,) * 5,
        cost_estimate=pl.CostEstimate(
            flops=4 * 10**9, transcendentals=10**6, bytes_accessed=4 * 10**6
        ),
        name="slot_forward",
    )(starts, q, k, v, la)


def attend_backward(q, k, v, la, starts, saved, dout):
    length, lanes = la.shape
    sds = jax.ShapeDtypeStruct
    return pl.pallas_call(
        backward_kernel,
        out_shape=(
            sds(q.shape, f32),
            sds(k.shape, f32),
            sds(v.shape, f32),
            sds((length, lanes), f32),
        ),
        in_specs=[SMEM] + [VMEM] * 9,
        out_specs=(VMEM,) * 4,
        cost_estimate=pl.CostEstimate(
            flops=12 * 10**9, transcendentals=10**6, bytes_accessed=8 * 10**6
        ),
        name="slot_backward",
    )(starts, q, k, v, la, *saved, dout)


eps = 1e-06
tau_inv = 0.125
INNER = 4
LAP = (0, 1, 3, 2)


def rms_scale(values):
    return lax.rsqrt(jnp.mean(values * values, axis=-1, keepdims=True) + eps)


def norm_back(values, scale, gain, upstream):
    gain_grad = jnp.sum(upstream * values * scale, axis=0, keepdims=True)
    weighted = upstream * gain
    input_grad = scale * weighted - values * (scale * scale * scale) * jnp.mean(
        weighted * values, axis=-1, keepdims=True
    )
    return (gain_grad, input_grad)


def silu_slope(values):
    sigmoid_val = jax.nn.sigmoid(values)
    return sigmoid_val * (1.0 + values * (1.0 - sigmoid_val))


class Grid:
    def __init__(self, dp):
        self.dp = dp
        self.outer = dp // INNER
        self.laps = [[o * INNER + i for i in LAP] for o in range(self.outer)]
        self.rows = [[o * INNER + i for i in range(INNER)] for o in range(self.outer)]
        self.cols = [[o * INNER + i for o in range(self.outer)] for i in range(INNER)]
        self.gathered = [o * INNER + i for i in LAP for o in range(self.outer)]
        self.natural = inverse(self.gathered)
        self.up = [(d, d + INNER) for d in range(dp - INNER)]
        self.down = [(d + INNER, d) for d in range(dp - INNER)]


def reorder(x, order):
    size = x.shape[-1] // len(order)
    return jnp.concatenate([x[..., b * size : (b + 1) * size] for b in order], axis=-1)


def inverse(order):
    back = [0] * len(order)
    for n, b in enumerate(order):
        back[b] = n
    return back


def swap(x):
    return lax.ppermute(x, "head", [(0, 1), (1, 0)])


def half_of(x, which):
    size = x.shape[0] // 2
    return lax.dynamic_slice_in_dim(x, which * size, size, 0)


def join(mine, other, core):
    size = mine.shape[0]
    out = jnp.zeros((2 * size,) + mine.shape[1:], mine.dtype)
    out = lax.dynamic_update_slice_in_dim(out, mine, core * size, 0)
    return lax.dynamic_update_slice_in_dim(out, other, (1 - core) * size, 0)


def on_rows(kernel, name, core, halves, wholes, outs):
    rows = halves[0].shape[0] // 2
    specs = [pl.BlockSpec((rows, x.shape[1]), lambda i, c: (c[0], 0)) for x in halves]
    specs += [pl.BlockSpec(x.shape, lambda i, c: (0, 0)) for x in wholes]
    return pl.pallas_call(
        kernel,
        out_shape=outs,
        grid_spec=pltpu.PrefetchScalarGridSpec(
            num_scalar_prefetch=1,
            grid=(1,),
            in_specs=specs,
            out_specs=[pl.BlockSpec(x.shape, lambda i, c: (0, 0)) for x in outs],
        ),
        name=name,
    )(core.reshape(1), *halves, *wholes)


def aligned(grid, width):
    return (width // grid.dp) % 128 == 0


def put_in_order(x, order, grid, inside):
    return reorder(x, order) if aligned(grid, x.shape[1]) == inside else x


def cotangent_rows(out_grad, core, grid):
    rows, width = out_grad.shape

    def kernel(core_ref, cot_ref, out_ref):
        out_ref[...] = put_in_order(cot_ref[...], grid.gathered, grid, True)

    outs = [jax.ShapeDtypeStruct((rows // 2, width), bf16)]
    (x,) = on_rows(kernel, "cotangent_rows", core, [out_grad], [], outs)
    return put_in_order(x, grid.gathered, grid, False)


def second_norm(block_in, mine, other, gain, core, grid):
    rows, width = mine.shape

    def kernel(core_ref, in_ref, mine_ref, other_ref, gain_ref, hidden_ref, normed_ref):
        hidden = in_ref[...].astype(f32) + (mine_ref[...] + other_ref[...])
        hidden_ref[...] = hidden
        normed = (hidden * rms_scale(hidden) * gain_ref[...]).astype(bf16)
        normed_ref[...] = put_in_order(normed, grid.gathered, grid, True)

    outs = [jax.ShapeDtypeStruct((rows, width), f32), jax.ShapeDtypeStruct((rows, width), bf16)]
    hidden, normed = on_rows(
        kernel, "second_norm", core, [block_in], [mine, other, gain[None]], outs
    )
    return hidden, put_in_order(normed, grid.gathered, grid, False)


def second_norm_back(out_grad, hidden, gain, parts, core, grid):
    rows, width = hidden.shape
    parts = [put_in_order(x, grid.natural, grid, False) for x in parts]

    def kernel(core_ref, cot_ref, hidden_ref, gain_ref, *refs):
        upstream = sum(x[...].astype(f32) for x in refs[: len(parts)])
        upstream = put_in_order(upstream, grid.natural, grid, True)
        grad_ref, low_ref, gain_grad_ref = refs[len(parts) :]
        hidden = hidden_ref[...]
        gain_grad, grad = norm_back(hidden, rms_scale(hidden), gain_ref[...], upstream)
        grad = grad + cot_ref[...].astype(f32)
        grad_ref[...] = grad
        low_ref[...] = grad.astype(bf16)
        gain_grad_ref[...] = gain_grad

    sds = jax.ShapeDtypeStruct
    outs = [sds((rows, width), f32), sds((rows, width), bf16), sds((1, width), f32)]
    return on_rows(
        kernel, "second_norm_back", core, [out_grad], [hidden, gain[None], *parts], outs
    )


def first_norm_back(block_in, grad, gain, mine, other, core):
    rows, width = grad.shape

    def kernel(core_ref, in_ref, grad_ref, gain_ref, mine_ref, other_ref, out_ref, gain_grad_ref):
        inputs = in_ref[...].astype(f32)
        upstream = mine_ref[...] + other_ref[...]
        gain_grad, out = norm_back(inputs, rms_scale(inputs), gain_ref[...], upstream)
        out_ref[...] = out + grad_ref[...]
        gain_grad_ref[...] = gain_grad

    sds = jax.ShapeDtypeStruct
    outs = [sds((rows, width), f32), sds((1, width), f32)]
    return on_rows(
        kernel, "first_norm_back", core, [block_in], [grad, gain[None], mine, other], outs
    )


def block_result(block_in, hidden, parts, core, grid):
    rows, width = hidden.shape
    parts = [put_in_order(x, grid.natural, grid, False) for x in parts]

    def kernel(core_ref, in_ref, hidden_ref, *refs):
        out = sum(x[...].astype(f32) for x in refs[: len(parts)])
        out = put_in_order(out, grid.natural, grid, True)
        refs[-1][...] = (hidden_ref[...] + out).astype(bf16)

    outs = [jax.ShapeDtypeStruct((rows, width), bf16)]
    (x,) = on_rows(kernel, "block_result", core, [block_in], [hidden, *parts], outs)
    return x


def exchange(x, split, concat, groups):
    return lax.all_to_all(x, "dp", split, concat, tiled=True, axis_index_groups=groups)


def tie(*values):
    return lax.optimization_barrier(values)


def gather_along(x, grid, place, beside=()):
    n = grid.outer
    above = below = x
    from_below, from_above, done = [], [], []
    for k in range(n - 1):
        below = lax.ppermute(below, "dp", grid.up)
        above = lax.ppermute(above, "dp", grid.down)
        extra = beside[k] if k < len(beside) else ()
        below, above, *extra = tie(below, above, *extra)
        from_below.append(below)
        from_above.append(above)
        done += extra
    blocks = [x]
    for k in range(1, n):
        blocks.append(jnp.where(place + k < n, from_above[k - 1], from_below[n - 1 - k]))
    return jnp.concatenate(blocks, axis=0), done


def with_other_core(own):
    return jnp.concatenate([own, swap(own)], axis=0)


def scatter_tokens(x, grid, beside=()):
    n = grid.outer
    size = x.shape[0] // (2 * n)
    block = [x[k * size : (k + 1) * size] for k in range(2 * n)]
    order = [k for s in range(1, n) for k in (n - s, s)]
    order = list(dict.fromkeys(order)) + [0]
    swapped = {k: swap(block[n + k].astype(bf16)) for k in order}
    own = {k: block[k] + swapped[k].astype(f32) for k in order}
    up = down = None
    done = []
    for k in range(n - 1):
        up = own[n - 1 - k] if up is None else own[n - 1 - k] + up.astype(f32)
        down = own[1 + k] if down is None else own[1 + k] + down.astype(f32)
        up = lax.ppermute(up.astype(bf16), "dp", grid.up)
        down = lax.ppermute(down.astype(bf16), "dp", grid.down)
        extra = beside[k] if k < len(beside) else ()
        up, down, *extra = tie(up, down, *extra)
        done += extra
    return (own[0], up, down), done


def plane_gather(x, grid, inner):
    out = jnp.zeros((INNER,) + x.shape, x.dtype)
    for k in range(INNER):
        y = x
        if k:
            y = lax.ppermute(x, "dp", [(d, d ^ k) for d in range(grid.dp)])
        out = lax.dynamic_update_slice_in_dim(out, y[None], inner ^ k, 0)
    return out.reshape(INNER * x.shape[0], x.shape[1])


def on_device(
    block_in,
    out_grad,
    attn_gain,
    mlp_gain,
    w_query,
    w_key,
    w_value,
    w_forget,
    w_output,
    w_gate,
    w_up,
    w_down,
    doc_starts,
    grid,
):
    core = lax.axis_index("head")
    place = lax.axis_index("dp") // INNER
    inner = lax.axis_index("dp") % INNER

    def columns(w):
        return exchange(w, 1, 0, grid.cols)

    def gather_rows(w):
        return lax.all_gather(w, "dp", axis=0, tiled=True, axis_index_groups=grid.laps)

    gate_piece, up_piece, down_piece = columns(w_gate), columns(w_up), columns(w_down)

    inputs_f = block_in.astype(f32)
    normed = (inputs_f * rms_scale(inputs_f) * attn_gain).astype(bf16)
    query_pre = nn(normed, w_query)
    later, query_pre, gate_piece = tie(normed, query_pre, gate_piece)
    full_gate = gather_rows(gate_piece)
    key_pre = nn(later, w_key)
    value_pre = nn(later, w_value)
    forget_pre = nn(later, w_forget)
    query = jax.nn.silu(query_pre).astype(bf16)
    key = jax.nn.silu(key_pre).astype(bf16)
    value = jax.nn.silu(value_pre).astype(bf16)
    log_keep = jax.nn.log_sigmoid(forget_pre) * tau_inv
    key, value, log_keep, up_piece = tie(key, value, log_keep, up_piece)
    full_up = gather_rows(up_piece)
    mixed, *saved = attend_forward(query, key, value, log_keep, doc_starts)

    branch_other = swap(nt(half_of(mixed, 1 - core), w_output))
    branch_mine = nt(half_of(mixed, core), w_output)
    branch_mine, down_piece = tie(branch_mine, down_piece)
    full_down = gather_rows(down_piece)
    hidden, normed_two = second_norm(block_in, branch_mine, branch_other, mlp_gain, core, grid)
    def plane_tokens(half):
        own = plane_gather(half, grid, inner)
        return own, swap(own)

    def plane_columns(parts):
        rows = parts[0].shape[0]
        x = jnp.concatenate([p.reshape(rows, INNER, -1) for p in parts], axis=2)
        size = x.shape[2]
        x = exchange(x.reshape(rows, INNER * size), 1, 0, grid.rows)
        x = x.reshape(INNER, 2, rows // 2, size)
        return tuple(
            lax.dynamic_index_in_dim(x, c, 1, keepdims=False).reshape(-1, size)
            for c in (core, 1 - core)
        )

    def plane_product(left, right):
        return (tn(left[0], right[0]) + tn(left[1], right[1])).astype(bf16)

    def plane_sum(g):
        return lax.psum_scatter(
            g, "dp", scatter_dimension=0, tiled=True, axis_index_groups=grid.cols
        )

    def from_plane(g):
        size = g.shape[1]
        return exchange(g, 0, 1, grid.rows).reshape(-1, INNER, size).astype(f32)

    cot_rows = cotangent_rows(out_grad, core, grid)
    own, (cot_rows, full_gate, full_up) = gather_along(
        normed_two, grid, place, ((cot_rows,), (full_gate,), (full_up,))
    )
    tokens = with_other_core(own)
    own, (gate_act, up_act, full_down) = gather_along(
        cot_rows, grid, place, ((nn(tokens, full_gate),), (nn(tokens, full_up),), (full_down,))
    )
    cot_all = with_other_core(own)

    def scatter_rows(g):
        return lax.psum_scatter(
            g, "dp", scatter_dimension=0, tiled=True, axis_index_groups=grid.laps
        )

    mixed_plane = plane_columns([mixed])
    normed_plane = plane_tokens(half_of(normed, core))
    inner_grad = nn(cot_all, full_down)
    gate_grad = (inner_grad * up_act * silu_slope(gate_act)).astype(bf16)
    up_grad = (inner_grad * jax.nn.silu(gate_act)).astype(bf16)
    inner_act = (jax.nn.silu(gate_act) * up_act).astype(bf16)
    back_parts, (down_rows, gate_rows, mixed_own, mixed_rest, up_rows, *normed_plane) = scatter_tokens(
        nt(gate_grad, full_gate) + nt(up_grad, full_up),
        grid,
        (
            (tn(cot_all, inner_act).astype(bf16),),
            (tn(tokens, gate_grad).astype(bf16), *mixed_plane),
            (tn(tokens, up_grad).astype(bf16), *normed_plane),
        ),
    )
    mixed_plane = (mixed_own, mixed_rest)
    down_rows, gate_rows, up_rows = (scatter_rows(g) for g in (down_rows, gate_rows, up_rows))
    hidden_grad, low_half, mlp_gain_part = second_norm_back(
        out_grad, hidden, mlp_gain, back_parts, core, grid
    )
    branch_grad = join(low_half, swap(low_half), core)
    mixed_grad = nn(branch_grad, w_output).astype(bf16)
    mixed_grad, down_rows, later_act = tie(mixed_grad, down_rows, inner_act)
    saved_grads = attend_backward(query, key, value, log_keep, doc_starts, saved, mixed_grad)
    query_grad, key_grad, value_grad, log_grad = saved_grads
    query_pre_grad = (query_grad * silu_slope(query_pre)).astype(bf16)
    key_pre_grad = (key_grad * silu_slope(key_pre)).astype(bf16)
    value_pre_grad = (value_grad * silu_slope(value_pre)).astype(bf16)
    forget_pre_grad = (log_grad * tau_inv * jax.nn.sigmoid(-forget_pre)).astype(bf16)
    pre_grads = (query_pre_grad, key_pre_grad, value_pre_grad, forget_pre_grad)

    query_pre_grad, gate_rows = tie(query_pre_grad, gate_rows)
    pre_grads = (query_pre_grad,) + pre_grads[1:]
    out_parts, (query_pre_grad, *grad_columns) = scatter_tokens(
        nt(later_act, full_down), grid, ((query_pre_grad,), tuple(plane_columns(pre_grads)))
    )
    pre_grads = (query_pre_grad,) + pre_grads[1:]
    output_grad = plane_product(plane_tokens(low_half), mixed_plane)
    pre_grad, up_rows, output_grad = tie(
        plane_product(normed_plane, grad_columns), up_rows, output_grad
    )
    output_sum = from_plane(plane_sum(output_grad))
    sums = plane_sum(pre_grad)

    result = block_result(block_in, hidden, out_parts, core, grid)
    result = join(result, swap(result), core)

    sums = from_plane(sums)
    ends = [0]
    for g in pre_grads:
        ends.append(ends[-1] + g.shape[1] // INNER)
    query_sum, key_sum, value_sum, forget_sum = (
        sums[:, :, a:b].reshape(sums.shape[0], -1) for a, b in zip(ends, ends[1:])
    )

    def normed_part(which):
        q, k, v, f = (half_of(g, which) for g in pre_grads)
        return nt(q, w_query) + nt(k, w_key) + nt(v, w_value) + nt(f, w_forget)

    part_other = swap(normed_part(1 - core))
    input_grad, attn_gain_part = first_norm_back(
        block_in, hidden_grad, attn_gain, normed_part(core), part_other, core
    )
    input_grad = join(input_grad, swap(input_grad), core)

    gains = jnp.concatenate([attn_gain_part, mlp_gain_part], axis=0)
    gains = gains + swap(gains)
    gains = jnp.swapaxes(gains.reshape(2, grid.dp, -1), 0, 1)
    gains = jnp.sum(lax.all_to_all(gains, "dp", 0, 0, tiled=True), axis=0)

    def to_columns(g):
        return exchange(g, 0, 1, grid.cols).astype(f32)

    return (
        result,
        input_grad,
        gains[0],
        gains[1],
        query_sum,
        key_sum,
        value_sum,
        forget_sum,
        output_sum.reshape(output_sum.shape[0], -1),
        to_columns(gate_rows),
        to_columns(up_rows),
        to_columns(down_rows),
    )


def solution(mesh):
    placed = (
        P("dp", None),
        P("dp", None),
        P(),
        P(),
        P(None, "head"),
        P(None, "head"),
        P(None, "head"),
        P(None, "head"),
        P(None, "head"),
        P("dp", "head"),
        P("dp", "head"),
        P("dp", "head"),
        P("dp", None),
    )
    return jax.shard_map(
        partial(on_device, grid=Grid(mesh.shape["dp"])),
        mesh=mesh,
        in_specs=placed,
        out_specs=(P("dp", None), P("dp", None), P("dp"), P("dp")) + (P("dp", "head"),) * 8,
        check_vma=False,
    )
```

```python
import math
from functools import partial
import jax
import jax.numpy as jnp
from jax import lax
from jax.experimental import pallas as pl
from jax.experimental.pallas import tpu as pltpu
from jax.sharding import PartitionSpec as P

DK = 512
DV = 512
M = 64
B = 16
f32 = jnp.float32
bf16 = jnp.bfloat16


def nn(a, b):
    return jnp.dot(a.astype(bf16), b.astype(bf16), preferred_element_type=f32)


def nt(a, b):
    return lax.dot_general(
        a.astype(bf16), b.astype(bf16), (((1,), (1,)), ((), ())), preferred_element_type=f32
    )


def tn(a, b):
    return lax.dot_general(
        a.astype(bf16), b.astype(bf16), (((0,), (0,)), ((), ())), preferred_element_type=f32
    )


def nn3(a, b):
    ah, bh = a.astype(bf16), b.astype(bf16)
    al, bl = (a - ah.astype(f32)).astype(bf16), (b - bh.astype(f32)).astype(bf16)
    return nn(ah, bh) + (nn(al, bh) + nn(ah, bl))


def shift_up(x, s):
    return pltpu.roll(x, x.shape[0] - s, 0)


def shift_down(x, s):
    return pltpu.roll(x, s, 0)


def segment_at(pos, starts):
    seg = jnp.zeros(pos.shape, jnp.int32)
    for s in starts:
        seg = seg + (pos >= s).astype(jnp.int32)
    return seg


def same_document(t, j, starts):
    ok = None
    for s in starts:
        same = (t >= s) == (j >= s)
        ok = same if ok is None else ok & same
    return ok


def level_sizes(length):
    sizes = []
    h = length // 2
    while h >= B:
        sizes.append(h)
        h //= 2
    return sizes


def row_pick(x, size, row):
    n, lanes = x.shape
    x3 = x.reshape(n // size, size, lanes)
    return jnp.broadcast_to(x3[:, row : row + 1, :], x3.shape).reshape(n, lanes)


class Common:
    def __init__(self, la, starts):
        length, lanes = la.shape
        self.length, self.lanes = length, lanes
        rows = lax.broadcasted_iota(jnp.int32, (length, lanes), 0)
        self.rows = rows
        self.lane_head = lax.broadcasted_iota(jnp.int32, (length, lanes), 1) // M
        c = la
        s = 1
        while s < length:
            c = c + jnp.where(rows >= s, shift_down(c, s), 0.0)
            s *= 2
        self.c = c
        self.alpha = jnp.exp(la)
        self.om = 1.0 - self.alpha
        self.levels = level_sizes(length)
        self.x = []
        for h in self.levels:
            mid = row_pick(c, 2 * h, h - 1)
            self.x.append(jnp.exp(-jnp.abs(c - mid)))
        t = lax.broadcasted_iota(jnp.int32, (length, length), 0)
        j = lax.broadcasted_iota(jnp.int32, (length, length), 1)
        same = same_document(t, j, starts)
        self.masks = [
            same & ((t // (2 * h)) == (j // (2 * h))) & ((t & h) != 0) & ((j & h) == 0)
            for h in self.levels
        ]
        tc = lax.broadcasted_iota(jnp.int32, (length, B), 0)
        off = lax.broadcasted_iota(jnp.int32, (length, B), 1)
        jc = (tc - tc % B) + off
        self.mask_c = same_document(tc, jc, starts) & (jc <= tc)

    def by_head(self, parts):
        out = parts[0]
        for i in range(1, len(parts)):
            out = jnp.where(self.lane_head == i, parts[i], out)
        return out

    def only(self, x, i):
        return jnp.where(self.lane_head == i, x, 0.0)

    def decay_from(self, jj):
        return jnp.exp(jnp.minimum(self.c - row_pick(self.c, B, jj), 0.0))

    def om_at(self, jj):
        return row_pick(self.om, B, jj)


def blocks(x):
    return x.reshape(x.shape[0] // B, B, x.shape[1])


def block_nt(a, b):
    r = lax.dot_general(
        blocks(a.astype(bf16)),
        blocks(b.astype(bf16)),
        (((2,), (2,)), ((0,), (0,))),
        preferred_element_type=f32,
    )
    return r.reshape(a.shape[0], B)


def block_nn(a, b):
    r = lax.dot_general(
        blocks(a.astype(bf16)),
        blocks(b.astype(bf16)),
        (((2,), (1,)), ((0,), (0,))),
        preferred_element_type=f32,
    )
    return r.reshape(a.shape[0], b.shape[1])


def block_tn(a, b):
    at = jnp.swapaxes(blocks(a), 1, 2).astype(bf16)
    r = lax.dot_general(
        at, blocks(b.astype(bf16)), (((2,), (1,)), ((0,), (0,))), preferred_element_type=f32
    )
    return r.reshape(a.shape[0], b.shape[1])


def collect(lanes, heads):
    r = lax.broadcasted_iota(jnp.int32, (B * lanes, heads * 128), 0)
    col = lax.broadcasted_iota(jnp.int32, (B * lanes, heads * 128), 1)
    jj, head = r // lanes, (r % lanes) // M
    return jnp.where(col == head * 128 + jj, 1.0, 0.0).astype(bf16)


def wide(x, jj):
    return jnp.broadcast_to(x[:, jj : jj + 1], (x.shape[0], 128))


def forward_math(q, k, v, la, starts):
    heads = q.shape[1] // DK
    scale = 1.0 / math.sqrt(DK)
    cm = Common(la, starts)
    qs = [q[:, i * DK : (i + 1) * DK] for i in range(heads)]
    ks = [k[:, i * DK : (i + 1) * DK] for i in range(heads)]
    vs = [v[:, i * DV : (i + 1) * DV] for i in range(heads)]
    aff = [nt(qs[i], ks[i]) * scale for i in range(heads)]
    affc = [jnp.where(cm.mask_c, block_nt(qs[i], ks[i]) * scale, 0.0) for i in range(heads)]
    s = jnp.zeros_like(la)
    parts = []
    for x, mask in zip(cm.x, cm.masks):
        g = x * cm.om
        part = x * cm.by_head([nn3(jnp.where(mask, aff[i], 0.0), g) for i in range(heads)])
        parts.append(part)
        s = s + part
    for jj in range(B):
        s = s + cm.by_head([wide(affc[i], jj) for i in range(heads)]) * (
            cm.decay_from(jj) * cm.om_at(jj)
        )
    top = cm.by_head(
        [
            jnp.max(jnp.where(cm.lane_head == i, s, -jnp.inf), axis=1, keepdims=True)
            for i in range(heads)
        ]
    )
    e = jnp.exp(s - top)
    total = cm.by_head([jnp.sum(cm.only(e, i), axis=1, keepdims=True) for i in range(heads)])
    p = e / total
    mix = [jnp.zeros((cm.length, cm.length), f32) for _ in range(heads)]
    for x, mask in zip(cm.x, cm.masks):
        g = x * cm.om
        px = p * x
        for i in range(heads):
            mix[i] = mix[i] + jnp.where(mask, nt(cm.only(px, i), g), 0.0)
    mix = [m.astype(bf16) for m in mix]
    pieces = [(p * (cm.decay_from(jj) * cm.om_at(jj))).astype(bf16) for jj in range(B)]
    mixc = nn(jnp.concatenate(pieces, axis=1), collect(cm.lanes, heads))
    mixc = [
        jnp.where(cm.mask_c, mixc[:, i * 128 : i * 128 + B], 0.0) for i in range(heads)
    ]
    outs = [nn(mix[i], vs[i]) + block_nn(mixc[i], vs[i]) for i in range(heads)]
    return outs, p, parts, mix, mixc


def backward_math(q, k, v, la, starts, p, parts, mix, mixc, dout):
    heads = q.shape[1] // DK
    scale = 1.0 / math.sqrt(DK)
    cm = Common(la, starts)
    qs = [q[:, i * DK : (i + 1) * DK] for i in range(heads)]
    ks = [k[:, i * DK : (i + 1) * DK] for i in range(heads)]
    vs = [v[:, i * DV : (i + 1) * DV] for i in range(heads)]
    dos = [dout[:, i * DV : (i + 1) * DV].astype(bf16) for i in range(heads)]
    aff = [nt(qs[i], ks[i]) * scale for i in range(heads)]
    affc = [jnp.where(cm.mask_c, block_nt(qs[i], ks[i]) * scale, 0.0) for i in range(heads)]
    dmix = [nt(dos[i], vs[i]) for i in range(heads)]
    dmixc = [jnp.where(cm.mask_c, block_nt(dos[i], vs[i]), 0.0) for i in range(heads)]
    dp = jnp.zeros_like(la)
    dparts = []
    for x, mask in zip(cm.x, cm.masks):
        g = x * cm.om
        part = x * cm.by_head([nn3(jnp.where(mask, dmix[i], 0.0), g) for i in range(heads)])
        dparts.append(part)
        dp = dp + part
    for jj in range(B):
        dp = dp + cm.by_head([wide(dmixc[i], jj) for i in range(heads)]) * (
            cm.decay_from(jj) * cm.om_at(jj)
        )
    pdp = p * dp
    inner = cm.by_head([jnp.sum(cm.only(pdp, i), axis=1, keepdims=True) for i in range(heads)])
    ds = pdp - p * inner
    daff = [jnp.zeros((cm.length, cm.length), f32) for _ in range(heads)]
    dla = jnp.zeros_like(la)
    reach = jnp.zeros_like(la)
    for n, h in enumerate(cm.levels):
        x, mask = cm.x[n], cm.masks[n]
        g = x * cm.om
        dsx, px = ds * x, p * x
        both = jnp.concatenate([dsx, px], axis=0).astype(bf16)
        cols = []
        for i in range(heads):
            daff[i] = daff[i] + jnp.where(mask, nt(cm.only(dsx, i), g), 0.0)
            left = jnp.concatenate(
                [jnp.where(mask, aff[i], 0.0), jnp.where(mask, dmix[i], 0.0)], axis=0
            )
            cols.append(tn(left, both))
        r = x * cm.by_head(cols)
        reach = reach + r
        right = (cm.rows & h) != 0
        flow = jnp.where(right, ds * parts[n] + p * dparts[n], cm.om * r)
        s = 1
        while s < h:
            flow = flow + jnp.where((cm.rows & (h - 1)) < h - s, shift_up(flow, s), 0.0)
            s *= 2
        dla = dla + jnp.where(right, flow, row_pick(flow, h, 0) - flow)
    flow = jnp.zeros_like(la)
    near = jnp.zeros_like(la)
    pieces = []
    for jj in range(B):
        w = cm.decay_from(jj)
        omj = cm.om_at(jj)
        aj = cm.by_head([wide(affc[i], jj) for i in range(heads)])
        dj = cm.by_head([wide(dmixc[i], jj) for i in range(heads)])
        pieces.append((ds * (w * omj)).astype(bf16))
        z = w * (aj * ds + dj * p)
        flow = flow + omj * z
        z3 = blocks(z)
        tot = jnp.broadcast_to(jnp.sum(z3, axis=1, keepdims=True), z3.shape).reshape(z.shape)
        near = jnp.where((cm.rows & (B - 1)) == jj, tot, near)
    flow = flow - cm.om * near
    s = 1
    while s < B:
        flow = flow + jnp.where((cm.rows & (B - 1)) < B - s, shift_up(flow, s), 0.0)
        s *= 2
    dla = dla + flow - cm.alpha * (reach + near)
    daffc = nn(jnp.concatenate(pieces, axis=1), collect(cm.lanes, heads))
    daffc = [
        jnp.where(cm.mask_c, daffc[:, i * 128 : i * 128 + B], 0.0) for i in range(heads)
    ]
    dq, dk, dv = [], [], []
    for i in range(heads):
        da = daff[i].astype(bf16)
        dq.append((nn(da, ks[i]) + block_nn(daffc[i], ks[i])) * scale)
        dk.append((tn(da, qs[i]) + block_tn(daffc[i], qs[i])) * scale)
        dv.append(tn(mix[i], dos[i]) + block_tn(mixc[i], dos[i]))
    return dq, dk, dv, dla


def head_split(outs, ref, width):
    for i, x in enumerate(outs):
        ref[:, i * width : (i + 1) * width] = x.astype(ref.dtype)


def forward_kernel(starts_ref, q_ref, k_ref, v_ref, la_ref, o_ref, p_ref, parts_ref, mix_ref, mixc_ref):
    starts = [starts_ref[0, n] for n in range(starts_ref.shape[1])]
    outs, p, parts, mix, mixc = forward_math(
        q_ref[...], k_ref[...], v_ref[...], la_ref[...], starts
    )
    head_split(outs, o_ref, DV)
    p_ref[...] = p
    for n, x in enumerate(parts):
        parts_ref[n] = x
    for i in range(len(mix)):
        mix_ref[i] = mix[i]
        mixc_ref[i] = mixc[i].astype(bf16)


def backward_kernel(
    starts_ref, q_ref, k_ref, v_ref, la_ref, p_ref, parts_ref, mix_ref, mixc_ref, do_ref,
    dq_ref, dk_ref, dv_ref, dla_ref,
):
    starts = [starts_ref[0, n] for n in range(starts_ref.shape[1])]
    heads = mix_ref.shape[0]
    dq, dk, dv, dla = backward_math(
        q_ref[...],
        k_ref[...],
        v_ref[...],
        la_ref[...],
        starts,
        p_ref[...],
        [parts_ref[n] for n in range(parts_ref.shape[0])],
        [mix_ref[i] for i in range(heads)],
        [mixc_ref[i] for i in range(heads)],
        do_ref[...],
    )
    head_split(dq, dq_ref, DK)
    head_split(dk, dk_ref, DK)
    head_split(dv, dv_ref, DV)
    dla_ref[...] = dla


SMEM = pl.BlockSpec(memory_space=pltpu.SMEM)
VMEM = pl.BlockSpec(memory_space=pltpu.VMEM)


def attend_forward(q, k, v, la, starts):
    length, lanes = la.shape
    heads = q.shape[1] // DK
    sds = jax.ShapeDtypeStruct
    return pl.pallas_call(
        forward_kernel,
        out_shape=(
            sds((length, heads * DV), bf16),
            sds((length, lanes), f32),
            sds((len(level_sizes(length)), length, lanes), f32),
            sds((heads, length, length), bf16),
            sds((heads, length, B), bf16),
        ),
        in_specs=[SMEM] + [VMEM] * 4,
        out_specs=(VMEM,) * 5,
        cost_estimate=pl.CostEstimate(
            flops=4 * 10**9, transcendentals=10**6, bytes_accessed=4 * 10**6
        ),
        name="slot_forward",
    )(starts, q, k, v, la)


def attend_backward(q, k, v, la, starts, saved, dout):
    length, lanes = la.shape
    sds = jax.ShapeDtypeStruct
    return pl.pallas_call(
        backward_kernel,
        out_shape=(
            sds(q.shape, f32),
            sds(k.shape, f32),
            sds(v.shape, f32),
            sds((length, lanes), f32),
        ),
        in_specs=[SMEM] + [VMEM] * 9,
        out_specs=(VMEM,) * 4,
        cost_estimate=pl.CostEstimate(
            flops=12 * 10**9, transcendentals=10**6, bytes_accessed=8 * 10**6
        ),
        name="slot_backward",
    )(starts, q, k, v, la, *saved, dout)


eps = 1e-06
tau_inv = 0.125
INNER = 4
LAP = (0, 1, 3, 2)


def rms_scale(values):
    return lax.rsqrt(jnp.mean(values * values, axis=-1, keepdims=True) + eps)


def norm_back(values, scale, gain, upstream):
    gain_grad = jnp.sum(upstream * values * scale, axis=0, keepdims=True)
    weighted = upstream * gain
    input_grad = scale * weighted - values * (scale * scale * scale) * jnp.mean(
        weighted * values, axis=-1, keepdims=True
    )
    return (gain_grad, input_grad)


def silu_slope(values):
    sigmoid_val = jax.nn.sigmoid(values)
    return sigmoid_val * (1.0 + values * (1.0 - sigmoid_val))


class Grid:
    def __init__(self, dp):
        self.dp = dp
        self.outer = dp // INNER
        self.laps = [[o * INNER + i for i in LAP] for o in range(self.outer)]
        self.rows = [[o * INNER + i for i in range(INNER)] for o in range(self.outer)]
        self.cols = [[o * INNER + i for o in range(self.outer)] for i in range(INNER)]
        self.gathered = [o * INNER + i for i in LAP for o in range(self.outer)]
        self.natural = inverse(self.gathered)
        self.up = [(d, d + INNER) for d in range(dp - INNER)]
        self.down = [(d + INNER, d) for d in range(dp - INNER)]


def reorder(x, order):
    size = x.shape[-1] // len(order)
    return jnp.concatenate([x[..., b * size : (b + 1) * size] for b in order], axis=-1)


def inverse(order):
    back = [0] * len(order)
    for n, b in enumerate(order):
        back[b] = n
    return back


def swap(x):
    return lax.ppermute(x, "head", [(0, 1), (1, 0)])


def half_of(x, which):
    size = x.shape[0] // 2
    return lax.dynamic_slice_in_dim(x, which * size, size, 0)


def join(mine, other, core):
    size = mine.shape[0]
    out = jnp.zeros((2 * size,) + mine.shape[1:], mine.dtype)
    out = lax.dynamic_update_slice_in_dim(out, mine, core * size, 0)
    return lax.dynamic_update_slice_in_dim(out, other, (1 - core) * size, 0)


def on_rows(kernel, name, core, halves, wholes, outs):
    rows = halves[0].shape[0] // 2
    specs = [pl.BlockSpec((rows, x.shape[1]), lambda i, c: (c[0], 0)) for x in halves]
    specs += [pl.BlockSpec(x.shape, lambda i, c: (0, 0)) for x in wholes]
    return pl.pallas_call(
        kernel,
        out_shape=outs,
        grid_spec=pltpu.PrefetchScalarGridSpec(
            num_scalar_prefetch=1,
            grid=(1,),
            in_specs=specs,
            out_specs=[pl.BlockSpec(x.shape, lambda i, c: (0, 0)) for x in outs],
        ),
        name=name,
    )(core.reshape(1), *halves, *wholes)


def aligned(grid, width):
    return (width // grid.dp) % 128 == 0


def put_in_order(x, order, grid, inside):
    return reorder(x, order) if aligned(grid, x.shape[1]) == inside else x


def cotangent_rows(out_grad, core, grid):
    rows, width = out_grad.shape

    def kernel(core_ref, cot_ref, out_ref):
        out_ref[...] = put_in_order(cot_ref[...], grid.gathered, grid, True)

    outs = [jax.ShapeDtypeStruct((rows // 2, width), bf16)]
    (x,) = on_rows(kernel, "cotangent_rows", core, [out_grad], [], outs)
    return put_in_order(x, grid.gathered, grid, False)


def second_norm(block_in, mine, other, gain, core, grid):
    rows, width = mine.shape

    def kernel(core_ref, in_ref, mine_ref, other_ref, gain_ref, hidden_ref, normed_ref):
        hidden = in_ref[...].astype(f32) + (mine_ref[...] + other_ref[...])
        hidden_ref[...] = hidden
        normed = (hidden * rms_scale(hidden) * gain_ref[...]).astype(bf16)
        normed_ref[...] = put_in_order(normed, grid.gathered, grid, True)

    outs = [jax.ShapeDtypeStruct((rows, width), f32), jax.ShapeDtypeStruct((rows, width), bf16)]
    hidden, normed = on_rows(
        kernel, "second_norm", core, [block_in], [mine, other, gain[None]], outs
    )
    return hidden, put_in_order(normed, grid.gathered, grid, False)


def second_norm_back(out_grad, hidden, gain, parts, core, grid):
    rows, width = hidden.shape
    parts = [put_in_order(x, grid.natural, grid, False) for x in parts]

    def kernel(core_ref, cot_ref, hidden_ref, gain_ref, *refs):
        upstream = sum(x[...].astype(f32) for x in refs[: len(parts)])
        upstream = put_in_order(upstream, grid.natural, grid, True)
        grad_ref, low_ref, gain_grad_ref = refs[len(parts) :]
        hidden = hidden_ref[...]
        gain_grad, grad = norm_back(hidden, rms_scale(hidden), gain_ref[...], upstream)
        grad = grad + cot_ref[...].astype(f32)
        grad_ref[...] = grad
        low_ref[...] = grad.astype(bf16)
        gain_grad_ref[...] = gain_grad

    sds = jax.ShapeDtypeStruct
    outs = [sds((rows, width), f32), sds((rows, width), bf16), sds((1, width), f32)]
    return on_rows(
        kernel, "second_norm_back", core, [out_grad], [hidden, gain[None], *parts], outs
    )


def first_norm_back(block_in, grad, gain, mine, other, core):
    rows, width = grad.shape

    def kernel(core_ref, in_ref, grad_ref, gain_ref, mine_ref, other_ref, out_ref, gain_grad_ref):
        inputs = in_ref[...].astype(f32)
        upstream = mine_ref[...] + other_ref[...]
        gain_grad, out = norm_back(inputs, rms_scale(inputs), gain_ref[...], upstream)
        out_ref[...] = out + grad_ref[...]
        gain_grad_ref[...] = gain_grad

    sds = jax.ShapeDtypeStruct
    outs = [sds((rows, width), f32), sds((1, width), f32)]
    return on_rows(
        kernel, "first_norm_back", core, [block_in], [grad, gain[None], mine, other], outs
    )


def block_result(block_in, hidden, parts, core, grid):
    rows, width = hidden.shape
    parts = [put_in_order(x, grid.natural, grid, False) for x in parts]

    def kernel(core_ref, in_ref, hidden_ref, *refs):
        out = sum(x[...].astype(f32) for x in refs[: len(parts)])
        out = put_in_order(out, grid.natural, grid, True)
        refs[-1][...] = (hidden_ref[...] + out).astype(bf16)

    outs = [jax.ShapeDtypeStruct((rows, width), bf16)]
    (x,) = on_rows(kernel, "block_result", core, [block_in], [hidden, *parts], outs)
    return x


def exchange(x, split, concat, groups):
    return lax.all_to_all(x, "dp", split, concat, tiled=True, axis_index_groups=groups)


def tie(*values):
    return lax.optimization_barrier(values)


def gather_along(x, grid, place, beside=()):
    n = grid.outer
    above = below = x
    from_below, from_above, done = [], [], []
    for k in range(n - 1):
        below = lax.ppermute(below, "dp", grid.up)
        above = lax.ppermute(above, "dp", grid.down)
        extra = beside[k] if k < len(beside) else ()
        below, above, *extra = tie(below, above, *extra)
        from_below.append(below)
        from_above.append(above)
        done += extra
    blocks = [x]
    for k in range(1, n):
        blocks.append(jnp.where(place + k < n, from_above[k - 1], from_below[n - 1 - k]))
    return jnp.concatenate(blocks, axis=0), done


def with_other_core(own):
    return jnp.concatenate([own, swap(own)], axis=0)


def scatter_tokens(x, grid, beside=()):
    n = grid.outer
    size = x.shape[0] // (2 * n)
    block = [x[k * size : (k + 1) * size] for k in range(2 * n)]
    order = [k for s in range(1, n) for k in (n - s, s)]
    order = list(dict.fromkeys(order)) + [0]
    swapped = {k: swap(block[n + k].astype(bf16)) for k in order}
    own = {k: block[k] + swapped[k].astype(f32) for k in order}
    up = down = None
    done = []
    for k in range(n - 1):
        up = own[n - 1 - k] if up is None else own[n - 1 - k] + up.astype(f32)
        down = own[1 + k] if down is None else own[1 + k] + down.astype(f32)
        up = lax.ppermute(up.astype(bf16), "dp", grid.up)
        down = lax.ppermute(down.astype(bf16), "dp", grid.down)
        extra = beside[k] if k < len(beside) else ()
        up, down, *extra = tie(up, down, *extra)
        done += extra
    return (own[0], up, down), done


def plane_gather(x, grid, inner):
    out = jnp.zeros((INNER,) + x.shape, x.dtype)
    for k in range(INNER):
        y = x
        if k:
            y = lax.ppermute(x, "dp", [(d, d ^ k) for d in range(grid.dp)])
        out = lax.dynamic_update_slice_in_dim(out, y[None], inner ^ k, 0)
    return out.reshape(INNER * x.shape[0], x.shape[1])


def on_device(
    block_in,
    out_grad,
    attn_gain,
    mlp_gain,
    w_query,
    w_key,
    w_value,
    w_forget,
    w_output,
    w_gate,
    w_up,
    w_down,
    doc_starts,
    grid,
):
    core = lax.axis_index("head")
    place = lax.axis_index("dp") // INNER
    inner = lax.axis_index("dp") % INNER

    def columns(w):
        return exchange(w, 1, 0, grid.cols)

    def gather_rows(w):
        return lax.all_gather(w, "dp", axis=0, tiled=True, axis_index_groups=grid.laps)

    def column_pairs(a, b):
        rows = a.shape[0]
        both = [w.reshape(rows, grid.outer, -1) for w in (a, b)]
        both = columns(jnp.concatenate(both, axis=2).reshape(rows, -1))
        return jnp.split(both, 2, axis=1)

    gate_piece, up_piece = column_pairs(w_gate, w_up)
    inputs_f = block_in.astype(f32)
    normed = (inputs_f * rms_scale(inputs_f) * attn_gain).astype(bf16)
    query_pre = nn(normed, w_query)
    key_pre = nn(normed, w_key)
    value_pre = nn(normed, w_value)
    forget_pre = nn(normed, w_forget)
    query = jax.nn.silu(query_pre).astype(bf16)
    key = jax.nn.silu(key_pre).astype(bf16)
    value = jax.nn.silu(value_pre).astype(bf16)
    log_keep = jax.nn.log_sigmoid(forget_pre) * tau_inv
    mixed, *saved = attend_forward(query, key, value, log_keep, doc_starts)
    mixed, gate_piece, up_piece, down_later = tie(mixed, gate_piece, up_piece, w_down)
    full_gate, full_up = gather_rows(gate_piece), gather_rows(up_piece)
    down_piece = columns(down_later)

    branch_other = swap(nt(half_of(mixed, 1 - core), w_output))
    branch_mine = nt(half_of(mixed, core), w_output)
    hidden, normed_two = second_norm(block_in, branch_mine, branch_other, mlp_gain, core, grid)
    def plane_tokens(half):
        own = plane_gather(half, grid, inner)
        return own, swap(own)

    def plane_columns(parts):
        rows = parts[0].shape[0]
        x = jnp.concatenate([p.reshape(rows, INNER, -1) for p in parts], axis=2)
        size = x.shape[2]
        x = exchange(x.reshape(rows, INNER * size), 1, 0, grid.rows)
        x = x.reshape(INNER, 2, rows // 2, size)
        return tuple(
            lax.dynamic_index_in_dim(x, c, 1, keepdims=False).reshape(-1, size)
            for c in (core, 1 - core)
        )

    def plane_product(left, right):
        return (tn(left[0], right[0]) + tn(left[1], right[1])).astype(bf16)

    def plane_sum(g):
        return lax.psum_scatter(
            g, "dp", scatter_dimension=0, tiled=True, axis_index_groups=grid.cols
        )

    def from_plane(g):
        size = g.shape[1]
        return exchange(g, 0, 1, grid.rows).reshape(-1, INNER, size).astype(f32)

    cot_rows = cotangent_rows(out_grad, core, grid)
    own, (cot_rows, down_piece, normed_own, normed_rest, full_gate) = gather_along(
        normed_two,
        grid,
        place,
        ((cot_rows, down_piece), plane_tokens(half_of(normed, core)), (full_gate,)),
    )
    normed_plane = (normed_own, normed_rest)
    full_down = gather_rows(down_piece)
    tokens = with_other_core(own)
    own, (gate_act, full_up, mixed_own, mixed_rest, up_act, full_down) = gather_along(
        cot_rows,
        grid,
        place,
        (
            (nn(tokens, full_gate), full_up),
            plane_columns([mixed]),
            (nn(tokens, full_up), full_down),
        ),
    )
    mixed_plane = (mixed_own, mixed_rest)
    cot_all = with_other_core(own)

    def scatter_rows(g):
        return lax.psum_scatter(
            g, "dp", scatter_dimension=0, tiled=True, axis_index_groups=grid.laps
        )

    def to_columns(g):
        return exchange(g, 0, 1, grid.cols).astype(f32)

    inner_grad = nn(cot_all, full_down)
    gate_grad = (inner_grad * up_act * silu_slope(gate_act)).astype(bf16)
    up_grad = (inner_grad * jax.nn.silu(gate_act)).astype(bf16)
    inner_act = (jax.nn.silu(gate_act) * up_act).astype(bf16)
    back_parts, (down_rows, gate_rows, up_rows) = scatter_tokens(
        nt(gate_grad, full_gate) + nt(up_grad, full_up),
        grid,
        (
            (tn(cot_all, inner_act).astype(bf16),),
            (tn(tokens, gate_grad).astype(bf16),),
            (tn(tokens, up_grad).astype(bf16),),
        ),
    )
    down_rows, gate_rows, up_rows = (scatter_rows(g) for g in (down_rows, gate_rows, up_rows))
    hidden_grad, low_half, mlp_gain_part = second_norm_back(
        out_grad, hidden, mlp_gain, back_parts, core, grid
    )
    branch_grad = join(low_half, swap(low_half), core)
    mixed_grad = nn(branch_grad, w_output).astype(bf16)
    mixed_grad, down_rows, later_act = tie(mixed_grad, down_rows, inner_act)
    saved_grads = attend_backward(query, key, value, log_keep, doc_starts, saved, mixed_grad)
    query_grad, key_grad, value_grad, log_grad = saved_grads
    query_pre_grad = (query_grad * silu_slope(query_pre)).astype(bf16)
    key_pre_grad = (key_grad * silu_slope(key_pre)).astype(bf16)
    value_pre_grad = (value_grad * silu_slope(value_pre)).astype(bf16)
    forget_pre_grad = (log_grad * tau_inv * jax.nn.sigmoid(-forget_pre)).astype(bf16)
    pre_grads = (query_pre_grad, key_pre_grad, value_pre_grad, forget_pre_grad)

    down_sum = to_columns(down_rows)
    query_pre_grad, gate_rows, down_sum, low_half = tie(
        query_pre_grad, gate_rows, down_sum, low_half
    )
    pre_grads = (query_pre_grad,) + pre_grads[1:]
    out_parts, (query_pre_grad, *grad_columns) = scatter_tokens(
        nt(later_act, full_down), grid, ((query_pre_grad,), tuple(plane_columns(pre_grads)))
    )
    pre_grads = (query_pre_grad,) + pre_grads[1:]
    output_grad = plane_product(plane_tokens(low_half), mixed_plane)
    pre_grad = plane_product(normed_plane, grad_columns)
    pre_grad, up_rows = tie(jnp.concatenate([pre_grad, output_grad], axis=1), up_rows)
    sums = plane_sum(pre_grad)

    result = block_result(block_in, hidden, out_parts, core, grid)
    result = join(result, swap(result), core)

    sums = from_plane(sums)
    ends = [0]
    for g in (*pre_grads, mixed):
        ends.append(ends[-1] + g.shape[1] // INNER)
    query_sum, key_sum, value_sum, forget_sum, output_sum = (
        sums[:, :, a:b].reshape(sums.shape[0], -1) for a, b in zip(ends, ends[1:])
    )

    def normed_part(which):
        q, k, v, f = (half_of(g, which) for g in pre_grads)
        return nt(q, w_query) + nt(k, w_key) + nt(v, w_value) + nt(f, w_forget)

    part_other = swap(normed_part(1 - core))
    input_grad, attn_gain_part = first_norm_back(
        block_in, hidden_grad, attn_gain, normed_part(core), part_other, core
    )
    input_grad = join(input_grad, swap(input_grad), core)

    gains = jnp.concatenate([attn_gain_part, mlp_gain_part], axis=0)
    gains = gains + swap(gains)
    gains = jnp.swapaxes(gains.reshape(2, grid.dp, -1), 0, 1)
    gains = jnp.sum(lax.all_to_all(gains, "dp", 0, 0, tiled=True), axis=0)

    return (
        result,
        input_grad,
        gains[0],
        gains[1],
        query_sum,
        key_sum,
        value_sum,
        forget_sum,
        output_sum,
        to_columns(gate_rows),
        to_columns(up_rows),
        down_sum,
    )


def solution(mesh):
    placed = (
        P("dp", None),
        P("dp", None),
        P(),
        P(),
        P(None, "head"),
        P(None, "head"),
        P(None, "head"),
        P(None, "head"),
        P(None, "head"),
        P("dp", "head"),
        P("dp", "head"),
        P("dp", "head"),
        P("dp", None),
    )
    return jax.shard_map(
        partial(on_device, grid=Grid(mesh.shape["dp"])),
        mesh=mesh,
        in_specs=placed,
        out_specs=(P("dp", None), P("dp", None), P("dp"), P("dp")) + (P("dp", "head"),) * 8,
        check_vma=False,
    )
```

```python
import math
from functools import partial
import jax
import jax.numpy as jnp
from jax import lax
from jax.experimental import pallas as pl
from jax.experimental.pallas import tpu as pltpu
from jax.sharding import PartitionSpec as P

DK = 512
DV = 512
M = 64
B = 16
f32 = jnp.float32
bf16 = jnp.bfloat16


def nn(a, b):
    return jnp.dot(a.astype(bf16), b.astype(bf16), preferred_element_type=f32)


def nt(a, b):
    return lax.dot_general(
        a.astype(bf16), b.astype(bf16), (((1,), (1,)), ((), ())), preferred_element_type=f32
    )


def tn(a, b):
    return lax.dot_general(
        a.astype(bf16), b.astype(bf16), (((0,), (0,)), ((), ())), preferred_element_type=f32
    )


def nn3(a, b):
    ah, bh = a.astype(bf16), b.astype(bf16)
    al, bl = (a - ah.astype(f32)).astype(bf16), (b - bh.astype(f32)).astype(bf16)
    return nn(ah, bh) + (nn(al, bh) + nn(ah, bl))


def shift_up(x, s):
    return pltpu.roll(x, x.shape[0] - s, 0)


def shift_down(x, s):
    return pltpu.roll(x, s, 0)


def segment_at(pos, starts):
    seg = jnp.zeros(pos.shape, jnp.int32)
    for s in starts:
        seg = seg + (pos >= s).astype(jnp.int32)
    return seg


def same_document(t, j, starts):
    ok = None
    for s in starts:
        same = (t >= s) == (j >= s)
        ok = same if ok is None else ok & same
    return ok


def level_sizes(length):
    sizes = []
    h = length // 2
    while h >= B:
        sizes.append(h)
        h //= 2
    return sizes


def row_pick(x, size, row):
    n, lanes = x.shape
    x3 = x.reshape(n // size, size, lanes)
    return jnp.broadcast_to(x3[:, row : row + 1, :], x3.shape).reshape(n, lanes)


class Common:
    def __init__(self, la, starts):
        length, lanes = la.shape
        self.length, self.lanes = length, lanes
        rows = lax.broadcasted_iota(jnp.int32, (length, lanes), 0)
        self.rows = rows
        self.lane_head = lax.broadcasted_iota(jnp.int32, (length, lanes), 1) // M
        c = la
        s = 1
        while s < length:
            c = c + jnp.where(rows >= s, shift_down(c, s), 0.0)
            s *= 2
        self.c = c
        self.alpha = jnp.exp(la)
        self.om = 1.0 - self.alpha
        self.levels = level_sizes(length)
        self.x = []
        for h in self.levels:
            mid = row_pick(c, 2 * h, h - 1)
            self.x.append(jnp.exp(-jnp.abs(c - mid)))
        t = lax.broadcasted_iota(jnp.int32, (length, length), 0)
        j = lax.broadcasted_iota(jnp.int32, (length, length), 1)
        same = same_document(t, j, starts)
        self.masks = [
            same & ((t // (2 * h)) == (j // (2 * h))) & ((t & h) != 0) & ((j & h) == 0)
            for h in self.levels
        ]
        tc = lax.broadcasted_iota(jnp.int32, (length, B), 0)
        off = lax.broadcasted_iota(jnp.int32, (length, B), 1)
        jc = (tc - tc % B) + off
        self.mask_c = same_document(tc, jc, starts) & (jc <= tc)

    def by_head(self, parts):
        out = parts[0]
        for i in range(1, len(parts)):
            out = jnp.where(self.lane_head == i, parts[i], out)
        return out

    def only(self, x, i):
        return jnp.where(self.lane_head == i, x, 0.0)

    def decay_from(self, jj):
        return jnp.exp(jnp.minimum(self.c - row_pick(self.c, B, jj), 0.0))

    def om_at(self, jj):
        return row_pick(self.om, B, jj)


def blocks(x):
    return x.reshape(x.shape[0] // B, B, x.shape[1])


def block_nt(a, b):
    r = lax.dot_general(
        blocks(a.astype(bf16)),
        blocks(b.astype(bf16)),
        (((2,), (2,)), ((0,), (0,))),
        preferred_element_type=f32,
    )
    return r.reshape(a.shape[0], B)


def block_nn(a, b):
    r = lax.dot_general(
        blocks(a.astype(bf16)),
        blocks(b.astype(bf16)),
        (((2,), (1,)), ((0,), (0,))),
        preferred_element_type=f32,
    )
    return r.reshape(a.shape[0], b.shape[1])


def block_tn(a, b):
    at = jnp.swapaxes(blocks(a), 1, 2).astype(bf16)
    r = lax.dot_general(
        at, blocks(b.astype(bf16)), (((2,), (1,)), ((0,), (0,))), preferred_element_type=f32
    )
    return r.reshape(a.shape[0], b.shape[1])


def collect(lanes, heads):
    r = lax.broadcasted_iota(jnp.int32, (B * lanes, heads * 128), 0)
    col = lax.broadcasted_iota(jnp.int32, (B * lanes, heads * 128), 1)
    jj, head = r // lanes, (r % lanes) // M
    return jnp.where(col == head * 128 + jj, 1.0, 0.0).astype(bf16)


def wide(x, jj):
    return jnp.broadcast_to(x[:, jj : jj + 1], (x.shape[0], 128))


def forward_math(q, k, v, la, starts):
    heads = q.shape[1] // DK
    scale = 1.0 / math.sqrt(DK)
    cm = Common(la, starts)
    qs = [q[:, i * DK : (i + 1) * DK] for i in range(heads)]
    ks = [k[:, i * DK : (i + 1) * DK] for i in range(heads)]
    vs = [v[:, i * DV : (i + 1) * DV] for i in range(heads)]
    aff = [nt(qs[i], ks[i]) * scale for i in range(heads)]
    affc = [jnp.where(cm.mask_c, block_nt(qs[i], ks[i]) * scale, 0.0) for i in range(heads)]
    s = jnp.zeros_like(la)
    parts = []
    for x, mask in zip(cm.x, cm.masks):
        g = x * cm.om
        part = x * cm.by_head([nn3(jnp.where(mask, aff[i], 0.0), g) for i in range(heads)])
        parts.append(part)
        s = s + part
    for jj in range(B):
        s = s + cm.by_head([wide(affc[i], jj) for i in range(heads)]) * (
            cm.decay_from(jj) * cm.om_at(jj)
        )
    top = cm.by_head(
        [
            jnp.max(jnp.where(cm.lane_head == i, s, -jnp.inf), axis=1, keepdims=True)
            for i in range(heads)
        ]
    )
    e = jnp.exp(s - top)
    total = cm.by_head([jnp.sum(cm.only(e, i), axis=1, keepdims=True) for i in range(heads)])
    p = e / total
    mix = [jnp.zeros((cm.length, cm.length), f32) for _ in range(heads)]
    for x, mask in zip(cm.x, cm.masks):
        g = x * cm.om
        px = p * x
        for i in range(heads):
            mix[i] = mix[i] + jnp.where(mask, nt(cm.only(px, i), g), 0.0)
    mix = [m.astype(bf16) for m in mix]
    pieces = [(p * (cm.decay_from(jj) * cm.om_at(jj))).astype(bf16) for jj in range(B)]
    mixc = nn(jnp.concatenate(pieces, axis=1), collect(cm.lanes, heads))
    mixc = [
        jnp.where(cm.mask_c, mixc[:, i * 128 : i * 128 + B], 0.0) for i in range(heads)
    ]
    outs = [nn(mix[i], vs[i]) + block_nn(mixc[i], vs[i]) for i in range(heads)]
    return outs, p, parts, mix, mixc


def backward_math(q, k, v, la, starts, p, parts, mix, mixc, dout):
    heads = q.shape[1] // DK
    scale = 1.0 / math.sqrt(DK)
    cm = Common(la, starts)
    qs = [q[:, i * DK : (i + 1) * DK] for i in range(heads)]
    ks = [k[:, i * DK : (i + 1) * DK] for i in range(heads)]
    vs = [v[:, i * DV : (i + 1) * DV] for i in range(heads)]
    dos = [dout[:, i * DV : (i + 1) * DV].astype(bf16) for i in range(heads)]
    aff = [nt(qs[i], ks[i]) * scale for i in range(heads)]
    affc = [jnp.where(cm.mask_c, block_nt(qs[i], ks[i]) * scale, 0.0) for i in range(heads)]
    dmix = [nt(dos[i], vs[i]) for i in range(heads)]
    dmixc = [jnp.where(cm.mask_c, block_nt(dos[i], vs[i]), 0.0) for i in range(heads)]
    dp = jnp.zeros_like(la)
    dparts = []
    for x, mask in zip(cm.x, cm.masks):
        g = x * cm.om
        part = x * cm.by_head([nn3(jnp.where(mask, dmix[i], 0.0), g) for i in range(heads)])
        dparts.append(part)
        dp = dp + part
    for jj in range(B):
        dp = dp + cm.by_head([wide(dmixc[i], jj) for i in range(heads)]) * (
            cm.decay_from(jj) * cm.om_at(jj)
        )
    pdp = p * dp
    inner = cm.by_head([jnp.sum(cm.only(pdp, i), axis=1, keepdims=True) for i in range(heads)])
    ds = pdp - p * inner
    daff = [jnp.zeros((cm.length, cm.length), f32) for _ in range(heads)]
    dla = jnp.zeros_like(la)
    reach = jnp.zeros_like(la)
    for n, h in enumerate(cm.levels):
        x, mask = cm.x[n], cm.masks[n]
        g = x * cm.om
        dsx, px = ds * x, p * x
        both = jnp.concatenate([dsx, px], axis=0).astype(bf16)
        cols = []
        for i in range(heads):
            daff[i] = daff[i] + jnp.where(mask, nt(cm.only(dsx, i), g), 0.0)
            left = jnp.concatenate(
                [jnp.where(mask, aff[i], 0.0), jnp.where(mask, dmix[i], 0.0)], axis=0
            )
            cols.append(tn(left, both))
        r = x * cm.by_head(cols)
        reach = reach + r
        right = (cm.rows & h) != 0
        flow = jnp.where(right, ds * parts[n] + p * dparts[n], cm.om * r)
        s = 1
        while s < h:
            flow = flow + jnp.where((cm.rows & (h - 1)) < h - s, shift_up(flow, s), 0.0)
            s *= 2
        dla = dla + jnp.where(right, flow, row_pick(flow, h, 0) - flow)
    flow = jnp.zeros_like(la)
    near = jnp.zeros_like(la)
    pieces = []
    for jj in range(B):
        w = cm.decay_from(jj)
        omj = cm.om_at(jj)
        aj = cm.by_head([wide(affc[i], jj) for i in range(heads)])
        dj = cm.by_head([wide(dmixc[i], jj) for i in range(heads)])
        pieces.append((ds * (w * omj)).astype(bf16))
        z = w * (aj * ds + dj * p)
        flow = flow + omj * z
        z3 = blocks(z)
        tot = jnp.broadcast_to(jnp.sum(z3, axis=1, keepdims=True), z3.shape).reshape(z.shape)
        near = jnp.where((cm.rows & (B - 1)) == jj, tot, near)
    flow = flow - cm.om * near
    s = 1
    while s < B:
        flow = flow + jnp.where((cm.rows & (B - 1)) < B - s, shift_up(flow, s), 0.0)
        s *= 2
    dla = dla + flow - cm.alpha * (reach + near)
    daffc = nn(jnp.concatenate(pieces, axis=1), collect(cm.lanes, heads))
    daffc = [
        jnp.where(cm.mask_c, daffc[:, i * 128 : i * 128 + B], 0.0) for i in range(heads)
    ]
    dq, dk, dv = [], [], []
    for i in range(heads):
        da = daff[i].astype(bf16)
        dq.append((nn(da, ks[i]) + block_nn(daffc[i], ks[i])) * scale)
        dk.append((tn(da, qs[i]) + block_tn(daffc[i], qs[i])) * scale)
        dv.append(tn(mix[i], dos[i]) + block_tn(mixc[i], dos[i]))
    return dq, dk, dv, dla


def head_split(outs, ref, width):
    for i, x in enumerate(outs):
        ref[:, i * width : (i + 1) * width] = x.astype(ref.dtype)


def forward_kernel(starts_ref, q_ref, k_ref, v_ref, la_ref, o_ref, p_ref, parts_ref, mix_ref, mixc_ref):
    starts = [starts_ref[0, n] for n in range(starts_ref.shape[1])]
    outs, p, parts, mix, mixc = forward_math(
        q_ref[...], k_ref[...], v_ref[...], la_ref[...], starts
    )
    head_split(outs, o_ref, DV)
    p_ref[...] = p
    for n, x in enumerate(parts):
        parts_ref[n] = x
    for i in range(len(mix)):
        mix_ref[i] = mix[i]
        mixc_ref[i] = mixc[i].astype(bf16)


def backward_kernel(
    starts_ref, q_ref, k_ref, v_ref, la_ref, p_ref, parts_ref, mix_ref, mixc_ref, do_ref,
    dq_ref, dk_ref, dv_ref, dla_ref,
):
    starts = [starts_ref[0, n] for n in range(starts_ref.shape[1])]
    heads = mix_ref.shape[0]
    dq, dk, dv, dla = backward_math(
        q_ref[...],
        k_ref[...],
        v_ref[...],
        la_ref[...],
        starts,
        p_ref[...],
        [parts_ref[n] for n in range(parts_ref.shape[0])],
        [mix_ref[i] for i in range(heads)],
        [mixc_ref[i] for i in range(heads)],
        do_ref[...],
    )
    head_split(dq, dq_ref, DK)
    head_split(dk, dk_ref, DK)
    head_split(dv, dv_ref, DV)
    dla_ref[...] = dla


SMEM = pl.BlockSpec(memory_space=pltpu.SMEM)
VMEM = pl.BlockSpec(memory_space=pltpu.VMEM)


def attend_forward(q, k, v, la, starts):
    length, lanes = la.shape
    heads = q.shape[1] // DK
    sds = jax.ShapeDtypeStruct
    return pl.pallas_call(
        forward_kernel,
        out_shape=(
            sds((length, heads * DV), bf16),
            sds((length, lanes), f32),
            sds((len(level_sizes(length)), length, lanes), f32),
            sds((heads, length, length), bf16),
            sds((heads, length, B), bf16),
        ),
        in_specs=[SMEM] + [VMEM] * 4,
        out_specs=(VMEM,) * 5,
        cost_estimate=pl.CostEstimate(
            flops=4 * 10**9, transcendentals=10**6, bytes_accessed=4 * 10**6
        ),
        name="slot_forward",
    )(starts, q, k, v, la)


def attend_backward(q, k, v, la, starts, saved, dout):
    length, lanes = la.shape
    sds = jax.ShapeDtypeStruct
    return pl.pallas_call(
        backward_kernel,
        out_shape=(
            sds(q.shape, f32),
            sds(k.shape, f32),
            sds(v.shape, f32),
            sds((length, lanes), f32),
        ),
        in_specs=[SMEM] + [VMEM] * 9,
        out_specs=(VMEM,) * 4,
        cost_estimate=pl.CostEstimate(
            flops=12 * 10**9, transcendentals=10**6, bytes_accessed=8 * 10**6
        ),
        name="slot_backward",
    )(starts, q, k, v, la, *saved, dout)


eps = 1e-06
tau_inv = 0.125
INNER = 4
LAP = (0, 1, 3, 2)


def rms_scale(values):
    return lax.rsqrt(jnp.mean(values * values, axis=-1, keepdims=True) + eps)


def norm_back(values, scale, gain, upstream):
    gain_grad = jnp.sum(upstream * values * scale, axis=0, keepdims=True)
    weighted = upstream * gain
    input_grad = scale * weighted - values * (scale * scale * scale) * jnp.mean(
        weighted * values, axis=-1, keepdims=True
    )
    return (gain_grad, input_grad)


def silu_slope(values):
    sigmoid_val = jax.nn.sigmoid(values)
    return sigmoid_val * (1.0 + values * (1.0 - sigmoid_val))


class Grid:
    def __init__(self, dp):
        self.dp = dp
        self.outer = dp // INNER
        self.laps = [[o * INNER + i for i in LAP] for o in range(self.outer)]
        self.rows = [[o * INNER + i for i in range(INNER)] for o in range(self.outer)]
        self.cols = [[o * INNER + i for o in range(self.outer)] for i in range(INNER)]
        self.gathered = [o * INNER + i for i in LAP for o in range(self.outer)]
        self.natural = inverse(self.gathered)
        self.up = [(d, d + INNER) for d in range(dp - INNER)]
        self.down = [(d + INNER, d) for d in range(dp - INNER)]


def reorder(x, order):
    size = x.shape[-1] // len(order)
    return jnp.concatenate([x[..., b * size : (b + 1) * size] for b in order], axis=-1)


def inverse(order):
    back = [0] * len(order)
    for n, b in enumerate(order):
        back[b] = n
    return back


def swap(x):
    return lax.ppermute(x, "head", [(0, 1), (1, 0)])


def half_of(x, which):
    size = x.shape[0] // 2
    return lax.dynamic_slice_in_dim(x, which * size, size, 0)


def join(mine, other, core):
    size = mine.shape[0]
    out = jnp.zeros((2 * size,) + mine.shape[1:], mine.dtype)
    out = lax.dynamic_update_slice_in_dim(out, mine, core * size, 0)
    return lax.dynamic_update_slice_in_dim(out, other, (1 - core) * size, 0)


def on_rows(kernel, name, core, halves, wholes, outs):
    rows = halves[0].shape[0] // 2
    specs = [pl.BlockSpec((rows, x.shape[1]), lambda i, c: (c[0], 0)) for x in halves]
    specs += [pl.BlockSpec(x.shape, lambda i, c: (0, 0)) for x in wholes]
    return pl.pallas_call(
        kernel,
        out_shape=outs,
        grid_spec=pltpu.PrefetchScalarGridSpec(
            num_scalar_prefetch=1,
            grid=(1,),
            in_specs=specs,
            out_specs=[pl.BlockSpec(x.shape, lambda i, c: (0, 0)) for x in outs],
        ),
        name=name,
    )(core.reshape(1), *halves, *wholes)


def aligned(grid, width):
    return (width // grid.dp) % 128 == 0


def put_in_order(x, order, grid, inside):
    return reorder(x, order) if aligned(grid, x.shape[1]) == inside else x


def cotangent_rows(out_grad, core, grid):
    rows, width = out_grad.shape

    def kernel(core_ref, cot_ref, out_ref):
        out_ref[...] = put_in_order(cot_ref[...], grid.gathered, grid, True)

    outs = [jax.ShapeDtypeStruct((rows // 2, width), bf16)]
    (x,) = on_rows(kernel, "cotangent_rows", core, [out_grad], [], outs)
    return put_in_order(x, grid.gathered, grid, False)


def second_norm(block_in, mine, other, gain, core, grid):
    rows, width = mine.shape

    def kernel(core_ref, in_ref, mine_ref, other_ref, gain_ref, hidden_ref, normed_ref):
        hidden = in_ref[...].astype(f32) + (mine_ref[...] + other_ref[...])
        hidden_ref[...] = hidden
        normed = (hidden * rms_scale(hidden) * gain_ref[...]).astype(bf16)
        normed_ref[...] = put_in_order(normed, grid.gathered, grid, True)

    outs = [jax.ShapeDtypeStruct((rows, width), f32), jax.ShapeDtypeStruct((rows, width), bf16)]
    hidden, normed = on_rows(
        kernel, "second_norm", core, [block_in], [mine, other, gain[None]], outs
    )
    return hidden, put_in_order(normed, grid.gathered, grid, False)


def second_norm_back(out_grad, hidden, gain, parts, core, grid):
    rows, width = hidden.shape
    parts = [put_in_order(x, grid.natural, grid, False) for x in parts]

    def kernel(core_ref, cot_ref, hidden_ref, gain_ref, *refs):
        upstream = sum(x[...].astype(f32) for x in refs[: len(parts)])
        upstream = put_in_order(upstream, grid.natural, grid, True)
        grad_ref, low_ref, gain_grad_ref = refs[len(parts) :]
        hidden = hidden_ref[...]
        gain_grad, grad = norm_back(hidden, rms_scale(hidden), gain_ref[...], upstream)
        grad = grad + cot_ref[...].astype(f32)
        grad_ref[...] = grad
        low_ref[...] = grad.astype(bf16)
        gain_grad_ref[...] = gain_grad

    sds = jax.ShapeDtypeStruct
    outs = [sds((rows, width), f32), sds((rows, width), bf16), sds((1, width), f32)]
    return on_rows(
        kernel, "second_norm_back", core, [out_grad], [hidden, gain[None], *parts], outs
    )


def first_norm_back(block_in, grad, gain, mine, other, core):
    rows, width = grad.shape

    def kernel(core_ref, in_ref, grad_ref, gain_ref, mine_ref, other_ref, out_ref, gain_grad_ref):
        inputs = in_ref[...].astype(f32)
        upstream = mine_ref[...] + other_ref[...]
        gain_grad, out = norm_back(inputs, rms_scale(inputs), gain_ref[...], upstream)
        out_ref[...] = out + grad_ref[...]
        gain_grad_ref[...] = gain_grad

    sds = jax.ShapeDtypeStruct
    outs = [sds((rows, width), f32), sds((1, width), f32)]
    return on_rows(
        kernel, "first_norm_back", core, [block_in], [grad, gain[None], mine, other], outs
    )


def block_result(block_in, hidden, parts, core, grid):
    rows, width = hidden.shape
    parts = [put_in_order(x, grid.natural, grid, False) for x in parts]

    def kernel(core_ref, in_ref, hidden_ref, *refs):
        out = sum(x[...].astype(f32) for x in refs[: len(parts)])
        out = put_in_order(out, grid.natural, grid, True)
        refs[-1][...] = (hidden_ref[...] + out).astype(bf16)

    outs = [jax.ShapeDtypeStruct((rows, width), bf16)]
    (x,) = on_rows(kernel, "block_result", core, [block_in], [hidden, *parts], outs)
    return x


def exchange(x, split, concat, groups):
    return lax.all_to_all(x, "dp", split, concat, tiled=True, axis_index_groups=groups)


def tie(*values):
    return lax.optimization_barrier(values)


def gather_along(x, grid, place, beside=()):
    n = grid.outer
    above = below = x
    from_below, from_above, done = [], [], []
    for k in range(n - 1):
        below = lax.ppermute(below, "dp", grid.up)
        above = lax.ppermute(above, "dp", grid.down)
        extra = beside[k] if k < len(beside) else ()
        extra = extra(*done) if callable(extra) else extra
        below, above, *extra = tie(below, above, *extra)
        from_below.append(below)
        from_above.append(above)
        done += extra
    blocks = [x]
    for k in range(1, n):
        blocks.append(jnp.where(place + k < n, from_above[k - 1], from_below[n - 1 - k]))
    return jnp.concatenate(blocks, axis=0), done


def with_other_core(own):
    return jnp.concatenate([own, swap(own)], axis=0)


def add_other_core(x, grid):
    n = grid.outer
    size = x.shape[0] // (2 * n)
    block = [x[k * size : (k + 1) * size] for k in range(2 * n)]
    return [block[k] + swap(block[n + k].astype(bf16)).astype(f32) for k in range(n)]


def scatter_along(own, grid, beside=()):
    n = grid.outer
    up = down = None
    done = []
    for k in range(n - 1):
        up = own[n - 1 - k] if up is None else own[n - 1 - k] + up.astype(f32)
        down = own[1 + k] if down is None else own[1 + k] + down.astype(f32)
        up = lax.ppermute(up.astype(bf16), "dp", grid.up)
        down = lax.ppermute(down.astype(bf16), "dp", grid.down)
        extra = beside[k] if k < len(beside) else ()
        extra = extra(*done) if callable(extra) else extra
        up, down, *extra = tie(up, down, *extra)
        done += extra
    return (own[0], up, down), done


def plane_gather(x, grid, inner):
    out = jnp.zeros((INNER,) + x.shape, x.dtype)
    for k in range(INNER):
        y = x
        if k:
            y = lax.ppermute(x, "dp", [(d, d ^ k) for d in range(grid.dp)])
        out = lax.dynamic_update_slice_in_dim(out, y[None], inner ^ k, 0)
    return out


def on_device(
    block_in,
    out_grad,
    attn_gain,
    mlp_gain,
    w_query,
    w_key,
    w_value,
    w_forget,
    w_output,
    w_gate,
    w_up,
    w_down,
    doc_starts,
    grid,
):
    core = lax.axis_index("head")
    place = lax.axis_index("dp") // INNER
    inner = lax.axis_index("dp") % INNER

    def columns(w):
        return exchange(w, 1, 0, grid.cols)

    def gather_rows(w):
        return lax.all_gather(w, "dp", axis=0, tiled=True, axis_index_groups=grid.laps)

    def column_pairs(a, b):
        rows = a.shape[0]
        both = [w.reshape(rows, grid.outer, -1) for w in (a, b)]
        both = columns(jnp.concatenate(both, axis=2).reshape(rows, -1))
        return jnp.split(both, 2, axis=1)

    gate_piece, up_piece = column_pairs(w_gate, w_up)
    inputs_f = block_in.astype(f32)
    normed = (inputs_f * rms_scale(inputs_f) * attn_gain).astype(bf16)
    query_pre = nn(normed, w_query)
    key_pre = nn(normed, w_key)
    value_pre = nn(normed, w_value)
    forget_pre = nn(normed, w_forget)
    query = jax.nn.silu(query_pre).astype(bf16)
    key = jax.nn.silu(key_pre).astype(bf16)
    value = jax.nn.silu(value_pre).astype(bf16)
    log_keep = jax.nn.log_sigmoid(forget_pre) * tau_inv
    mixed, *saved = attend_forward(query, key, value, log_keep, doc_starts)
    normed_own = lax.all_gather(
        half_of(normed, core), "dp", axis=0, tiled=True, axis_index_groups=grid.rows
    )
    mixed, gate_piece, up_piece, down_later, normed_own = tie(
        mixed, gate_piece, up_piece, w_down, normed_own
    )
    full_gate, full_up = gather_rows(gate_piece), gather_rows(up_piece)
    down_piece = columns(down_later)

    branch_other = swap(nt(half_of(mixed, 1 - core), w_output))
    branch_mine = nt(half_of(mixed, core), w_output)
    hidden, normed_two = second_norm(block_in, branch_mine, branch_other, mlp_gain, core, grid)
    def plane_tokens(own):
        own = own.reshape(INNER, 1, -1, own.shape[-1])
        out = jnp.zeros((INNER, 2) + own.shape[2:], own.dtype)
        out = lax.dynamic_update_slice_in_dim(out, own, core, 1)
        out = lax.dynamic_update_slice_in_dim(out, swap(own), 1 - core, 1)
        return out.reshape(-1, own.shape[-1])

    def plane_columns(parts):
        rows = parts[0].shape[0]
        x = jnp.concatenate([p.reshape(rows, INNER, -1) for p in parts], axis=2)
        return exchange(x.reshape(rows, -1), 1, 0, grid.rows)

    def plane_product(left, right):
        return tn(left, right).astype(bf16)

    def plane_sum(g):
        return lax.psum_scatter(
            g, "dp", scatter_dimension=0, tiled=True, axis_index_groups=grid.cols
        )

    def from_plane(g):
        size = g.shape[1]
        return exchange(g, 0, 1, grid.rows).reshape(-1, INNER, size).astype(f32)

    cot_rows = cotangent_rows(out_grad, core, grid)
    own, (cot_rows, down_piece, normed_plane, full_gate) = gather_along(
        normed_two,
        grid,
        place,
        ((cot_rows, down_piece), (plane_tokens(normed_own),), (full_gate,)),
    )
    full_down = gather_rows(down_piece)
    tokens = with_other_core(own)
    own, (gate_act, full_up, mixed_plane, up_act, full_down) = gather_along(
        cot_rows,
        grid,
        place,
        (
            (nn(tokens, full_gate), full_up),
            (plane_columns([mixed]),),
            (nn(tokens, full_up), full_down),
        ),
    )
    cot_all = with_other_core(own)

    def scatter_rows(g):
        return lax.psum_scatter(
            g, "dp", scatter_dimension=0, tiled=True, axis_index_groups=grid.laps
        )

    def to_columns(g):
        return exchange(g, 0, 1, grid.cols).astype(f32)

    inner_grad = nn(cot_all, full_down)
    gate_grad = (inner_grad * up_act * silu_slope(gate_act)).astype(bf16)
    up_grad = (inner_grad * jax.nn.silu(gate_act)).astype(bf16)
    inner_act = (jax.nn.silu(gate_act) * up_act).astype(bf16)
    back_parts, (down_rows, *out_own, gate_rows, up_rows) = scatter_along(
        add_other_core(nt(gate_grad, full_gate) + nt(up_grad, full_up), grid),
        grid,
        (
            (tn(cot_all, inner_act).astype(bf16),),
            (*add_other_core(nt(inner_act, full_down), grid), tn(tokens, gate_grad).astype(bf16)),
            (tn(tokens, up_grad).astype(bf16),),
        ),
    )
    down_rows, gate_rows, up_rows = (scatter_rows(g) for g in (down_rows, gate_rows, up_rows))
    hidden_grad, low_half, mlp_gain_part = second_norm_back(
        out_grad, hidden, mlp_gain, back_parts, core, grid
    )
    branch_grad = join(low_half, swap(low_half), core)
    mixed_grad = nn(branch_grad, w_output).astype(bf16)
    mixed_grad, down_rows = tie(mixed_grad, down_rows)
    saved_grads = attend_backward(query, key, value, log_keep, doc_starts, saved, mixed_grad)
    query_grad, key_grad, value_grad, log_grad = saved_grads
    query_pre_grad = (query_grad * silu_slope(query_pre)).astype(bf16)
    key_pre_grad = (key_grad * silu_slope(key_pre)).astype(bf16)
    value_pre_grad = (value_grad * silu_slope(value_pre)).astype(bf16)
    forget_pre_grad = (log_grad * tau_inv * jax.nn.sigmoid(-forget_pre)).astype(bf16)
    pre_grads = (query_pre_grad, key_pre_grad, value_pre_grad, forget_pre_grad)

    query_pre_grad, *out_own = tie(query_pre_grad, *out_own)
    pre_grads = (query_pre_grad,) + pre_grads[1:]
    grad_columns = plane_columns(pre_grads)
    out_parts, (grad_columns, pre_grad, low_half) = scatter_along(
        out_own,
        grid,
        ((grad_columns,), lambda columns: (plane_product(normed_plane, columns), low_half)),
    )
    low_plane = plane_tokens(plane_gather(low_half, grid, inner))
    sums, output_grad = tie(plane_sum(pre_grad), plane_product(low_plane, mixed_plane))
    output_sum = plane_sum(output_grad)
    result = block_result(block_in, hidden, out_parts, core, grid)
    result = join(result, swap(result), core)

    sums = from_plane(sums)
    output_sum = from_plane(output_sum).reshape(sums.shape[0], -1)
    ends = [0]
    for g in pre_grads:
        ends.append(ends[-1] + g.shape[1] // INNER)
    query_sum, key_sum, value_sum, forget_sum = (
        sums[:, :, a:b].reshape(sums.shape[0], -1) for a, b in zip(ends, ends[1:])
    )

    def normed_part(which):
        q, k, v, f = (half_of(g, which) for g in pre_grads)
        return nt(q, w_query) + nt(k, w_key) + nt(v, w_value) + nt(f, w_forget)

    part_other = swap(normed_part(1 - core))
    input_grad, attn_gain_part = first_norm_back(
        block_in, hidden_grad, attn_gain, normed_part(core), part_other, core
    )
    input_grad = join(input_grad, swap(input_grad), core)

    gains = jnp.concatenate([attn_gain_part, mlp_gain_part], axis=0)
    gains = gains + swap(gains)
    gains = jnp.swapaxes(gains.reshape(2, grid.dp, -1), 0, 1)
    gains = jnp.sum(lax.all_to_all(gains, "dp", 0, 0, tiled=True), axis=0)

    return (
        result,
        input_grad,
        gains[0],
        gains[1],
        query_sum,
        key_sum,
        value_sum,
        forget_sum,
        output_sum,
        to_columns(gate_rows),
        to_columns(up_rows),
        to_columns(down_rows),
    )


def solution(mesh):
    placed = (
        P("dp", None),
        P("dp", None),
        P(),
        P(),
        P(None, "head"),
        P(None, "head"),
        P(None, "head"),
        P(None, "head"),
        P(None, "head"),
        P("dp", "head"),
        P("dp", "head"),
        P("dp", "head"),
        P("dp", None),
    )
    return jax.shard_map(
        partial(on_device, grid=Grid(mesh.shape["dp"])),
        mesh=mesh,
        in_specs=placed,
        out_specs=(P("dp", None), P("dp", None), P("dp"), P("dp")) + (P("dp", "head"),) * 8,
        check_vma=False,
    )
```

```python
import math
from functools import partial
import jax
import jax.numpy as jnp
from jax import lax
from jax.experimental import pallas as pl
from jax.experimental.pallas import tpu as pltpu
from jax.sharding import PartitionSpec as P

DK = 512
DV = 512
M = 64
B = 16
f32 = jnp.float32
bf16 = jnp.bfloat16


def nn(a, b):
    return jnp.dot(a.astype(bf16), b.astype(bf16), preferred_element_type=f32)


def nt(a, b):
    return lax.dot_general(
        a.astype(bf16), b.astype(bf16), (((1,), (1,)), ((), ())), preferred_element_type=f32
    )


def tn(a, b):
    return lax.dot_general(
        a.astype(bf16), b.astype(bf16), (((0,), (0,)), ((), ())), preferred_element_type=f32
    )


def nn3(a, b):
    ah, bh = a.astype(bf16), b.astype(bf16)
    al, bl = (a - ah.astype(f32)).astype(bf16), (b - bh.astype(f32)).astype(bf16)
    return nn(ah, bh) + (nn(al, bh) + nn(ah, bl))


def shift_up(x, s):
    return pltpu.roll(x, x.shape[0] - s, 0)


def shift_down(x, s):
    return pltpu.roll(x, s, 0)


def segment_at(pos, starts):
    seg = jnp.zeros(pos.shape, jnp.int32)
    for s in starts:
        seg = seg + (pos >= s).astype(jnp.int32)
    return seg


def same_document(t, j, starts):
    ok = None
    for s in starts:
        same = (t >= s) == (j >= s)
        ok = same if ok is None else ok & same
    return ok


def level_sizes(length):
    sizes = []
    h = length // 2
    while h >= B:
        sizes.append(h)
        h //= 2
    return sizes


def row_pick(x, size, row):
    n, lanes = x.shape
    x3 = x.reshape(n // size, size, lanes)
    return jnp.broadcast_to(x3[:, row : row + 1, :], x3.shape).reshape(n, lanes)


class Common:
    def __init__(self, la, starts):
        length, lanes = la.shape
        self.length, self.lanes = length, lanes
        rows = lax.broadcasted_iota(jnp.int32, (length, lanes), 0)
        self.rows = rows
        self.lane_head = lax.broadcasted_iota(jnp.int32, (length, lanes), 1) // M
        c = la
        s = 1
        while s < length:
            c = c + jnp.where(rows >= s, shift_down(c, s), 0.0)
            s *= 2
        self.c = c
        self.alpha = jnp.exp(la)
        self.om = 1.0 - self.alpha
        self.levels = level_sizes(length)
        self.x = []
        for h in self.levels:
            mid = row_pick(c, 2 * h, h - 1)
            self.x.append(jnp.exp(-jnp.abs(c - mid)))
        t = lax.broadcasted_iota(jnp.int32, (length, length), 0)
        j = lax.broadcasted_iota(jnp.int32, (length, length), 1)
        same = same_document(t, j, starts)
        self.masks = [
            same & ((t // (2 * h)) == (j // (2 * h))) & ((t & h) != 0) & ((j & h) == 0)
            for h in self.levels
        ]
        tc = lax.broadcasted_iota(jnp.int32, (length, B), 0)
        off = lax.broadcasted_iota(jnp.int32, (length, B), 1)
        jc = (tc - tc % B) + off
        self.mask_c = same_document(tc, jc, starts) & (jc <= tc)

    def by_head(self, parts):
        out = parts[0]
        for i in range(1, len(parts)):
            out = jnp.where(self.lane_head == i, parts[i], out)
        return out

    def only(self, x, i):
        return jnp.where(self.lane_head == i, x, 0.0)

    def decay_from(self, jj):
        return jnp.exp(jnp.minimum(self.c - row_pick(self.c, B, jj), 0.0))

    def om_at(self, jj):
        return row_pick(self.om, B, jj)


def blocks(x):
    return x.reshape(x.shape[0] // B, B, x.shape[1])


def block_nt(a, b):
    r = lax.dot_general(
        blocks(a.astype(bf16)),
        blocks(b.astype(bf16)),
        (((2,), (2,)), ((0,), (0,))),
        preferred_element_type=f32,
    )
    return r.reshape(a.shape[0], B)


def block_nn(a, b):
    r = lax.dot_general(
        blocks(a.astype(bf16)),
        blocks(b.astype(bf16)),
        (((2,), (1,)), ((0,), (0,))),
        preferred_element_type=f32,
    )
    return r.reshape(a.shape[0], b.shape[1])


def block_tn(a, b):
    at = jnp.swapaxes(blocks(a), 1, 2).astype(bf16)
    r = lax.dot_general(
        at, blocks(b.astype(bf16)), (((2,), (1,)), ((0,), (0,))), preferred_element_type=f32
    )
    return r.reshape(a.shape[0], b.shape[1])


def collect(lanes, heads):
    r = lax.broadcasted_iota(jnp.int32, (B * lanes, heads * 128), 0)
    col = lax.broadcasted_iota(jnp.int32, (B * lanes, heads * 128), 1)
    jj, head = r // lanes, (r % lanes) // M
    return jnp.where(col == head * 128 + jj, 1.0, 0.0).astype(bf16)


def wide(x, jj):
    return jnp.broadcast_to(x[:, jj : jj + 1], (x.shape[0], 128))


def forward_math(q, k, v, la, starts):
    heads = q.shape[1] // DK
    scale = 1.0 / math.sqrt(DK)
    cm = Common(la, starts)
    qs = [q[:, i * DK : (i + 1) * DK] for i in range(heads)]
    ks = [k[:, i * DK : (i + 1) * DK] for i in range(heads)]
    vs = [v[:, i * DV : (i + 1) * DV] for i in range(heads)]
    aff = [nt(qs[i], ks[i]) * scale for i in range(heads)]
    affc = [jnp.where(cm.mask_c, block_nt(qs[i], ks[i]) * scale, 0.0) for i in range(heads)]
    s = jnp.zeros_like(la)
    parts = []
    for x, mask in zip(cm.x, cm.masks):
        g = x * cm.om
        part = x * cm.by_head([nn3(jnp.where(mask, aff[i], 0.0), g) for i in range(heads)])
        parts.append(part)
        s = s + part
    for jj in range(B):
        s = s + cm.by_head([wide(affc[i], jj) for i in range(heads)]) * (
            cm.decay_from(jj) * cm.om_at(jj)
        )
    top = cm.by_head(
        [
            jnp.max(jnp.where(cm.lane_head == i, s, -jnp.inf), axis=1, keepdims=True)
            for i in range(heads)
        ]
    )
    e = jnp.exp(s - top)
    total = cm.by_head([jnp.sum(cm.only(e, i), axis=1, keepdims=True) for i in range(heads)])
    p = e / total
    mix = [jnp.zeros((cm.length, cm.length), f32) for _ in range(heads)]
    for x, mask in zip(cm.x, cm.masks):
        g = x * cm.om
        px = p * x
        for i in range(heads):
            mix[i] = mix[i] + jnp.where(mask, nt(cm.only(px, i), g), 0.0)
    mix = [m.astype(bf16) for m in mix]
    pieces = [(p * (cm.decay_from(jj) * cm.om_at(jj))).astype(bf16) for jj in range(B)]
    mixc = nn(jnp.concatenate(pieces, axis=1), collect(cm.lanes, heads))
    mixc = [
        jnp.where(cm.mask_c, mixc[:, i * 128 : i * 128 + B], 0.0) for i in range(heads)
    ]
    outs = [nn(mix[i], vs[i]) + block_nn(mixc[i], vs[i]) for i in range(heads)]
    return outs, p, parts, mix, mixc


def backward_math(q, k, v, la, starts, p, parts, mix, mixc, dout):
    heads = q.shape[1] // DK
    scale = 1.0 / math.sqrt(DK)
    cm = Common(la, starts)
    qs = [q[:, i * DK : (i + 1) * DK] for i in range(heads)]
    ks = [k[:, i * DK : (i + 1) * DK] for i in range(heads)]
    vs = [v[:, i * DV : (i + 1) * DV] for i in range(heads)]
    dos = [dout[:, i * DV : (i + 1) * DV].astype(bf16) for i in range(heads)]
    aff = [nt(qs[i], ks[i]) * scale for i in range(heads)]
    affc = [jnp.where(cm.mask_c, block_nt(qs[i], ks[i]) * scale, 0.0) for i in range(heads)]
    dmix = [nt(dos[i], vs[i]) for i in range(heads)]
    dmixc = [jnp.where(cm.mask_c, block_nt(dos[i], vs[i]), 0.0) for i in range(heads)]
    dp = jnp.zeros_like(la)
    dparts = []
    for x, mask in zip(cm.x, cm.masks):
        g = x * cm.om
        part = x * cm.by_head([nn3(jnp.where(mask, dmix[i], 0.0), g) for i in range(heads)])
        dparts.append(part)
        dp = dp + part
    for jj in range(B):
        dp = dp + cm.by_head([wide(dmixc[i], jj) for i in range(heads)]) * (
            cm.decay_from(jj) * cm.om_at(jj)
        )
    pdp = p * dp
    inner = cm.by_head([jnp.sum(cm.only(pdp, i), axis=1, keepdims=True) for i in range(heads)])
    ds = pdp - p * inner
    daff = [jnp.zeros((cm.length, cm.length), f32) for _ in range(heads)]
    dla = jnp.zeros_like(la)
    reach = jnp.zeros_like(la)
    for n, h in enumerate(cm.levels):
        x, mask = cm.x[n], cm.masks[n]
        g = x * cm.om
        dsx, px = ds * x, p * x
        both = jnp.concatenate([dsx, px], axis=0).astype(bf16)
        cols = []
        for i in range(heads):
            daff[i] = daff[i] + jnp.where(mask, nt(cm.only(dsx, i), g), 0.0)
            left = jnp.concatenate(
                [jnp.where(mask, aff[i], 0.0), jnp.where(mask, dmix[i], 0.0)], axis=0
            )
            cols.append(tn(left, both))
        r = x * cm.by_head(cols)
        reach = reach + r
        right = (cm.rows & h) != 0
        flow = jnp.where(right, ds * parts[n] + p * dparts[n], cm.om * r)
        s = 1
        while s < h:
            flow = flow + jnp.where((cm.rows & (h - 1)) < h - s, shift_up(flow, s), 0.0)
            s *= 2
        dla = dla + jnp.where(right, flow, row_pick(flow, h, 0) - flow)
    flow = jnp.zeros_like(la)
    near = jnp.zeros_like(la)
    pieces = []
    for jj in range(B):
        w = cm.decay_from(jj)
        omj = cm.om_at(jj)
        aj = cm.by_head([wide(affc[i], jj) for i in range(heads)])
        dj = cm.by_head([wide(dmixc[i], jj) for i in range(heads)])
        pieces.append((ds * (w * omj)).astype(bf16))
        z = w * (aj * ds + dj * p)
        flow = flow + omj * z
        z3 = blocks(z)
        tot = jnp.broadcast_to(jnp.sum(z3, axis=1, keepdims=True), z3.shape).reshape(z.shape)
        near = jnp.where((cm.rows & (B - 1)) == jj, tot, near)
    flow = flow - cm.om * near
    s = 1
    while s < B:
        flow = flow + jnp.where((cm.rows & (B - 1)) < B - s, shift_up(flow, s), 0.0)
        s *= 2
    dla = dla + flow - cm.alpha * (reach + near)
    daffc = nn(jnp.concatenate(pieces, axis=1), collect(cm.lanes, heads))
    daffc = [
        jnp.where(cm.mask_c, daffc[:, i * 128 : i * 128 + B], 0.0) for i in range(heads)
    ]
    dq, dk, dv = [], [], []
    for i in range(heads):
        da = daff[i].astype(bf16)
        dq.append((nn(da, ks[i]) + block_nn(daffc[i], ks[i])) * scale)
        dk.append((tn(da, qs[i]) + block_tn(daffc[i], qs[i])) * scale)
        dv.append(tn(mix[i], dos[i]) + block_tn(mixc[i], dos[i]))
    return dq, dk, dv, dla


def head_split(outs, ref, width):
    for i, x in enumerate(outs):
        ref[:, i * width : (i + 1) * width] = x.astype(ref.dtype)


def forward_kernel(starts_ref, q_ref, k_ref, v_ref, la_ref, o_ref, p_ref, parts_ref, mix_ref, mixc_ref):
    starts = [starts_ref[0, n] for n in range(starts_ref.shape[1])]
    outs, p, parts, mix, mixc = forward_math(
        q_ref[...], k_ref[...], v_ref[...], la_ref[...], starts
    )
    head_split(outs, o_ref, DV)
    p_ref[...] = p
    for n, x in enumerate(parts):
        parts_ref[n] = x
    for i in range(len(mix)):
        mix_ref[i] = mix[i]
        mixc_ref[i] = mixc[i].astype(bf16)


tau_inv = 0.125


def silu_slope(values):
    sigmoid_val = jax.nn.sigmoid(values)
    return sigmoid_val * (1.0 + values * (1.0 - sigmoid_val))


def through_silu(grads, z):
    width = grads[0].shape[1]
    return [g * silu_slope(z[:, i * width : (i + 1) * width]) for i, g in enumerate(grads)]


def through_gate(dla, zf):
    return dla * tau_inv * jax.nn.sigmoid(-zf)


INNER = 4


def share_columns(wide_parts, dzf, shares_ref):
    lanes = dzf.shape[1]
    size = lanes // INNER
    lane = lax.broadcasted_iota(jnp.int32, dzf.shape, 1)
    for n in range(INNER):
        at = 0
        for x in wide_parts:
            width = x.shape[1] // INNER
            shares_ref[n, :, at : at + width] = x[:, n * width : (n + 1) * width]
            at += width
        turned = pltpu.roll(dzf, (lanes - n * size) % lanes, 1) if n else dzf
        shares_ref[n, :, at : at + lanes] = jnp.where(lane < size, turned, 0.0).astype(bf16)


def backward_kernel(
    starts_ref, q_ref, k_ref, v_ref, la_ref, p_ref, parts_ref, mix_ref, mixc_ref, do_ref,
    zq_ref, zk_ref, zv_ref, zf_ref, dzq_ref, dzk_ref, dzv_ref, dzf_ref, shares_ref,
):
    starts = [starts_ref[0, n] for n in range(starts_ref.shape[1])]
    heads = mix_ref.shape[0]
    dq, dk, dv, dla = backward_math(
        q_ref[...],
        k_ref[...],
        v_ref[...],
        la_ref[...],
        starts,
        p_ref[...],
        [parts_ref[n] for n in range(parts_ref.shape[0])],
        [mix_ref[i] for i in range(heads)],
        [mixc_ref[i] for i in range(heads)],
        do_ref[...],
    )
    for grads, z_ref, dz_ref in ((dq, zq_ref, dzq_ref), (dk, zk_ref, dzk_ref), (dv, zv_ref, dzv_ref)):
        head_split(through_silu(grads, z_ref[...]), dz_ref, grads[0].shape[1])
    dzf = through_gate(dla, zf_ref[...])
    dzf_ref[...] = dzf.astype(bf16)
    share_columns([dzq_ref[...], dzk_ref[...], dzv_ref[...]], dzf, shares_ref)


SMEM = pl.BlockSpec(memory_space=pltpu.SMEM)
VMEM = pl.BlockSpec(memory_space=pltpu.VMEM)


def attend_forward(q, k, v, la, starts):
    length, lanes = la.shape
    heads = q.shape[1] // DK
    sds = jax.ShapeDtypeStruct
    return pl.pallas_call(
        forward_kernel,
        out_shape=(
            sds((length, heads * DV), bf16),
            sds((length, lanes), f32),
            sds((len(level_sizes(length)), length, lanes), f32),
            sds((heads, length, length), bf16),
            sds((heads, length, B), bf16),
        ),
        in_specs=[SMEM] + [VMEM] * 4,
        out_specs=(VMEM,) * 5,
        cost_estimate=pl.CostEstimate(
            flops=4 * 10**9, transcendentals=10**6, bytes_accessed=4 * 10**6
        ),
        name="slot_forward",
    )(starts, q, k, v, la)


def attend_backward(q, k, v, la, starts, saved, dout, pres):
    sds = jax.ShapeDtypeStruct
    return pl.pallas_call(
        backward_kernel,
        out_shape=(
            sds(q.shape, bf16),
            sds(k.shape, bf16),
            sds(v.shape, bf16),
            sds(la.shape, bf16),
            sds((INNER, q.shape[0], (2 * DK + DV) * (q.shape[1] // DK) // INNER + la.shape[1]), bf16),
        ),
        in_specs=[SMEM] + [VMEM] * 13,
        out_specs=(VMEM,) * 5,
        cost_estimate=pl.CostEstimate(
            flops=12 * 10**9, transcendentals=10**6, bytes_accessed=8 * 10**6
        ),
        name="slot_backward",
    )(starts, q, k, v, la, *saved, dout, *pres)


eps = 1e-06
LAP = (0, 1, 3, 2)


def rms_scale(values):
    return lax.rsqrt(jnp.mean(values * values, axis=-1, keepdims=True) + eps)


def norm_back(values, scale, gain, upstream):
    gain_grad = jnp.sum(upstream * values * scale, axis=0, keepdims=True)
    weighted = upstream * gain
    input_grad = scale * weighted - values * (scale * scale * scale) * jnp.mean(
        weighted * values, axis=-1, keepdims=True
    )
    return (gain_grad, input_grad)


class Grid:
    def __init__(self, dp):
        self.dp = dp
        self.outer = dp // INNER
        self.laps = [[o * INNER + i for i in LAP] for o in range(self.outer)]
        self.rows = [[o * INNER + i for i in range(INNER)] for o in range(self.outer)]
        self.cols = [[o * INNER + i for o in range(self.outer)] for i in range(INNER)]
        self.gathered = [o * INNER + i for i in LAP for o in range(self.outer)]
        self.natural = inverse(self.gathered)
        self.up = [(d, d + INNER) for d in range(dp - INNER)]
        self.down = [(d + INNER, d) for d in range(dp - INNER)]


def reorder(x, order):
    size = x.shape[-1] // len(order)
    return jnp.concatenate([x[..., b * size : (b + 1) * size] for b in order], axis=-1)


def inverse(order):
    back = [0] * len(order)
    for n, b in enumerate(order):
        back[b] = n
    return back


def swap(x):
    return lax.ppermute(x, "head", [(0, 1), (1, 0)])


def half_of(x, which):
    size = x.shape[0] // 2
    return lax.dynamic_slice_in_dim(x, which * size, size, 0)


def join(mine, other, core):
    size = mine.shape[0]
    out = jnp.zeros((2 * size,) + mine.shape[1:], mine.dtype)
    out = lax.dynamic_update_slice_in_dim(out, mine, core * size, 0)
    return lax.dynamic_update_slice_in_dim(out, other, (1 - core) * size, 0)


def on_rows(kernel, name, core, halves, wholes, outs):
    rows = halves[0].shape[0] // 2
    specs = [pl.BlockSpec((rows, x.shape[1]), lambda i, c: (c[0], 0)) for x in halves]
    specs += [pl.BlockSpec(x.shape, lambda i, c: (0, 0)) for x in wholes]
    return pl.pallas_call(
        kernel,
        out_shape=outs,
        grid_spec=pltpu.PrefetchScalarGridSpec(
            num_scalar_prefetch=1,
            grid=(1,),
            in_specs=specs,
            out_specs=[pl.BlockSpec(x.shape, lambda i, c: (0, 0)) for x in outs],
        ),
        name=name,
    )(core.reshape(1), *halves, *wholes)


def aligned(grid, width):
    return (width // grid.dp) % 128 == 0


def put_in_order(x, order, grid, inside):
    return reorder(x, order) if aligned(grid, x.shape[1]) == inside else x


def cotangent_rows(out_grad, core, grid):
    rows, width = out_grad.shape

    def kernel(core_ref, cot_ref, out_ref):
        out_ref[...] = put_in_order(cot_ref[...], grid.gathered, grid, True)

    outs = [jax.ShapeDtypeStruct((rows // 2, width), bf16)]
    (x,) = on_rows(kernel, "cotangent_rows", core, [out_grad], [], outs)
    return put_in_order(x, grid.gathered, grid, False)


def second_norm(block_in, mine, other, gain, core, grid):
    rows, width = mine.shape

    def kernel(core_ref, in_ref, mine_ref, other_ref, gain_ref, hidden_ref, normed_ref):
        hidden = in_ref[...].astype(f32) + (mine_ref[...] + other_ref[...])
        hidden_ref[...] = hidden
        normed = (hidden * rms_scale(hidden) * gain_ref[...]).astype(bf16)
        normed_ref[...] = put_in_order(normed, grid.gathered, grid, True)

    outs = [jax.ShapeDtypeStruct((rows, width), f32), jax.ShapeDtypeStruct((rows, width), bf16)]
    hidden, normed = on_rows(
        kernel, "second_norm", core, [block_in], [mine, other, gain[None]], outs
    )
    return hidden, put_in_order(normed, grid.gathered, grid, False)


def second_norm_back(out_grad, hidden, gain, parts, core, grid):
    rows, width = hidden.shape
    parts = [put_in_order(x, grid.natural, grid, False) for x in parts]

    def kernel(core_ref, cot_ref, hidden_ref, gain_ref, *refs):
        upstream = sum(x[...].astype(f32) for x in refs[: len(parts)])
        upstream = put_in_order(upstream, grid.natural, grid, True)
        grad_ref, low_ref, gain_grad_ref = refs[len(parts) :]
        hidden = hidden_ref[...]
        gain_grad, grad = norm_back(hidden, rms_scale(hidden), gain_ref[...], upstream)
        grad = grad + cot_ref[...].astype(f32)
        grad_ref[...] = grad
        low_ref[...] = grad.astype(bf16)
        gain_grad_ref[...] = gain_grad

    sds = jax.ShapeDtypeStruct
    outs = [sds((rows, width), f32), sds((rows, width), bf16), sds((1, width), f32)]
    return on_rows(
        kernel, "second_norm_back", core, [out_grad], [hidden, gain[None], *parts], outs
    )


def first_norm_back(block_in, grad, gain, mine, other, core):
    rows, width = grad.shape

    def kernel(core_ref, in_ref, grad_ref, gain_ref, mine_ref, other_ref, out_ref, gain_grad_ref):
        inputs = in_ref[...].astype(f32)
        upstream = mine_ref[...] + other_ref[...]
        gain_grad, out = norm_back(inputs, rms_scale(inputs), gain_ref[...], upstream)
        out_ref[...] = out + grad_ref[...]
        gain_grad_ref[...] = gain_grad

    sds = jax.ShapeDtypeStruct
    outs = [sds((rows, width), f32), sds((1, width), f32)]
    return on_rows(
        kernel, "first_norm_back", core, [block_in], [grad, gain[None], mine, other], outs
    )


def block_result(block_in, hidden, parts, core, grid):
    rows, width = hidden.shape
    parts = [put_in_order(x, grid.natural, grid, False) for x in parts]

    def kernel(core_ref, in_ref, hidden_ref, *refs):
        out = sum(x[...].astype(f32) for x in refs[: len(parts)])
        out = put_in_order(out, grid.natural, grid, True)
        refs[-1][...] = (hidden_ref[...] + out).astype(bf16)

    outs = [jax.ShapeDtypeStruct((rows, width), bf16)]
    (x,) = on_rows(kernel, "block_result", core, [block_in], [hidden, *parts], outs)
    return x


def exchange(x, split, concat, groups):
    return lax.all_to_all(x, "dp", split, concat, tiled=True, axis_index_groups=groups)


def tie(*values):
    return lax.optimization_barrier(values)


def gather_along(x, grid, place, beside=()):
    n = grid.outer
    above = below = x
    from_below, from_above, done = [], [], []
    other = swap(x)
    for k in range(n - 1):
        below = lax.ppermute(below, "dp", grid.up)
        above = lax.ppermute(above, "dp", grid.down)
        extra = beside[k] if k < len(beside) else ()
        extra = extra(*done) if callable(extra) else extra
        below, above, *extra = tie(below, above, *extra)
        from_below.append((below, swap(below)))
        from_above.append((above, swap(above)))
        done += extra
    blocks = [x]
    for c in range(2):
        blocks += [other] if c else []
        for k in range(1, n):
            blocks.append(
                jnp.where(place + k < n, from_above[k - 1][c], from_below[n - 1 - k][c])
            )
    return jnp.concatenate(blocks, axis=0), done


def add_other_core(x, grid):
    n = grid.outer
    size = x.shape[0] // (2 * n)
    block = [x[k * size : (k + 1) * size] for k in range(2 * n)]
    other = tie(*[swap(block[n + k].astype(bf16)) for k in range(n)])
    return [block[k] + other[k].astype(f32) for k in range(n)]


def scatter_along(own, grid, beside=()):
    n = grid.outer
    up = down = None
    done = []
    for k in range(n - 1):
        up = own[n - 1 - k] if up is None else own[n - 1 - k] + up.astype(f32)
        down = own[1 + k] if down is None else own[1 + k] + down.astype(f32)
        up = lax.ppermute(up.astype(bf16), "dp", grid.up)
        down = lax.ppermute(down.astype(bf16), "dp", grid.down)
        extra = beside[k] if k < len(beside) else ()
        extra = extra(*done) if callable(extra) else extra
        up, down, *extra = tie(up, down, *extra)
        done += extra
    return (own[0], up, down), done


def plane_gather(x, grid, inner):
    out = jnp.zeros((INNER,) + x.shape, x.dtype)
    for k in range(INNER):
        y = x
        if k:
            y = lax.ppermute(x, "dp", [(d, d ^ k) for d in range(grid.dp)])
        out = lax.dynamic_update_slice_in_dim(out, y[None], inner ^ k, 0)
    return out


def on_device(
    block_in,
    out_grad,
    attn_gain,
    mlp_gain,
    w_query,
    w_key,
    w_value,
    w_forget,
    w_output,
    w_gate,
    w_up,
    w_down,
    doc_starts,
    grid,
):
    core = lax.axis_index("head")
    place = lax.axis_index("dp") // INNER
    inner = lax.axis_index("dp") % INNER

    def columns(w):
        return exchange(w, 1, 0, grid.cols)

    def gather_rows(w):
        return lax.all_gather(w, "dp", axis=0, tiled=True, axis_index_groups=grid.laps)

    def column_pairs(a, b):
        rows = a.shape[0]
        both = [w.reshape(rows, grid.outer, -1) for w in (a, b)]
        both = columns(jnp.concatenate(both, axis=2).reshape(rows, -1))
        return jnp.split(both, 2, axis=1)

    gate_piece, up_piece = column_pairs(w_gate, w_up)
    inputs_f = block_in.astype(f32)
    normed = (inputs_f * rms_scale(inputs_f) * attn_gain).astype(bf16)
    query_pre = nn(normed, w_query)
    key_pre = nn(normed, w_key)
    value_pre = nn(normed, w_value)
    forget_pre = nn(normed, w_forget)
    query = jax.nn.silu(query_pre).astype(bf16)
    key = jax.nn.silu(key_pre).astype(bf16)
    value = jax.nn.silu(value_pre).astype(bf16)
    log_keep = jax.nn.log_sigmoid(forget_pre) * tau_inv
    mixed, *saved = attend_forward(query, key, value, log_keep, doc_starts)
    normed_own = lax.all_gather(
        half_of(normed, core), "dp", axis=0, tiled=True, axis_index_groups=grid.rows
    )
    branch_other = swap(nt(half_of(mixed, 1 - core), w_output))
    branch_mine = nt(half_of(mixed, core), w_output)
    branch_mine, gate_piece, up_piece, down_later, normed_own = tie(
        branch_mine, gate_piece, up_piece, w_down, normed_own
    )
    full_gate, full_up = gather_rows(gate_piece), gather_rows(up_piece)
    down_piece = columns(down_later)

    hidden, normed_two = second_norm(block_in, branch_mine, branch_other, mlp_gain, core, grid)
    def plane_tokens(own):
        own = own.reshape(INNER, 1, -1, own.shape[-1])
        out = jnp.zeros((INNER, 2) + own.shape[2:], own.dtype)
        out = lax.dynamic_update_slice_in_dim(out, own, core, 1)
        out = lax.dynamic_update_slice_in_dim(out, swap(own), 1 - core, 1)
        return out.reshape(-1, own.shape[-1])

    def plane_columns(shares):
        return exchange(shares.reshape(-1, shares.shape[2]), 0, 0, grid.rows)

    def plane_product(left, right):
        return tn(left, right).astype(bf16)

    def plane_sum(g):
        return lax.psum_scatter(
            g, "dp", scatter_dimension=0, tiled=True, axis_index_groups=grid.cols
        )

    def from_plane(g):
        size = g.shape[1]
        return exchange(g, 0, 1, grid.rows).reshape(-1, INNER, size).astype(f32)

    cot_rows = cotangent_rows(out_grad, core, grid)
    tokens, (cot_rows, down_piece, normed_plane, full_gate) = gather_along(
        normed_two,
        grid,
        place,
        ((cot_rows, down_piece), (plane_tokens(normed_own),), (full_gate,)),
    )
    full_down = gather_rows(down_piece)
    cot_all, (gate_act, full_up, up_act, full_down) = gather_along(
        cot_rows,
        grid,
        place,
        (
            (nn(tokens, full_gate), full_up),
            (),
            (nn(tokens, full_up), full_down),
        ),
    )

    def scatter_rows(g):
        return lax.psum_scatter(
            g, "dp", scatter_dimension=0, tiled=True, axis_index_groups=grid.laps
        )

    def to_columns(g):
        return exchange(g, 0, 1, grid.cols).astype(f32)

    inner_grad = nn(cot_all, full_down)
    gate_grad = (inner_grad * up_act * silu_slope(gate_act)).astype(bf16)
    up_grad = (inner_grad * jax.nn.silu(gate_act)).astype(bf16)
    inner_act = (jax.nn.silu(gate_act) * up_act).astype(bf16)
    back_parts, (down_rows, gate_rows, *out_own, up_rows) = scatter_along(
        add_other_core(nt(gate_grad, full_gate) + nt(up_grad, full_up), grid),
        grid,
        (
            (tn(cot_all, inner_act).astype(bf16), tn(tokens, gate_grad).astype(bf16)),
            add_other_core(nt(inner_act, full_down), grid),
            (tn(tokens, up_grad).astype(bf16),),
        ),
    )
    down_rows, gate_rows = scatter_rows(down_rows), scatter_rows(gate_rows)
    out_blocks = jnp.zeros((grid.outer,) + out_own[0].shape, bf16)
    for k, x in enumerate(out_own):
        at = (place + k) % grid.outer
        out_blocks = lax.dynamic_update_slice_in_dim(out_blocks, x.astype(bf16)[None], at, 0)
    out_blocks = out_blocks.reshape(-1, out_blocks.shape[2])
    out_sum = lax.psum_scatter(
        out_blocks, "dp", scatter_dimension=0, tiled=True, axis_index_groups=grid.cols
    )
    up_rows = scatter_rows(up_rows)
    hidden_grad, low_half, mlp_gain_part = second_norm_back(
        out_grad, hidden, mlp_gain, back_parts, core, grid
    )
    branch_grad = join(low_half, swap(low_half), core)
    mixed_grad = nn(branch_grad, w_output).astype(bf16)
    mixed_grad, down_rows = tie(mixed_grad, down_rows)
    *pre_grads, shares = attend_backward(
        query, key, value, log_keep, doc_starts, saved, mixed_grad,
        (query_pre, key_pre, value_pre, forget_pre),
    )
    down_sum = to_columns(down_rows)
    down_sum, shares, *pre_grads = tie(down_sum, shares, *pre_grads)
    pre_grad = plane_product(normed_plane, plane_columns(shares))
    _, low_half, mixed = tie(pre_grad, low_half, mixed)
    mixed_plane = plane_columns(jnp.stack(jnp.split(mixed, INNER, axis=1)))
    low_plane = plane_tokens(plane_gather(low_half, grid, inner))
    sums, output_grad = tie(plane_sum(pre_grad), plane_product(low_plane, mixed_plane))
    output_sum = plane_sum(output_grad)
    result = block_result(block_in, hidden, [out_sum], core, grid)
    result = join(result, swap(result), core)

    sums = from_plane(sums)
    output_sum = from_plane(output_sum).reshape(sums.shape[0], -1)
    ends = [0]
    for g in pre_grads:
        ends.append(ends[-1] + g.shape[1] // INNER)
    query_sum, key_sum, value_sum, forget_sum = (
        sums[:, :, a:b].reshape(sums.shape[0], -1) for a, b in zip(ends, ends[1:])
    )

    def normed_part(which):
        q, k, v, f = (half_of(g, which) for g in pre_grads)
        return nt(q, w_query) + nt(k, w_key) + nt(v, w_value) + nt(f, w_forget)

    part_other = swap(normed_part(1 - core))
    input_grad, attn_gain_part = first_norm_back(
        block_in, hidden_grad, attn_gain, normed_part(core), part_other, core
    )
    input_grad = join(input_grad, swap(input_grad), core)

    gains = jnp.concatenate([attn_gain_part, mlp_gain_part], axis=0)
    gains = gains + swap(gains)
    gains = jnp.swapaxes(gains.reshape(2, grid.dp, -1), 0, 1)
    gains = jnp.sum(lax.all_to_all(gains, "dp", 0, 0, tiled=True), axis=0)

    return (
        result,
        input_grad,
        gains[0],
        gains[1],
        query_sum,
        key_sum,
        value_sum,
        forget_sum,
        output_sum,
        to_columns(gate_rows),
        to_columns(up_rows),
        down_sum,
    )


def solution(mesh):
    placed = (
        P("dp", None),
        P("dp", None),
        P(),
        P(),
        P(None, "head"),
        P(None, "head"),
        P(None, "head"),
        P(None, "head"),
        P(None, "head"),
        P("dp", "head"),
        P("dp", "head"),
        P("dp", "head"),
        P("dp", None),
    )
    return jax.shard_map(
        partial(on_device, grid=Grid(mesh.shape["dp"])),
        mesh=mesh,
        in_specs=placed,
        out_specs=(P("dp", None), P("dp", None), P("dp"), P("dp")) + (P("dp", "head"),) * 8,
        check_vma=False,
    )
```

```python
import math
from functools import partial
import jax
import jax.numpy as jnp
from jax import lax
from jax.experimental import pallas as pl
from jax.experimental.pallas import tpu as pltpu
from jax.sharding import PartitionSpec as P

DK = 512
DV = 512
M = 64
B = 16
f32 = jnp.float32
bf16 = jnp.bfloat16


def nn(a, b):
    return jnp.dot(a.astype(bf16), b.astype(bf16), preferred_element_type=f32)


def nt(a, b):
    return lax.dot_general(
        a.astype(bf16), b.astype(bf16), (((1,), (1,)), ((), ())), preferred_element_type=f32
    )


def tn(a, b):
    return lax.dot_general(
        a.astype(bf16), b.astype(bf16), (((0,), (0,)), ((), ())), preferred_element_type=f32
    )


def nn3(a, b):
    ah, bh = a.astype(bf16), b.astype(bf16)
    al, bl = (a - ah.astype(f32)).astype(bf16), (b - bh.astype(f32)).astype(bf16)
    return nn(ah, bh) + (nn(al, bh) + nn(ah, bl))


def shift_up(x, s):
    return pltpu.roll(x, x.shape[0] - s, 0)


def shift_down(x, s):
    return pltpu.roll(x, s, 0)


def segment_at(pos, starts):
    seg = jnp.zeros(pos.shape, jnp.int32)
    for s in starts:
        seg = seg + (pos >= s).astype(jnp.int32)
    return seg


def same_document(t, j, starts):
    ok = None
    for s in starts:
        same = (t >= s) == (j >= s)
        ok = same if ok is None else ok & same
    return ok


def level_sizes(length):
    sizes = []
    h = length // 2
    while h >= B:
        sizes.append(h)
        h //= 2
    return sizes


def row_pick(x, size, row):
    n, lanes = x.shape
    x3 = x.reshape(n // size, size, lanes)
    return jnp.broadcast_to(x3[:, row : row + 1, :], x3.shape).reshape(n, lanes)


class Common:
    def __init__(self, la, starts):
        length, lanes = la.shape
        self.length, self.lanes = length, lanes
        rows = lax.broadcasted_iota(jnp.int32, (length, lanes), 0)
        self.rows = rows
        self.lane_head = lax.broadcasted_iota(jnp.int32, (length, lanes), 1) // M
        c = la
        s = 1
        while s < length:
            c = c + jnp.where(rows >= s, shift_down(c, s), 0.0)
            s *= 2
        self.c = c
        self.alpha = jnp.exp(la)
        self.om = 1.0 - self.alpha
        self.levels = level_sizes(length)
        self.x = []
        for h in self.levels:
            mid = row_pick(c, 2 * h, h - 1)
            self.x.append(jnp.exp(-jnp.abs(c - mid)))
        t = lax.broadcasted_iota(jnp.int32, (length, length), 0)
        j = lax.broadcasted_iota(jnp.int32, (length, length), 1)
        same = same_document(t, j, starts)
        self.masks = [
            same & ((t // (2 * h)) == (j // (2 * h))) & ((t & h) != 0) & ((j & h) == 0)
            for h in self.levels
        ]
        tc = lax.broadcasted_iota(jnp.int32, (length, B), 0)
        off = lax.broadcasted_iota(jnp.int32, (length, B), 1)
        jc = (tc - tc % B) + off
        self.mask_c = same_document(tc, jc, starts) & (jc <= tc)

    def by_head(self, parts):
        out = parts[0]
        for i in range(1, len(parts)):
            out = jnp.where(self.lane_head == i, parts[i], out)
        return out

    def only(self, x, i):
        return jnp.where(self.lane_head == i, x, 0.0)

    def decay_from(self, jj):
        return jnp.exp(jnp.minimum(self.c - row_pick(self.c, B, jj), 0.0))

    def om_at(self, jj):
        return row_pick(self.om, B, jj)


def blocks(x):
    return x.reshape(x.shape[0] // B, B, x.shape[1])


def block_nt(a, b):
    r = lax.dot_general(
        blocks(a.astype(bf16)),
        blocks(b.astype(bf16)),
        (((2,), (2,)), ((0,), (0,))),
        preferred_element_type=f32,
    )
    return r.reshape(a.shape[0], B)


def block_nn(a, b):
    r = lax.dot_general(
        blocks(a.astype(bf16)),
        blocks(b.astype(bf16)),
        (((2,), (1,)), ((0,), (0,))),
        preferred_element_type=f32,
    )
    return r.reshape(a.shape[0], b.shape[1])


def block_tn(a, b):
    at = jnp.swapaxes(blocks(a), 1, 2).astype(bf16)
    r = lax.dot_general(
        at, blocks(b.astype(bf16)), (((2,), (1,)), ((0,), (0,))), preferred_element_type=f32
    )
    return r.reshape(a.shape[0], b.shape[1])


def collect(lanes, heads):
    r = lax.broadcasted_iota(jnp.int32, (B * lanes, heads * 128), 0)
    col = lax.broadcasted_iota(jnp.int32, (B * lanes, heads * 128), 1)
    jj, head = r // lanes, (r % lanes) // M
    return jnp.where(col == head * 128 + jj, 1.0, 0.0).astype(bf16)


def wide(x, jj):
    return jnp.broadcast_to(x[:, jj : jj + 1], (x.shape[0], 128))


def forward_math(q, k, v, la, starts):
    heads = q.shape[1] // DK
    scale = 1.0 / math.sqrt(DK)
    cm = Common(la, starts)
    qs = [q[:, i * DK : (i + 1) * DK] for i in range(heads)]
    ks = [k[:, i * DK : (i + 1) * DK] for i in range(heads)]
    vs = [v[:, i * DV : (i + 1) * DV] for i in range(heads)]
    aff = [nt(qs[i], ks[i]) * scale for i in range(heads)]
    affc = [jnp.where(cm.mask_c, block_nt(qs[i], ks[i]) * scale, 0.0) for i in range(heads)]
    s = jnp.zeros_like(la)
    parts = []
    for x, mask in zip(cm.x, cm.masks):
        g = x * cm.om
        part = x * cm.by_head([nn3(jnp.where(mask, aff[i], 0.0), g) for i in range(heads)])
        parts.append(part)
        s = s + part
    for jj in range(B):
        s = s + cm.by_head([wide(affc[i], jj) for i in range(heads)]) * (
            cm.decay_from(jj) * cm.om_at(jj)
        )
    top = cm.by_head(
        [
            jnp.max(jnp.where(cm.lane_head == i, s, -jnp.inf), axis=1, keepdims=True)
            for i in range(heads)
        ]
    )
    e = jnp.exp(s - top)
    total = cm.by_head([jnp.sum(cm.only(e, i), axis=1, keepdims=True) for i in range(heads)])
    p = e / total
    mix = [jnp.zeros((cm.length, cm.length), f32) for _ in range(heads)]
    for x, mask in zip(cm.x, cm.masks):
        g = x * cm.om
        px = p * x
        for i in range(heads):
            mix[i] = mix[i] + jnp.where(mask, nt(cm.only(px, i), g), 0.0)
    mix = [m.astype(bf16) for m in mix]
    pieces = [(p * (cm.decay_from(jj) * cm.om_at(jj))).astype(bf16) for jj in range(B)]
    mixc = nn(jnp.concatenate(pieces, axis=1), collect(cm.lanes, heads))
    mixc = [
        jnp.where(cm.mask_c, mixc[:, i * 128 : i * 128 + B], 0.0) for i in range(heads)
    ]
    outs = [nn(mix[i], vs[i]) + block_nn(mixc[i], vs[i]) for i in range(heads)]
    return outs, p, parts, mix, mixc


def backward_math(q, k, v, la, starts, p, parts, mix, mixc, dout):
    heads = q.shape[1] // DK
    scale = 1.0 / math.sqrt(DK)
    cm = Common(la, starts)
    qs = [q[:, i * DK : (i + 1) * DK] for i in range(heads)]
    ks = [k[:, i * DK : (i + 1) * DK] for i in range(heads)]
    vs = [v[:, i * DV : (i + 1) * DV] for i in range(heads)]
    dos = [dout[:, i * DV : (i + 1) * DV].astype(bf16) for i in range(heads)]
    aff = [nt(qs[i], ks[i]) * scale for i in range(heads)]
    affc = [jnp.where(cm.mask_c, block_nt(qs[i], ks[i]) * scale, 0.0) for i in range(heads)]
    dmix = [nt(dos[i], vs[i]) for i in range(heads)]
    dmixc = [jnp.where(cm.mask_c, block_nt(dos[i], vs[i]), 0.0) for i in range(heads)]
    dp = jnp.zeros_like(la)
    dparts = []
    for x, mask in zip(cm.x, cm.masks):
        g = x * cm.om
        part = x * cm.by_head([nn3(jnp.where(mask, dmix[i], 0.0), g) for i in range(heads)])
        dparts.append(part)
        dp = dp + part
    for jj in range(B):
        dp = dp + cm.by_head([wide(dmixc[i], jj) for i in range(heads)]) * (
            cm.decay_from(jj) * cm.om_at(jj)
        )
    pdp = p * dp
    inner = cm.by_head([jnp.sum(cm.only(pdp, i), axis=1, keepdims=True) for i in range(heads)])
    ds = pdp - p * inner
    daff = [jnp.zeros((cm.length, cm.length), f32) for _ in range(heads)]
    dla = jnp.zeros_like(la)
    reach = jnp.zeros_like(la)
    for n, h in enumerate(cm.levels):
        x, mask = cm.x[n], cm.masks[n]
        g = x * cm.om
        dsx, px = ds * x, p * x
        both = jnp.concatenate([dsx, px], axis=0).astype(bf16)
        cols = []
        for i in range(heads):
            daff[i] = daff[i] + jnp.where(mask, nt(cm.only(dsx, i), g), 0.0)
            left = jnp.concatenate(
                [jnp.where(mask, aff[i], 0.0), jnp.where(mask, dmix[i], 0.0)], axis=0
            )
            cols.append(tn(left, both))
        r = x * cm.by_head(cols)
        reach = reach + r
        right = (cm.rows & h) != 0
        flow = jnp.where(right, ds * parts[n] + p * dparts[n], cm.om * r)
        s = 1
        while s < h:
            flow = flow + jnp.where((cm.rows & (h - 1)) < h - s, shift_up(flow, s), 0.0)
            s *= 2
        dla = dla + jnp.where(right, flow, row_pick(flow, h, 0) - flow)
    flow = jnp.zeros_like(la)
    near = jnp.zeros_like(la)
    pieces = []
    for jj in range(B):
        w = cm.decay_from(jj)
        omj = cm.om_at(jj)
        aj = cm.by_head([wide(affc[i], jj) for i in range(heads)])
        dj = cm.by_head([wide(dmixc[i], jj) for i in range(heads)])
        pieces.append((ds * (w * omj)).astype(bf16))
        z = w * (aj * ds + dj * p)
        flow = flow + omj * z
        z3 = blocks(z)
        tot = jnp.broadcast_to(jnp.sum(z3, axis=1, keepdims=True), z3.shape).reshape(z.shape)
        near = jnp.where((cm.rows & (B - 1)) == jj, tot, near)
    flow = flow - cm.om * near
    s = 1
    while s < B:
        flow = flow + jnp.where((cm.rows & (B - 1)) < B - s, shift_up(flow, s), 0.0)
        s *= 2
    dla = dla + flow - cm.alpha * (reach + near)
    daffc = nn(jnp.concatenate(pieces, axis=1), collect(cm.lanes, heads))
    daffc = [
        jnp.where(cm.mask_c, daffc[:, i * 128 : i * 128 + B], 0.0) for i in range(heads)
    ]
    dq, dk, dv = [], [], []
    for i in range(heads):
        da = daff[i].astype(bf16)
        dq.append((nn(da, ks[i]) + block_nn(daffc[i], ks[i])) * scale)
        dk.append((tn(da, qs[i]) + block_tn(daffc[i], qs[i])) * scale)
        dv.append(tn(mix[i], dos[i]) + block_tn(mixc[i], dos[i]))
    return dq, dk, dv, dla


def head_split(outs, ref, width):
    for i, x in enumerate(outs):
        ref[:, i * width : (i + 1) * width] = x.astype(ref.dtype)


def forward_kernel(starts_ref, q_ref, k_ref, v_ref, la_ref, o_ref, p_ref, parts_ref, mix_ref, mixc_ref):
    starts = [starts_ref[0, n] for n in range(starts_ref.shape[1])]
    outs, p, parts, mix, mixc = forward_math(
        q_ref[...], k_ref[...], v_ref[...], la_ref[...], starts
    )
    head_split(outs, o_ref, DV)
    p_ref[...] = p
    for n, x in enumerate(parts):
        parts_ref[n] = x
    for i in range(len(mix)):
        mix_ref[i] = mix[i]
        mixc_ref[i] = mixc[i].astype(bf16)


tau_inv = 0.125


def silu_slope(values):
    sigmoid_val = jax.nn.sigmoid(values)
    return sigmoid_val * (1.0 + values * (1.0 - sigmoid_val))


def through_silu(grads, z):
    width = grads[0].shape[1]
    return [g * silu_slope(z[:, i * width : (i + 1) * width]) for i, g in enumerate(grads)]


def through_gate(dla, zf):
    return dla * tau_inv * jax.nn.sigmoid(-zf)


INNER = 4


def share_columns(wide_parts, dzf, shares_ref):
    lanes = dzf.shape[1]
    size = lanes // INNER
    lane = lax.broadcasted_iota(jnp.int32, dzf.shape, 1)
    for n in range(INNER):
        at = 0
        for x in wide_parts:
            width = x.shape[1] // INNER
            shares_ref[n, :, at : at + width] = x[:, n * width : (n + 1) * width]
            at += width
        turned = pltpu.roll(dzf, (lanes - n * size) % lanes, 1) if n else dzf
        shares_ref[n, :, at : at + lanes] = jnp.where(lane < size, turned, 0.0).astype(bf16)


def backward_kernel(
    starts_ref, q_ref, k_ref, v_ref, la_ref, p_ref, parts_ref, mix_ref, mixc_ref, do_ref,
    zq_ref, zk_ref, zv_ref, zf_ref, dzq_ref, dzk_ref, dzv_ref, dzf_ref, shares_ref,
):
    starts = [starts_ref[0, n] for n in range(starts_ref.shape[1])]
    heads = mix_ref.shape[0]
    dq, dk, dv, dla = backward_math(
        q_ref[...],
        k_ref[...],
        v_ref[...],
        la_ref[...],
        starts,
        p_ref[...],
        [parts_ref[n] for n in range(parts_ref.shape[0])],
        [mix_ref[i] for i in range(heads)],
        [mixc_ref[i] for i in range(heads)],
        do_ref[...],
    )
    for grads, z_ref, dz_ref in ((dq, zq_ref, dzq_ref), (dk, zk_ref, dzk_ref), (dv, zv_ref, dzv_ref)):
        head_split(through_silu(grads, z_ref[...]), dz_ref, grads[0].shape[1])
    dzf = through_gate(dla, zf_ref[...])
    dzf_ref[...] = dzf.astype(bf16)
    share_columns([dzq_ref[...], dzk_ref[...], dzv_ref[...]], dzf, shares_ref)


SMEM = pl.BlockSpec(memory_space=pltpu.SMEM)
VMEM = pl.BlockSpec(memory_space=pltpu.VMEM)


def attend_forward(q, k, v, la, starts):
    length, lanes = la.shape
    heads = q.shape[1] // DK
    sds = jax.ShapeDtypeStruct
    return pl.pallas_call(
        forward_kernel,
        out_shape=(
            sds((length, heads * DV), bf16),
            sds((length, lanes), f32),
            sds((len(level_sizes(length)), length, lanes), f32),
            sds((heads, length, length), bf16),
            sds((heads, length, B), bf16),
        ),
        in_specs=[SMEM] + [VMEM] * 4,
        out_specs=(VMEM,) * 5,
        cost_estimate=pl.CostEstimate(
            flops=4 * 10**9, transcendentals=10**6, bytes_accessed=4 * 10**6
        ),
        name="slot_forward",
    )(starts, q, k, v, la)


def attend_backward(q, k, v, la, starts, saved, dout, pres):
    sds = jax.ShapeDtypeStruct
    return pl.pallas_call(
        backward_kernel,
        out_shape=(
            sds(q.shape, bf16),
            sds(k.shape, bf16),
            sds(v.shape, bf16),
            sds(la.shape, bf16),
            sds((INNER, q.shape[0], (2 * DK + DV) * (q.shape[1] // DK) // INNER + la.shape[1]), bf16),
        ),
        in_specs=[SMEM] + [VMEM] * 13,
        out_specs=(VMEM,) * 5,
        cost_estimate=pl.CostEstimate(
            flops=12 * 10**9, transcendentals=10**6, bytes_accessed=8 * 10**6
        ),
        name="slot_backward",
    )(starts, q, k, v, la, *saved, dout, *pres)


eps = 1e-06
LAP = (0, 1, 3, 2)


def rms_scale(values):
    return lax.rsqrt(jnp.mean(values * values, axis=-1, keepdims=True) + eps)


def norm_back(values, scale, gain, upstream):
    gain_grad = jnp.sum(upstream * values * scale, axis=0, keepdims=True)
    weighted = upstream * gain
    input_grad = scale * weighted - values * (scale * scale * scale) * jnp.mean(
        weighted * values, axis=-1, keepdims=True
    )
    return (gain_grad, input_grad)


class Grid:
    def __init__(self, dp):
        self.dp = dp
        self.outer = dp // INNER
        self.laps = [[o * INNER + i for i in LAP] for o in range(self.outer)]
        self.rows = [[o * INNER + i for i in range(INNER)] for o in range(self.outer)]
        self.cols = [[o * INNER + i for o in range(self.outer)] for i in range(INNER)]
        self.gathered = [o * INNER + i for i in LAP for o in range(self.outer)]
        self.natural = inverse(self.gathered)
        self.up = [(d, d + INNER) for d in range(dp - INNER)]
        self.down = [(d + INNER, d) for d in range(dp - INNER)]


def reorder(x, order):
    size = x.shape[-1] // len(order)
    return jnp.concatenate([x[..., b * size : (b + 1) * size] for b in order], axis=-1)


def inverse(order):
    back = [0] * len(order)
    for n, b in enumerate(order):
        back[b] = n
    return back


def swap(x):
    return lax.ppermute(x, "head", [(0, 1), (1, 0)])


def half_of(x, which):
    size = x.shape[0] // 2
    return lax.dynamic_slice_in_dim(x, which * size, size, 0)


def join(mine, other, core):
    size = mine.shape[0]
    out = jnp.zeros((2 * size,) + mine.shape[1:], mine.dtype)
    out = lax.dynamic_update_slice_in_dim(out, mine, core * size, 0)
    return lax.dynamic_update_slice_in_dim(out, other, (1 - core) * size, 0)


def on_rows(kernel, name, core, halves, wholes, outs):
    rows = halves[0].shape[0] // 2
    specs = [pl.BlockSpec((rows, x.shape[1]), lambda i, c: (c[0], 0)) for x in halves]
    specs += [pl.BlockSpec(x.shape, lambda i, c: (0, 0)) for x in wholes]
    return pl.pallas_call(
        kernel,
        out_shape=outs,
        grid_spec=pltpu.PrefetchScalarGridSpec(
            num_scalar_prefetch=1,
            grid=(1,),
            in_specs=specs,
            out_specs=[pl.BlockSpec(x.shape, lambda i, c: (0, 0)) for x in outs],
        ),
        name=name,
    )(core.reshape(1), *halves, *wholes)


def aligned(grid, width):
    return (width // grid.dp) % 128 == 0


def put_in_order(x, order, grid, inside):
    return reorder(x, order) if aligned(grid, x.shape[1]) == inside else x


def cotangent_rows(out_grad, core, grid):
    rows, width = out_grad.shape

    def kernel(core_ref, cot_ref, out_ref):
        out_ref[...] = put_in_order(cot_ref[...], grid.gathered, grid, True)

    outs = [jax.ShapeDtypeStruct((rows // 2, width), bf16)]
    (x,) = on_rows(kernel, "cotangent_rows", core, [out_grad], [], outs)
    return put_in_order(x, grid.gathered, grid, False)


def second_norm(block_in, mine, other, gain, core, grid):
    rows, width = mine.shape

    def kernel(core_ref, in_ref, mine_ref, other_ref, gain_ref, hidden_ref, normed_ref):
        hidden = in_ref[...].astype(f32) + (mine_ref[...] + other_ref[...])
        hidden_ref[...] = hidden
        normed = (hidden * rms_scale(hidden) * gain_ref[...]).astype(bf16)
        normed_ref[...] = put_in_order(normed, grid.gathered, grid, True)

    outs = [jax.ShapeDtypeStruct((rows, width), f32), jax.ShapeDtypeStruct((rows, width), bf16)]
    hidden, normed = on_rows(
        kernel, "second_norm", core, [block_in], [mine, other, gain[None]], outs
    )
    return hidden, put_in_order(normed, grid.gathered, grid, False)


def second_norm_back(out_grad, hidden, gain, parts, core, grid):
    rows, width = hidden.shape
    parts = [put_in_order(x, grid.natural, grid, False) for x in parts]

    def kernel(core_ref, cot_ref, hidden_ref, gain_ref, *refs):
        upstream = sum(x[...].astype(f32) for x in refs[: len(parts)])
        upstream = put_in_order(upstream, grid.natural, grid, True)
        grad_ref, low_ref, gain_grad_ref = refs[len(parts) :]
        hidden = hidden_ref[...]
        gain_grad, grad = norm_back(hidden, rms_scale(hidden), gain_ref[...], upstream)
        grad = grad + cot_ref[...].astype(f32)
        grad_ref[...] = grad
        low_ref[...] = grad.astype(bf16)
        gain_grad_ref[...] = gain_grad

    sds = jax.ShapeDtypeStruct
    outs = [sds((rows, width), f32), sds((rows, width), bf16), sds((1, width), f32)]
    return on_rows(
        kernel, "second_norm_back", core, [out_grad], [hidden, gain[None], *parts], outs
    )


def first_norm_back(block_in, grad, gain, mine, other, core):
    rows, width = grad.shape

    def kernel(core_ref, in_ref, grad_ref, gain_ref, mine_ref, other_ref, out_ref, gain_grad_ref):
        inputs = in_ref[...].astype(f32)
        upstream = mine_ref[...] + other_ref[...]
        gain_grad, out = norm_back(inputs, rms_scale(inputs), gain_ref[...], upstream)
        out_ref[...] = out + grad_ref[...]
        gain_grad_ref[...] = gain_grad

    sds = jax.ShapeDtypeStruct
    outs = [sds((rows, width), f32), sds((1, width), f32)]
    return on_rows(
        kernel, "first_norm_back", core, [block_in], [grad, gain[None], mine, other], outs
    )


def block_result(block_in, hidden, parts, core, grid):
    rows, width = hidden.shape
    parts = [put_in_order(x, grid.natural, grid, False) for x in parts]

    def kernel(core_ref, in_ref, hidden_ref, *refs):
        out = sum(x[...].astype(f32) for x in refs[: len(parts)])
        out = put_in_order(out, grid.natural, grid, True)
        refs[-1][...] = (hidden_ref[...] + out).astype(bf16)

    outs = [jax.ShapeDtypeStruct((rows, width), bf16)]
    (x,) = on_rows(kernel, "block_result", core, [block_in], [hidden, *parts], outs)
    return x


def exchange(x, split, concat, groups):
    return lax.all_to_all(x, "dp", split, concat, tiled=True, axis_index_groups=groups)


def tie(*values):
    return lax.optimization_barrier(values)


def gather_along(x, grid, place, beside=()):
    n = grid.outer
    above = below = x
    from_below, from_above, done = [], [], []
    other = swap(x)
    for k in range(n - 1):
        below = lax.ppermute(below, "dp", grid.up)
        above = lax.ppermute(above, "dp", grid.down)
        extra = beside[k] if k < len(beside) else ()
        extra = extra(*done) if callable(extra) else extra
        below, above, *extra = tie(below, above, *extra)
        from_below.append((below, swap(below)))
        from_above.append((above, swap(above)))
        done += extra
    blocks = [x]
    for c in range(2):
        blocks += [other] if c else []
        for k in range(1, n):
            blocks.append(
                jnp.where(place + k < n, from_above[k - 1][c], from_below[n - 1 - k][c])
            )
    return jnp.concatenate(blocks, axis=0), done


def by_core(x):
    size = x.shape[0] // 2
    return x[:size], x[size:].astype(bf16)


def add_other_core(mine, other, grid):
    n = grid.outer
    other = tie(*[swap(y) for y in jnp.split(other, n)])
    return [x + y.astype(f32) for x, y in zip(jnp.split(mine, n), other)]


def scatter_along(own, grid, beside=()):
    n = grid.outer
    up = down = None
    done = []
    for k in range(n - 1):
        up = own[n - 1 - k] if up is None else own[n - 1 - k] + up.astype(f32)
        down = own[1 + k] if down is None else own[1 + k] + down.astype(f32)
        up = lax.ppermute(up.astype(bf16), "dp", grid.up)
        down = lax.ppermute(down.astype(bf16), "dp", grid.down)
        extra = beside[k] if k < len(beside) else ()
        extra = extra(*done) if callable(extra) else extra
        up, down, *extra = tie(up, down, *extra)
        done += extra
    return (own[0], up, down), done


def plane_gather(x, grid, inner):
    out = jnp.zeros((INNER,) + x.shape, x.dtype)
    for k in range(INNER):
        y = x
        if k:
            y = lax.ppermute(x, "dp", [(d, d ^ k) for d in range(grid.dp)])
        out = lax.dynamic_update_slice_in_dim(out, y[None], inner ^ k, 0)
    return out


def on_device(
    block_in,
    out_grad,
    attn_gain,
    mlp_gain,
    w_query,
    w_key,
    w_value,
    w_forget,
    w_output,
    w_gate,
    w_up,
    w_down,
    doc_starts,
    grid,
):
    core = lax.axis_index("head")
    place = lax.axis_index("dp") // INNER
    inner = lax.axis_index("dp") % INNER

    def columns(w):
        return exchange(w, 1, 0, grid.cols)

    def gather_rows(w):
        return lax.all_gather(w, "dp", axis=0, tiled=True, axis_index_groups=grid.laps)

    def column_pairs(a, b):
        rows = a.shape[0]
        both = [w.reshape(rows, grid.outer, -1) for w in (a, b)]
        both = columns(jnp.concatenate(both, axis=2).reshape(rows, -1))
        return jnp.split(both, 2, axis=1)

    gate_piece, up_piece = column_pairs(w_gate, w_up)
    inputs_f = block_in.astype(f32)
    normed = (inputs_f * rms_scale(inputs_f) * attn_gain).astype(bf16)
    query_pre = nn(normed, w_query)
    key_pre = nn(normed, w_key)
    value_pre = nn(normed, w_value)
    forget_pre = nn(normed, w_forget)
    query = jax.nn.silu(query_pre).astype(bf16)
    key = jax.nn.silu(key_pre).astype(bf16)
    value = jax.nn.silu(value_pre).astype(bf16)
    log_keep = jax.nn.log_sigmoid(forget_pre) * tau_inv
    mixed, *saved = attend_forward(query, key, value, log_keep, doc_starts)
    normed_own = lax.all_gather(
        half_of(normed, core), "dp", axis=0, tiled=True, axis_index_groups=grid.rows
    )
    branch_other = swap(nt(half_of(mixed, 1 - core), w_output))
    branch_mine = nt(half_of(mixed, core), w_output)
    branch_mine, gate_piece, up_piece, down_later, normed_own = tie(
        branch_mine, gate_piece, up_piece, w_down, normed_own
    )
    full_gate, full_up = gather_rows(gate_piece), gather_rows(up_piece)
    down_piece = columns(down_later)

    hidden, normed_two = second_norm(block_in, branch_mine, branch_other, mlp_gain, core, grid)
    def plane_tokens(own):
        own = own.reshape(INNER, 1, -1, own.shape[-1])
        out = jnp.zeros((INNER, 2) + own.shape[2:], own.dtype)
        out = lax.dynamic_update_slice_in_dim(out, own, core, 1)
        out = lax.dynamic_update_slice_in_dim(out, swap(own), 1 - core, 1)
        return out.reshape(-1, own.shape[-1])

    def plane_columns(shares):
        return exchange(shares.reshape(-1, shares.shape[2]), 0, 0, grid.rows)

    def plane_product(left, right):
        return tn(left, right).astype(bf16)

    def plane_sum(g):
        return lax.psum_scatter(
            g, "dp", scatter_dimension=0, tiled=True, axis_index_groups=grid.cols
        )

    def from_plane(g):
        size = g.shape[1]
        return exchange(g, 0, 1, grid.rows).reshape(-1, INNER, size).astype(f32)

    cot_rows = cotangent_rows(out_grad, core, grid)
    tokens, (cot_rows, down_piece, normed_plane, full_gate) = gather_along(
        normed_two,
        grid,
        place,
        ((cot_rows, down_piece), (plane_tokens(normed_own),), (full_gate,)),
    )
    full_down = gather_rows(down_piece)
    def gated(gate, up):
        return (jax.nn.silu(gate) * up).astype(bf16)

    cot_all, (gate_act, full_up, up_act, full_down, out_mine, out_other) = gather_along(
        cot_rows,
        grid,
        place,
        (
            (nn(tokens, full_gate), full_up),
            lambda gate, w_up_all: (nn(tokens, w_up_all), full_down),
            lambda gate, _, up, w_down_all: by_core(nt(gated(gate, up), w_down_all)),
        ),
    )
    out_own = add_other_core(out_mine, out_other, grid)
    out_blocks = jnp.zeros((grid.outer,) + out_own[0].shape, bf16)
    for k, x in enumerate(out_own):
        at = (place + k) % grid.outer
        out_blocks = lax.dynamic_update_slice_in_dim(out_blocks, x.astype(bf16)[None], at, 0)
    out_blocks, cot_all = tie(out_blocks.reshape(-1, out_blocks.shape[2]), cot_all)
    out_sum = lax.psum_scatter(
        out_blocks, "dp", scatter_dimension=0, tiled=True, axis_index_groups=grid.cols
    )

    def scatter_rows(g):
        return lax.psum_scatter(
            g, "dp", scatter_dimension=0, tiled=True, axis_index_groups=grid.laps
        )

    def to_columns(g):
        return exchange(g, 0, 1, grid.cols).astype(f32)

    inner_grad = nn(cot_all, full_down)
    gate_grad = (inner_grad * up_act * silu_slope(gate_act)).astype(bf16)
    up_grad = (inner_grad * jax.nn.silu(gate_act)).astype(bf16)
    inner_act = gated(gate_act, up_act)
    back_parts, (down_rows, out_sum, gate_rows, up_rows) = scatter_along(
        add_other_core(*by_core(nt(gate_grad, full_gate) + nt(up_grad, full_up)), grid),
        grid,
        (
            (tn(cot_all, inner_act).astype(bf16), out_sum),
            (tn(tokens, gate_grad).astype(bf16),),
            (tn(tokens, up_grad).astype(bf16),),
        ),
    )
    down_rows, gate_rows, up_rows = (scatter_rows(g) for g in (down_rows, gate_rows, up_rows))
    hidden_grad, low_half, mlp_gain_part = second_norm_back(
        out_grad, hidden, mlp_gain, back_parts, core, grid
    )
    branch_grad = join(low_half, swap(low_half), core)
    mixed_grad = nn(branch_grad, w_output).astype(bf16)
    mixed_grad, down_rows = tie(mixed_grad, down_rows)
    *pre_grads, shares = attend_backward(
        query, key, value, log_keep, doc_starts, saved, mixed_grad,
        (query_pre, key_pre, value_pre, forget_pre),
    )
    down_sum = to_columns(down_rows)
    down_sum, shares, *pre_grads = tie(down_sum, shares, *pre_grads)
    pre_grad = plane_product(normed_plane, plane_columns(shares))
    _, low_half, mixed = tie(pre_grad, low_half, mixed)
    mixed_plane = plane_columns(jnp.stack(jnp.split(mixed, INNER, axis=1)))
    low_plane = plane_tokens(plane_gather(low_half, grid, inner))
    sums, output_grad = tie(plane_sum(pre_grad), plane_product(low_plane, mixed_plane))
    output_sum = plane_sum(output_grad)
    result = block_result(block_in, hidden, [out_sum], core, grid)
    result = join(result, swap(result), core)

    sums = from_plane(sums)
    output_sum = from_plane(output_sum).reshape(sums.shape[0], -1)
    ends = [0]
    for g in pre_grads:
        ends.append(ends[-1] + g.shape[1] // INNER)
    query_sum, key_sum, value_sum, forget_sum = (
        sums[:, :, a:b].reshape(sums.shape[0], -1) for a, b in zip(ends, ends[1:])
    )

    def normed_part(which):
        q, k, v, f = (half_of(g, which) for g in pre_grads)
        return nt(q, w_query) + nt(k, w_key) + nt(v, w_value) + nt(f, w_forget)

    part_other = swap(normed_part(1 - core))
    input_grad, attn_gain_part = first_norm_back(
        block_in, hidden_grad, attn_gain, normed_part(core), part_other, core
    )
    input_grad = join(input_grad, swap(input_grad), core)

    gains = jnp.concatenate([attn_gain_part, mlp_gain_part], axis=0)
    gains = gains + swap(gains)
    gains = jnp.swapaxes(gains.reshape(2, grid.dp, -1), 0, 1)
    gains = jnp.sum(lax.all_to_all(gains, "dp", 0, 0, tiled=True), axis=0)

    return (
        result,
        input_grad,
        gains[0],
        gains[1],
        query_sum,
        key_sum,
        value_sum,
        forget_sum,
        output_sum,
        to_columns(gate_rows),
        to_columns(up_rows),
        down_sum,
    )


def solution(mesh):
    placed = (
        P("dp", None),
        P("dp", None),
        P(),
        P(),
        P(None, "head"),
        P(None, "head"),
        P(None, "head"),
        P(None, "head"),
        P(None, "head"),
        P("dp", "head"),
        P("dp", "head"),
        P("dp", "head"),
        P("dp", None),
    )
    return jax.shard_map(
        partial(on_device, grid=Grid(mesh.shape["dp"])),
        mesh=mesh,
        in_specs=placed,
        out_specs=(P("dp", None), P("dp", None), P("dp"), P("dp")) + (P("dp", "head"),) * 8,
        check_vma=False,
    )
```

```python
import math
from functools import partial
import jax
import jax.numpy as jnp
from jax import lax
from jax.experimental import pallas as pl
from jax.experimental.pallas import tpu as pltpu
from jax.sharding import PartitionSpec as P

DK = 512
DV = 512
M = 64
B = 16
f32 = jnp.float32
bf16 = jnp.bfloat16


def nn(a, b):
    return jnp.dot(a.astype(bf16), b.astype(bf16), preferred_element_type=f32)


def nt(a, b):
    return lax.dot_general(
        a.astype(bf16), b.astype(bf16), (((1,), (1,)), ((), ())), preferred_element_type=f32
    )


def tn(a, b):
    return lax.dot_general(
        a.astype(bf16), b.astype(bf16), (((0,), (0,)), ((), ())), preferred_element_type=f32
    )


def nn3(a, b):
    ah, bh = a.astype(bf16), b.astype(bf16)
    al, bl = (a - ah.astype(f32)).astype(bf16), (b - bh.astype(f32)).astype(bf16)
    return nn(ah, bh) + (nn(al, bh) + nn(ah, bl))


def shift_up(x, s):
    return pltpu.roll(x, x.shape[0] - s, 0)


def shift_down(x, s):
    return pltpu.roll(x, s, 0)


def segment_at(pos, starts):
    seg = jnp.zeros(pos.shape, jnp.int32)
    for s in starts:
        seg = seg + (pos >= s).astype(jnp.int32)
    return seg


def same_document(t, j, starts):
    ok = None
    for s in starts:
        same = (t >= s) == (j >= s)
        ok = same if ok is None else ok & same
    return ok


def level_sizes(length):
    sizes = []
    h = length // 2
    while h >= B:
        sizes.append(h)
        h //= 2
    return sizes


def row_pick(x, size, row):
    n, lanes = x.shape
    x3 = x.reshape(n // size, size, lanes)
    return jnp.broadcast_to(x3[:, row : row + 1, :], x3.shape).reshape(n, lanes)


class Common:
    def __init__(self, la, starts):
        length, lanes = la.shape
        self.length, self.lanes = length, lanes
        rows = lax.broadcasted_iota(jnp.int32, (length, lanes), 0)
        self.rows = rows
        self.lane_head = lax.broadcasted_iota(jnp.int32, (length, lanes), 1) // M
        c = la
        s = 1
        while s < length:
            c = c + jnp.where(rows >= s, shift_down(c, s), 0.0)
            s *= 2
        self.c = c
        self.alpha = jnp.exp(la)
        self.om = 1.0 - self.alpha
        self.levels = level_sizes(length)
        self.x = []
        for h in self.levels:
            mid = row_pick(c, 2 * h, h - 1)
            self.x.append(jnp.exp(-jnp.abs(c - mid)))
        t = lax.broadcasted_iota(jnp.int32, (length, length), 0)
        j = lax.broadcasted_iota(jnp.int32, (length, length), 1)
        same = same_document(t, j, starts)
        self.masks = [
            same & ((t // (2 * h)) == (j // (2 * h))) & ((t & h) != 0) & ((j & h) == 0)
            for h in self.levels
        ]
        tc = lax.broadcasted_iota(jnp.int32, (length, B), 0)
        off = lax.broadcasted_iota(jnp.int32, (length, B), 1)
        jc = (tc - tc % B) + off
        self.mask_c = same_document(tc, jc, starts) & (jc <= tc)

    def by_head(self, parts):
        out = parts[0]
        for i in range(1, len(parts)):
            out = jnp.where(self.lane_head == i, parts[i], out)
        return out

    def only(self, x, i):
        return jnp.where(self.lane_head == i, x, 0.0)

    def decay_from(self, jj):
        return jnp.exp(jnp.minimum(self.c - row_pick(self.c, B, jj), 0.0))

    def om_at(self, jj):
        return row_pick(self.om, B, jj)


def blocks(x):
    return x.reshape(x.shape[0] // B, B, x.shape[1])


def block_nt(a, b):
    r = lax.dot_general(
        blocks(a.astype(bf16)),
        blocks(b.astype(bf16)),
        (((2,), (2,)), ((0,), (0,))),
        preferred_element_type=f32,
    )
    return r.reshape(a.shape[0], B)


def block_nn(a, b):
    r = lax.dot_general(
        blocks(a.astype(bf16)),
        blocks(b.astype(bf16)),
        (((2,), (1,)), ((0,), (0,))),
        preferred_element_type=f32,
    )
    return r.reshape(a.shape[0], b.shape[1])


def block_tn(a, b):
    at = jnp.swapaxes(blocks(a), 1, 2).astype(bf16)
    r = lax.dot_general(
        at, blocks(b.astype(bf16)), (((2,), (1,)), ((0,), (0,))), preferred_element_type=f32
    )
    return r.reshape(a.shape[0], b.shape[1])


def collect(lanes, heads):
    r = lax.broadcasted_iota(jnp.int32, (B * lanes, heads * 128), 0)
    col = lax.broadcasted_iota(jnp.int32, (B * lanes, heads * 128), 1)
    jj, head = r // lanes, (r % lanes) // M
    return jnp.where(col == head * 128 + jj, 1.0, 0.0).astype(bf16)


def wide(x, jj):
    return jnp.broadcast_to(x[:, jj : jj + 1], (x.shape[0], 128))


def forward_math(q, k, v, la, starts):
    heads = q.shape[1] // DK
    scale = 1.0 / math.sqrt(DK)
    cm = Common(la, starts)
    qs = [q[:, i * DK : (i + 1) * DK] for i in range(heads)]
    ks = [k[:, i * DK : (i + 1) * DK] for i in range(heads)]
    vs = [v[:, i * DV : (i + 1) * DV] for i in range(heads)]
    aff = [nt(qs[i], ks[i]) * scale for i in range(heads)]
    affc = [jnp.where(cm.mask_c, block_nt(qs[i], ks[i]) * scale, 0.0) for i in range(heads)]
    s = jnp.zeros_like(la)
    parts = []
    for x, mask in zip(cm.x, cm.masks):
        g = x * cm.om
        part = x * cm.by_head([nn3(jnp.where(mask, aff[i], 0.0), g) for i in range(heads)])
        parts.append(part)
        s = s + part
    for jj in range(B):
        s = s + cm.by_head([wide(affc[i], jj) for i in range(heads)]) * (
            cm.decay_from(jj) * cm.om_at(jj)
        )
    top = cm.by_head(
        [
            jnp.max(jnp.where(cm.lane_head == i, s, -jnp.inf), axis=1, keepdims=True)
            for i in range(heads)
        ]
    )
    e = jnp.exp(s - top)
    total = cm.by_head([jnp.sum(cm.only(e, i), axis=1, keepdims=True) for i in range(heads)])
    p = e / total
    mix = [jnp.zeros((cm.length, cm.length), f32) for _ in range(heads)]
    for x, mask in zip(cm.x, cm.masks):
        g = x * cm.om
        px = p * x
        for i in range(heads):
            mix[i] = mix[i] + jnp.where(mask, nt(cm.only(px, i), g), 0.0)
    mix = [m.astype(bf16) for m in mix]
    pieces = [(p * (cm.decay_from(jj) * cm.om_at(jj))).astype(bf16) for jj in range(B)]
    mixc = nn(jnp.concatenate(pieces, axis=1), collect(cm.lanes, heads))
    mixc = [
        jnp.where(cm.mask_c, mixc[:, i * 128 : i * 128 + B], 0.0) for i in range(heads)
    ]
    outs = [nn(mix[i], vs[i]) + block_nn(mixc[i], vs[i]) for i in range(heads)]
    return outs, p, parts, mix, mixc


def backward_math(q, k, v, la, starts, p, parts, mix, mixc, dout):
    heads = q.shape[1] // DK
    scale = 1.0 / math.sqrt(DK)
    cm = Common(la, starts)
    qs = [q[:, i * DK : (i + 1) * DK] for i in range(heads)]
    ks = [k[:, i * DK : (i + 1) * DK] for i in range(heads)]
    vs = [v[:, i * DV : (i + 1) * DV] for i in range(heads)]
    dos = [dout[:, i * DV : (i + 1) * DV].astype(bf16) for i in range(heads)]
    aff = [nt(qs[i], ks[i]) * scale for i in range(heads)]
    affc = [jnp.where(cm.mask_c, block_nt(qs[i], ks[i]) * scale, 0.0) for i in range(heads)]
    dmix = [nt(dos[i], vs[i]) for i in range(heads)]
    dmixc = [jnp.where(cm.mask_c, block_nt(dos[i], vs[i]), 0.0) for i in range(heads)]
    dp = jnp.zeros_like(la)
    dparts = []
    for x, mask in zip(cm.x, cm.masks):
        g = x * cm.om
        part = x * cm.by_head([nn3(jnp.where(mask, dmix[i], 0.0), g) for i in range(heads)])
        dparts.append(part)
        dp = dp + part
    for jj in range(B):
        dp = dp + cm.by_head([wide(dmixc[i], jj) for i in range(heads)]) * (
            cm.decay_from(jj) * cm.om_at(jj)
        )
    pdp = p * dp
    inner = cm.by_head([jnp.sum(cm.only(pdp, i), axis=1, keepdims=True) for i in range(heads)])
    ds = pdp - p * inner
    daff = [jnp.zeros((cm.length, cm.length), f32) for _ in range(heads)]
    dla = jnp.zeros_like(la)
    reach = jnp.zeros_like(la)
    for n, h in enumerate(cm.levels):
        x, mask = cm.x[n], cm.masks[n]
        g = x * cm.om
        dsx, px = ds * x, p * x
        both = jnp.concatenate([dsx, px], axis=0).astype(bf16)
        cols = []
        for i in range(heads):
            daff[i] = daff[i] + jnp.where(mask, nt(cm.only(dsx, i), g), 0.0)
            left = jnp.concatenate(
                [jnp.where(mask, aff[i], 0.0), jnp.where(mask, dmix[i], 0.0)], axis=0
            )
            cols.append(tn(left, both))
        r = x * cm.by_head(cols)
        reach = reach + r
        right = (cm.rows & h) != 0
        flow = jnp.where(right, ds * parts[n] + p * dparts[n], cm.om * r)
        s = 1
        while s < h:
            flow = flow + jnp.where((cm.rows & (h - 1)) < h - s, shift_up(flow, s), 0.0)
            s *= 2
        dla = dla + jnp.where(right, flow, row_pick(flow, h, 0) - flow)
    flow = jnp.zeros_like(la)
    near = jnp.zeros_like(la)
    pieces = []
    for jj in range(B):
        w = cm.decay_from(jj)
        omj = cm.om_at(jj)
        aj = cm.by_head([wide(affc[i], jj) for i in range(heads)])
        dj = cm.by_head([wide(dmixc[i], jj) for i in range(heads)])
        pieces.append((ds * (w * omj)).astype(bf16))
        z = w * (aj * ds + dj * p)
        flow = flow + omj * z
        z3 = blocks(z)
        tot = jnp.broadcast_to(jnp.sum(z3, axis=1, keepdims=True), z3.shape).reshape(z.shape)
        near = jnp.where((cm.rows & (B - 1)) == jj, tot, near)
    flow = flow - cm.om * near
    s = 1
    while s < B:
        flow = flow + jnp.where((cm.rows & (B - 1)) < B - s, shift_up(flow, s), 0.0)
        s *= 2
    dla = dla + flow - cm.alpha * (reach + near)
    daffc = nn(jnp.concatenate(pieces, axis=1), collect(cm.lanes, heads))
    daffc = [
        jnp.where(cm.mask_c, daffc[:, i * 128 : i * 128 + B], 0.0) for i in range(heads)
    ]
    dq, dk, dv = [], [], []
    for i in range(heads):
        da = daff[i].astype(bf16)
        dq.append((nn(da, ks[i]) + block_nn(daffc[i], ks[i])) * scale)
        dk.append((tn(da, qs[i]) + block_tn(daffc[i], qs[i])) * scale)
        dv.append(tn(mix[i], dos[i]) + block_tn(mixc[i], dos[i]))
    return dq, dk, dv, dla


def head_split(outs, ref, width):
    for i, x in enumerate(outs):
        ref[:, i * width : (i + 1) * width] = x.astype(ref.dtype)


def forward_kernel(starts_ref, q_ref, k_ref, v_ref, la_ref, o_ref, p_ref, parts_ref, mix_ref, mixc_ref):
    starts = [starts_ref[0, n] for n in range(starts_ref.shape[1])]
    outs, p, parts, mix, mixc = forward_math(
        q_ref[...], k_ref[...], v_ref[...], la_ref[...], starts
    )
    head_split(outs, o_ref, DV)
    p_ref[...] = p
    for n, x in enumerate(parts):
        parts_ref[n] = x
    for i in range(len(mix)):
        mix_ref[i] = mix[i]
        mixc_ref[i] = mixc[i].astype(bf16)


tau_inv = 0.125


def silu_slope(values):
    sigmoid_val = jax.nn.sigmoid(values)
    return sigmoid_val * (1.0 + values * (1.0 - sigmoid_val))


def through_silu(grads, z):
    width = grads[0].shape[1]
    return [g * silu_slope(z[:, i * width : (i + 1) * width]) for i, g in enumerate(grads)]


def through_gate(dla, zf):
    return dla * tau_inv * jax.nn.sigmoid(-zf)


INNER = 4


def share_columns(wide_parts, dzf, shares_ref):
    lanes = dzf.shape[1]
    size = lanes // INNER
    lane = lax.broadcasted_iota(jnp.int32, dzf.shape, 1)
    for n in range(INNER):
        at = 0
        for x in wide_parts:
            width = x.shape[1] // INNER
            shares_ref[n, :, at : at + width] = x[:, n * width : (n + 1) * width]
            at += width
        turned = pltpu.roll(dzf, (lanes - n * size) % lanes, 1) if n else dzf
        shares_ref[n, :, at : at + lanes] = jnp.where(lane < size, turned, 0.0).astype(bf16)


def backward_kernel(
    starts_ref, q_ref, k_ref, v_ref, la_ref, p_ref, parts_ref, mix_ref, mixc_ref, do_ref,
    zq_ref, zk_ref, zv_ref, zf_ref, dzq_ref, dzk_ref, dzv_ref, dzf_ref, shares_ref,
):
    starts = [starts_ref[0, n] for n in range(starts_ref.shape[1])]
    heads = mix_ref.shape[0]
    dq, dk, dv, dla = backward_math(
        q_ref[...],
        k_ref[...],
        v_ref[...],
        la_ref[...],
        starts,
        p_ref[...],
        [parts_ref[n] for n in range(parts_ref.shape[0])],
        [mix_ref[i] for i in range(heads)],
        [mixc_ref[i] for i in range(heads)],
        do_ref[...],
    )
    for grads, z_ref, dz_ref in ((dq, zq_ref, dzq_ref), (dk, zk_ref, dzk_ref), (dv, zv_ref, dzv_ref)):
        head_split(through_silu(grads, z_ref[...]), dz_ref, grads[0].shape[1])
    dzf = through_gate(dla, zf_ref[...])
    dzf_ref[...] = dzf.astype(bf16)
    share_columns([dzq_ref[...], dzk_ref[...], dzv_ref[...]], dzf, shares_ref)


SMEM = pl.BlockSpec(memory_space=pltpu.SMEM)
VMEM = pl.BlockSpec(memory_space=pltpu.VMEM)


def attend_forward(q, k, v, la, starts):
    length, lanes = la.shape
    heads = q.shape[1] // DK
    sds = jax.ShapeDtypeStruct
    return pl.pallas_call(
        forward_kernel,
        out_shape=(
            sds((length, heads * DV), bf16),
            sds((length, lanes), f32),
            sds((len(level_sizes(length)), length, lanes), f32),
            sds((heads, length, length), bf16),
            sds((heads, length, B), bf16),
        ),
        in_specs=[SMEM] + [VMEM] * 4,
        out_specs=(VMEM,) * 5,
        cost_estimate=pl.CostEstimate(
            flops=4 * 10**9, transcendentals=10**6, bytes_accessed=4 * 10**6
        ),
        name="slot_forward",
    )(starts, q, k, v, la)


def attend_backward(q, k, v, la, starts, saved, dout, pres):
    sds = jax.ShapeDtypeStruct
    return pl.pallas_call(
        backward_kernel,
        out_shape=(
            sds(q.shape, bf16),
            sds(k.shape, bf16),
            sds(v.shape, bf16),
            sds(la.shape, bf16),
            sds((INNER, q.shape[0], (2 * DK + DV) * (q.shape[1] // DK) // INNER + la.shape[1]), bf16),
        ),
        in_specs=[SMEM] + [VMEM] * 13,
        out_specs=(VMEM,) * 5,
        cost_estimate=pl.CostEstimate(
            flops=12 * 10**9, transcendentals=10**6, bytes_accessed=8 * 10**6
        ),
        name="slot_backward",
    )(starts, q, k, v, la, *saved, dout, *pres)


eps = 1e-06
LAP = (0, 1, 3, 2)


def rms_scale(values):
    return lax.rsqrt(jnp.mean(values * values, axis=-1, keepdims=True) + eps)


def norm_back(values, scale, gain, upstream):
    gain_grad = jnp.sum(upstream * values * scale, axis=0, keepdims=True)
    weighted = upstream * gain
    input_grad = scale * weighted - values * (scale * scale * scale) * jnp.mean(
        weighted * values, axis=-1, keepdims=True
    )
    return (gain_grad, input_grad)


class Grid:
    def __init__(self, dp):
        self.dp = dp
        self.outer = dp // INNER
        self.laps = [[o * INNER + i for i in LAP] for o in range(self.outer)]
        self.rows = [[o * INNER + i for i in range(INNER)] for o in range(self.outer)]
        self.cols = [[o * INNER + i for o in range(self.outer)] for i in range(INNER)]
        self.gathered = [o * INNER + i for i in LAP for o in range(self.outer)]
        self.natural = inverse(self.gathered)
        self.up = [(d, d + INNER) for d in range(dp - INNER)]
        self.down = [(d + INNER, d) for d in range(dp - INNER)]


def reorder(x, order):
    size = x.shape[-1] // len(order)
    return jnp.concatenate([x[..., b * size : (b + 1) * size] for b in order], axis=-1)


def inverse(order):
    back = [0] * len(order)
    for n, b in enumerate(order):
        back[b] = n
    return back


def swap(x):
    return lax.ppermute(x, "head", [(0, 1), (1, 0)])


def half_of(x, which):
    size = x.shape[0] // 2
    return lax.dynamic_slice_in_dim(x, which * size, size, 0)


def join(mine, other, core):
    size = mine.shape[0]
    out = jnp.zeros((2 * size,) + mine.shape[1:], mine.dtype)
    out = lax.dynamic_update_slice_in_dim(out, mine, core * size, 0)
    return lax.dynamic_update_slice_in_dim(out, other, (1 - core) * size, 0)


def on_rows(kernel, name, core, halves, wholes, outs):
    rows = halves[0].shape[0] // 2
    specs = [pl.BlockSpec((rows, x.shape[1]), lambda i, c: (c[0], 0)) for x in halves]
    specs += [pl.BlockSpec(x.shape, lambda i, c: (0, 0)) for x in wholes]
    return pl.pallas_call(
        kernel,
        out_shape=outs,
        grid_spec=pltpu.PrefetchScalarGridSpec(
            num_scalar_prefetch=1,
            grid=(1,),
            in_specs=specs,
            out_specs=[pl.BlockSpec(x.shape, lambda i, c: (0, 0)) for x in outs],
        ),
        name=name,
    )(core.reshape(1), *halves, *wholes)


def aligned(grid, width):
    return (width // grid.dp) % 128 == 0


def put_in_order(x, order, grid, inside):
    return reorder(x, order) if aligned(grid, x.shape[1]) == inside else x


def cotangent_rows(out_grad, core, grid):
    rows, width = out_grad.shape

    def kernel(core_ref, cot_ref, out_ref):
        out_ref[...] = put_in_order(cot_ref[...], grid.gathered, grid, True)

    outs = [jax.ShapeDtypeStruct((rows // 2, width), bf16)]
    (x,) = on_rows(kernel, "cotangent_rows", core, [out_grad], [], outs)
    return put_in_order(x, grid.gathered, grid, False)


def second_norm(block_in, mine, other, gain, core, grid):
    rows, width = mine.shape

    def kernel(core_ref, in_ref, mine_ref, other_ref, gain_ref, hidden_ref, normed_ref):
        hidden = in_ref[...].astype(f32) + (mine_ref[...] + other_ref[...])
        hidden_ref[...] = hidden
        normed = (hidden * rms_scale(hidden) * gain_ref[...]).astype(bf16)
        normed_ref[...] = put_in_order(normed, grid.gathered, grid, True)

    outs = [jax.ShapeDtypeStruct((rows, width), f32), jax.ShapeDtypeStruct((rows, width), bf16)]
    hidden, normed = on_rows(
        kernel, "second_norm", core, [block_in], [mine, other, gain[None]], outs
    )
    return hidden, put_in_order(normed, grid.gathered, grid, False)


def second_norm_back(out_grad, hidden, gain, parts, core, grid):
    rows, width = hidden.shape
    parts = [put_in_order(x, grid.natural, grid, False) for x in parts]

    def kernel(core_ref, cot_ref, hidden_ref, gain_ref, *refs):
        upstream = sum(x[...].astype(f32) for x in refs[: len(parts)])
        upstream = put_in_order(upstream, grid.natural, grid, True)
        grad_ref, low_ref, gain_grad_ref = refs[len(parts) :]
        hidden = hidden_ref[...]
        gain_grad, grad = norm_back(hidden, rms_scale(hidden), gain_ref[...], upstream)
        grad = grad + cot_ref[...].astype(f32)
        grad_ref[...] = grad
        low_ref[...] = grad.astype(bf16)
        gain_grad_ref[...] = gain_grad

    sds = jax.ShapeDtypeStruct
    outs = [sds((rows, width), f32), sds((rows, width), bf16), sds((1, width), f32)]
    return on_rows(
        kernel, "second_norm_back", core, [out_grad], [hidden, gain[None], *parts], outs
    )


def first_norm_back(block_in, grad, gain, mine, other, core):
    rows, width = grad.shape

    def kernel(core_ref, in_ref, grad_ref, gain_ref, mine_ref, other_ref, out_ref, gain_grad_ref):
        inputs = in_ref[...].astype(f32)
        upstream = mine_ref[...] + other_ref[...]
        gain_grad, out = norm_back(inputs, rms_scale(inputs), gain_ref[...], upstream)
        out_ref[...] = out + grad_ref[...]
        gain_grad_ref[...] = gain_grad

    sds = jax.ShapeDtypeStruct
    outs = [sds((rows, width), f32), sds((1, width), f32)]
    return on_rows(
        kernel, "first_norm_back", core, [block_in], [grad, gain[None], mine, other], outs
    )


def block_result(block_in, hidden, parts, core, grid):
    rows, width = hidden.shape
    parts = [put_in_order(x, grid.natural, grid, False) for x in parts]

    def kernel(core_ref, in_ref, hidden_ref, *refs):
        out = sum(x[...].astype(f32) for x in refs[: len(parts)])
        out = put_in_order(out, grid.natural, grid, True)
        refs[-1][...] = (hidden_ref[...] + out).astype(bf16)

    outs = [jax.ShapeDtypeStruct((rows, width), bf16)]
    (x,) = on_rows(kernel, "block_result", core, [block_in], [hidden, *parts], outs)
    return x


def exchange(x, split, concat, groups):
    return lax.all_to_all(x, "dp", split, concat, tiled=True, axis_index_groups=groups)


def tie(*values):
    return lax.optimization_barrier(values)


def gather_along(x, grid, place, beside=()):
    n = grid.outer
    above = below = x
    from_below, from_above, done = [], [], []
    other = swap(x)
    for k in range(n - 1):
        below = lax.ppermute(below, "dp", grid.up)
        above = lax.ppermute(above, "dp", grid.down)
        extra = beside[k] if k < len(beside) else ()
        extra = extra(*done) if callable(extra) else extra
        below, above, *extra = tie(below, above, *extra)
        from_below.append((below, swap(below)))
        from_above.append((above, swap(above)))
        done += extra
    blocks = [x]
    for c in range(2):
        blocks += [other] if c else []
        for k in range(1, n):
            blocks.append(
                jnp.where(place + k < n, from_above[k - 1][c], from_below[n - 1 - k][c])
            )
    return jnp.concatenate(blocks, axis=0), done


def by_core(x):
    size = x.shape[0] // 2
    return x[:size], x[size:].astype(bf16)


def add_other_core(mine, other, grid):
    n = grid.outer
    other = tie(*[swap(y) for y in jnp.split(other, n)])
    return [x + y.astype(f32) for x, y in zip(jnp.split(mine, n), other)]


def scatter_along(own, grid, beside=()):
    n = grid.outer
    up = down = None
    done = []
    for k in range(n - 1):
        up = own[n - 1 - k] if up is None else own[n - 1 - k] + up.astype(f32)
        down = own[1 + k] if down is None else own[1 + k] + down.astype(f32)
        up = lax.ppermute(up.astype(bf16), "dp", grid.up)
        down = lax.ppermute(down.astype(bf16), "dp", grid.down)
        extra = beside[k] if k < len(beside) else ()
        extra = extra(*done) if callable(extra) else extra
        up, down, *extra = tie(up, down, *extra)
        done += extra
    return (own[0], up, down), done


def plane_gather(x, grid, inner):
    out = jnp.zeros((INNER,) + x.shape, x.dtype)
    for k in range(INNER):
        y = x
        if k:
            y = lax.ppermute(x, "dp", [(d, d ^ k) for d in range(grid.dp)])
        out = lax.dynamic_update_slice_in_dim(out, y[None], inner ^ k, 0)
    return out


def on_device(
    block_in,
    out_grad,
    attn_gain,
    mlp_gain,
    w_query,
    w_key,
    w_value,
    w_forget,
    w_output,
    w_gate,
    w_up,
    w_down,
    doc_starts,
    grid,
):
    core = lax.axis_index("head")
    place = lax.axis_index("dp") // INNER
    inner = lax.axis_index("dp") % INNER

    def columns(w):
        return exchange(w, 1, 0, grid.cols)

    def gather_rows(w):
        return lax.all_gather(w, "dp", axis=0, tiled=True, axis_index_groups=grid.laps)

    def column_pairs(a, b):
        rows = a.shape[0]
        both = [w.reshape(rows, grid.outer, -1) for w in (a, b)]
        both = columns(jnp.concatenate(both, axis=2).reshape(rows, -1))
        return jnp.split(both, 2, axis=1)

    gate_piece, up_piece = column_pairs(w_gate, w_up)
    inputs_f = block_in.astype(f32)
    normed = (inputs_f * rms_scale(inputs_f) * attn_gain).astype(bf16)
    query_pre = nn(normed, w_query)
    key_pre = nn(normed, w_key)
    value_pre = nn(normed, w_value)
    forget_pre = nn(normed, w_forget)
    query = jax.nn.silu(query_pre).astype(bf16)
    key = jax.nn.silu(key_pre).astype(bf16)
    value = jax.nn.silu(value_pre).astype(bf16)
    log_keep = jax.nn.log_sigmoid(forget_pre) * tau_inv
    mixed, *saved = attend_forward(query, key, value, log_keep, doc_starts)
    normed_own = lax.all_gather(
        half_of(normed, core), "dp", axis=0, tiled=True, axis_index_groups=grid.rows
    )
    branch_other = swap(nt(half_of(mixed, 1 - core), w_output))
    branch_mine = nt(half_of(mixed, core), w_output)
    branch_mine, gate_piece, up_piece, down_later, normed_own = tie(
        branch_mine, gate_piece, up_piece, w_down, normed_own
    )
    full_gate, full_up = gather_rows(gate_piece), gather_rows(up_piece)
    down_piece = columns(down_later)

    hidden, normed_two = second_norm(block_in, branch_mine, branch_other, mlp_gain, core, grid)
    def plane_tokens(own):
        own = own.reshape(INNER, 1, -1, own.shape[-1])
        out = jnp.zeros((INNER, 2) + own.shape[2:], own.dtype)
        out = lax.dynamic_update_slice_in_dim(out, own, core, 1)
        out = lax.dynamic_update_slice_in_dim(out, swap(own), 1 - core, 1)
        return out.reshape(-1, own.shape[-1])

    def plane_columns(shares):
        return exchange(shares.reshape(-1, shares.shape[2]), 0, 0, grid.rows)

    def plane_product(left, right):
        return tn(left, right).astype(bf16)

    def plane_sum(g):
        return lax.psum_scatter(
            g, "dp", scatter_dimension=0, tiled=True, axis_index_groups=grid.cols
        )

    def from_plane(g):
        size = g.shape[1]
        return exchange(g, 0, 1, grid.rows).reshape(-1, INNER, size).astype(f32)

    cot_rows = cotangent_rows(out_grad, core, grid)
    tokens, (cot_rows, down_piece, normed_plane, full_gate) = gather_along(
        normed_two,
        grid,
        place,
        ((cot_rows, down_piece), (plane_tokens(normed_own),), (full_gate,)),
    )
    full_down = gather_rows(down_piece)
    def gated(gate, up):
        return (jax.nn.silu(gate) * up).astype(bf16)

    cot_all, (gate_act, full_up, up_act, full_down, out_mine, out_other) = gather_along(
        cot_rows,
        grid,
        place,
        (
            (nn(tokens, full_gate), full_up),
            lambda gate, w_up_all: (nn(tokens, w_up_all), full_down),
            lambda gate, _, up, w_down_all: by_core(nt(gated(gate, up), w_down_all)),
        ),
    )
    out_own = add_other_core(out_mine, out_other, grid)
    out_blocks = jnp.zeros((grid.outer,) + out_own[0].shape, bf16)
    for k, x in enumerate(out_own):
        at = (place + k) % grid.outer
        out_blocks = lax.dynamic_update_slice_in_dim(out_blocks, x.astype(bf16)[None], at, 0)
    out_blocks, cot_all = tie(out_blocks.reshape(-1, out_blocks.shape[2]), cot_all)


    def scatter_rows(g):
        return lax.psum_scatter(
            g, "dp", scatter_dimension=0, tiled=True, axis_index_groups=grid.laps
        )

    def to_columns(g):
        return exchange(g, 0, 1, grid.cols).astype(f32)

    inner_grad = nn(cot_all, full_down)
    gate_grad = (inner_grad * up_act * silu_slope(gate_act)).astype(bf16)
    up_grad = (inner_grad * jax.nn.silu(gate_act)).astype(bf16)
    inner_act = gated(gate_act, up_act)
    back_parts, (down_rows, gate_rows, up_rows) = scatter_along(
        add_other_core(*by_core(nt(gate_grad, full_gate) + nt(up_grad, full_up)), grid),
        grid,
        (
            (tn(cot_all, inner_act).astype(bf16),),
            (tn(tokens, gate_grad).astype(bf16),),
            (tn(tokens, up_grad).astype(bf16),),
        ),
    )
    down_rows, gate_rows, up_rows = (scatter_rows(g) for g in (down_rows, gate_rows, up_rows))
    hidden_grad, low_half, mlp_gain_part = second_norm_back(
        out_grad, hidden, mlp_gain, back_parts, core, grid
    )
    branch_grad = join(low_half, swap(low_half), core)
    mixed_grad = nn(branch_grad, w_output).astype(bf16)
    mixed_grad, down_rows = tie(mixed_grad, down_rows)
    *pre_grads, shares = attend_backward(
        query, key, value, log_keep, doc_starts, saved, mixed_grad,
        (query_pre, key_pre, value_pre, forget_pre),
    )
    down_sum = to_columns(down_rows)
    down_sum, shares, *pre_grads = tie(down_sum, shares, *pre_grads)

    def normed_part(which):
        q, k, v, f = (half_of(g, which) for g in pre_grads)
        return nt(q, w_query) + nt(k, w_key) + nt(v, w_value) + nt(f, w_forget)

    columns_here, part_other, part_mine, out_blocks, gate_rows, up_rows = tie(
        plane_columns(shares),
        normed_part(1 - core),
        normed_part(core),
        out_blocks,
        gate_rows,
        up_rows,
    )
    out_sum = lax.psum_scatter(
        out_blocks, "dp", scatter_dimension=0, tiled=True, axis_index_groups=grid.cols
    )
    pre_grad = plane_product(normed_plane, columns_here)
    _, low_half, mixed, out_sum = tie(pre_grad, low_half, mixed, out_sum)
    mixed_plane = plane_columns(jnp.stack(jnp.split(mixed, INNER, axis=1)))
    low_plane = plane_tokens(plane_gather(low_half, grid, inner))
    sums, output_grad = tie(plane_sum(pre_grad), plane_product(low_plane, mixed_plane))
    output_sum = plane_sum(output_grad)
    result = block_result(block_in, hidden, [out_sum], core, grid)
    result = join(result, swap(result), core)

    sums = from_plane(sums)
    output_sum = from_plane(output_sum).reshape(sums.shape[0], -1)
    ends = [0]
    for g in pre_grads:
        ends.append(ends[-1] + g.shape[1] // INNER)
    query_sum, key_sum, value_sum, forget_sum = (
        sums[:, :, a:b].reshape(sums.shape[0], -1) for a, b in zip(ends, ends[1:])
    )

    input_grad, attn_gain_part = first_norm_back(
        block_in, hidden_grad, attn_gain, part_mine, swap(part_other), core
    )
    input_grad = join(input_grad, swap(input_grad), core)

    gains = jnp.concatenate([attn_gain_part, mlp_gain_part], axis=0)
    gains = gains + swap(gains)
    gains = jnp.swapaxes(gains.reshape(2, grid.dp, -1), 0, 1)
    gains = jnp.sum(lax.all_to_all(gains, "dp", 0, 0, tiled=True), axis=0)

    return (
        result,
        input_grad,
        gains[0],
        gains[1],
        query_sum,
        key_sum,
        value_sum,
        forget_sum,
        output_sum,
        to_columns(gate_rows),
        to_columns(up_rows),
        down_sum,
    )


def solution(mesh):
    placed = (
        P("dp", None),
        P("dp", None),
        P(),
        P(),
        P(None, "head"),
        P(None, "head"),
        P(None, "head"),
        P(None, "head"),
        P(None, "head"),
        P("dp", "head"),
        P("dp", "head"),
        P("dp", "head"),
        P("dp", None),
    )
    return jax.shard_map(
        partial(on_device, grid=Grid(mesh.shape["dp"])),
        mesh=mesh,
        in_specs=placed,
        out_specs=(P("dp", None), P("dp", None), P("dp"), P("dp")) + (P("dp", "head"),) * 8,
        check_vma=False,
    )
```

```python
import math
from functools import partial
import jax
import jax.numpy as jnp
from jax import lax
from jax.experimental import pallas as pl
from jax.experimental.pallas import tpu as pltpu
from jax.sharding import PartitionSpec as P

DK = 512
DV = 512
M = 64
B = 16
f32 = jnp.float32
bf16 = jnp.bfloat16


def nn(a, b):
    return jnp.dot(a.astype(bf16), b.astype(bf16), preferred_element_type=f32)


def nt(a, b):
    return lax.dot_general(
        a.astype(bf16), b.astype(bf16), (((1,), (1,)), ((), ())), preferred_element_type=f32
    )


def tn(a, b):
    return lax.dot_general(
        a.astype(bf16), b.astype(bf16), (((0,), (0,)), ((), ())), preferred_element_type=f32
    )


def nn3(a, b):
    ah, bh = a.astype(bf16), b.astype(bf16)
    al, bl = (a - ah.astype(f32)).astype(bf16), (b - bh.astype(f32)).astype(bf16)
    return nn(ah, bh) + (nn(al, bh) + nn(ah, bl))


def shift_up(x, s):
    return pltpu.roll(x, x.shape[0] - s, 0)


def shift_down(x, s):
    return pltpu.roll(x, s, 0)


def segment_at(pos, starts):
    seg = jnp.zeros(pos.shape, jnp.int32)
    for s in starts:
        seg = seg + (pos >= s).astype(jnp.int32)
    return seg


def same_document(t, j, starts):
    ok = None
    for s in starts:
        same = (t >= s) == (j >= s)
        ok = same if ok is None else ok & same
    return ok


def level_sizes(length):
    sizes = []
    h = length // 2
    while h >= B:
        sizes.append(h)
        h //= 2
    return sizes


def row_pick(x, size, row):
    n, lanes = x.shape
    x3 = x.reshape(n // size, size, lanes)
    return jnp.broadcast_to(x3[:, row : row + 1, :], x3.shape).reshape(n, lanes)


class Common:
    def __init__(self, la, starts):
        length, lanes = la.shape
        self.length, self.lanes = length, lanes
        rows = lax.broadcasted_iota(jnp.int32, (length, lanes), 0)
        self.rows = rows
        self.lane_head = lax.broadcasted_iota(jnp.int32, (length, lanes), 1) // M
        c = la
        s = 1
        while s < length:
            c = c + jnp.where(rows >= s, shift_down(c, s), 0.0)
            s *= 2
        self.c = c
        self.alpha = jnp.exp(la)
        self.om = 1.0 - self.alpha
        self.levels = level_sizes(length)
        self.x = []
        for h in self.levels:
            mid = row_pick(c, 2 * h, h - 1)
            self.x.append(jnp.exp(-jnp.abs(c - mid)))
        t = lax.broadcasted_iota(jnp.int32, (length, length), 0)
        j = lax.broadcasted_iota(jnp.int32, (length, length), 1)
        same = same_document(t, j, starts)
        self.masks = [
            same & ((t // (2 * h)) == (j // (2 * h))) & ((t & h) != 0) & ((j & h) == 0)
            for h in self.levels
        ]
        tc = lax.broadcasted_iota(jnp.int32, (length, B), 0)
        off = lax.broadcasted_iota(jnp.int32, (length, B), 1)
        jc = (tc - tc % B) + off
        self.mask_c = same_document(tc, jc, starts) & (jc <= tc)

    def by_head(self, parts):
        out = parts[0]
        for i in range(1, len(parts)):
            out = jnp.where(self.lane_head == i, parts[i], out)
        return out

    def only(self, x, i):
        return jnp.where(self.lane_head == i, x, 0.0)

    def decay_from(self, jj):
        return jnp.exp(jnp.minimum(self.c - row_pick(self.c, B, jj), 0.0))

    def om_at(self, jj):
        return row_pick(self.om, B, jj)


def blocks(x):
    return x.reshape(x.shape[0] // B, B, x.shape[1])


def block_nt(a, b):
    r = lax.dot_general(
        blocks(a.astype(bf16)),
        blocks(b.astype(bf16)),
        (((2,), (2,)), ((0,), (0,))),
        preferred_element_type=f32,
    )
    return r.reshape(a.shape[0], B)


def block_nn(a, b):
    r = lax.dot_general(
        blocks(a.astype(bf16)),
        blocks(b.astype(bf16)),
        (((2,), (1,)), ((0,), (0,))),
        preferred_element_type=f32,
    )
    return r.reshape(a.shape[0], b.shape[1])


def block_tn(a, b):
    at = jnp.swapaxes(blocks(a), 1, 2).astype(bf16)
    r = lax.dot_general(
        at, blocks(b.astype(bf16)), (((2,), (1,)), ((0,), (0,))), preferred_element_type=f32
    )
    return r.reshape(a.shape[0], b.shape[1])


def collect(lanes, heads):
    r = lax.broadcasted_iota(jnp.int32, (B * lanes, heads * 128), 0)
    col = lax.broadcasted_iota(jnp.int32, (B * lanes, heads * 128), 1)
    jj, head = r // lanes, (r % lanes) // M
    return jnp.where(col == head * 128 + jj, 1.0, 0.0).astype(bf16)


def wide(x, jj):
    return jnp.broadcast_to(x[:, jj : jj + 1], (x.shape[0], 128))


def forward_math(q, k, v, la, starts):
    heads = q.shape[1] // DK
    scale = 1.0 / math.sqrt(DK)
    cm = Common(la, starts)
    qs = [q[:, i * DK : (i + 1) * DK] for i in range(heads)]
    ks = [k[:, i * DK : (i + 1) * DK] for i in range(heads)]
    vs = [v[:, i * DV : (i + 1) * DV] for i in range(heads)]
    aff = [nt(qs[i], ks[i]) * scale for i in range(heads)]
    affc = [jnp.where(cm.mask_c, block_nt(qs[i], ks[i]) * scale, 0.0) for i in range(heads)]
    s = jnp.zeros_like(la)
    parts = []
    for x, mask in zip(cm.x, cm.masks):
        g = x * cm.om
        part = x * cm.by_head([nn3(jnp.where(mask, aff[i], 0.0), g) for i in range(heads)])
        parts.append(part)
        s = s + part
    for jj in range(B):
        s = s + cm.by_head([wide(affc[i], jj) for i in range(heads)]) * (
            cm.decay_from(jj) * cm.om_at(jj)
        )
    top = cm.by_head(
        [
            jnp.max(jnp.where(cm.lane_head == i, s, -jnp.inf), axis=1, keepdims=True)
            for i in range(heads)
        ]
    )
    e = jnp.exp(s - top)
    total = cm.by_head([jnp.sum(cm.only(e, i), axis=1, keepdims=True) for i in range(heads)])
    p = e / total
    mix = [jnp.zeros((cm.length, cm.length), f32) for _ in range(heads)]
    for x, mask in zip(cm.x, cm.masks):
        g = x * cm.om
        px = p * x
        for i in range(heads):
            mix[i] = mix[i] + jnp.where(mask, nt(cm.only(px, i), g), 0.0)
    mix = [m.astype(bf16) for m in mix]
    pieces = [(p * (cm.decay_from(jj) * cm.om_at(jj))).astype(bf16) for jj in range(B)]
    mixc = nn(jnp.concatenate(pieces, axis=1), collect(cm.lanes, heads))
    mixc = [
        jnp.where(cm.mask_c, mixc[:, i * 128 : i * 128 + B], 0.0) for i in range(heads)
    ]
    outs = [nn(mix[i], vs[i]) + block_nn(mixc[i], vs[i]) for i in range(heads)]
    return outs, p, parts, mix, mixc


def backward_math(q, k, v, la, starts, p, parts, mix, mixc, dout):
    heads = q.shape[1] // DK
    scale = 1.0 / math.sqrt(DK)
    cm = Common(la, starts)
    qs = [q[:, i * DK : (i + 1) * DK] for i in range(heads)]
    ks = [k[:, i * DK : (i + 1) * DK] for i in range(heads)]
    vs = [v[:, i * DV : (i + 1) * DV] for i in range(heads)]
    dos = [dout[:, i * DV : (i + 1) * DV].astype(bf16) for i in range(heads)]
    aff = [nt(qs[i], ks[i]) * scale for i in range(heads)]
    affc = [jnp.where(cm.mask_c, block_nt(qs[i], ks[i]) * scale, 0.0) for i in range(heads)]
    dmix = [nt(dos[i], vs[i]) for i in range(heads)]
    dmixc = [jnp.where(cm.mask_c, block_nt(dos[i], vs[i]), 0.0) for i in range(heads)]
    dp = jnp.zeros_like(la)
    dparts = []
    for x, mask in zip(cm.x, cm.masks):
        g = x * cm.om
        part = x * cm.by_head([nn3(jnp.where(mask, dmix[i], 0.0), g) for i in range(heads)])
        dparts.append(part)
        dp = dp + part
    for jj in range(B):
        dp = dp + cm.by_head([wide(dmixc[i], jj) for i in range(heads)]) * (
            cm.decay_from(jj) * cm.om_at(jj)
        )
    pdp = p * dp
    inner = cm.by_head([jnp.sum(cm.only(pdp, i), axis=1, keepdims=True) for i in range(heads)])
    ds = pdp - p * inner
    daff = [jnp.zeros((cm.length, cm.length), f32) for _ in range(heads)]
    dla = jnp.zeros_like(la)
    reach = jnp.zeros_like(la)
    for n, h in enumerate(cm.levels):
        x, mask = cm.x[n], cm.masks[n]
        g = x * cm.om
        dsx, px = ds * x, p * x
        both = jnp.concatenate([dsx, px], axis=0).astype(bf16)
        cols = []
        for i in range(heads):
            daff[i] = daff[i] + jnp.where(mask, nt(cm.only(dsx, i), g), 0.0)
            left = jnp.concatenate(
                [jnp.where(mask, aff[i], 0.0), jnp.where(mask, dmix[i], 0.0)], axis=0
            )
            cols.append(tn(left, both))
        r = x * cm.by_head(cols)
        reach = reach + r
        right = (cm.rows & h) != 0
        flow = jnp.where(right, ds * parts[n] + p * dparts[n], cm.om * r)
        s = 1
        while s < h:
            flow = flow + jnp.where((cm.rows & (h - 1)) < h - s, shift_up(flow, s), 0.0)
            s *= 2
        dla = dla + jnp.where(right, flow, row_pick(flow, h, 0) - flow)
    flow = jnp.zeros_like(la)
    near = jnp.zeros_like(la)
    pieces = []
    for jj in range(B):
        w = cm.decay_from(jj)
        omj = cm.om_at(jj)
        aj = cm.by_head([wide(affc[i], jj) for i in range(heads)])
        dj = cm.by_head([wide(dmixc[i], jj) for i in range(heads)])
        pieces.append((ds * (w * omj)).astype(bf16))
        z = w * (aj * ds + dj * p)
        flow = flow + omj * z
        z3 = blocks(z)
        tot = jnp.broadcast_to(jnp.sum(z3, axis=1, keepdims=True), z3.shape).reshape(z.shape)
        near = jnp.where((cm.rows & (B - 1)) == jj, tot, near)
    flow = flow - cm.om * near
    s = 1
    while s < B:
        flow = flow + jnp.where((cm.rows & (B - 1)) < B - s, shift_up(flow, s), 0.0)
        s *= 2
    dla = dla + flow - cm.alpha * (reach + near)
    daffc = nn(jnp.concatenate(pieces, axis=1), collect(cm.lanes, heads))
    daffc = [
        jnp.where(cm.mask_c, daffc[:, i * 128 : i * 128 + B], 0.0) for i in range(heads)
    ]
    dq, dk, dv = [], [], []
    for i in range(heads):
        da = daff[i].astype(bf16)
        dq.append((nn(da, ks[i]) + block_nn(daffc[i], ks[i])) * scale)
        dk.append((tn(da, qs[i]) + block_tn(daffc[i], qs[i])) * scale)
        dv.append(tn(mix[i], dos[i]) + block_tn(mixc[i], dos[i]))
    return dq, dk, dv, dla


def head_split(outs, ref, width):
    for i, x in enumerate(outs):
        ref[:, i * width : (i + 1) * width] = x.astype(ref.dtype)


def forward_kernel(starts_ref, q_ref, k_ref, v_ref, la_ref, o_ref, p_ref, parts_ref, mix_ref, mixc_ref):
    starts = [starts_ref[0, n] for n in range(starts_ref.shape[1])]
    outs, p, parts, mix, mixc = forward_math(
        q_ref[...], k_ref[...], v_ref[...], la_ref[...], starts
    )
    head_split(outs, o_ref, DV)
    p_ref[...] = p
    for n, x in enumerate(parts):
        parts_ref[n] = x
    for i in range(len(mix)):
        mix_ref[i] = mix[i]
        mixc_ref[i] = mixc[i].astype(bf16)


tau_inv = 0.125


def silu_slope(values):
    sigmoid_val = jax.nn.sigmoid(values)
    return sigmoid_val * (1.0 + values * (1.0 - sigmoid_val))


def through_silu(grads, z):
    width = grads[0].shape[1]
    return [g * silu_slope(z[:, i * width : (i + 1) * width]) for i, g in enumerate(grads)]


def through_gate(dla, zf):
    return dla * tau_inv * jax.nn.sigmoid(-zf)


INNER = 4


def share_columns(wide_parts, dzf, shares_ref):
    lanes = dzf.shape[1]
    size = lanes // INNER
    lane = lax.broadcasted_iota(jnp.int32, dzf.shape, 1)
    for n in range(INNER):
        at = 0
        for x in wide_parts:
            width = x.shape[1] // INNER
            shares_ref[n, :, at : at + width] = x[:, n * width : (n + 1) * width]
            at += width
        turned = pltpu.roll(dzf, (lanes - n * size) % lanes, 1) if n else dzf
        shares_ref[n, :, at : at + lanes] = jnp.where(lane < size, turned, 0.0).astype(bf16)


def backward_kernel(
    starts_ref, q_ref, k_ref, v_ref, la_ref, p_ref, parts_ref, mix_ref, mixc_ref, do_ref,
    zq_ref, zk_ref, zv_ref, zf_ref, dzq_ref, dzk_ref, dzv_ref, dzf_ref, shares_ref,
):
    starts = [starts_ref[0, n] for n in range(starts_ref.shape[1])]
    heads = mix_ref.shape[0]
    dq, dk, dv, dla = backward_math(
        q_ref[...],
        k_ref[...],
        v_ref[...],
        la_ref[...],
        starts,
        p_ref[...],
        [parts_ref[n] for n in range(parts_ref.shape[0])],
        [mix_ref[i] for i in range(heads)],
        [mixc_ref[i] for i in range(heads)],
        do_ref[...],
    )
    for grads, z_ref, dz_ref in ((dq, zq_ref, dzq_ref), (dk, zk_ref, dzk_ref), (dv, zv_ref, dzv_ref)):
        head_split(through_silu(grads, z_ref[...]), dz_ref, grads[0].shape[1])
    dzf = through_gate(dla, zf_ref[...])
    dzf_ref[...] = dzf.astype(bf16)
    share_columns([dzq_ref[...], dzk_ref[...], dzv_ref[...]], dzf, shares_ref)


SMEM = pl.BlockSpec(memory_space=pltpu.SMEM)
VMEM = pl.BlockSpec(memory_space=pltpu.VMEM)


def attend_forward(q, k, v, la, starts):
    length, lanes = la.shape
    heads = q.shape[1] // DK
    sds = jax.ShapeDtypeStruct
    return pl.pallas_call(
        forward_kernel,
        out_shape=(
            sds((length, heads * DV), bf16),
            sds((length, lanes), f32),
            sds((len(level_sizes(length)), length, lanes), f32),
            sds((heads, length, length), bf16),
            sds((heads, length, B), bf16),
        ),
        in_specs=[SMEM] + [VMEM] * 4,
        out_specs=(VMEM,) * 5,
        cost_estimate=pl.CostEstimate(
            flops=4 * 10**9, transcendentals=10**6, bytes_accessed=4 * 10**6
        ),
        name="slot_forward",
    )(starts, q, k, v, la)


def attend_backward(q, k, v, la, starts, saved, dout, pres):
    sds = jax.ShapeDtypeStruct
    return pl.pallas_call(
        backward_kernel,
        out_shape=(
            sds(q.shape, bf16),
            sds(k.shape, bf16),
            sds(v.shape, bf16),
            sds(la.shape, bf16),
            sds((INNER, q.shape[0], (2 * DK + DV) * (q.shape[1] // DK) // INNER + la.shape[1]), bf16),
        ),
        in_specs=[SMEM] + [VMEM] * 13,
        out_specs=(VMEM,) * 5,
        cost_estimate=pl.CostEstimate(
            flops=12 * 10**9, transcendentals=10**6, bytes_accessed=8 * 10**6
        ),
        name="slot_backward",
    )(starts, q, k, v, la, *saved, dout, *pres)


eps = 1e-06
LAP = (0, 1, 3, 2)


def rms_scale(values):
    return lax.rsqrt(jnp.mean(values * values, axis=-1, keepdims=True) + eps)


def norm_back(values, scale, gain, upstream):
    gain_grad = jnp.sum(upstream * values * scale, axis=0, keepdims=True)
    weighted = upstream * gain
    input_grad = scale * weighted - values * (scale * scale * scale) * jnp.mean(
        weighted * values, axis=-1, keepdims=True
    )
    return (gain_grad, input_grad)


class Grid:
    def __init__(self, dp):
        self.dp = dp
        self.outer = dp // INNER
        self.laps = [[o * INNER + i for i in LAP] for o in range(self.outer)]
        self.rows = [[o * INNER + i for i in range(INNER)] for o in range(self.outer)]
        self.cols = [[o * INNER + i for o in range(self.outer)] for i in range(INNER)]
        self.gathered = [o * INNER + i for i in LAP for o in range(self.outer)]
        self.natural = inverse(self.gathered)
        self.up = [(d, d + INNER) for d in range(dp - INNER)]
        self.down = [(d + INNER, d) for d in range(dp - INNER)]


def reorder(x, order):
    size = x.shape[-1] // len(order)
    return jnp.concatenate([x[..., b * size : (b + 1) * size] for b in order], axis=-1)


def inverse(order):
    back = [0] * len(order)
    for n, b in enumerate(order):
        back[b] = n
    return back


def swap(x):
    return lax.ppermute(x, "head", [(0, 1), (1, 0)])


def half_of(x, which):
    size = x.shape[0] // 2
    return lax.dynamic_slice_in_dim(x, which * size, size, 0)


def join(mine, other, core):
    size = mine.shape[0]
    out = jnp.zeros((2 * size,) + mine.shape[1:], mine.dtype)
    out = lax.dynamic_update_slice_in_dim(out, mine, core * size, 0)
    return lax.dynamic_update_slice_in_dim(out, other, (1 - core) * size, 0)


def on_rows(kernel, name, core, halves, wholes, outs):
    rows = halves[0].shape[0] // 2
    specs = [pl.BlockSpec((rows, x.shape[1]), lambda i, c: (c[0], 0)) for x in halves]
    specs += [pl.BlockSpec(x.shape, lambda i, c: (0, 0)) for x in wholes]
    return pl.pallas_call(
        kernel,
        out_shape=outs,
        grid_spec=pltpu.PrefetchScalarGridSpec(
            num_scalar_prefetch=1,
            grid=(1,),
            in_specs=specs,
            out_specs=[pl.BlockSpec(x.shape, lambda i, c: (0, 0)) for x in outs],
        ),
        name=name,
    )(core.reshape(1), *halves, *wholes)


def aligned(grid, width):
    return (width // grid.dp) % 128 == 0


def put_in_order(x, order, grid, inside):
    return reorder(x, order) if aligned(grid, x.shape[1]) == inside else x


def cotangent_rows(out_grad, core, grid):
    rows, width = out_grad.shape

    def kernel(core_ref, cot_ref, out_ref):
        out_ref[...] = put_in_order(cot_ref[...], grid.gathered, grid, True)

    outs = [jax.ShapeDtypeStruct((rows // 2, width), bf16)]
    (x,) = on_rows(kernel, "cotangent_rows", core, [out_grad], [], outs)
    return put_in_order(x, grid.gathered, grid, False)


def second_norm(block_in, mine, other, gain, core, grid):
    rows, width = mine.shape

    def kernel(core_ref, in_ref, mine_ref, other_ref, gain_ref, hidden_ref, normed_ref):
        hidden = in_ref[...].astype(f32) + (mine_ref[...] + other_ref[...])
        hidden_ref[...] = hidden
        normed = (hidden * rms_scale(hidden) * gain_ref[...]).astype(bf16)
        normed_ref[...] = put_in_order(normed, grid.gathered, grid, True)

    outs = [jax.ShapeDtypeStruct((rows, width), f32), jax.ShapeDtypeStruct((rows, width), bf16)]
    hidden, normed = on_rows(
        kernel, "second_norm", core, [block_in], [mine, other, gain[None]], outs
    )
    return hidden, put_in_order(normed, grid.gathered, grid, False)


def second_norm_back(out_grad, hidden, gain, parts, core, grid):
    rows, width = hidden.shape
    parts = [put_in_order(x, grid.natural, grid, False) for x in parts]

    def kernel(core_ref, cot_ref, hidden_ref, gain_ref, *refs):
        upstream = sum(x[...].astype(f32) for x in refs[: len(parts)])
        upstream = put_in_order(upstream, grid.natural, grid, True)
        grad_ref, low_ref, gain_grad_ref = refs[len(parts) :]
        hidden = hidden_ref[...]
        gain_grad, grad = norm_back(hidden, rms_scale(hidden), gain_ref[...], upstream)
        grad = grad + cot_ref[...].astype(f32)
        grad_ref[...] = grad
        low_ref[...] = grad.astype(bf16)
        gain_grad_ref[...] = gain_grad

    sds = jax.ShapeDtypeStruct
    outs = [sds((rows, width), f32), sds((rows, width), bf16), sds((1, width), f32)]
    return on_rows(
        kernel, "second_norm_back", core, [out_grad], [hidden, gain[None], *parts], outs
    )


def first_norm_back(block_in, grad, gain, mine, other, core):
    rows, width = grad.shape

    def kernel(core_ref, in_ref, grad_ref, gain_ref, mine_ref, other_ref, out_ref, gain_grad_ref):
        inputs = in_ref[...].astype(f32)
        upstream = mine_ref[...] + other_ref[...]
        gain_grad, out = norm_back(inputs, rms_scale(inputs), gain_ref[...], upstream)
        out_ref[...] = out + grad_ref[...]
        gain_grad_ref[...] = gain_grad

    sds = jax.ShapeDtypeStruct
    outs = [sds((rows, width), f32), sds((1, width), f32)]
    return on_rows(
        kernel, "first_norm_back", core, [block_in], [grad, gain[None], mine, other], outs
    )


def block_result(block_in, hidden, parts, core, grid):
    rows, width = hidden.shape
    parts = [put_in_order(x, grid.natural, grid, False) for x in parts]

    def kernel(core_ref, in_ref, hidden_ref, *refs):
        out = sum(x[...].astype(f32) for x in refs[: len(parts)])
        out = put_in_order(out, grid.natural, grid, True)
        refs[-1][...] = (hidden_ref[...] + out).astype(bf16)

    outs = [jax.ShapeDtypeStruct((rows, width), bf16)]
    (x,) = on_rows(kernel, "block_result", core, [block_in], [hidden, *parts], outs)
    return x


def exchange(x, split, concat, groups):
    return lax.all_to_all(x, "dp", split, concat, tiled=True, axis_index_groups=groups)


def tie(*values):
    return lax.optimization_barrier(values)


def gather_along(x, grid, place, beside=()):
    n = grid.outer
    above = below = x
    from_below, from_above, done = [], [], []
    other = swap(x)
    for k in range(n - 1):
        below = lax.ppermute(below, "dp", grid.up)
        above = lax.ppermute(above, "dp", grid.down)
        extra = beside[k] if k < len(beside) else ()
        extra = extra(*done) if callable(extra) else extra
        below, above, *extra = tie(below, above, *extra)
        from_below.append((below, swap(below)))
        from_above.append((above, swap(above)))
        done += extra
    blocks = [x]
    for c in range(2):
        blocks += [other] if c else []
        for k in range(1, n):
            blocks.append(
                jnp.where(place + k < n, from_above[k - 1][c], from_below[n - 1 - k][c])
            )
    return jnp.concatenate(blocks, axis=0), done


def by_core(x):
    size = x.shape[0] // 2
    return x[:size], x[size:].astype(bf16)


def add_other_core(mine, other, grid):
    n = grid.outer
    other = tie(*[swap(y) for y in jnp.split(other, n)])
    return [x + y.astype(f32) for x, y in zip(jnp.split(mine, n), other)]


def scatter_along(own, grid, beside=()):
    n = grid.outer
    up = down = None
    done = []
    for k in range(n - 1):
        up = own[n - 1 - k] if up is None else own[n - 1 - k] + up.astype(f32)
        down = own[1 + k] if down is None else own[1 + k] + down.astype(f32)
        up = lax.ppermute(up.astype(bf16), "dp", grid.up)
        down = lax.ppermute(down.astype(bf16), "dp", grid.down)
        extra = beside[k] if k < len(beside) else ()
        extra = extra(*done) if callable(extra) else extra
        up, down, *extra = tie(up, down, *extra)
        done += extra
    return (own[0], up, down), done


def plane_gather(x, grid, inner):
    out = jnp.zeros((INNER,) + x.shape, x.dtype)
    for k in range(INNER):
        y = x
        if k:
            y = lax.ppermute(x, "dp", [(d, d ^ k) for d in range(grid.dp)])
        out = lax.dynamic_update_slice_in_dim(out, y[None], inner ^ k, 0)
    return out


def on_device(
    block_in,
    out_grad,
    attn_gain,
    mlp_gain,
    w_query,
    w_key,
    w_value,
    w_forget,
    w_output,
    w_gate,
    w_up,
    w_down,
    doc_starts,
    grid,
):
    core = lax.axis_index("head")
    place = lax.axis_index("dp") // INNER
    inner = lax.axis_index("dp") % INNER

    def columns(w):
        return exchange(w, 1, 0, grid.cols)

    def gather_rows(w):
        return lax.all_gather(w, "dp", axis=0, tiled=True, axis_index_groups=grid.laps)

    def column_pairs(a, b):
        rows = a.shape[0]
        both = [w.reshape(rows, grid.outer, -1) for w in (a, b)]
        both = columns(jnp.concatenate(both, axis=2).reshape(rows, -1))
        return jnp.split(both, 2, axis=1)

    gate_piece, up_piece = column_pairs(w_gate, w_up)
    inputs_f = block_in.astype(f32)
    normed = (inputs_f * rms_scale(inputs_f) * attn_gain).astype(bf16)
    query_pre = nn(normed, w_query)
    key_pre = nn(normed, w_key)
    value_pre = nn(normed, w_value)
    forget_pre = nn(normed, w_forget)
    query = jax.nn.silu(query_pre).astype(bf16)
    key = jax.nn.silu(key_pre).astype(bf16)
    value = jax.nn.silu(value_pre).astype(bf16)
    log_keep = jax.nn.log_sigmoid(forget_pre) * tau_inv
    mixed, *saved = attend_forward(query, key, value, log_keep, doc_starts)
    normed_own = lax.all_gather(
        half_of(normed, core), "dp", axis=0, tiled=True, axis_index_groups=grid.rows
    )
    branch_other = swap(nt(half_of(mixed, 1 - core), w_output))
    branch_mine = nt(half_of(mixed, core), w_output)
    branch_mine, gate_piece, up_piece, down_later, normed_own = tie(
        branch_mine, gate_piece, up_piece, w_down, normed_own
    )
    full_gate, full_up = gather_rows(gate_piece), gather_rows(up_piece)
    down_piece = columns(down_later)

    hidden, normed_two = second_norm(block_in, branch_mine, branch_other, mlp_gain, core, grid)
    def plane_tokens(own):
        own = own.reshape(INNER, 1, -1, own.shape[-1])
        out = jnp.zeros((INNER, 2) + own.shape[2:], own.dtype)
        out = lax.dynamic_update_slice_in_dim(out, own, core, 1)
        out = lax.dynamic_update_slice_in_dim(out, swap(own), 1 - core, 1)
        return out.reshape(-1, own.shape[-1])

    def plane_columns(shares):
        return exchange(shares.reshape(-1, shares.shape[2]), 0, 0, grid.rows)

    def plane_product(left, right):
        return tn(left, right).astype(bf16)

    def plane_sum(g):
        return lax.psum_scatter(
            g, "dp", scatter_dimension=0, tiled=True, axis_index_groups=grid.cols
        )

    def from_plane(g):
        size = g.shape[1]
        return exchange(g, 0, 1, grid.rows).reshape(-1, INNER, size).astype(f32)

    cot_rows = cotangent_rows(out_grad, core, grid)
    tokens, (cot_rows, down_piece, normed_plane, full_gate) = gather_along(
        normed_two,
        grid,
        place,
        ((cot_rows, down_piece), (plane_tokens(normed_own),), (full_gate,)),
    )
    full_down = gather_rows(down_piece)
    def gated(gate, up):
        return (jax.nn.silu(gate) * up).astype(bf16)

    cot_all, (gate_act, full_up, up_act, full_down, out_mine, out_other) = gather_along(
        cot_rows,
        grid,
        place,
        (
            (nn(tokens, full_gate), full_up),
            lambda gate, w_up_all: (nn(tokens, w_up_all), full_down),
            lambda gate, _, up, w_down_all: by_core(nt(gated(gate, up), w_down_all)),
        ),
    )
    out_own = add_other_core(out_mine, out_other, grid)
    out_blocks = jnp.zeros((grid.outer,) + out_own[0].shape, bf16)
    for k, x in enumerate(out_own):
        at = (place + k) % grid.outer
        out_blocks = lax.dynamic_update_slice_in_dim(out_blocks, x.astype(bf16)[None], at, 0)
    out_blocks, cot_all = tie(out_blocks.reshape(-1, out_blocks.shape[2]), cot_all)
    out_sum = lax.psum_scatter(
        out_blocks, "dp", scatter_dimension=0, tiled=True, axis_index_groups=grid.cols
    )

    def scatter_rows(g):
        return lax.psum_scatter(
            g, "dp", scatter_dimension=0, tiled=True, axis_index_groups=grid.laps
        )

    def to_columns(g):
        return exchange(g, 0, 1, grid.cols).astype(f32)

    inner_grad = nn(cot_all, full_down)
    gate_grad = (inner_grad * up_act * silu_slope(gate_act)).astype(bf16)
    up_grad = (inner_grad * jax.nn.silu(gate_act)).astype(bf16)
    inner_act = gated(gate_act, up_act)
    back_parts, (down_rows, out_sum, mixed_plane, gate_rows) = scatter_along(
        add_other_core(*by_core(nt(gate_grad, full_gate) + nt(up_grad, full_up)), grid),
        grid,
        (
            (
                tn(cot_all, inner_act).astype(bf16),
                out_sum,
                plane_columns(jnp.stack(jnp.split(mixed, INNER, axis=1))),
            ),
            (tn(tokens, gate_grad).astype(bf16),),
        ),
    )
    down_rows, gate_rows = scatter_rows(down_rows), scatter_rows(gate_rows)
    hidden_grad, low_half, mlp_gain_part = second_norm_back(
        out_grad, hidden, mlp_gain, back_parts, core, grid
    )
    branch_grad = join(low_half, swap(low_half), core)
    mixed_grad = nn(branch_grad, w_output).astype(bf16)
    mixed_grad, down_rows = tie(mixed_grad, down_rows)
    *pre_grads, shares = attend_backward(
        query, key, value, log_keep, doc_starts, saved, mixed_grad,
        (query_pre, key_pre, value_pre, forget_pre),
    )
    down_sum = to_columns(down_rows)
    down_sum, shares, *pre_grads = tie(down_sum, shares, *pre_grads)

    def normed_part(which):
        q, k, v, f = (half_of(g, which) for g in pre_grads)
        return nt(q, w_query) + nt(k, w_key) + nt(v, w_value) + nt(f, w_forget)

    up_later, _ = tie(up_grad, shares)
    columns_here, part_other, part_mine, up_rows = tie(
        plane_columns(shares),
        normed_part(1 - core),
        normed_part(core),
        tn(tokens, up_later).astype(bf16),
    )
    pre_grad = plane_product(normed_plane, columns_here)
    up_rows = scatter_rows(up_rows)
    input_grad, attn_gain_part = first_norm_back(
        block_in, hidden_grad, attn_gain, part_mine, swap(part_other), core
    )
    _, low_half, attn_gain_part = tie(pre_grad, low_half, attn_gain_part)
    low_plane = plane_tokens(plane_gather(low_half, grid, inner))
    sums, output_grad = tie(plane_sum(pre_grad), plane_product(low_plane, mixed_plane))
    output_sum = plane_sum(output_grad)
    result = block_result(block_in, hidden, [out_sum], core, grid)
    result = join(result, swap(result), core)

    sums = from_plane(sums)
    output_sum = from_plane(output_sum).reshape(sums.shape[0], -1)
    ends = [0]
    for g in pre_grads:
        ends.append(ends[-1] + g.shape[1] // INNER)
    query_sum, key_sum, value_sum, forget_sum = (
        sums[:, :, a:b].reshape(sums.shape[0], -1) for a, b in zip(ends, ends[1:])
    )

    input_grad = join(input_grad, swap(input_grad), core)

    gains = jnp.concatenate([attn_gain_part, mlp_gain_part], axis=0)
    gains = gains + swap(gains)
    gains = jnp.swapaxes(gains.reshape(2, grid.dp, -1), 0, 1)
    gains = jnp.sum(lax.all_to_all(gains, "dp", 0, 0, tiled=True), axis=0)

    return (
        result,
        input_grad,
        gains[0],
        gains[1],
        query_sum,
        key_sum,
        value_sum,
        forget_sum,
        output_sum,
        to_columns(gate_rows),
        to_columns(up_rows),
        down_sum,
    )


def solution(mesh):
    placed = (
        P("dp", None),
        P("dp", None),
        P(),
        P(),
        P(None, "head"),
        P(None, "head"),
        P(None, "head"),
        P(None, "head"),
        P(None, "head"),
        P("dp", "head"),
        P("dp", "head"),
        P("dp", "head"),
        P("dp", None),
    )
    return jax.shard_map(
        partial(on_device, grid=Grid(mesh.shape["dp"])),
        mesh=mesh,
        in_specs=placed,
        out_specs=(P("dp", None), P("dp", None), P("dp"), P("dp")) + (P("dp", "head"),) * 8,
        check_vma=False,
    )
```

```python
import math
from functools import partial
import jax
import jax.numpy as jnp
from jax import lax
from jax.experimental import pallas as pl
from jax.experimental.pallas import tpu as pltpu
from jax.sharding import PartitionSpec as P

DK = 512
DV = 512
M = 64
B = 16
f32 = jnp.float32
bf16 = jnp.bfloat16


def nn(a, b):
    return jnp.dot(a.astype(bf16), b.astype(bf16), preferred_element_type=f32)


def nt(a, b):
    return lax.dot_general(
        a.astype(bf16), b.astype(bf16), (((1,), (1,)), ((), ())), preferred_element_type=f32
    )


def tn(a, b):
    return lax.dot_general(
        a.astype(bf16), b.astype(bf16), (((0,), (0,)), ((), ())), preferred_element_type=f32
    )


def nn3(a, b):
    ah, bh = a.astype(bf16), b.astype(bf16)
    al, bl = (a - ah.astype(f32)).astype(bf16), (b - bh.astype(f32)).astype(bf16)
    return nn(ah, bh) + (nn(al, bh) + nn(ah, bl))


def shift_up(x, s):
    return pltpu.roll(x, x.shape[0] - s, 0)


def shift_down(x, s):
    return pltpu.roll(x, s, 0)


def segment_at(pos, starts):
    seg = jnp.zeros(pos.shape, jnp.int32)
    for s in starts:
        seg = seg + (pos >= s).astype(jnp.int32)
    return seg


def same_document(t, j, starts):
    ok = None
    for s in starts:
        same = (t >= s) == (j >= s)
        ok = same if ok is None else ok & same
    return ok


def level_sizes(length):
    sizes = []
    h = length // 2
    while h >= B:
        sizes.append(h)
        h //= 2
    return sizes


def row_pick(x, size, row):
    n, lanes = x.shape
    x3 = x.reshape(n // size, size, lanes)
    return jnp.broadcast_to(x3[:, row : row + 1, :], x3.shape).reshape(n, lanes)


class Common:
    def __init__(self, la, starts):
        length, lanes = la.shape
        self.length, self.lanes = length, lanes
        rows = lax.broadcasted_iota(jnp.int32, (length, lanes), 0)
        self.rows = rows
        self.lane_head = lax.broadcasted_iota(jnp.int32, (length, lanes), 1) // M
        c = la
        s = 1
        while s < length:
            c = c + jnp.where(rows >= s, shift_down(c, s), 0.0)
            s *= 2
        self.c = c
        self.alpha = jnp.exp(la)
        self.om = 1.0 - self.alpha
        self.levels = level_sizes(length)
        self.x = []
        for h in self.levels:
            mid = row_pick(c, 2 * h, h - 1)
            self.x.append(jnp.exp(-jnp.abs(c - mid)))
        t = lax.broadcasted_iota(jnp.int32, (length, length), 0)
        j = lax.broadcasted_iota(jnp.int32, (length, length), 1)
        same = same_document(t, j, starts)
        self.masks = [
            same & ((t // (2 * h)) == (j // (2 * h))) & ((t & h) != 0) & ((j & h) == 0)
            for h in self.levels
        ]
        tc = lax.broadcasted_iota(jnp.int32, (length, B), 0)
        off = lax.broadcasted_iota(jnp.int32, (length, B), 1)
        jc = (tc - tc % B) + off
        self.mask_c = same_document(tc, jc, starts) & (jc <= tc)

    def by_head(self, parts):
        out = parts[0]
        for i in range(1, len(parts)):
            out = jnp.where(self.lane_head == i, parts[i], out)
        return out

    def only(self, x, i):
        return jnp.where(self.lane_head == i, x, 0.0)

    def decay_from(self, jj):
        return jnp.exp(jnp.minimum(self.c - row_pick(self.c, B, jj), 0.0))

    def om_at(self, jj):
        return row_pick(self.om, B, jj)


def blocks(x):
    return x.reshape(x.shape[0] // B, B, x.shape[1])


def block_nt(a, b):
    r = lax.dot_general(
        blocks(a.astype(bf16)),
        blocks(b.astype(bf16)),
        (((2,), (2,)), ((0,), (0,))),
        preferred_element_type=f32,
    )
    return r.reshape(a.shape[0], B)


def block_nn(a, b):
    r = lax.dot_general(
        blocks(a.astype(bf16)),
        blocks(b.astype(bf16)),
        (((2,), (1,)), ((0,), (0,))),
        preferred_element_type=f32,
    )
    return r.reshape(a.shape[0], b.shape[1])


def block_tn(a, b):
    at = jnp.swapaxes(blocks(a), 1, 2).astype(bf16)
    r = lax.dot_general(
        at, blocks(b.astype(bf16)), (((2,), (1,)), ((0,), (0,))), preferred_element_type=f32
    )
    return r.reshape(a.shape[0], b.shape[1])


def collect(lanes, heads):
    r = lax.broadcasted_iota(jnp.int32, (B * lanes, heads * 128), 0)
    col = lax.broadcasted_iota(jnp.int32, (B * lanes, heads * 128), 1)
    jj, head = r // lanes, (r % lanes) // M
    return jnp.where(col == head * 128 + jj, 1.0, 0.0).astype(bf16)


def wide(x, jj):
    return jnp.broadcast_to(x[:, jj : jj + 1], (x.shape[0], 128))


def forward_math(q, k, v, la, starts):
    heads = q.shape[1] // DK
    scale = 1.0 / math.sqrt(DK)
    cm = Common(la, starts)
    qs = [q[:, i * DK : (i + 1) * DK] for i in range(heads)]
    ks = [k[:, i * DK : (i + 1) * DK] for i in range(heads)]
    vs = [v[:, i * DV : (i + 1) * DV] for i in range(heads)]
    aff = [nt(qs[i], ks[i]) * scale for i in range(heads)]
    affc = [jnp.where(cm.mask_c, block_nt(qs[i], ks[i]) * scale, 0.0) for i in range(heads)]
    s = jnp.zeros_like(la)
    parts = []
    for x, mask in zip(cm.x, cm.masks):
        g = x * cm.om
        part = x * cm.by_head([nn3(jnp.where(mask, aff[i], 0.0), g) for i in range(heads)])
        parts.append(part)
        s = s + part
    for jj in range(B):
        s = s + cm.by_head([wide(affc[i], jj) for i in range(heads)]) * (
            cm.decay_from(jj) * cm.om_at(jj)
        )
    top = cm.by_head(
        [
            jnp.max(jnp.where(cm.lane_head == i, s, -jnp.inf), axis=1, keepdims=True)
            for i in range(heads)
        ]
    )
    e = jnp.exp(s - top)
    total = cm.by_head([jnp.sum(cm.only(e, i), axis=1, keepdims=True) for i in range(heads)])
    p = e / total
    mix = [jnp.zeros((cm.length, cm.length), f32) for _ in range(heads)]
    for x, mask in zip(cm.x, cm.masks):
        g = x * cm.om
        px = p * x
        for i in range(heads):
            mix[i] = mix[i] + jnp.where(mask, nt(cm.only(px, i), g), 0.0)
    mix = [m.astype(bf16) for m in mix]
    pieces = [(p * (cm.decay_from(jj) * cm.om_at(jj))).astype(bf16) for jj in range(B)]
    mixc = nn(jnp.concatenate(pieces, axis=1), collect(cm.lanes, heads))
    mixc = [
        jnp.where(cm.mask_c, mixc[:, i * 128 : i * 128 + B], 0.0) for i in range(heads)
    ]
    outs = [nn(mix[i], vs[i]) + block_nn(mixc[i], vs[i]) for i in range(heads)]
    return outs, p, parts, mix, mixc


def backward_math(q, k, v, la, starts, p, parts, mix, mixc, dout):
    heads = q.shape[1] // DK
    scale = 1.0 / math.sqrt(DK)
    cm = Common(la, starts)
    qs = [q[:, i * DK : (i + 1) * DK] for i in range(heads)]
    ks = [k[:, i * DK : (i + 1) * DK] for i in range(heads)]
    vs = [v[:, i * DV : (i + 1) * DV] for i in range(heads)]
    dos = [dout[:, i * DV : (i + 1) * DV].astype(bf16) for i in range(heads)]
    aff = [nt(qs[i], ks[i]) * scale for i in range(heads)]
    affc = [jnp.where(cm.mask_c, block_nt(qs[i], ks[i]) * scale, 0.0) for i in range(heads)]
    dmix = [nt(dos[i], vs[i]) for i in range(heads)]
    dmixc = [jnp.where(cm.mask_c, block_nt(dos[i], vs[i]), 0.0) for i in range(heads)]
    dp = jnp.zeros_like(la)
    dparts = []
    for x, mask in zip(cm.x, cm.masks):
        g = x * cm.om
        part = x * cm.by_head([nn3(jnp.where(mask, dmix[i], 0.0), g) for i in range(heads)])
        dparts.append(part)
        dp = dp + part
    for jj in range(B):
        dp = dp + cm.by_head([wide(dmixc[i], jj) for i in range(heads)]) * (
            cm.decay_from(jj) * cm.om_at(jj)
        )
    pdp = p * dp
    inner = cm.by_head([jnp.sum(cm.only(pdp, i), axis=1, keepdims=True) for i in range(heads)])
    ds = pdp - p * inner
    daff = [jnp.zeros((cm.length, cm.length), f32) for _ in range(heads)]
    dla = jnp.zeros_like(la)
    reach = jnp.zeros_like(la)
    for n, h in enumerate(cm.levels):
        x, mask = cm.x[n], cm.masks[n]
        g = x * cm.om
        dsx, px = ds * x, p * x
        both = jnp.concatenate([dsx, px], axis=0).astype(bf16)
        cols = []
        for i in range(heads):
            daff[i] = daff[i] + jnp.where(mask, nt(cm.only(dsx, i), g), 0.0)
            left = jnp.concatenate(
                [jnp.where(mask, aff[i], 0.0), jnp.where(mask, dmix[i], 0.0)], axis=0
            )
            cols.append(tn(left, both))
        r = x * cm.by_head(cols)
        reach = reach + r
        right = (cm.rows & h) != 0
        flow = jnp.where(right, ds * parts[n] + p * dparts[n], cm.om * r)
        s = 1
        while s < h:
            flow = flow + jnp.where((cm.rows & (h - 1)) < h - s, shift_up(flow, s), 0.0)
            s *= 2
        dla = dla + jnp.where(right, flow, row_pick(flow, h, 0) - flow)
    flow = jnp.zeros_like(la)
    near = jnp.zeros_like(la)
    pieces = []
    for jj in range(B):
        w = cm.decay_from(jj)
        omj = cm.om_at(jj)
        aj = cm.by_head([wide(affc[i], jj) for i in range(heads)])
        dj = cm.by_head([wide(dmixc[i], jj) for i in range(heads)])
        pieces.append((ds * (w * omj)).astype(bf16))
        z = w * (aj * ds + dj * p)
        flow = flow + omj * z
        z3 = blocks(z)
        tot = jnp.broadcast_to(jnp.sum(z3, axis=1, keepdims=True), z3.shape).reshape(z.shape)
        near = jnp.where((cm.rows & (B - 1)) == jj, tot, near)
    flow = flow - cm.om * near
    s = 1
    while s < B:
        flow = flow + jnp.where((cm.rows & (B - 1)) < B - s, shift_up(flow, s), 0.0)
        s *= 2
    dla = dla + flow - cm.alpha * (reach + near)
    daffc = nn(jnp.concatenate(pieces, axis=1), collect(cm.lanes, heads))
    daffc = [
        jnp.where(cm.mask_c, daffc[:, i * 128 : i * 128 + B], 0.0) for i in range(heads)
    ]
    dq, dk, dv = [], [], []
    for i in range(heads):
        da = daff[i].astype(bf16)
        dq.append((nn(da, ks[i]) + block_nn(daffc[i], ks[i])) * scale)
        dk.append((tn(da, qs[i]) + block_tn(daffc[i], qs[i])) * scale)
        dv.append(tn(mix[i], dos[i]) + block_tn(mixc[i], dos[i]))
    return dq, dk, dv, dla


def head_split(outs, ref, width):
    for i, x in enumerate(outs):
        ref[:, i * width : (i + 1) * width] = x.astype(ref.dtype)


def forward_kernel(starts_ref, q_ref, k_ref, v_ref, la_ref, o_ref, p_ref, parts_ref, mix_ref, mixc_ref):
    starts = [starts_ref[0, n] for n in range(starts_ref.shape[1])]
    outs, p, parts, mix, mixc = forward_math(
        q_ref[...], k_ref[...], v_ref[...], la_ref[...], starts
    )
    head_split(outs, o_ref, DV)
    p_ref[...] = p
    for n, x in enumerate(parts):
        parts_ref[n] = x
    for i in range(len(mix)):
        mix_ref[i] = mix[i]
        mixc_ref[i] = mixc[i].astype(bf16)


tau_inv = 0.125


def silu_slope(values):
    sigmoid_val = jax.nn.sigmoid(values)
    return sigmoid_val * (1.0 + values * (1.0 - sigmoid_val))


def through_silu(grads, z):
    width = grads[0].shape[1]
    return [g * silu_slope(z[:, i * width : (i + 1) * width]) for i, g in enumerate(grads)]


def through_gate(dla, zf):
    return dla * tau_inv * jax.nn.sigmoid(-zf)


INNER = 4


def share_columns(wide_parts, dzf, shares_ref):
    lanes = dzf.shape[1]
    size = lanes // INNER
    lane = lax.broadcasted_iota(jnp.int32, dzf.shape, 1)
    for n in range(INNER):
        at = 0
        for x in wide_parts:
            width = x.shape[1] // INNER
            shares_ref[n, :, at : at + width] = x[:, n * width : (n + 1) * width]
            at += width
        turned = pltpu.roll(dzf, (lanes - n * size) % lanes, 1) if n else dzf
        shares_ref[n, :, at : at + lanes] = jnp.where(lane < size, turned, 0.0).astype(bf16)


def backward_kernel(
    starts_ref, q_ref, k_ref, v_ref, la_ref, p_ref, parts_ref, mix_ref, mixc_ref, do_ref,
    zq_ref, zk_ref, zv_ref, zf_ref, dzq_ref, dzk_ref, dzv_ref, dzf_ref, shares_ref,
):
    starts = [starts_ref[0, n] for n in range(starts_ref.shape[1])]
    heads = mix_ref.shape[0]
    dq, dk, dv, dla = backward_math(
        q_ref[...],
        k_ref[...],
        v_ref[...],
        la_ref[...],
        starts,
        p_ref[...],
        [parts_ref[n] for n in range(parts_ref.shape[0])],
        [mix_ref[i] for i in range(heads)],
        [mixc_ref[i] for i in range(heads)],
        do_ref[...],
    )
    for grads, z_ref, dz_ref in ((dq, zq_ref, dzq_ref), (dk, zk_ref, dzk_ref), (dv, zv_ref, dzv_ref)):
        head_split(through_silu(grads, z_ref[...]), dz_ref, grads[0].shape[1])
    dzf = through_gate(dla, zf_ref[...])
    dzf_ref[...] = dzf.astype(bf16)
    share_columns([dzq_ref[...], dzk_ref[...], dzv_ref[...]], dzf, shares_ref)


SMEM = pl.BlockSpec(memory_space=pltpu.SMEM)
VMEM = pl.BlockSpec(memory_space=pltpu.VMEM)


def attend_forward(q, k, v, la, starts):
    length, lanes = la.shape
    heads = q.shape[1] // DK
    sds = jax.ShapeDtypeStruct
    return pl.pallas_call(
        forward_kernel,
        out_shape=(
            sds((length, heads * DV), bf16),
            sds((length, lanes), f32),
            sds((len(level_sizes(length)), length, lanes), f32),
            sds((heads, length, length), bf16),
            sds((heads, length, B), bf16),
        ),
        in_specs=[SMEM] + [VMEM] * 4,
        out_specs=(VMEM,) * 5,
        cost_estimate=pl.CostEstimate(
            flops=4 * 10**9, transcendentals=10**6, bytes_accessed=4 * 10**6
        ),
        name="slot_forward",
    )(starts, q, k, v, la)


def attend_backward(q, k, v, la, starts, saved, dout, pres):
    sds = jax.ShapeDtypeStruct
    return pl.pallas_call(
        backward_kernel,
        out_shape=(
            sds(q.shape, bf16),
            sds(k.shape, bf16),
            sds(v.shape, bf16),
            sds(la.shape, bf16),
            sds((INNER, q.shape[0], (2 * DK + DV) * (q.shape[1] // DK) // INNER + la.shape[1]), bf16),
        ),
        in_specs=[SMEM] + [VMEM] * 13,
        out_specs=(VMEM,) * 5,
        cost_estimate=pl.CostEstimate(
            flops=12 * 10**9, transcendentals=10**6, bytes_accessed=8 * 10**6
        ),
        name="slot_backward",
    )(starts, q, k, v, la, *saved, dout, *pres)


eps = 1e-06
LAP = (0, 1, 3, 2)


def rms_scale(values):
    return lax.rsqrt(jnp.mean(values * values, axis=-1, keepdims=True) + eps)


def norm_back(values, scale, gain, upstream):
    gain_grad = jnp.sum(upstream * values * scale, axis=0, keepdims=True)
    weighted = upstream * gain
    input_grad = scale * weighted - values * (scale * scale * scale) * jnp.mean(
        weighted * values, axis=-1, keepdims=True
    )
    return (gain_grad, input_grad)


class Grid:
    def __init__(self, dp):
        self.dp = dp
        self.outer = dp // INNER
        self.laps = [[o * INNER + i for i in LAP] for o in range(self.outer)]
        self.rows = [[o * INNER + i for i in range(INNER)] for o in range(self.outer)]
        self.cols = [[o * INNER + i for o in range(self.outer)] for i in range(INNER)]
        self.gathered = [o * INNER + i for i in LAP for o in range(self.outer)]
        self.natural = inverse(self.gathered)
        self.up = [(d, d + INNER) for d in range(dp - INNER)]
        self.down = [(d + INNER, d) for d in range(dp - INNER)]


def reorder(x, order):
    size = x.shape[-1] // len(order)
    return jnp.concatenate([x[..., b * size : (b + 1) * size] for b in order], axis=-1)


def inverse(order):
    back = [0] * len(order)
    for n, b in enumerate(order):
        back[b] = n
    return back


def swap(x):
    return lax.ppermute(x, "head", [(0, 1), (1, 0)])


def half_of(x, which):
    size = x.shape[0] // 2
    return lax.dynamic_slice_in_dim(x, which * size, size, 0)


def join(mine, other, core):
    size = mine.shape[0]
    out = jnp.zeros((2 * size,) + mine.shape[1:], mine.dtype)
    out = lax.dynamic_update_slice_in_dim(out, mine, core * size, 0)
    return lax.dynamic_update_slice_in_dim(out, other, (1 - core) * size, 0)


def on_rows(kernel, name, core, halves, wholes, outs):
    rows = halves[0].shape[0] // 2
    specs = [pl.BlockSpec((rows, x.shape[1]), lambda i, c: (c[0], 0)) for x in halves]
    specs += [pl.BlockSpec(x.shape, lambda i, c: (0, 0)) for x in wholes]
    return pl.pallas_call(
        kernel,
        out_shape=outs,
        grid_spec=pltpu.PrefetchScalarGridSpec(
            num_scalar_prefetch=1,
            grid=(1,),
            in_specs=specs,
            out_specs=[pl.BlockSpec(x.shape, lambda i, c: (0, 0)) for x in outs],
        ),
        name=name,
    )(core.reshape(1), *halves, *wholes)


def aligned(grid, width):
    return (width // grid.dp) % 128 == 0


def put_in_order(x, order, grid, inside):
    return reorder(x, order) if aligned(grid, x.shape[1]) == inside else x


def cotangent_rows(out_grad, core, grid):
    rows, width = out_grad.shape

    def kernel(core_ref, cot_ref, out_ref):
        out_ref[...] = put_in_order(cot_ref[...], grid.gathered, grid, True)

    outs = [jax.ShapeDtypeStruct((rows // 2, width), bf16)]
    (x,) = on_rows(kernel, "cotangent_rows", core, [out_grad], [], outs)
    return put_in_order(x, grid.gathered, grid, False)


def second_norm(block_in, mine, other, gain, core, grid):
    rows, width = mine.shape

    def kernel(core_ref, in_ref, mine_ref, other_ref, gain_ref, hidden_ref, normed_ref):
        hidden = in_ref[...].astype(f32) + (mine_ref[...] + other_ref[...])
        hidden_ref[...] = hidden
        normed = (hidden * rms_scale(hidden) * gain_ref[...]).astype(bf16)
        normed_ref[...] = put_in_order(normed, grid.gathered, grid, True)

    outs = [jax.ShapeDtypeStruct((rows, width), f32), jax.ShapeDtypeStruct((rows, width), bf16)]
    hidden, normed = on_rows(
        kernel, "second_norm", core, [block_in], [mine, other, gain[None]], outs
    )
    return hidden, put_in_order(normed, grid.gathered, grid, False)


def second_norm_back(out_grad, hidden, gain, parts, core, grid):
    rows, width = hidden.shape
    parts = [put_in_order(x, grid.natural, grid, False) for x in parts]

    def kernel(core_ref, cot_ref, hidden_ref, gain_ref, *refs):
        upstream = sum(x[...].astype(f32) for x in refs[: len(parts)])
        upstream = put_in_order(upstream, grid.natural, grid, True)
        grad_ref, low_ref, gain_grad_ref = refs[len(parts) :]
        hidden = hidden_ref[...]
        gain_grad, grad = norm_back(hidden, rms_scale(hidden), gain_ref[...], upstream)
        grad = grad + cot_ref[...].astype(f32)
        grad_ref[...] = grad
        low_ref[...] = grad.astype(bf16)
        gain_grad_ref[...] = gain_grad

    sds = jax.ShapeDtypeStruct
    outs = [sds((rows, width), f32), sds((rows, width), bf16), sds((1, width), f32)]
    return on_rows(
        kernel, "second_norm_back", core, [out_grad], [hidden, gain[None], *parts], outs
    )


def first_norm_back(block_in, grad, gain, mine, other, core):
    rows, width = grad.shape

    def kernel(core_ref, in_ref, grad_ref, gain_ref, mine_ref, other_ref, out_ref, gain_grad_ref):
        inputs = in_ref[...].astype(f32)
        upstream = mine_ref[...] + other_ref[...]
        gain_grad, out = norm_back(inputs, rms_scale(inputs), gain_ref[...], upstream)
        out_ref[...] = out + grad_ref[...]
        gain_grad_ref[...] = gain_grad

    sds = jax.ShapeDtypeStruct
    outs = [sds((rows, width), f32), sds((1, width), f32)]
    return on_rows(
        kernel, "first_norm_back", core, [block_in], [grad, gain[None], mine, other], outs
    )


def block_result(block_in, hidden, parts, core, grid):
    rows, width = hidden.shape
    parts = [put_in_order(x, grid.natural, grid, False) for x in parts]

    def kernel(core_ref, in_ref, hidden_ref, *refs):
        out = sum(x[...].astype(f32) for x in refs[: len(parts)])
        out = put_in_order(out, grid.natural, grid, True)
        refs[-1][...] = (hidden_ref[...] + out).astype(bf16)

    outs = [jax.ShapeDtypeStruct((rows, width), bf16)]
    (x,) = on_rows(kernel, "block_result", core, [block_in], [hidden, *parts], outs)
    return x


def exchange(x, split, concat, groups):
    return lax.all_to_all(x, "dp", split, concat, tiled=True, axis_index_groups=groups)


def tie(*values):
    return lax.optimization_barrier(values)


def gather_along(x, grid, place, beside=()):
    n = grid.outer
    above = below = x
    from_below, from_above, done = [], [], []
    other = swap(x)
    for k in range(n - 1):
        below = lax.ppermute(below, "dp", grid.up)
        above = lax.ppermute(above, "dp", grid.down)
        extra = beside[k] if k < len(beside) else ()
        extra = extra(*done) if callable(extra) else extra
        below, above, *extra = tie(below, above, *extra)
        from_below.append((below, swap(below)))
        from_above.append((above, swap(above)))
        done += extra
    blocks = [x]
    for c in range(2):
        blocks += [other] if c else []
        for k in range(1, n):
            blocks.append(
                jnp.where(place + k < n, from_above[k - 1][c], from_below[n - 1 - k][c])
            )
    return jnp.concatenate(blocks, axis=0), done


def by_core(x):
    size = x.shape[0] // 2
    return x[:size], x[size:].astype(bf16)


def add_other_core(mine, other, grid):
    n = grid.outer
    other = tie(*[swap(y) for y in jnp.split(other, n)])
    return [x + y.astype(f32) for x, y in zip(jnp.split(mine, n), other)]


def scatter_along(own, grid, beside=()):
    n = grid.outer
    up = down = None
    done = []
    for k in range(n - 1):
        up = own[n - 1 - k] if up is None else own[n - 1 - k] + up.astype(f32)
        down = own[1 + k] if down is None else own[1 + k] + down.astype(f32)
        up = lax.ppermute(up.astype(bf16), "dp", grid.up)
        down = lax.ppermute(down.astype(bf16), "dp", grid.down)
        extra = beside[k] if k < len(beside) else ()
        extra = extra(*done) if callable(extra) else extra
        up, down, *extra = tie(up, down, *extra)
        done += extra
    return (own[0], up, down), done


def plane_gather(x, grid, inner):
    out = jnp.zeros((INNER,) + x.shape, x.dtype)
    for k in range(INNER):
        y = x
        if k:
            y = lax.ppermute(x, "dp", [(d, d ^ k) for d in range(grid.dp)])
        out = lax.dynamic_update_slice_in_dim(out, y[None], inner ^ k, 0)
    return out


def on_device(
    block_in,
    out_grad,
    attn_gain,
    mlp_gain,
    w_query,
    w_key,
    w_value,
    w_forget,
    w_output,
    w_gate,
    w_up,
    w_down,
    doc_starts,
    grid,
):
    core = lax.axis_index("head")
    place = lax.axis_index("dp") // INNER
    inner = lax.axis_index("dp") % INNER

    def columns(w):
        return exchange(w, 1, 0, grid.cols)

    def gather_rows(w):
        return lax.all_gather(w, "dp", axis=0, tiled=True, axis_index_groups=grid.laps)

    def column_pairs(a, b):
        rows = a.shape[0]
        both = [w.reshape(rows, grid.outer, -1) for w in (a, b)]
        both = columns(jnp.concatenate(both, axis=2).reshape(rows, -1))
        return jnp.split(both, 2, axis=1)

    gate_piece, up_piece = column_pairs(w_gate, w_up)
    inputs_f = block_in.astype(f32)
    normed = (inputs_f * rms_scale(inputs_f) * attn_gain).astype(bf16)
    query_pre = nn(normed, w_query)
    key_pre = nn(normed, w_key)
    value_pre = nn(normed, w_value)
    forget_pre = nn(normed, w_forget)
    query = jax.nn.silu(query_pre).astype(bf16)
    key = jax.nn.silu(key_pre).astype(bf16)
    value = jax.nn.silu(value_pre).astype(bf16)
    log_keep = jax.nn.log_sigmoid(forget_pre) * tau_inv
    mixed, *saved = attend_forward(query, key, value, log_keep, doc_starts)
    normed_own = lax.all_gather(
        half_of(normed, core), "dp", axis=0, tiled=True, axis_index_groups=grid.rows
    )
    branch_other = swap(nt(half_of(mixed, 1 - core), w_output))
    branch_mine = nt(half_of(mixed, core), w_output)
    branch_mine, gate_piece, up_piece, down_later, normed_own = tie(
        branch_mine, gate_piece, up_piece, w_down, normed_own
    )
    full_gate, full_up = gather_rows(gate_piece), gather_rows(up_piece)
    down_piece = columns(down_later)

    hidden, normed_two = second_norm(block_in, branch_mine, branch_other, mlp_gain, core, grid)
    def plane_tokens(own):
        own = own.reshape(INNER, 1, -1, own.shape[-1])
        out = jnp.zeros((INNER, 2) + own.shape[2:], own.dtype)
        out = lax.dynamic_update_slice_in_dim(out, own, core, 1)
        out = lax.dynamic_update_slice_in_dim(out, swap(own), 1 - core, 1)
        return out.reshape(-1, own.shape[-1])

    def plane_columns(shares):
        return exchange(shares.reshape(-1, shares.shape[2]), 0, 0, grid.rows)

    def plane_product(left, right):
        return tn(left, right).astype(bf16)

    def plane_sum(g):
        return lax.psum_scatter(
            g, "dp", scatter_dimension=0, tiled=True, axis_index_groups=grid.cols
        )

    def from_plane(g):
        size = g.shape[1]
        return exchange(g, 0, 1, grid.rows).reshape(-1, INNER, size).astype(f32)

    cot_rows = cotangent_rows(out_grad, core, grid)
    tokens, (cot_rows, down_piece, normed_plane, full_gate) = gather_along(
        normed_two,
        grid,
        place,
        ((cot_rows, down_piece), (plane_tokens(normed_own),), (full_gate,)),
    )
    full_down = gather_rows(down_piece)
    def gated(gate, up):
        return (jax.nn.silu(gate) * up).astype(bf16)

    cot_all, (gate_act, full_up, up_act, full_down, out_mine, out_other) = gather_along(
        cot_rows,
        grid,
        place,
        (
            (nn(tokens, full_gate), full_up),
            lambda gate, w_up_all: (nn(tokens, w_up_all), full_down),
            lambda gate, _, up, w_down_all: by_core(nt(gated(gate, up), w_down_all)),
        ),
    )
    out_own = add_other_core(out_mine, out_other, grid)
    out_blocks = jnp.zeros((grid.outer,) + out_own[0].shape, bf16)
    for k, x in enumerate(out_own):
        at = (place + k) % grid.outer
        out_blocks = lax.dynamic_update_slice_in_dim(out_blocks, x.astype(bf16)[None], at, 0)
    out_blocks, cot_all = tie(out_blocks.reshape(-1, out_blocks.shape[2]), cot_all)
    out_sum = lax.psum_scatter(
        out_blocks, "dp", scatter_dimension=0, tiled=True, axis_index_groups=grid.cols
    )

    def scatter_rows(g):
        return lax.psum_scatter(
            g, "dp", scatter_dimension=0, tiled=True, axis_index_groups=grid.laps
        )

    def to_columns(g):
        return exchange(g, 0, 1, grid.cols).astype(f32)

    def to_columns_beside(g):
        n = grid.outer
        if n & (n - 1) or n > 4:
            return to_columns(g)
        blocks = g.reshape(n, -1, g.shape[1])
        out = jnp.zeros_like(blocks)
        for s in range(n):
            piece = lax.dynamic_slice_in_dim(blocks, place ^ s, 1, 0)
            if s:
                pairs = [(d, (d // INNER ^ s) * INNER + d % INNER) for d in range(grid.dp)]
                piece = lax.ppermute(piece, "dp", pairs)
            out = lax.dynamic_update_slice_in_dim(out, piece, place ^ s, 0)
        return jnp.swapaxes(out, 0, 1).reshape(blocks.shape[1], -1).astype(f32)

    inner_grad = nn(cot_all, full_down)
    gate_grad = (inner_grad * up_act * silu_slope(gate_act)).astype(bf16)
    up_grad = (inner_grad * jax.nn.silu(gate_act)).astype(bf16)
    inner_act = gated(gate_act, up_act)
    back_parts, (down_rows, out_sum, mixed_plane, gate_rows, up_rows) = scatter_along(
        add_other_core(*by_core(nt(gate_grad, full_gate) + nt(up_grad, full_up)), grid),
        grid,
        (
            (
                tn(cot_all, inner_act).astype(bf16),
                out_sum,
                plane_columns(jnp.stack(jnp.split(mixed, INNER, axis=1))),
            ),
            (tn(tokens, gate_grad).astype(bf16),),
            (tn(tokens, up_grad).astype(bf16),),
        ),
    )
    down_rows, gate_rows, up_rows = (scatter_rows(g) for g in (down_rows, gate_rows, up_rows))
    hidden_grad, low_half, mlp_gain_part = second_norm_back(
        out_grad, hidden, mlp_gain, back_parts, core, grid
    )
    branch_grad = join(low_half, swap(low_half), core)
    mixed_grad = nn(branch_grad, w_output).astype(bf16)
    mixed_grad, down_rows = tie(mixed_grad, down_rows)
    *pre_grads, shares = attend_backward(
        query, key, value, log_keep, doc_starts, saved, mixed_grad,
        (query_pre, key_pre, value_pre, forget_pre),
    )

    def normed_part(which):
        q, k, v, f = (half_of(g, which) for g in pre_grads)
        return nt(q, w_query) + nt(k, w_key) + nt(v, w_value) + nt(f, w_forget)

    columns_here, part_other, part_mine, down_sum, gate_sum = tie(
        plane_columns(shares),
        normed_part(1 - core),
        normed_part(core),
        to_columns_beside(down_rows),
        to_columns_beside(gate_rows),
    )
    pre_grad = plane_product(normed_plane, columns_here)
    input_grad, attn_gain_part = first_norm_back(
        block_in, hidden_grad, attn_gain, part_mine, swap(part_other), core
    )
    _, low_half, attn_gain_part = tie(pre_grad, low_half, attn_gain_part)
    low_plane = plane_tokens(plane_gather(low_half, grid, inner))
    sums, output_grad = tie(plane_sum(pre_grad), plane_product(low_plane, mixed_plane))
    output_sum = plane_sum(output_grad)
    result = block_result(block_in, hidden, [out_sum], core, grid)
    result = join(result, swap(result), core)

    sums = from_plane(sums)
    output_sum = from_plane(output_sum).reshape(sums.shape[0], -1)
    ends = [0]
    for g in pre_grads:
        ends.append(ends[-1] + g.shape[1] // INNER)
    query_sum, key_sum, value_sum, forget_sum = (
        sums[:, :, a:b].reshape(sums.shape[0], -1) for a, b in zip(ends, ends[1:])
    )

    input_grad = join(input_grad, swap(input_grad), core)

    gains = jnp.concatenate([attn_gain_part, mlp_gain_part], axis=0)
    gains = gains + swap(gains)
    gains = jnp.swapaxes(gains.reshape(2, grid.dp, -1), 0, 1)
    gains = jnp.sum(lax.all_to_all(gains, "dp", 0, 0, tiled=True), axis=0)

    return (
        result,
        input_grad,
        gains[0],
        gains[1],
        query_sum,
        key_sum,
        value_sum,
        forget_sum,
        output_sum,
        gate_sum,
        to_columns(up_rows),
        down_sum,
    )


def solution(mesh):
    placed = (
        P("dp", None),
        P("dp", None),
        P(),
        P(),
        P(None, "head"),
        P(None, "head"),
        P(None, "head"),
        P(None, "head"),
        P(None, "head"),
        P("dp", "head"),
        P("dp", "head"),
        P("dp", "head"),
        P("dp", None),
    )
    return jax.shard_map(
        partial(on_device, grid=Grid(mesh.shape["dp"])),
        mesh=mesh,
        in_specs=placed,
        out_specs=(P("dp", None), P("dp", None), P("dp"), P("dp")) + (P("dp", "head"),) * 8,
        check_vma=False,
    )
```

```python
import math
from functools import partial
import jax
import jax.numpy as jnp
from jax import lax
from jax.experimental import pallas as pl
from jax.experimental.pallas import tpu as pltpu
from jax.sharding import PartitionSpec as P

DK = 512
DV = 512
M = 64
B = 16
f32 = jnp.float32
bf16 = jnp.bfloat16


def nn(a, b):
    return jnp.dot(a.astype(bf16), b.astype(bf16), preferred_element_type=f32)


def nt(a, b):
    return lax.dot_general(
        a.astype(bf16), b.astype(bf16), (((1,), (1,)), ((), ())), preferred_element_type=f32
    )


def tn(a, b):
    return lax.dot_general(
        a.astype(bf16), b.astype(bf16), (((0,), (0,)), ((), ())), preferred_element_type=f32
    )


def nn3(a, b):
    ah, bh = a.astype(bf16), b.astype(bf16)
    al, bl = (a - ah.astype(f32)).astype(bf16), (b - bh.astype(f32)).astype(bf16)
    return nn(ah, bh) + (nn(al, bh) + nn(ah, bl))


def shift_up(x, s):
    return pltpu.roll(x, x.shape[0] - s, 0)


def shift_down(x, s):
    return pltpu.roll(x, s, 0)


def segment_at(pos, starts):
    seg = jnp.zeros(pos.shape, jnp.int32)
    for s in starts:
        seg = seg + (pos >= s).astype(jnp.int32)
    return seg


def same_document(t, j, starts):
    ok = None
    for s in starts:
        same = (t >= s) == (j >= s)
        ok = same if ok is None else ok & same
    return ok


def level_sizes(length):
    sizes = []
    h = length // 2
    while h >= B:
        sizes.append(h)
        h //= 2
    return sizes


def row_pick(x, size, row):
    n, lanes = x.shape
    x3 = x.reshape(n // size, size, lanes)
    return jnp.broadcast_to(x3[:, row : row + 1, :], x3.shape).reshape(n, lanes)


class Common:
    def __init__(self, la, starts):
        length, lanes = la.shape
        self.length, self.lanes = length, lanes
        rows = lax.broadcasted_iota(jnp.int32, (length, lanes), 0)
        self.rows = rows
        self.lane_head = lax.broadcasted_iota(jnp.int32, (length, lanes), 1) // M
        c = la
        s = 1
        while s < length:
            c = c + jnp.where(rows >= s, shift_down(c, s), 0.0)
            s *= 2
        self.c = c
        self.alpha = jnp.exp(la)
        self.om = 1.0 - self.alpha
        self.levels = level_sizes(length)
        self.x = []
        for h in self.levels:
            mid = row_pick(c, 2 * h, h - 1)
            self.x.append(jnp.exp(-jnp.abs(c - mid)))
        t = lax.broadcasted_iota(jnp.int32, (length, length), 0)
        j = lax.broadcasted_iota(jnp.int32, (length, length), 1)
        same = same_document(t, j, starts)
        self.masks = [
            same & ((t // (2 * h)) == (j // (2 * h))) & ((t & h) != 0) & ((j & h) == 0)
            for h in self.levels
        ]
        tc = lax.broadcasted_iota(jnp.int32, (length, B), 0)
        off = lax.broadcasted_iota(jnp.int32, (length, B), 1)
        jc = (tc - tc % B) + off
        self.mask_c = same_document(tc, jc, starts) & (jc <= tc)

    def by_head(self, parts):
        out = parts[0]
        for i in range(1, len(parts)):
            out = jnp.where(self.lane_head == i, parts[i], out)
        return out

    def only(self, x, i):
        return jnp.where(self.lane_head == i, x, 0.0)

    def decay_from(self, jj):
        return jnp.exp(jnp.minimum(self.c - row_pick(self.c, B, jj), 0.0))

    def om_at(self, jj):
        return row_pick(self.om, B, jj)


def blocks(x):
    return x.reshape(x.shape[0] // B, B, x.shape[1])


def block_nt(a, b):
    r = lax.dot_general(
        blocks(a.astype(bf16)),
        blocks(b.astype(bf16)),
        (((2,), (2,)), ((0,), (0,))),
        preferred_element_type=f32,
    )
    return r.reshape(a.shape[0], B)


def block_nn(a, b):
    r = lax.dot_general(
        blocks(a.astype(bf16)),
        blocks(b.astype(bf16)),
        (((2,), (1,)), ((0,), (0,))),
        preferred_element_type=f32,
    )
    return r.reshape(a.shape[0], b.shape[1])


def block_tn(a, b):
    at = jnp.swapaxes(blocks(a), 1, 2).astype(bf16)
    r = lax.dot_general(
        at, blocks(b.astype(bf16)), (((2,), (1,)), ((0,), (0,))), preferred_element_type=f32
    )
    return r.reshape(a.shape[0], b.shape[1])


def collect(lanes, heads):
    r = lax.broadcasted_iota(jnp.int32, (B * lanes, heads * 128), 0)
    col = lax.broadcasted_iota(jnp.int32, (B * lanes, heads * 128), 1)
    jj, head = r // lanes, (r % lanes) // M
    return jnp.where(col == head * 128 + jj, 1.0, 0.0).astype(bf16)


def wide(x, jj):
    return jnp.broadcast_to(x[:, jj : jj + 1], (x.shape[0], 128))


def forward_math(q, k, v, la, starts):
    heads = q.shape[1] // DK
    scale = 1.0 / math.sqrt(DK)
    cm = Common(la, starts)
    qs = [q[:, i * DK : (i + 1) * DK] for i in range(heads)]
    ks = [k[:, i * DK : (i + 1) * DK] for i in range(heads)]
    vs = [v[:, i * DV : (i + 1) * DV] for i in range(heads)]
    aff = [nt(qs[i], ks[i]) * scale for i in range(heads)]
    affc = [jnp.where(cm.mask_c, block_nt(qs[i], ks[i]) * scale, 0.0) for i in range(heads)]
    s = jnp.zeros_like(la)
    parts = []
    for x, mask in zip(cm.x, cm.masks):
        g = x * cm.om
        part = x * cm.by_head([nn3(jnp.where(mask, aff[i], 0.0), g) for i in range(heads)])
        parts.append(part)
        s = s + part
    for jj in range(B):
        s = s + cm.by_head([wide(affc[i], jj) for i in range(heads)]) * (
            cm.decay_from(jj) * cm.om_at(jj)
        )
    top = cm.by_head(
        [
            jnp.max(jnp.where(cm.lane_head == i, s, -jnp.inf), axis=1, keepdims=True)
            for i in range(heads)
        ]
    )
    e = jnp.exp(s - top)
    total = cm.by_head([jnp.sum(cm.only(e, i), axis=1, keepdims=True) for i in range(heads)])
    p = e / total
    mix = [jnp.zeros((cm.length, cm.length), f32) for _ in range(heads)]
    for x, mask in zip(cm.x, cm.masks):
        g = x * cm.om
        px = p * x
        for i in range(heads):
            mix[i] = mix[i] + jnp.where(mask, nt(cm.only(px, i), g), 0.0)
    mix = [m.astype(bf16) for m in mix]
    pieces = [(p * (cm.decay_from(jj) * cm.om_at(jj))).astype(bf16) for jj in range(B)]
    mixc = nn(jnp.concatenate(pieces, axis=1), collect(cm.lanes, heads))
    mixc = [
        jnp.where(cm.mask_c, mixc[:, i * 128 : i * 128 + B], 0.0) for i in range(heads)
    ]
    outs = [nn(mix[i], vs[i]) + block_nn(mixc[i], vs[i]) for i in range(heads)]
    return outs, p, parts, mix, mixc


def backward_math(q, k, v, la, starts, p, parts, mix, mixc, dout):
    heads = q.shape[1] // DK
    scale = 1.0 / math.sqrt(DK)
    cm = Common(la, starts)
    qs = [q[:, i * DK : (i + 1) * DK] for i in range(heads)]
    ks = [k[:, i * DK : (i + 1) * DK] for i in range(heads)]
    vs = [v[:, i * DV : (i + 1) * DV] for i in range(heads)]
    dos = [dout[:, i * DV : (i + 1) * DV].astype(bf16) for i in range(heads)]
    aff = [nt(qs[i], ks[i]) * scale for i in range(heads)]
    affc = [jnp.where(cm.mask_c, block_nt(qs[i], ks[i]) * scale, 0.0) for i in range(heads)]
    dmix = [nt(dos[i], vs[i]) for i in range(heads)]
    dmixc = [jnp.where(cm.mask_c, block_nt(dos[i], vs[i]), 0.0) for i in range(heads)]
    dp = jnp.zeros_like(la)
    dparts = []
    for x, mask in zip(cm.x, cm.masks):
        g = x * cm.om
        part = x * cm.by_head([nn3(jnp.where(mask, dmix[i], 0.0), g) for i in range(heads)])
        dparts.append(part)
        dp = dp + part
    for jj in range(B):
        dp = dp + cm.by_head([wide(dmixc[i], jj) for i in range(heads)]) * (
            cm.decay_from(jj) * cm.om_at(jj)
        )
    pdp = p * dp
    inner = cm.by_head([jnp.sum(cm.only(pdp, i), axis=1, keepdims=True) for i in range(heads)])
    ds = pdp - p * inner
    daff = [jnp.zeros((cm.length, cm.length), f32) for _ in range(heads)]
    dla = jnp.zeros_like(la)
    reach = jnp.zeros_like(la)
    for n, h in enumerate(cm.levels):
        x, mask = cm.x[n], cm.masks[n]
        g = x * cm.om
        dsx, px = ds * x, p * x
        both = jnp.concatenate([dsx, px], axis=0).astype(bf16)
        cols = []
        for i in range(heads):
            daff[i] = daff[i] + jnp.where(mask, nt(cm.only(dsx, i), g), 0.0)
            left = jnp.concatenate(
                [jnp.where(mask, aff[i], 0.0), jnp.where(mask, dmix[i], 0.0)], axis=0
            )
            cols.append(tn(left, both))
        r = x * cm.by_head(cols)
        reach = reach + r
        right = (cm.rows & h) != 0
        flow = jnp.where(right, ds * parts[n] + p * dparts[n], cm.om * r)
        s = 1
        while s < h:
            flow = flow + jnp.where((cm.rows & (h - 1)) < h - s, shift_up(flow, s), 0.0)
            s *= 2
        dla = dla + jnp.where(right, flow, row_pick(flow, h, 0) - flow)
    flow = jnp.zeros_like(la)
    near = jnp.zeros_like(la)
    pieces = []
    for jj in range(B):
        w = cm.decay_from(jj)
        omj = cm.om_at(jj)
        aj = cm.by_head([wide(affc[i], jj) for i in range(heads)])
        dj = cm.by_head([wide(dmixc[i], jj) for i in range(heads)])
        pieces.append((ds * (w * omj)).astype(bf16))
        z = w * (aj * ds + dj * p)
        flow = flow + omj * z
        z3 = blocks(z)
        tot = jnp.broadcast_to(jnp.sum(z3, axis=1, keepdims=True), z3.shape).reshape(z.shape)
        near = jnp.where((cm.rows & (B - 1)) == jj, tot, near)
    flow = flow - cm.om * near
    s = 1
    while s < B:
        flow = flow + jnp.where((cm.rows & (B - 1)) < B - s, shift_up(flow, s), 0.0)
        s *= 2
    dla = dla + flow - cm.alpha * (reach + near)
    daffc = nn(jnp.concatenate(pieces, axis=1), collect(cm.lanes, heads))
    daffc = [
        jnp.where(cm.mask_c, daffc[:, i * 128 : i * 128 + B], 0.0) for i in range(heads)
    ]
    dq, dk, dv = [], [], []
    for i in range(heads):
        da = daff[i].astype(bf16)
        dq.append((nn(da, ks[i]) + block_nn(daffc[i], ks[i])) * scale)
        dk.append((tn(da, qs[i]) + block_tn(daffc[i], qs[i])) * scale)
        dv.append(tn(mix[i], dos[i]) + block_tn(mixc[i], dos[i]))
    return dq, dk, dv, dla


def head_split(outs, ref, width):
    for i, x in enumerate(outs):
        ref[:, i * width : (i + 1) * width] = x.astype(ref.dtype)


def forward_kernel(starts_ref, q_ref, k_ref, v_ref, la_ref, o_ref, p_ref, parts_ref, mix_ref, mixc_ref):
    starts = [starts_ref[0, n] for n in range(starts_ref.shape[1])]
    outs, p, parts, mix, mixc = forward_math(
        q_ref[...], k_ref[...], v_ref[...], la_ref[...], starts
    )
    head_split(outs, o_ref, DV)
    p_ref[...] = p
    for n, x in enumerate(parts):
        parts_ref[n] = x
    for i in range(len(mix)):
        mix_ref[i] = mix[i]
        mixc_ref[i] = mixc[i].astype(bf16)


tau_inv = 0.125


def silu_slope(values):
    sigmoid_val = jax.nn.sigmoid(values)
    return sigmoid_val * (1.0 + values * (1.0 - sigmoid_val))


def through_silu(grads, z):
    width = grads[0].shape[1]
    return [g * silu_slope(z[:, i * width : (i + 1) * width]) for i, g in enumerate(grads)]


def through_gate(dla, zf):
    return dla * tau_inv * jax.nn.sigmoid(-zf)


INNER = 4


def share_columns(wide_parts, dzf, shares_ref):
    lanes = dzf.shape[1]
    size = lanes // INNER
    lane = lax.broadcasted_iota(jnp.int32, dzf.shape, 1)
    for n in range(INNER):
        at = 0
        for x in wide_parts:
            width = x.shape[1] // INNER
            shares_ref[n, :, at : at + width] = x[:, n * width : (n + 1) * width]
            at += width
        turned = pltpu.roll(dzf, (lanes - n * size) % lanes, 1) if n else dzf
        shares_ref[n, :, at : at + lanes] = jnp.where(lane < size, turned, 0.0).astype(bf16)


def backward_kernel(
    starts_ref, q_ref, k_ref, v_ref, la_ref, p_ref, parts_ref, mix_ref, mixc_ref, do_ref,
    zq_ref, zk_ref, zv_ref, zf_ref, dzq_ref, dzk_ref, dzv_ref, dzf_ref, shares_ref,
):
    starts = [starts_ref[0, n] for n in range(starts_ref.shape[1])]
    heads = mix_ref.shape[0]
    dq, dk, dv, dla = backward_math(
        q_ref[...],
        k_ref[...],
        v_ref[...],
        la_ref[...],
        starts,
        p_ref[...],
        [parts_ref[n] for n in range(parts_ref.shape[0])],
        [mix_ref[i] for i in range(heads)],
        [mixc_ref[i] for i in range(heads)],
        do_ref[...],
    )
    for grads, z_ref, dz_ref in ((dq, zq_ref, dzq_ref), (dk, zk_ref, dzk_ref), (dv, zv_ref, dzv_ref)):
        head_split(through_silu(grads, z_ref[...]), dz_ref, grads[0].shape[1])
    dzf = through_gate(dla, zf_ref[...])
    dzf_ref[...] = dzf.astype(bf16)
    share_columns([dzq_ref[...], dzk_ref[...], dzv_ref[...]], dzf, shares_ref)


SMEM = pl.BlockSpec(memory_space=pltpu.SMEM)
VMEM = pl.BlockSpec(memory_space=pltpu.VMEM)


def attend_forward(q, k, v, la, starts):
    length, lanes = la.shape
    heads = q.shape[1] // DK
    sds = jax.ShapeDtypeStruct
    return pl.pallas_call(
        forward_kernel,
        out_shape=(
            sds((length, heads * DV), bf16),
            sds((length, lanes), f32),
            sds((len(level_sizes(length)), length, lanes), f32),
            sds((heads, length, length), bf16),
            sds((heads, length, B), bf16),
        ),
        in_specs=[SMEM] + [VMEM] * 4,
        out_specs=(VMEM,) * 5,
        cost_estimate=pl.CostEstimate(
            flops=4 * 10**9, transcendentals=10**6, bytes_accessed=4 * 10**6
        ),
        name="slot_forward",
    )(starts, q, k, v, la)


def attend_backward(q, k, v, la, starts, saved, dout, pres):
    sds = jax.ShapeDtypeStruct
    return pl.pallas_call(
        backward_kernel,
        out_shape=(
            sds(q.shape, bf16),
            sds(k.shape, bf16),
            sds(v.shape, bf16),
            sds(la.shape, bf16),
            sds((INNER, q.shape[0], (2 * DK + DV) * (q.shape[1] // DK) // INNER + la.shape[1]), bf16),
        ),
        in_specs=[SMEM] + [VMEM] * 13,
        out_specs=(VMEM,) * 5,
        cost_estimate=pl.CostEstimate(
            flops=12 * 10**9, transcendentals=10**6, bytes_accessed=8 * 10**6
        ),
        name="slot_backward",
    )(starts, q, k, v, la, *saved, dout, *pres)


eps = 1e-06
LAP = (0, 1, 3, 2)


def rms_scale(values):
    return lax.rsqrt(jnp.mean(values * values, axis=-1, keepdims=True) + eps)


def norm_back(values, scale, gain, upstream):
    gain_grad = jnp.sum(upstream * values * scale, axis=0, keepdims=True)
    weighted = upstream * gain
    input_grad = scale * weighted - values * (scale * scale * scale) * jnp.mean(
        weighted * values, axis=-1, keepdims=True
    )
    return (gain_grad, input_grad)


class Grid:
    def __init__(self, dp):
        self.dp = dp
        self.outer = dp // INNER
        self.laps = [[o * INNER + i for i in LAP] for o in range(self.outer)]
        self.rows = [[o * INNER + i for i in range(INNER)] for o in range(self.outer)]
        self.cols = [[o * INNER + i for o in range(self.outer)] for i in range(INNER)]
        self.gathered = [o * INNER + i for i in LAP for o in range(self.outer)]
        self.natural = inverse(self.gathered)
        self.up = [(d, d + INNER) for d in range(dp - INNER)]
        self.down = [(d + INNER, d) for d in range(dp - INNER)]


def reorder(x, order):
    size = x.shape[-1] // len(order)
    return jnp.concatenate([x[..., b * size : (b + 1) * size] for b in order], axis=-1)


def inverse(order):
    back = [0] * len(order)
    for n, b in enumerate(order):
        back[b] = n
    return back


def swap(x):
    return lax.ppermute(x, "head", [(0, 1), (1, 0)])


def half_of(x, which):
    size = x.shape[0] // 2
    return lax.dynamic_slice_in_dim(x, which * size, size, 0)


def join(mine, other, core):
    size = mine.shape[0]
    out = jnp.zeros((2 * size,) + mine.shape[1:], mine.dtype)
    out = lax.dynamic_update_slice_in_dim(out, mine, core * size, 0)
    return lax.dynamic_update_slice_in_dim(out, other, (1 - core) * size, 0)


def on_rows(kernel, name, core, halves, wholes, outs):
    rows = halves[0].shape[0] // 2
    specs = [pl.BlockSpec((rows, x.shape[1]), lambda i, c: (c[0], 0)) for x in halves]
    specs += [pl.BlockSpec(x.shape, lambda i, c: (0, 0)) for x in wholes]
    return pl.pallas_call(
        kernel,
        out_shape=outs,
        grid_spec=pltpu.PrefetchScalarGridSpec(
            num_scalar_prefetch=1,
            grid=(1,),
            in_specs=specs,
            out_specs=[pl.BlockSpec(x.shape, lambda i, c: (0, 0)) for x in outs],
        ),
        name=name,
    )(core.reshape(1), *halves, *wholes)


def aligned(grid, width):
    return (width // grid.dp) % 128 == 0


def put_in_order(x, order, grid, inside):
    return reorder(x, order) if aligned(grid, x.shape[1]) == inside else x


def cotangent_rows(out_grad, core, grid):
    rows, width = out_grad.shape

    def kernel(core_ref, cot_ref, out_ref):
        out_ref[...] = put_in_order(cot_ref[...], grid.gathered, grid, True)

    outs = [jax.ShapeDtypeStruct((rows // 2, width), bf16)]
    (x,) = on_rows(kernel, "cotangent_rows", core, [out_grad], [], outs)
    return put_in_order(x, grid.gathered, grid, False)


def second_norm(block_in, mine, other, gain, core, grid):
    rows, width = mine.shape

    def kernel(core_ref, in_ref, mine_ref, other_ref, gain_ref, hidden_ref, normed_ref):
        hidden = in_ref[...].astype(f32) + (mine_ref[...] + other_ref[...])
        hidden_ref[...] = hidden
        normed = (hidden * rms_scale(hidden) * gain_ref[...]).astype(bf16)
        normed_ref[...] = put_in_order(normed, grid.gathered, grid, True)

    outs = [jax.ShapeDtypeStruct((rows, width), f32), jax.ShapeDtypeStruct((rows, width), bf16)]
    hidden, normed = on_rows(
        kernel, "second_norm", core, [block_in], [mine, other, gain[None]], outs
    )
    return hidden, put_in_order(normed, grid.gathered, grid, False)


def second_norm_back(out_grad, hidden, gain, parts, core, grid):
    rows, width = hidden.shape
    parts = [put_in_order(x, grid.natural, grid, False) for x in parts]

    def kernel(core_ref, cot_ref, hidden_ref, gain_ref, *refs):
        upstream = sum(x[...].astype(f32) for x in refs[: len(parts)])
        upstream = put_in_order(upstream, grid.natural, grid, True)
        grad_ref, low_ref, gain_grad_ref = refs[len(parts) :]
        hidden = hidden_ref[...]
        gain_grad, grad = norm_back(hidden, rms_scale(hidden), gain_ref[...], upstream)
        grad = grad + cot_ref[...].astype(f32)
        grad_ref[...] = grad
        low_ref[...] = grad.astype(bf16)
        gain_grad_ref[...] = gain_grad

    sds = jax.ShapeDtypeStruct
    outs = [sds((rows, width), f32), sds((rows, width), bf16), sds((1, width), f32)]
    return on_rows(
        kernel, "second_norm_back", core, [out_grad], [hidden, gain[None], *parts], outs
    )


def first_norm_back(block_in, grad, gain, mine, other, core):
    rows, width = grad.shape

    def kernel(core_ref, in_ref, grad_ref, gain_ref, mine_ref, other_ref, out_ref, gain_grad_ref):
        inputs = in_ref[...].astype(f32)
        upstream = mine_ref[...] + other_ref[...]
        gain_grad, out = norm_back(inputs, rms_scale(inputs), gain_ref[...], upstream)
        out_ref[...] = out + grad_ref[...]
        gain_grad_ref[...] = gain_grad

    sds = jax.ShapeDtypeStruct
    outs = [sds((rows, width), f32), sds((1, width), f32)]
    return on_rows(
        kernel, "first_norm_back", core, [block_in], [grad, gain[None], mine, other], outs
    )


def block_result(block_in, hidden, parts, core, grid):
    rows, width = hidden.shape
    parts = [put_in_order(x, grid.natural, grid, False) for x in parts]

    def kernel(core_ref, in_ref, hidden_ref, *refs):
        out = sum(x[...].astype(f32) for x in refs[: len(parts)])
        out = put_in_order(out, grid.natural, grid, True)
        refs[-1][...] = (hidden_ref[...] + out).astype(bf16)

    outs = [jax.ShapeDtypeStruct((rows, width), bf16)]
    (x,) = on_rows(kernel, "block_result", core, [block_in], [hidden, *parts], outs)
    return x


def exchange(x, split, concat, groups):
    return lax.all_to_all(x, "dp", split, concat, tiled=True, axis_index_groups=groups)


def tie(*values):
    return lax.optimization_barrier(values)


def gather_along(x, grid, place, beside=()):
    n = grid.outer
    above = below = x
    from_below, from_above, done = [], [], []
    other = swap(x)
    for k in range(n - 1):
        below = lax.ppermute(below, "dp", grid.up)
        above = lax.ppermute(above, "dp", grid.down)
        extra = beside[k] if k < len(beside) else ()
        extra = extra(*done) if callable(extra) else extra
        below, above, *extra = tie(below, above, *extra)
        from_below.append((below, swap(below)))
        from_above.append((above, swap(above)))
        done += extra
    blocks = [x]
    for c in range(2):
        blocks += [other] if c else []
        for k in range(1, n):
            blocks.append(
                jnp.where(place + k < n, from_above[k - 1][c], from_below[n - 1 - k][c])
            )
    return jnp.concatenate(blocks, axis=0), done


def by_core(x):
    size = x.shape[0] // 2
    return x[:size], x[size:].astype(bf16)


def add_other_core(mine, other, grid):
    n = grid.outer
    other = tie(*[swap(y) for y in jnp.split(other, n)])
    return [x + y.astype(f32) for x, y in zip(jnp.split(mine, n), other)]


def scatter_along(own, grid, beside=()):
    n = grid.outer
    up = down = None
    done = []
    for k in range(n - 1):
        up = own[n - 1 - k] if up is None else own[n - 1 - k] + up.astype(f32)
        down = own[1 + k] if down is None else own[1 + k] + down.astype(f32)
        up = lax.ppermute(up.astype(bf16), "dp", grid.up)
        down = lax.ppermute(down.astype(bf16), "dp", grid.down)
        extra = beside[k] if k < len(beside) else ()
        extra = extra(*done) if callable(extra) else extra
        up, down, *extra = tie(up, down, *extra)
        done += extra
    return (own[0], up, down), done


def plane_gather(x, grid, inner):
    out = jnp.zeros((INNER,) + x.shape, x.dtype)
    for k in range(INNER):
        y = x
        if k:
            y = lax.ppermute(x, "dp", [(d, d ^ k) for d in range(grid.dp)])
        out = lax.dynamic_update_slice_in_dim(out, y[None], inner ^ k, 0)
    return out


def on_device(
    block_in,
    out_grad,
    attn_gain,
    mlp_gain,
    w_query,
    w_key,
    w_value,
    w_forget,
    w_output,
    w_gate,
    w_up,
    w_down,
    doc_starts,
    grid,
):
    core = lax.axis_index("head")
    place = lax.axis_index("dp") // INNER
    inner = lax.axis_index("dp") % INNER

    def columns(w):
        return exchange(w, 1, 0, grid.cols)

    def gather_rows(w):
        return lax.all_gather(w, "dp", axis=0, tiled=True, axis_index_groups=grid.laps)

    def column_pairs(a, b):
        rows = a.shape[0]
        both = [w.reshape(rows, grid.outer, -1) for w in (a, b)]
        both = columns(jnp.concatenate(both, axis=2).reshape(rows, -1))
        return jnp.split(both, 2, axis=1)

    gate_piece, up_piece = column_pairs(w_gate, w_up)
    inputs_f = block_in.astype(f32)
    normed = (inputs_f * rms_scale(inputs_f) * attn_gain).astype(bf16)
    query_pre = nn(normed, w_query)
    key_pre = nn(normed, w_key)
    value_pre = nn(normed, w_value)
    forget_pre = nn(normed, w_forget)
    query = jax.nn.silu(query_pre).astype(bf16)
    key = jax.nn.silu(key_pre).astype(bf16)
    value = jax.nn.silu(value_pre).astype(bf16)
    log_keep = jax.nn.log_sigmoid(forget_pre) * tau_inv
    mixed, *saved = attend_forward(query, key, value, log_keep, doc_starts)
    normed_own = lax.all_gather(
        half_of(normed, core), "dp", axis=0, tiled=True, axis_index_groups=grid.rows
    )
    branch_other = swap(nt(half_of(mixed, 1 - core), w_output))
    branch_mine = nt(half_of(mixed, core), w_output)
    branch_mine, gate_piece, up_piece, down_later, normed_own = tie(
        branch_mine, gate_piece, up_piece, w_down, normed_own
    )
    full_gate, full_up = gather_rows(gate_piece), gather_rows(up_piece)
    down_piece = columns(down_later)

    hidden, normed_two = second_norm(block_in, branch_mine, branch_other, mlp_gain, core, grid)
    def plane_tokens(own):
        own = own.reshape(INNER, 1, -1, own.shape[-1])
        out = jnp.zeros((INNER, 2) + own.shape[2:], own.dtype)
        out = lax.dynamic_update_slice_in_dim(out, own, core, 1)
        out = lax.dynamic_update_slice_in_dim(out, swap(own), 1 - core, 1)
        return out.reshape(-1, own.shape[-1])

    def plane_columns(shares):
        return exchange(shares.reshape(-1, shares.shape[2]), 0, 0, grid.rows)

    def plane_product(left, right):
        return tn(left, right).astype(bf16)

    def plane_sum(g):
        return lax.psum_scatter(
            g, "dp", scatter_dimension=0, tiled=True, axis_index_groups=grid.cols
        )

    def from_plane(g):
        size = g.shape[1]
        return exchange(g, 0, 1, grid.rows).reshape(-1, INNER, size).astype(f32)

    cot_rows = cotangent_rows(out_grad, core, grid)
    tokens, (cot_rows, down_piece, normed_plane, full_gate) = gather_along(
        normed_two,
        grid,
        place,
        ((cot_rows, down_piece), (plane_tokens(normed_own),), (full_gate,)),
    )
    full_down = gather_rows(down_piece)
    def gated(gate, up):
        return (jax.nn.silu(gate) * up).astype(bf16)

    cot_all, (gate_act, full_up, up_act, full_down, out_mine, out_other) = gather_along(
        cot_rows,
        grid,
        place,
        (
            (nn(tokens, full_gate), full_up),
            lambda gate, w_up_all: (nn(tokens, w_up_all), full_down),
            lambda gate, _, up, w_down_all: by_core(nt(gated(gate, up), w_down_all)),
        ),
    )
    out_own = add_other_core(out_mine, out_other, grid)
    out_blocks = jnp.zeros((grid.outer,) + out_own[0].shape, bf16)
    for k, x in enumerate(out_own):
        at = (place + k) % grid.outer
        out_blocks = lax.dynamic_update_slice_in_dim(out_blocks, x.astype(bf16)[None], at, 0)
    out_blocks, cot_all = tie(out_blocks.reshape(-1, out_blocks.shape[2]), cot_all)
    out_sum = lax.psum_scatter(
        out_blocks, "dp", scatter_dimension=0, tiled=True, axis_index_groups=grid.cols
    )

    def scatter_rows(g):
        return lax.psum_scatter(
            g, "dp", scatter_dimension=0, tiled=True, axis_index_groups=grid.laps
        )

    def to_columns(g):
        return exchange(g, 0, 1, grid.cols).astype(f32)

    def to_columns_beside(g):
        n = grid.outer
        if n & (n - 1) or n > 4:
            return to_columns(g)
        blocks = g.reshape(n, -1, g.shape[1])
        out = jnp.zeros_like(blocks)
        for s in range(n):
            piece = lax.dynamic_slice_in_dim(blocks, place ^ s, 1, 0)
            if s:
                pairs = [(d, (d // INNER ^ s) * INNER + d % INNER) for d in range(grid.dp)]
                piece = lax.ppermute(piece, "dp", pairs)
            out = lax.dynamic_update_slice_in_dim(out, piece, place ^ s, 0)
        return jnp.swapaxes(out, 0, 1).reshape(blocks.shape[1], -1).astype(f32)

    inner_grad = nn(cot_all, full_down)
    gate_grad = (inner_grad * up_act * silu_slope(gate_act)).astype(bf16)
    up_grad = (inner_grad * jax.nn.silu(gate_act)).astype(bf16)
    inner_act = gated(gate_act, up_act)
    back_parts, (down_rows, out_sum, gate_rows, up_rows) = scatter_along(
        add_other_core(*by_core(nt(gate_grad, full_gate) + nt(up_grad, full_up)), grid),
        grid,
        (
            (tn(cot_all, inner_act).astype(bf16), out_sum),
            (tn(tokens, gate_grad).astype(bf16),),
            (tn(tokens, up_grad).astype(bf16),),
        ),
    )
    down_rows, gate_rows, up_rows = (scatter_rows(g) for g in (down_rows, gate_rows, up_rows))
    hidden_grad, low_half, mlp_gain_part = second_norm_back(
        out_grad, hidden, mlp_gain, back_parts, core, grid
    )
    branch_grad = join(low_half, swap(low_half), core)
    mixed_grad = nn(branch_grad, w_output).astype(bf16)
    mixed_grad, down_rows = tie(mixed_grad, down_rows)
    *pre_grads, shares = attend_backward(
        query, key, value, log_keep, doc_starts, saved, mixed_grad,
        (query_pre, key_pre, value_pre, forget_pre),
    )

    def normed_part(which):
        q, k, v, f = (half_of(g, which) for g in pre_grads)
        return nt(q, w_query) + nt(k, w_key) + nt(v, w_value) + nt(f, w_forget)

    columns_here, part_other, part_mine, down_sum, gate_sum = tie(
        plane_columns(shares),
        normed_part(1 - core),
        normed_part(core),
        to_columns_beside(down_rows),
        to_columns_beside(gate_rows),
    )
    pre_grad = plane_product(normed_plane, columns_here)
    input_grad, attn_gain_part = first_norm_back(
        block_in, hidden_grad, attn_gain, part_mine, swap(part_other), core
    )
    _, low_half, attn_gain_part, mixed = tie(pre_grad, low_half, attn_gain_part, mixed)
    mixed_plane = plane_columns(jnp.stack(jnp.split(mixed, INNER, axis=1)))
    low_plane = plane_tokens(plane_gather(low_half, grid, inner))
    gains = jnp.concatenate([attn_gain_part, mlp_gain_part], axis=0)
    gains = gains + swap(gains)
    gains = jnp.swapaxes(gains.reshape(2, grid.dp, -1), 0, 1)
    gains = jnp.sum(lax.all_to_all(gains, "dp", 0, 0, tiled=True), axis=0)
    output_grad, gains = tie(plane_product(low_plane, mixed_plane), gains)
    sums, output_grad = tie(plane_sum(pre_grad), output_grad)
    output_sum = plane_sum(output_grad)
    result = block_result(block_in, hidden, [out_sum], core, grid)
    result = join(result, swap(result), core)

    sums = from_plane(sums)
    output_sum = from_plane(output_sum).reshape(sums.shape[0], -1)
    ends = [0]
    for g in pre_grads:
        ends.append(ends[-1] + g.shape[1] // INNER)
    query_sum, key_sum, value_sum, forget_sum = (
        sums[:, :, a:b].reshape(sums.shape[0], -1) for a, b in zip(ends, ends[1:])
    )

    input_grad = join(input_grad, swap(input_grad), core)

    return (
        result,
        input_grad,
        gains[0],
        gains[1],
        query_sum,
        key_sum,
        value_sum,
        forget_sum,
        output_sum,
        gate_sum,
        to_columns(up_rows),
        down_sum,
    )


def solution(mesh):
    placed = (
        P("dp", None),
        P("dp", None),
        P(),
        P(),
        P(None, "head"),
        P(None, "head"),
        P(None, "head"),
        P(None, "head"),
        P(None, "head"),
        P("dp", "head"),
        P("dp", "head"),
        P("dp", "head"),
        P("dp", None),
    )
    return jax.shard_map(
        partial(on_device, grid=Grid(mesh.shape["dp"])),
        mesh=mesh,
        in_specs=placed,
        out_specs=(P("dp", None), P("dp", None), P("dp"), P("dp")) + (P("dp", "head"),) * 8,
        check_vma=False,
    )
```

```python
import math
from functools import partial
import jax
import jax.numpy as jnp
from jax import lax
from jax.experimental import pallas as pl
from jax.experimental.pallas import tpu as pltpu
from jax.sharding import PartitionSpec as P

DK = 512
DV = 512
M = 64
B = 16
f32 = jnp.float32
bf16 = jnp.bfloat16


def nn(a, b):
    return jnp.dot(a.astype(bf16), b.astype(bf16), preferred_element_type=f32)


def nt(a, b):
    return lax.dot_general(
        a.astype(bf16), b.astype(bf16), (((1,), (1,)), ((), ())), preferred_element_type=f32
    )


def tn(a, b):
    return lax.dot_general(
        a.astype(bf16), b.astype(bf16), (((0,), (0,)), ((), ())), preferred_element_type=f32
    )


def nn3(a, b):
    ah, bh = a.astype(bf16), b.astype(bf16)
    al, bl = (a - ah.astype(f32)).astype(bf16), (b - bh.astype(f32)).astype(bf16)
    return nn(ah, bh) + (nn(al, bh) + nn(ah, bl))


def shift_up(x, s):
    return pltpu.roll(x, x.shape[0] - s, 0)


def shift_down(x, s):
    return pltpu.roll(x, s, 0)


def segment_at(pos, starts):
    seg = jnp.zeros(pos.shape, jnp.int32)
    for s in starts:
        seg = seg + (pos >= s).astype(jnp.int32)
    return seg


def same_document(t, j, starts):
    ok = None
    for s in starts:
        same = (t >= s) == (j >= s)
        ok = same if ok is None else ok & same
    return ok


def level_sizes(length):
    sizes = []
    h = length // 2
    while h >= B:
        sizes.append(h)
        h //= 2
    return sizes


def row_pick(x, size, row):
    n, lanes = x.shape
    x3 = x.reshape(n // size, size, lanes)
    return jnp.broadcast_to(x3[:, row : row + 1, :], x3.shape).reshape(n, lanes)


class Common:
    def __init__(self, la, starts):
        length, lanes = la.shape
        self.length, self.lanes = length, lanes
        rows = lax.broadcasted_iota(jnp.int32, (length, lanes), 0)
        self.rows = rows
        self.lane_head = lax.broadcasted_iota(jnp.int32, (length, lanes), 1) // M
        c = la
        s = 1
        while s < length:
            c = c + jnp.where(rows >= s, shift_down(c, s), 0.0)
            s *= 2
        self.c = c
        self.alpha = jnp.exp(la)
        self.om = 1.0 - self.alpha
        self.levels = level_sizes(length)
        self.x = []
        for h in self.levels:
            mid = row_pick(c, 2 * h, h - 1)
            self.x.append(jnp.exp(-jnp.abs(c - mid)))
        t = lax.broadcasted_iota(jnp.int32, (length, length), 0)
        j = lax.broadcasted_iota(jnp.int32, (length, length), 1)
        same = same_document(t, j, starts)
        self.masks = [
            same & ((t // (2 * h)) == (j // (2 * h))) & ((t & h) != 0) & ((j & h) == 0)
            for h in self.levels
        ]
        tc = lax.broadcasted_iota(jnp.int32, (length, B), 0)
        off = lax.broadcasted_iota(jnp.int32, (length, B), 1)
        jc = (tc - tc % B) + off
        self.mask_c = same_document(tc, jc, starts) & (jc <= tc)

    def by_head(self, parts):
        out = parts[0]
        for i in range(1, len(parts)):
            out = jnp.where(self.lane_head == i, parts[i], out)
        return out

    def only(self, x, i):
        return jnp.where(self.lane_head == i, x, 0.0)

    def decay_from(self, jj):
        return jnp.exp(jnp.minimum(self.c - row_pick(self.c, B, jj), 0.0))

    def om_at(self, jj):
        return row_pick(self.om, B, jj)


def blocks(x):
    return x.reshape(x.shape[0] // B, B, x.shape[1])


def block_nt(a, b):
    r = lax.dot_general(
        blocks(a.astype(bf16)),
        blocks(b.astype(bf16)),
        (((2,), (2,)), ((0,), (0,))),
        preferred_element_type=f32,
    )
    return r.reshape(a.shape[0], B)


def block_nn(a, b):
    r = lax.dot_general(
        blocks(a.astype(bf16)),
        blocks(b.astype(bf16)),
        (((2,), (1,)), ((0,), (0,))),
        preferred_element_type=f32,
    )
    return r.reshape(a.shape[0], b.shape[1])


def block_tn(a, b):
    at = jnp.swapaxes(blocks(a), 1, 2).astype(bf16)
    r = lax.dot_general(
        at, blocks(b.astype(bf16)), (((2,), (1,)), ((0,), (0,))), preferred_element_type=f32
    )
    return r.reshape(a.shape[0], b.shape[1])


def collect(lanes, heads):
    r = lax.broadcasted_iota(jnp.int32, (B * lanes, heads * 128), 0)
    col = lax.broadcasted_iota(jnp.int32, (B * lanes, heads * 128), 1)
    jj, head = r // lanes, (r % lanes) // M
    return jnp.where(col == head * 128 + jj, 1.0, 0.0).astype(bf16)


def wide(x, jj):
    return jnp.broadcast_to(x[:, jj : jj + 1], (x.shape[0], 128))


def forward_math(q, k, v, la, starts):
    heads = q.shape[1] // DK
    scale = 1.0 / math.sqrt(DK)
    cm = Common(la, starts)
    qs = [q[:, i * DK : (i + 1) * DK] for i in range(heads)]
    ks = [k[:, i * DK : (i + 1) * DK] for i in range(heads)]
    vs = [v[:, i * DV : (i + 1) * DV] for i in range(heads)]
    aff = [nt(qs[i], ks[i]) * scale for i in range(heads)]
    affc = [jnp.where(cm.mask_c, block_nt(qs[i], ks[i]) * scale, 0.0) for i in range(heads)]
    s = jnp.zeros_like(la)
    parts = []
    for x, mask in zip(cm.x, cm.masks):
        g = x * cm.om
        part = x * cm.by_head([nn3(jnp.where(mask, aff[i], 0.0), g) for i in range(heads)])
        parts.append(part)
        s = s + part
    for jj in range(B):
        s = s + cm.by_head([wide(affc[i], jj) for i in range(heads)]) * (
            cm.decay_from(jj) * cm.om_at(jj)
        )
    top = cm.by_head(
        [
            jnp.max(jnp.where(cm.lane_head == i, s, -jnp.inf), axis=1, keepdims=True)
            for i in range(heads)
        ]
    )
    e = jnp.exp(s - top)
    total = cm.by_head([jnp.sum(cm.only(e, i), axis=1, keepdims=True) for i in range(heads)])
    p = e / total
    mix = [jnp.zeros((cm.length, cm.length), f32) for _ in range(heads)]
    for x, mask in zip(cm.x, cm.masks):
        g = x * cm.om
        px = p * x
        for i in range(heads):
            mix[i] = mix[i] + jnp.where(mask, nt(cm.only(px, i), g), 0.0)
    mix = [m.astype(bf16) for m in mix]
    pieces = [(p * (cm.decay_from(jj) * cm.om_at(jj))).astype(bf16) for jj in range(B)]
    mixc = nn(jnp.concatenate(pieces, axis=1), collect(cm.lanes, heads))
    mixc = [
        jnp.where(cm.mask_c, mixc[:, i * 128 : i * 128 + B], 0.0) for i in range(heads)
    ]
    outs = [nn(mix[i], vs[i]) + block_nn(mixc[i], vs[i]) for i in range(heads)]
    return outs, p, parts, mix, mixc


def backward_math(q, k, v, la, starts, p, parts, mix, mixc, dout):
    heads = q.shape[1] // DK
    scale = 1.0 / math.sqrt(DK)
    cm = Common(la, starts)
    qs = [q[:, i * DK : (i + 1) * DK] for i in range(heads)]
    ks = [k[:, i * DK : (i + 1) * DK] for i in range(heads)]
    vs = [v[:, i * DV : (i + 1) * DV] for i in range(heads)]
    dos = [dout[:, i * DV : (i + 1) * DV].astype(bf16) for i in range(heads)]
    aff = [nt(qs[i], ks[i]) * scale for i in range(heads)]
    affc = [jnp.where(cm.mask_c, block_nt(qs[i], ks[i]) * scale, 0.0) for i in range(heads)]
    dmix = [nt(dos[i], vs[i]) for i in range(heads)]
    dmixc = [jnp.where(cm.mask_c, block_nt(dos[i], vs[i]), 0.0) for i in range(heads)]
    dp = jnp.zeros_like(la)
    dparts = []
    for x, mask in zip(cm.x, cm.masks):
        g = x * cm.om
        part = x * cm.by_head([nn3(jnp.where(mask, dmix[i], 0.0), g) for i in range(heads)])
        dparts.append(part)
        dp = dp + part
    for jj in range(B):
        dp = dp + cm.by_head([wide(dmixc[i], jj) for i in range(heads)]) * (
            cm.decay_from(jj) * cm.om_at(jj)
        )
    pdp = p * dp
    inner = cm.by_head([jnp.sum(cm.only(pdp, i), axis=1, keepdims=True) for i in range(heads)])
    ds = pdp - p * inner
    daff = [jnp.zeros((cm.length, cm.length), f32) for _ in range(heads)]
    dla = jnp.zeros_like(la)
    reach = jnp.zeros_like(la)
    for n, h in enumerate(cm.levels):
        x, mask = cm.x[n], cm.masks[n]
        g = x * cm.om
        dsx, px = ds * x, p * x
        both = jnp.concatenate([dsx, px], axis=0).astype(bf16)
        cols = []
        for i in range(heads):
            daff[i] = daff[i] + jnp.where(mask, nt(cm.only(dsx, i), g), 0.0)
            left = jnp.concatenate(
                [jnp.where(mask, aff[i], 0.0), jnp.where(mask, dmix[i], 0.0)], axis=0
            )
            cols.append(tn(left, both))
        r = x * cm.by_head(cols)
        reach = reach + r
        right = (cm.rows & h) != 0
        flow = jnp.where(right, ds * parts[n] + p * dparts[n], cm.om * r)
        s = 1
        while s < h:
            flow = flow + jnp.where((cm.rows & (h - 1)) < h - s, shift_up(flow, s), 0.0)
            s *= 2
        dla = dla + jnp.where(right, flow, row_pick(flow, h, 0) - flow)
    flow = jnp.zeros_like(la)
    near = jnp.zeros_like(la)
    pieces = []
    for jj in range(B):
        w = cm.decay_from(jj)
        omj = cm.om_at(jj)
        aj = cm.by_head([wide(affc[i], jj) for i in range(heads)])
        dj = cm.by_head([wide(dmixc[i], jj) for i in range(heads)])
        pieces.append((ds * (w * omj)).astype(bf16))
        z = w * (aj * ds + dj * p)
        flow = flow + omj * z
        z3 = blocks(z)
        tot = jnp.broadcast_to(jnp.sum(z3, axis=1, keepdims=True), z3.shape).reshape(z.shape)
        near = jnp.where((cm.rows & (B - 1)) == jj, tot, near)
    flow = flow - cm.om * near
    s = 1
    while s < B:
        flow = flow + jnp.where((cm.rows & (B - 1)) < B - s, shift_up(flow, s), 0.0)
        s *= 2
    dla = dla + flow - cm.alpha * (reach + near)
    daffc = nn(jnp.concatenate(pieces, axis=1), collect(cm.lanes, heads))
    daffc = [
        jnp.where(cm.mask_c, daffc[:, i * 128 : i * 128 + B], 0.0) for i in range(heads)
    ]
    dq, dk, dv = [], [], []
    for i in range(heads):
        da = daff[i].astype(bf16)
        dq.append((nn(da, ks[i]) + block_nn(daffc[i], ks[i])) * scale)
        dk.append((tn(da, qs[i]) + block_tn(daffc[i], qs[i])) * scale)
        dv.append(tn(mix[i], dos[i]) + block_tn(mixc[i], dos[i]))
    return dq, dk, dv, dla


def head_split(outs, ref, width):
    for i, x in enumerate(outs):
        ref[:, i * width : (i + 1) * width] = x.astype(ref.dtype)


def forward_kernel(starts_ref, q_ref, k_ref, v_ref, la_ref, o_ref, p_ref, parts_ref, mix_ref, mixc_ref):
    starts = [starts_ref[0, n] for n in range(starts_ref.shape[1])]
    outs, p, parts, mix, mixc = forward_math(
        q_ref[...], k_ref[...], v_ref[...], la_ref[...], starts
    )
    head_split(outs, o_ref, DV)
    p_ref[...] = p
    for n, x in enumerate(parts):
        parts_ref[n] = x
    for i in range(len(mix)):
        mix_ref[i] = mix[i]
        mixc_ref[i] = mixc[i].astype(bf16)


tau_inv = 0.125


def silu_slope(values):
    sigmoid_val = jax.nn.sigmoid(values)
    return sigmoid_val * (1.0 + values * (1.0 - sigmoid_val))


def through_silu(grads, z):
    width = grads[0].shape[1]
    return [g * silu_slope(z[:, i * width : (i + 1) * width]) for i, g in enumerate(grads)]


def through_gate(dla, zf):
    return dla * tau_inv * jax.nn.sigmoid(-zf)


INNER = 4


def share_columns(wide_parts, dzf, shares_ref):
    lanes = dzf.shape[1]
    size = lanes // INNER
    lane = lax.broadcasted_iota(jnp.int32, dzf.shape, 1)
    for n in range(INNER):
        at = 0
        for x in wide_parts:
            width = x.shape[1] // INNER
            shares_ref[n, :, at : at + width] = x[:, n * width : (n + 1) * width]
            at += width
        turned = pltpu.roll(dzf, (lanes - n * size) % lanes, 1) if n else dzf
        shares_ref[n, :, at : at + lanes] = jnp.where(lane < size, turned, 0.0).astype(bf16)


def backward_kernel(
    starts_ref, q_ref, k_ref, v_ref, la_ref, p_ref, parts_ref, mix_ref, mixc_ref, do_ref,
    zq_ref, zk_ref, zv_ref, zf_ref, dzq_ref, dzk_ref, dzv_ref, dzf_ref, shares_ref,
):
    starts = [starts_ref[0, n] for n in range(starts_ref.shape[1])]
    heads = mix_ref.shape[0]
    dq, dk, dv, dla = backward_math(
        q_ref[...],
        k_ref[...],
        v_ref[...],
        la_ref[...],
        starts,
        p_ref[...],
        [parts_ref[n] for n in range(parts_ref.shape[0])],
        [mix_ref[i] for i in range(heads)],
        [mixc_ref[i] for i in range(heads)],
        do_ref[...],
    )
    for grads, z_ref, dz_ref in ((dq, zq_ref, dzq_ref), (dk, zk_ref, dzk_ref), (dv, zv_ref, dzv_ref)):
        head_split(through_silu(grads, z_ref[...]), dz_ref, grads[0].shape[1])
    dzf = through_gate(dla, zf_ref[...])
    dzf_ref[...] = dzf.astype(bf16)
    share_columns([dzq_ref[...], dzk_ref[...], dzv_ref[...]], dzf, shares_ref)


SMEM = pl.BlockSpec(memory_space=pltpu.SMEM)
VMEM = pl.BlockSpec(memory_space=pltpu.VMEM)


def attend_forward(q, k, v, la, starts):
    length, lanes = la.shape
    heads = q.shape[1] // DK
    sds = jax.ShapeDtypeStruct
    return pl.pallas_call(
        forward_kernel,
        out_shape=(
            sds((length, heads * DV), bf16),
            sds((length, lanes), f32),
            sds((len(level_sizes(length)), length, lanes), f32),
            sds((heads, length, length), bf16),
            sds((heads, length, B), bf16),
        ),
        in_specs=[SMEM] + [VMEM] * 4,
        out_specs=(VMEM,) * 5,
        cost_estimate=pl.CostEstimate(
            flops=4 * 10**9, transcendentals=10**6, bytes_accessed=4 * 10**6
        ),
        name="slot_forward",
    )(starts, q, k, v, la)


def attend_backward(q, k, v, la, starts, saved, dout, pres):
    sds = jax.ShapeDtypeStruct
    return pl.pallas_call(
        backward_kernel,
        out_shape=(
            sds(q.shape, bf16),
            sds(k.shape, bf16),
            sds(v.shape, bf16),
            sds(la.shape, bf16),
            sds((INNER, q.shape[0], (2 * DK + DV) * (q.shape[1] // DK) // INNER + la.shape[1]), bf16),
        ),
        in_specs=[SMEM] + [VMEM] * 13,
        out_specs=(VMEM,) * 5,
        cost_estimate=pl.CostEstimate(
            flops=12 * 10**9, transcendentals=10**6, bytes_accessed=8 * 10**6
        ),
        name="slot_backward",
    )(starts, q, k, v, la, *saved, dout, *pres)


eps = 1e-06
LAP = (0, 1, 3, 2)


def rms_scale(values):
    return lax.rsqrt(jnp.mean(values * values, axis=-1, keepdims=True) + eps)


def norm_back(values, scale, gain, upstream):
    gain_grad = jnp.sum(upstream * values * scale, axis=0, keepdims=True)
    weighted = upstream * gain
    input_grad = scale * weighted - values * (scale * scale * scale) * jnp.mean(
        weighted * values, axis=-1, keepdims=True
    )
    return (gain_grad, input_grad)


class Grid:
    def __init__(self, dp):
        self.dp = dp
        self.outer = dp // INNER
        self.laps = [[o * INNER + i for i in LAP] for o in range(self.outer)]
        self.rows = [[o * INNER + i for i in range(INNER)] for o in range(self.outer)]
        self.cols = [[o * INNER + i for o in range(self.outer)] for i in range(INNER)]
        self.gathered = [o * INNER + i for i in LAP for o in range(self.outer)]
        self.natural = inverse(self.gathered)
        self.up = [(d, d + INNER) for d in range(dp - INNER)]
        self.down = [(d + INNER, d) for d in range(dp - INNER)]


def reorder(x, order):
    size = x.shape[-1] // len(order)
    return jnp.concatenate([x[..., b * size : (b + 1) * size] for b in order], axis=-1)


def inverse(order):
    back = [0] * len(order)
    for n, b in enumerate(order):
        back[b] = n
    return back


def swap(x):
    return lax.ppermute(x, "head", [(0, 1), (1, 0)])


def half_of(x, which):
    size = x.shape[0] // 2
    return lax.dynamic_slice_in_dim(x, which * size, size, 0)


def join(mine, other, core):
    size = mine.shape[0]
    out = jnp.zeros((2 * size,) + mine.shape[1:], mine.dtype)
    out = lax.dynamic_update_slice_in_dim(out, mine, core * size, 0)
    return lax.dynamic_update_slice_in_dim(out, other, (1 - core) * size, 0)


def on_rows(kernel, name, core, halves, wholes, outs):
    rows = halves[0].shape[0] // 2
    specs = [pl.BlockSpec((rows, x.shape[1]), lambda i, c: (c[0], 0)) for x in halves]
    specs += [pl.BlockSpec(x.shape, lambda i, c: (0, 0)) for x in wholes]
    return pl.pallas_call(
        kernel,
        out_shape=outs,
        grid_spec=pltpu.PrefetchScalarGridSpec(
            num_scalar_prefetch=1,
            grid=(1,),
            in_specs=specs,
            out_specs=[pl.BlockSpec(x.shape, lambda i, c: (0, 0)) for x in outs],
        ),
        name=name,
    )(core.reshape(1), *halves, *wholes)


def aligned(grid, width):
    return (width // grid.dp) % 128 == 0


def put_in_order(x, order, grid, inside):
    return reorder(x, order) if aligned(grid, x.shape[1]) == inside else x


def cotangent_rows(out_grad, core, grid):
    rows, width = out_grad.shape

    def kernel(core_ref, cot_ref, out_ref):
        out_ref[...] = put_in_order(cot_ref[...], grid.gathered, grid, True)

    outs = [jax.ShapeDtypeStruct((rows // 2, width), bf16)]
    (x,) = on_rows(kernel, "cotangent_rows", core, [out_grad], [], outs)
    return put_in_order(x, grid.gathered, grid, False)


def second_norm(block_in, mine, other, gain, core, grid):
    rows, width = mine.shape

    def kernel(core_ref, in_ref, mine_ref, other_ref, gain_ref, hidden_ref, normed_ref):
        hidden = in_ref[...].astype(f32) + (mine_ref[...] + other_ref[...])
        hidden_ref[...] = hidden
        normed = (hidden * rms_scale(hidden) * gain_ref[...]).astype(bf16)
        normed_ref[...] = put_in_order(normed, grid.gathered, grid, True)

    outs = [jax.ShapeDtypeStruct((rows, width), f32), jax.ShapeDtypeStruct((rows, width), bf16)]
    hidden, normed = on_rows(
        kernel, "second_norm", core, [block_in], [mine, other, gain[None]], outs
    )
    return hidden, put_in_order(normed, grid.gathered, grid, False)


def second_norm_back(out_grad, hidden, gain, parts, core, grid):
    rows, width = hidden.shape
    parts = [put_in_order(x, grid.natural, grid, False) for x in parts]

    def kernel(core_ref, cot_ref, hidden_ref, gain_ref, *refs):
        upstream = sum(x[...].astype(f32) for x in refs[: len(parts)])
        upstream = put_in_order(upstream, grid.natural, grid, True)
        grad_ref, low_ref, gain_grad_ref = refs[len(parts) :]
        hidden = hidden_ref[...]
        gain_grad, grad = norm_back(hidden, rms_scale(hidden), gain_ref[...], upstream)
        grad = grad + cot_ref[...].astype(f32)
        grad_ref[...] = grad
        low_ref[...] = grad.astype(bf16)
        gain_grad_ref[...] = gain_grad

    sds = jax.ShapeDtypeStruct
    outs = [sds((rows, width), f32), sds((rows, width), bf16), sds((1, width), f32)]
    return on_rows(
        kernel, "second_norm_back", core, [out_grad], [hidden, gain[None], *parts], outs
    )


def first_norm_back(block_in, grad, gain, mine, other, core):
    rows, width = grad.shape

    def kernel(core_ref, in_ref, grad_ref, gain_ref, mine_ref, other_ref, out_ref, gain_grad_ref):
        inputs = in_ref[...].astype(f32)
        upstream = mine_ref[...] + other_ref[...]
        gain_grad, out = norm_back(inputs, rms_scale(inputs), gain_ref[...], upstream)
        out_ref[...] = out + grad_ref[...]
        gain_grad_ref[...] = gain_grad

    sds = jax.ShapeDtypeStruct
    outs = [sds((rows, width), f32), sds((1, width), f32)]
    return on_rows(
        kernel, "first_norm_back", core, [block_in], [grad, gain[None], mine, other], outs
    )


def block_result(block_in, hidden, parts, core, grid):
    rows, width = hidden.shape
    parts = [put_in_order(x, grid.natural, grid, False) for x in parts]

    def kernel(core_ref, in_ref, hidden_ref, *refs):
        out = sum(x[...].astype(f32) for x in refs[: len(parts)])
        out = put_in_order(out, grid.natural, grid, True)
        refs[-1][...] = (hidden_ref[...] + out).astype(bf16)

    outs = [jax.ShapeDtypeStruct((rows, width), bf16)]
    (x,) = on_rows(kernel, "block_result", core, [block_in], [hidden, *parts], outs)
    return x


def exchange(x, split, concat, groups):
    return lax.all_to_all(x, "dp", split, concat, tiled=True, axis_index_groups=groups)


def tie(*values):
    return lax.optimization_barrier(values)


def gather_along(x, grid, place, beside=()):
    n = grid.outer
    above = below = x
    from_below, from_above, done = [], [], []
    other = swap(x)
    for k in range(n - 1):
        below = lax.ppermute(below, "dp", grid.up)
        above = lax.ppermute(above, "dp", grid.down)
        extra = beside[k] if k < len(beside) else ()
        extra = extra(*done) if callable(extra) else extra
        below, above, *extra = tie(below, above, *extra)
        from_below.append((below, swap(below)))
        from_above.append((above, swap(above)))
        done += extra
    blocks = [x]
    for c in range(2):
        blocks += [other] if c else []
        for k in range(1, n):
            blocks.append(
                jnp.where(place + k < n, from_above[k - 1][c], from_below[n - 1 - k][c])
            )
    return jnp.concatenate(blocks, axis=0), done


def by_core(x):
    size = x.shape[0] // 2
    return x[:size], x[size:].astype(bf16)


def add_other_core(mine, other, grid):
    n = grid.outer
    other = tie(*[swap(y) for y in jnp.split(other, n)])
    return [x + y.astype(f32) for x, y in zip(jnp.split(mine, n), other)]


def scatter_along(own, grid, beside=()):
    n = grid.outer
    up = down = None
    done = []
    for k in range(n - 1):
        up = own[n - 1 - k] if up is None else own[n - 1 - k] + up.astype(f32)
        down = own[1 + k] if down is None else own[1 + k] + down.astype(f32)
        up = lax.ppermute(up.astype(bf16), "dp", grid.up)
        down = lax.ppermute(down.astype(bf16), "dp", grid.down)
        extra = beside[k] if k < len(beside) else ()
        extra = extra(*done) if callable(extra) else extra
        up, down, *extra = tie(up, down, *extra)
        done += extra
    return (own[0], up, down), done


def plane_gather(x, grid, inner):
    out = jnp.zeros((INNER,) + x.shape, x.dtype)
    for k in range(INNER):
        y = x
        if k:
            y = lax.ppermute(x, "dp", [(d, d ^ k) for d in range(grid.dp)])
        out = lax.dynamic_update_slice_in_dim(out, y[None], inner ^ k, 0)
    return out


def on_device(
    block_in,
    out_grad,
    attn_gain,
    mlp_gain,
    w_query,
    w_key,
    w_value,
    w_forget,
    w_output,
    w_gate,
    w_up,
    w_down,
    doc_starts,
    grid,
):
    core = lax.axis_index("head")
    place = lax.axis_index("dp") // INNER
    inner = lax.axis_index("dp") % INNER

    def columns(w):
        return exchange(w, 1, 0, grid.cols)

    def gather_rows(w):
        return lax.all_gather(w, "dp", axis=0, tiled=True, axis_index_groups=grid.laps)

    def column_pairs(a, b):
        rows = a.shape[0]
        both = [w.reshape(rows, grid.outer, -1) for w in (a, b)]
        both = columns(jnp.concatenate(both, axis=2).reshape(rows, -1))
        return jnp.split(both, 2, axis=1)

    gate_piece, up_piece = column_pairs(w_gate, w_up)
    inputs_f = block_in.astype(f32)
    normed = (inputs_f * rms_scale(inputs_f) * attn_gain).astype(bf16)
    query_pre = nn(normed, w_query)
    key_pre = nn(normed, w_key)
    value_pre = nn(normed, w_value)
    forget_pre = nn(normed, w_forget)
    query = jax.nn.silu(query_pre).astype(bf16)
    key = jax.nn.silu(key_pre).astype(bf16)
    value = jax.nn.silu(value_pre).astype(bf16)
    log_keep = jax.nn.log_sigmoid(forget_pre) * tau_inv
    mixed, *saved = attend_forward(query, key, value, log_keep, doc_starts)
    normed_own = lax.all_gather(
        half_of(normed, core), "dp", axis=0, tiled=True, axis_index_groups=grid.rows
    )
    branch_other = swap(nt(half_of(mixed, 1 - core), w_output))
    branch_mine = nt(half_of(mixed, core), w_output)
    branch_mine, gate_piece, up_piece, down_later, normed_own = tie(
        branch_mine, gate_piece, up_piece, w_down, normed_own
    )
    full_gate, full_up = gather_rows(gate_piece), gather_rows(up_piece)
    down_piece = columns(down_later)

    hidden, normed_two = second_norm(block_in, branch_mine, branch_other, mlp_gain, core, grid)
    def plane_tokens(own):
        own = own.reshape(INNER, 1, -1, own.shape[-1])
        out = jnp.zeros((INNER, 2) + own.shape[2:], own.dtype)
        out = lax.dynamic_update_slice_in_dim(out, own, core, 1)
        out = lax.dynamic_update_slice_in_dim(out, swap(own), 1 - core, 1)
        return out.reshape(-1, own.shape[-1])

    def plane_columns(shares):
        return exchange(shares.reshape(-1, shares.shape[2]), 0, 0, grid.rows)

    def plane_product(left, right):
        return tn(left, right).astype(bf16)

    def plane_sum(g):
        return lax.psum_scatter(
            g, "dp", scatter_dimension=0, tiled=True, axis_index_groups=grid.cols
        )

    def from_plane(g):
        size = g.shape[1]
        return exchange(g, 0, 1, grid.rows).reshape(-1, INNER, size).astype(f32)

    cot_rows = cotangent_rows(out_grad, core, grid)
    tokens, (cot_rows, down_piece, normed_plane, full_gate) = gather_along(
        normed_two,
        grid,
        place,
        ((cot_rows, down_piece), (plane_tokens(normed_own),), (full_gate,)),
    )
    full_down = gather_rows(down_piece)
    def gated(gate, up):
        return (jax.nn.silu(gate) * up).astype(bf16)

    cot_all, (gate_act, full_up, up_act, full_down, out_mine, out_other) = gather_along(
        cot_rows,
        grid,
        place,
        (
            (nn(tokens, full_gate), full_up),
            lambda gate, w_up_all: (nn(tokens, w_up_all), full_down),
            lambda gate, _, up, w_down_all: by_core(nt(gated(gate, up), w_down_all)),
        ),
    )
    out_own = add_other_core(out_mine, out_other, grid)
    out_blocks = jnp.zeros((grid.outer,) + out_own[0].shape, bf16)
    for k, x in enumerate(out_own):
        at = (place + k) % grid.outer
        out_blocks = lax.dynamic_update_slice_in_dim(out_blocks, x.astype(bf16)[None], at, 0)
    out_blocks, cot_all = tie(out_blocks.reshape(-1, out_blocks.shape[2]), cot_all)
    out_sum = lax.psum_scatter(
        out_blocks, "dp", scatter_dimension=0, tiled=True, axis_index_groups=grid.cols
    )

    def scatter_rows(g):
        return lax.psum_scatter(
            g, "dp", scatter_dimension=0, tiled=True, axis_index_groups=grid.laps
        )

    def to_columns(g):
        return exchange(g, 0, 1, grid.cols).astype(f32)

    def to_columns_beside(g):
        n = grid.outer
        if n & (n - 1) or n > 4:
            return to_columns(g)
        blocks = g.reshape(n, -1, g.shape[1])
        out = jnp.zeros_like(blocks)
        for s in range(n):
            piece = lax.dynamic_slice_in_dim(blocks, place ^ s, 1, 0)
            if s:
                pairs = [(d, (d // INNER ^ s) * INNER + d % INNER) for d in range(grid.dp)]
                piece = lax.ppermute(piece, "dp", pairs)
            out = lax.dynamic_update_slice_in_dim(out, piece, place ^ s, 0)
        return jnp.swapaxes(out, 0, 1).reshape(blocks.shape[1], -1).astype(f32)

    inner_grad = nn(cot_all, full_down)
    gate_grad = (inner_grad * up_act * silu_slope(gate_act)).astype(bf16)
    up_grad = (inner_grad * jax.nn.silu(gate_act)).astype(bf16)
    inner_act = gated(gate_act, up_act)
    back_parts, (down_rows, out_sum, gate_rows, up_rows) = scatter_along(
        add_other_core(*by_core(nt(gate_grad, full_gate) + nt(up_grad, full_up)), grid),
        grid,
        (
            (tn(cot_all, inner_act).astype(bf16), out_sum),
            (tn(tokens, gate_grad).astype(bf16),),
            (tn(tokens, up_grad).astype(bf16),),
        ),
    )
    down_rows, gate_rows, up_rows = (scatter_rows(g) for g in (down_rows, gate_rows, up_rows))
    hidden_grad, low_half, mlp_gain_part = second_norm_back(
        out_grad, hidden, mlp_gain, back_parts, core, grid
    )
    branch_grad = join(low_half, swap(low_half), core)
    mixed_grad = nn(branch_grad, w_output).astype(bf16)
    mixed_grad, down_rows = tie(mixed_grad, down_rows)
    *pre_grads, shares = attend_backward(
        query, key, value, log_keep, doc_starts, saved, mixed_grad,
        (query_pre, key_pre, value_pre, forget_pre),
    )

    def normed_part(which):
        q, k, v, f = (half_of(g, which) for g in pre_grads)
        return nt(q, w_query) + nt(k, w_key) + nt(v, w_value) + nt(f, w_forget)

    columns_here, part_other, part_mine, down_sum, gate_sum = tie(
        plane_columns(shares),
        normed_part(1 - core),
        normed_part(core),
        to_columns_beside(down_rows),
        to_columns_beside(gate_rows),
    )
    pre_grad = plane_product(normed_plane, columns_here)
    input_grad, attn_gain_part = first_norm_back(
        block_in, hidden_grad, attn_gain, part_mine, swap(part_other), core
    )
    _, low_half, attn_gain_part, mixed, up_rows = tie(
        pre_grad, low_half, attn_gain_part, mixed, up_rows
    )
    mixed_plane = plane_columns(jnp.stack(jnp.split(mixed, INNER, axis=1)))
    low_plane = plane_tokens(plane_gather(low_half, grid, inner))
    gains = jnp.concatenate([attn_gain_part, mlp_gain_part], axis=0)
    gains = gains + swap(gains)
    gains = jnp.swapaxes(gains.reshape(2, grid.dp, -1), 0, 1)
    gains = jnp.sum(lax.all_to_all(gains, "dp", 0, 0, tiled=True), axis=0)
    output_grad, gains, up_sum = tie(
        plane_product(low_plane, mixed_plane), gains, to_columns_beside(up_rows)
    )
    sums, output_grad = tie(plane_sum(pre_grad), output_grad)
    output_sum = plane_sum(output_grad)
    result = block_result(block_in, hidden, [out_sum], core, grid)
    result = join(result, swap(result), core)

    sums = from_plane(sums)
    output_sum = from_plane(output_sum).reshape(sums.shape[0], -1)
    ends = [0]
    for g in pre_grads:
        ends.append(ends[-1] + g.shape[1] // INNER)
    query_sum, key_sum, value_sum, forget_sum = (
        sums[:, :, a:b].reshape(sums.shape[0], -1) for a, b in zip(ends, ends[1:])
    )

    input_grad = join(input_grad, swap(input_grad), core)

    return (
        result,
        input_grad,
        gains[0],
        gains[1],
        query_sum,
        key_sum,
        value_sum,
        forget_sum,
        output_sum,
        gate_sum,
        up_sum,
        down_sum,
    )


def solution(mesh):
    placed = (
        P("dp", None),
        P("dp", None),
        P(),
        P(),
        P(None, "head"),
        P(None, "head"),
        P(None, "head"),
        P(None, "head"),
        P(None, "head"),
        P("dp", "head"),
        P("dp", "head"),
        P("dp", "head"),
        P("dp", None),
    )
    return jax.shard_map(
        partial(on_device, grid=Grid(mesh.shape["dp"])),
        mesh=mesh,
        in_specs=placed,
        out_specs=(P("dp", None), P("dp", None), P("dp"), P("dp")) + (P("dp", "head"),) * 8,
        check_vma=False,
    )
```
